32 devices in a mesh: fsdp: 8 (over z, x), tp: 4 (over y, core).
Axes of the slice: x: 2, y: 2, z: 4, core: 2. Of those that a mesh axis runs over, the one named last changes fastest.
Arguments:
- inputs: float32 [16384, 768], P(('fsdp', 'tp')), may hold values from -6 to 6
- cotangent: float32 [16384, 768], P(('fsdp', 'tp')), may hold values from -6 to 6
- lengths: int32 [8, 4], P('fsdp'), may hold values from 1 to 768, as said below
- routes: int32 [16384, 2], P('fsdp'), may hold values from 0 to 11, all different within a row
- drop_order: int32 [16384, 2], P('fsdp'), may hold values from 0 to 4095, as said below
- prior_logits: float32 [16384, 12], P('fsdp'), may hold values from -6 to 6
- attn_gain: float32 [768], replicated, may hold values from 0.5 to 1.5
- w_query: bfloat16 [768, 768], P('fsdp', 'tp'), may hold values from -0.21875 to 0.21875
- w_key: bfloat16 [768, 768], P('fsdp', 'tp'), may hold values from -0.21875 to 0.21875
- w_value: bfloat16 [768, 768], P('fsdp', 'tp'), may hold values from -0.21875 to 0.21875
- w_out: bfloat16 [768, 768], P('tp', 'fsdp'), may hold values from -3.5 to 3.5
- moe_gain: float32 [768], replicated, may hold values from 0.5 to 1.5
- w_router: float32 [768, 12], replicated, may hold values from -0.21875 to 0.21875
- w_prior: float32 [12, 12], replicated, may hold values from -1.75 to 1.75
- w_const: float32 [2, 768, 2], replicated, may hold values from -0.21875 to 0.21875
- const_vector: float32 [2, 768], replicated, may hold values from -6 to 6
- w_gate: bfloat16 [8, 768, 2048], P(None, 'fsdp', 'tp'), may hold values from -0.21875 to 0.21875
- w_up: bfloat16 [8, 768, 2048], P(None, 'fsdp', 'tp'), may hold values from -0.21875 to 0.21875
- w_down: bfloat16 [8, 2048, 768], P(None, 'tp', 'fsdp'), may hold values from -2 to 2
Outputs:
- output: float32 [16384, 768], P(('fsdp', 'tp'))
- grad_inputs: float32 [16384, 768], P(('fsdp', 'tp'))
- grad_prior: float32 [16384, 12], P(('fsdp', 'tp'))
- grad_attn_gain: float32 [768], replicated
- grad_w_query: float32 [768, 768], P('fsdp', 'tp')
- grad_w_key: float32 [768, 768], P('fsdp', 'tp')
- grad_w_value: float32 [768, 768], P('fsdp', 'tp')
- grad_w_out: float32 [768, 768], P('tp', 'fsdp')
- grad_moe_gain: float32 [768], replicated
- grad_w_router: float32 [768, 12], replicated
- grad_w_prior: float32 [12, 12], replicated
- grad_w_const: float32 [2, 768, 2], replicated
- grad_const_vector: float32 [2, 768], replicated
- grad_w_gate: float32 [8, 768, 2048], P(None, 'fsdp', 'tp')
- grad_w_up: float32 [8, 768, 2048], P(None, 'fsdp', 'tp')
- grad_w_down: float32 [8, 2048, 768], P(None, 'tp', 'fsdp')
The draws below stay inside these ranges and needn't reach their ends.
Inputs may be any that keep to these rules, and one draw needn't show every extreme that they name: In each row the first 3 entries are the group's sequence lengths in order and the last counts padding tokens at the group's end; each row sums to 2048. Every sequence has 512 tokens or more, one sequence of each row has exactly 768, and the padding is 1 or more. `routes`: each token names two different experts: 0 to 7 feed-forward, 8 zero, 9 copy, 10 and 11 constant. `drop_order`: within each group the 4096 pairs carry each rank once.
All inputs are finite; a program needn't handle non-finite values.
Results may differ from the reference program's by a relative error of at most 0.015.
Values may be sent and summed in bfloat16 or wider, within the bound.
No kernel may reach another device: no remote copies, remote signals or barrier semaphores. Data moves between devices by JAX's collectives and lax.ppermute only.
A program may use at most 256 MiB of HBM per device.

```python
import jax
import jax.numpy as jnp
from jax import lax

D = 768
HEADS = 12
HEAD = 64
FF = 2048
EXPERTS = 8
ZERO_EXPERTS = 4
SEQS = 3
ROWS_GROUP = 2048
TOKENS = 16384
MAXLEN = 768


def draw_drop_order(key, part):
    groups = TOKENS // ROWS_GROUP
    group_keys = jax.random.split(key, groups)
    ranked = jax.vmap(lambda item: jax.random.permutation(item, 2 * ROWS_GROUP))(group_keys)
    return ranked.reshape(TOKENS, 2).astype(jnp.int32)


def draw_lengths(key, part):
    groups = TOKENS // ROWS_GROUP
    key_lengths = jax.random.fold_in(key, 11)
    key_longest = jax.random.fold_in(key, 23)
    others = jax.random.randint(key_lengths, (groups, SEQS), ROWS_GROUP // 4, 5 * ROWS_GROUP // 16).astype(jnp.int32)
    longest = jax.random.randint(key_longest, (groups,), 0, SEQS).astype(jnp.int32)
    marks = jnp.arange(SEQS, dtype=jnp.int32)[None, :] == longest[:, None]
    sequence_lengths = jnp.where(marks, MAXLEN, others).astype(jnp.int32)
    padding = (ROWS_GROUP - jnp.sum(sequence_lengths, axis=1, keepdims=True)).astype(jnp.int32)
    return jnp.concatenate([sequence_lengths, padding], axis=1).astype(jnp.int32)


def levels(stream_key, dims, shards, low, high):
    def one(dim, parts):
        steps = jax.random.uniform(jax.random.fold_in(jax.random.fold_in(stream_key, 6), dim), (parts,), jnp.float32, low / len(shards), high / len(shards))
        return jnp.repeat(jnp.exp(steps), dims[dim] // parts).reshape((-1,) + (1,) * (len(dims) - dim - 1))

    factor_of = one(*shards[0])
    for cut in shards[1:]:
        factor_of = factor_of * one(*cut)
    return factor_of


def distinct(key, rows, number_of, top, lift):
    sequence = jax.random.permutation(jax.random.fold_in(key, 1), number_of)
    favour = sequence
    for power in range(3):
        favour = favour * favour // number_of
    favour = favour * lift // number_of
    lots = jax.random.randint(jax.random.fold_in(key, 2), (rows, number_of), 0, 4096) + favour
    fixed_rows = jax.random.permutation(jax.random.fold_in(key, 3), rows)[jnp.arange(number_of) % rows]
    lots = jnp.where(jnp.arange(rows)[:, None] == fixed_rows[None, :], 1 << 14, lots)
    score = lots * number_of + jnp.arange(number_of)
    return lax.top_k(score.astype(jnp.int32), top)[1].astype(jnp.int32)


def noise(own_key, shape, width, bound, cuts=(), kind=jnp.bfloat16):
    array = jax.random.normal(own_key, shape, jnp.float32) * width
    if len(cuts) > 0:
        array = levels(own_key, shape, cuts, -0.22, 0.18) * array
    return jnp.clip(array, min=-bound, max=bound).astype(kind)


def setup_inputs(seed: int = 0) -> dict:
    splits = jax.random.split(jax.random.key(seed), 20)
    inputs = noise(splits[0], (TOKENS, D), 1.0, 6.0, ((0, 32),), jnp.float32)
    cotangent = noise(splits[1], (TOKENS, D), 1.0, 6.0, ((0, 32),), jnp.float32)
    lengths = draw_lengths(jax.random.fold_in(splits[19], 71), 0)
    routes = distinct(splits[3], TOKENS, EXPERTS + ZERO_EXPERTS, 2, 1365)
    drop_order = draw_drop_order(jax.random.fold_in(splits[19], 71), 0)
    prior_logits = noise(splits[5], (TOKENS, EXPERTS + ZERO_EXPERTS), 1.0, 6.0, ((0, 8),), jnp.float32)
    attn_gain = jnp.clip(1.0 + 0.1 * jax.random.normal(splits[6], (D,), jnp.float32), 0.5, 1.5)
    w_query = noise(splits[7], (D, D), D ** -0.5, 0.21875, ((0, 8), (1, 4)))
    w_key = noise(splits[8], (D, D), D ** -0.5, 0.21875, ((0, 8), (1, 4)))
    w_value = noise(splits[9], (D, D), D ** -0.5, 0.21875, ((0, 8), (1, 4)))
    w_out = noise(splits[10], (D, D), (max(D // 256, 1)) ** -0.5, 3.5, ((0, 4), (1, 8)))
    moe_gain = jnp.clip(1.0 + 0.1 * jax.random.normal(splits[11], (D,), jnp.float32), 0.5, 1.5)
    w_router = noise(splits[12], (D, EXPERTS + ZERO_EXPERTS), D ** -0.5, 0.21875, (), jnp.float32)
    w_prior = noise(splits[13], (EXPERTS + ZERO_EXPERTS, EXPERTS + ZERO_EXPERTS), (EXPERTS + ZERO_EXPERTS) ** -0.5, 1.75, (), jnp.float32)
    w_const = noise(splits[14], (2, D, 2), D ** -0.5, 0.21875, (), jnp.float32)
    const_vector = noise(splits[15], (2, D), 1.0, 6.0, (), jnp.float32)
    w_gate = noise(splits[16], (EXPERTS, D, FF), D ** -0.5, 0.21875, ((1, 8), (2, 4)))
    w_up = noise(splits[17], (EXPERTS, D, FF), D ** -0.5, 0.21875, ((1, 8), (2, 4)))
    w_down = noise(splits[18], (EXPERTS, FF, D), (max(FF // 256, 1)) ** -0.5, 2.0, ((1, 4), (2, 8)))
    return {"inputs": inputs, "cotangent": cotangent, "lengths": lengths, "routes": routes, "drop_order": drop_order, "prior_logits": prior_logits, "attn_gain": attn_gain, "w_query": w_query, "w_key": w_key, "w_value": w_value, "w_out": w_out, "moe_gain": moe_gain, "w_router": w_router, "w_prior": w_prior, "w_const": w_const, "const_vector": const_vector, "w_gate": w_gate, "w_up": w_up, "w_down": w_down}


EPSILON = 1e-06
PRECISE = lax.Precision.HIGHEST

@jax.custom_vjp
def low(v):
    return lax.optimization_barrier(v.astype(jnp.bfloat16)).astype(jnp.float32)

@jax.custom_vjp
def low_back(v):
    return v

def low_keep(v):
    return (low(v), None)

def low_pass(kept, grad):
    return (grad,)

def back_keep(v):
    return (v, None)

def back_low(kept, grad):
    return (low(grad),)
low.defvjp(low_keep, low_pass)
low_back.defvjp(back_keep, back_low)

def rms_norm(values, gain):
    return values * lax.rsqrt(lax.optimization_barrier(jnp.mean(values * values, axis=-1, keepdims=True)) + EPSILON) * gain

def segments_of(lengths_row, group):
    boundary = jnp.cumsum(lengths_row).astype(jnp.int32)
    places = jnp.arange(group, dtype=jnp.int32)
    return lax.optimization_barrier(jnp.sum((places[:, None] >= boundary[None, :]).astype(jnp.int32), axis=1)).astype(jnp.int32)

def routing(routes, drop_order, valid, capacity, experts):
    group = routes.shape[0]
    live = (routes < experts) & valid[:, None]
    target = jnp.where(live, routes, experts).astype(jnp.int32)
    flat_order = drop_order.reshape(-1).astype(jnp.int32)
    by_rank = jnp.zeros((2 * group,), jnp.int32).at[flat_order].set(target.reshape(-1))
    onehot = (by_rank[:, None] == jnp.arange(experts, dtype=jnp.int32)[None, :]).astype(jnp.int32)
    before = lax.optimization_barrier(jnp.sum((jnp.cumsum(onehot, axis=0).astype(jnp.int32) - onehot) * onehot, axis=1)).astype(jnp.int32)
    placed = before[flat_order].reshape(group, 2)
    kept = live & (placed < capacity)
    slot_ids = jnp.where(kept, routes * capacity + placed, experts * capacity).astype(jnp.int32)
    token_ids = jnp.broadcast_to(jnp.arange(group, dtype=jnp.int32)[:, None], (group, 2))
    slot_token = jnp.zeros((experts * capacity + 1,), jnp.int32).at[slot_ids.reshape(-1)].set(token_ids.reshape(-1))[:-1]
    used = jnp.zeros((experts * capacity + 1,), jnp.int32).at[slot_ids.reshape(-1)].set(1)[:-1]
    return (kept, slot_ids, slot_token, used)

def group_forward(inputs, lengths_row, routes, drop_order, prior_rows, params):
    attn_gain, w_query, w_key, w_value, w_out, moe_gain, w_router, w_prior, w_const, const_vector, w_gate, w_up, w_down = params
    group = inputs.shape[0]
    block = min(512, group)
    capacity = 3 * group // 16
    segment = segments_of(lengths_row, group)
    valid = segment < SEQS
    normed_one = low(rms_norm(inputs, attn_gain))

    def heads_of(weight):
        return low_back(low(jnp.dot(normed_one, weight, precision=PRECISE))).reshape(group, HEADS, HEAD)
    queries = heads_of(w_query)
    keys = heads_of(w_key)
    values = heads_of(w_value)
    columns = jnp.arange(group, dtype=jnp.int32)

    def attend(first_row):
        query_rows = lax.dynamic_slice_in_dim(queries, first_row, block)
        segment_rows = lax.dynamic_slice_in_dim(segment, first_row, block)
        places = first_row + jnp.arange(block, dtype=jnp.int32)
        allowed = (segment_rows[:, None] == segment[None, :]) & (columns[None, :] <= places[:, None])
        scores = low_back(jnp.einsum('qhd,khd->hqk', query_rows, keys, precision=PRECISE)) * 0.125
        scores = jnp.where(allowed[None], scores, -1e+30)
        weights = jnp.exp(scores - lax.optimization_barrier(jnp.max(scores, axis=-1, keepdims=True)))
        probs = weights / lax.optimization_barrier(jnp.sum(weights, axis=-1, keepdims=True))
        return jnp.einsum('hqk,khd->qhd', low(probs), values, precision=PRECISE)
    starts = jnp.arange(group // block, dtype=jnp.int32) * block
    mixed = lax.map(jax.checkpoint(attend), starts).reshape(group, D)
    mixed = low_back(low(mixed))
    hidden = inputs + low_back(jnp.dot(mixed, w_out, precision=PRECISE))
    normed_two = rms_norm(hidden, moe_gain)
    rounded_two = low(normed_two)
    logits = jnp.dot(rounded_two, w_router, precision=PRECISE) + jnp.dot(prior_rows, w_prior, precision=PRECISE)
    router = jax.nn.softmax(logits, axis=-1)
    picked = (routes[:, :, None] == jnp.arange(EXPERTS + ZERO_EXPERTS, dtype=jnp.int32)[None, None, :]).astype(jnp.float32)
    chosen = lax.optimization_barrier(jnp.sum(router[:, None, :] * picked, axis=-1))
    kept, slot_ids, slot_token, used = routing(routes, drop_order, valid, capacity, EXPERTS)
    dispatched = (jnp.take(rounded_two, slot_token, axis=0) * used[:, None].astype(jnp.float32)).reshape(EXPERTS, capacity, D)
    gate_pre = low_back(jnp.einsum('ecd,edf->ecf', dispatched, w_gate, precision=PRECISE))
    up_pre = low_back(jnp.einsum('ecd,edf->ecf', dispatched, w_up, precision=PRECISE))
    activated = low(jax.nn.silu(gate_pre) * up_pre)
    expert_out = low_back(jnp.einsum('ecf,efd->ecd', activated, w_down, precision=PRECISE)).reshape(EXPERTS * capacity, D)
    safe_slots = jnp.where(kept, slot_ids, 0).astype(jnp.int32)
    feed_terms = jnp.take(expert_out, safe_slots.reshape(-1), axis=0).reshape(group, 2, D) * kept[..., None].astype(jnp.float32)
    mix_one = jax.nn.softmax(jnp.dot(normed_two, w_const[0], precision=PRECISE), axis=-1)
    mix_two = jax.nn.softmax(jnp.dot(normed_two, w_const[1], precision=PRECISE), axis=-1)
    constant_one = mix_one[:, :1] * normed_two + mix_one[:, 1:] * const_vector[0]
    constant_two = mix_two[:, :1] * normed_two + mix_two[:, 1:] * const_vector[1]
    is_copy = (routes == EXPERTS + 1).astype(jnp.float32)[..., None]
    is_first = (routes == EXPERTS + 2).astype(jnp.float32)[..., None]
    is_second = (routes == EXPERTS + 3).astype(jnp.float32)[..., None]
    terms = feed_terms + is_copy * normed_two[:, None, :] + is_first * constant_one[:, None, :] + is_second * constant_two[:, None, :]
    expert_sum = lax.optimization_barrier(jnp.sum(chosen[..., None] * terms, axis=1))
    return valid[:, None].astype(jnp.float32) * (hidden + expert_sum)

def reference(inputs, cotangent, lengths, routes, drop_order, prior_logits, attn_gain, w_query, w_key, w_value, w_out, moe_gain, w_router, w_prior, w_const, const_vector, w_gate, w_up, w_down):
    groups = lengths.shape[0]
    group = inputs.shape[0] // groups
    params = tuple((item.astype(jnp.float32) for item in (attn_gain, w_query, w_key, w_value, w_out, moe_gain, w_router, w_prior, w_const, const_vector, w_gate, w_up, w_down)))

    def forward(layer_in, prior_in, weights):

        def one_group(carry, items):
            rows_in, lengths_row, routes_rows, order_rows, prior_rows = items
            return (carry, jax.checkpoint(group_forward)(rows_in, lengths_row, routes_rows, order_rows, prior_rows, weights))
        _, results = lax.scan(one_group, jnp.zeros((), jnp.float32), (layer_in.reshape(groups, group, D), lengths, routes.reshape(groups, group, 2), drop_order.reshape(groups, group, 2), prior_in.reshape(groups, group, EXPERTS + ZERO_EXPERTS)))
        return results.reshape(groups * group, D)
    output, pull = jax.vjp(forward, inputs, prior_logits, params)
    grad_inputs, grad_prior, grads = pull(cotangent)
    return (output, grad_inputs, grad_prior, grads[0], grads[1], grads[2], grads[3], grads[4], grads[5], grads[6], grads[7], grads[8], grads[9], grads[10], grads[11], grads[12])
```

```python
import functools

import jax
import jax.numpy as jnp
from jax import lax
from jax.experimental import pallas as pl
from jax.experimental.pallas import tpu as pltpu
from jax.sharding import Mesh
from jax.sharding import PartitionSpec as P

HEAD = 64
MAXLEN = 768
LOW = 4
EPSILON = 1e-06
PRECISE = lax.Precision.HIGHEST
NEGATIVE = -1e30
F32 = jnp.float32
BF16 = jnp.bfloat16


def rms_norm(values, gain):
    return values * lax.rsqrt(jnp.mean(values * values, axis=-1, keepdims=True) + EPSILON) * gain


def swap(value, axis):
    return lax.ppermute(value, axis, [(0, 1), (1, 0)])


def gather_pieces(value):
    other = swap(value, "y")
    return [value, swap(value, "c"), other, swap(other, "c")]


def natural(pieces, index):
    ordered = []
    for j in range(4):
        item = pieces[j]
        for t in range(1, 4):
            item = jnp.where(index == t, pieces[j ^ t], item)
        ordered.append(item)
    return jnp.stack(ordered)


def scatter_sum(blocks):
    sent = swap(jnp.stack([blocks[1], blocks[3]]).astype(BF16), "c")
    own = blocks[0] + sent[0].astype(F32)
    other = blocks[2] + sent[1].astype(F32)
    return own + swap(other.astype(BF16), "y").astype(F32)


def scores_mask(first_key, first_query, window, block, start_row):
    key_places = first_key + lax.broadcasted_iota(jnp.int32, (window, block), 0)
    query_places = first_query + lax.broadcasted_iota(jnp.int32, (window, block), 1)
    return (key_places >= start_row) & (key_places <= query_places)


def attend_kernel(block, pad, q_ref, k_ref, v_ref, start_ref, out_ref, lse_ref, key_rows, value_pad):
    group = q_ref.shape[1]
    window = pad + block
    quarter = group // 4
    key_rows[pl.ds(0, pad), :] = jnp.zeros((pad, HEAD), BF16)
    value_pad[:, pl.ds(0, pad)] = jnp.zeros((HEAD, pad), BF16)
    key_rows[pl.ds(pad, group), :] = k_ref[...].T
    value_pad[:, pl.ds(pad, group)] = v_ref[...]

    def one(i, carry):
        first = pl.multiple_of(i * block, block)
        scores = jnp.dot(
            key_rows[pl.ds(first, window), :],
            q_ref[:, pl.ds(first, block)],
            preferred_element_type=F32,
        )
        allowed = scores_mask(first - pad, first, window, block, start_ref[:, pl.ds(first, block)])
        scores = jnp.where(allowed, scores * 0.125, NEGATIVE)
        highest = jnp.max(scores, axis=0, keepdims=True)
        weights = jnp.exp(scores - highest)
        total = jnp.sum(weights, axis=0, keepdims=True)
        mixed = jnp.dot(
            value_pad[:, pl.ds(first, window)], weights.astype(BF16), preferred_element_type=F32
        )
        mixed = (mixed / total).astype(BF16)
        out_ref[first // quarter, :, pl.ds(pl.multiple_of(first % quarter, block), block)] = mixed
        lse_ref[0, :, pl.ds(first, block)] = highest + jnp.log(total)
        return carry

    lax.fori_loop(0, group // block, one, 0)


def attend(qkv, starts, heads):
    group = qkv.shape[1]
    block = 256
    return pl.pallas_call(
        functools.partial(attend_kernel, block, MAXLEN),
        grid=(heads,),
        in_specs=[
            pl.BlockSpec((HEAD, group), lambda h: (h, 0)),
            pl.BlockSpec((HEAD, group), lambda h: (h + heads, 0)),
            pl.BlockSpec((HEAD, group), lambda h: (h + 2 * heads, 0)),
            pl.BlockSpec((1, group), lambda h: (0, 0)),
        ],
        out_specs=[
            pl.BlockSpec((4, HEAD, group // 4), lambda h: (0, h, 0)),
            pl.BlockSpec((1, 1, group), lambda h: (h, 0, 0)),
        ],
        out_shape=[
            jax.ShapeDtypeStruct((4, heads * HEAD, group // 4), BF16),
            jax.ShapeDtypeStruct((heads, 1, group), F32),
        ],
        scratch_shapes=[
            pltpu.VMEM((MAXLEN + group, HEAD), BF16),
            pltpu.VMEM((HEAD, MAXLEN + group), BF16),
        ],
        compiler_params=pltpu.CompilerParams(vmem_limit_bytes=48 * 2**20),
        name="attend",
    )(qkv, qkv, qkv, starts)


def attend_back_kernel(
    block, pad, q_ref, k_ref, v_ref, g_ref, start_ref, lse_ref, out_ref,
    key_rows, value_rows, key_pad, grad_key, grad_value,
):
    group = q_ref.shape[1]
    window = pad + block
    quarter = group // 4
    contract_last = (((1,), (1,)), ((), ()))
    key_rows[pl.ds(0, pad), :] = jnp.zeros((pad, HEAD), BF16)
    value_rows[pl.ds(0, pad), :] = jnp.zeros((pad, HEAD), BF16)
    key_pad[:, pl.ds(0, pad)] = jnp.zeros((HEAD, pad), BF16)
    key_rows[pl.ds(pad, group), :] = k_ref[...].T
    value_rows[pl.ds(pad, group), :] = v_ref[...].T
    key_pad[:, pl.ds(pad, group)] = k_ref[...]
    grad_key[...] = jnp.zeros_like(grad_key)
    grad_value[...] = jnp.zeros_like(grad_value)

    def one(i, carry):
        first = pl.multiple_of(i * block, block)
        query = q_ref[:, pl.ds(first, block)]
        grad = g_ref[:, pl.ds(first, block)]
        scores = jnp.dot(key_rows[pl.ds(first, window), :], query, preferred_element_type=F32)
        allowed = scores_mask(first - pad, first, window, block, start_ref[:, pl.ds(first, block)])
        exponent = jnp.where(allowed, scores * 0.125 - lse_ref[0, :, pl.ds(first, block)], NEGATIVE)
        probs = jnp.exp(exponent)
        grad_probs = jnp.dot(
            value_rows[pl.ds(first, window), :], grad, preferred_element_type=F32
        )
        inner = jnp.sum(probs * grad_probs, axis=0, keepdims=True)
        raw = (0.125 * (probs * (grad_probs - inner))).astype(BF16)
        grad_query = jnp.dot(key_pad[:, pl.ds(first, window)], raw, preferred_element_type=F32)
        out_ref[
            first // quarter, 0, :, pl.ds(pl.multiple_of(first % quarter, block), block)
        ] = grad_query.astype(BF16)
        grad_value[:, pl.ds(first, window)] += lax.dot_general(
            grad, probs.astype(BF16), contract_last, preferred_element_type=F32
        )
        grad_key[:, pl.ds(first, window)] += lax.dot_general(
            query, raw, contract_last, preferred_element_type=F32
        )
        return carry

    lax.fori_loop(0, group // block, one, 0)
    for j in range(4):
        out_ref[j, 1] = grad_key[:, pl.ds(pad + j * quarter, quarter)].astype(BF16)
        out_ref[j, 2] = grad_value[:, pl.ds(pad + j * quarter, quarter)].astype(BF16)


def attend_back(qkv, grad_mixed, starts, lse, heads):
    group = qkv.shape[1]
    block = 256
    return pl.pallas_call(
        functools.partial(attend_back_kernel, block, MAXLEN),
        grid=(heads,),
        in_specs=[
            pl.BlockSpec((HEAD, group), lambda h: (h, 0)),
            pl.BlockSpec((HEAD, group), lambda h: (h + heads, 0)),
            pl.BlockSpec((HEAD, group), lambda h: (h + 2 * heads, 0)),
            pl.BlockSpec((HEAD, group), lambda h: (h, 0)),
            pl.BlockSpec((1, group), lambda h: (0, 0)),
            pl.BlockSpec((1, 1, group), lambda h: (h, 0, 0)),
        ],
        out_specs=pl.BlockSpec((4, 3, HEAD, group // 4), lambda h: (0, 0, h, 0)),
        out_shape=jax.ShapeDtypeStruct((4, 3, heads * HEAD, group // 4), BF16),
        scratch_shapes=[
            pltpu.VMEM((MAXLEN + group, HEAD), BF16),
            pltpu.VMEM((MAXLEN + group, HEAD), BF16),
            pltpu.VMEM((HEAD, MAXLEN + group), BF16),
            pltpu.VMEM((HEAD, MAXLEN + group), F32),
            pltpu.VMEM((HEAD, MAXLEN + group), F32),
        ],
        compiler_params=pltpu.CompilerParams(vmem_limit_bytes=48 * 2**20),
        name="attend_back",
    )(qkv, qkv, qkv, grad_mixed, starts, lse)


def slots_of(routes, drop_order, valid, capacity, experts, parity, half):
    group = routes.shape[0]
    live = (routes < experts) & valid[:, None]
    target = jnp.where(live, routes, experts).reshape(-1)
    span = 2 * group
    code = target * span + drop_order.reshape(-1)
    smaller = jnp.sum((code[:, None] < code[None, :]).astype(jnp.int32), axis=0)
    ids = jnp.arange(experts + 1, dtype=jnp.int32)
    earlier = jnp.sum((target[:, None] < ids[None, :]).astype(jnp.int32), axis=0)
    base = jnp.sum(jnp.where(target[:, None] == ids[None, :], earlier[None, :], 0), axis=1)
    place = smaller - base
    share = capacity // 2
    mine = (
        (target < experts)
        & (place < capacity)
        & (target % 2 == parity)
        & (place // share == half)
    )
    slot = (target // 2) * share + place - half * share
    return jnp.where(mine, slot, -1).reshape(group, 2)


def router_of(rounded, prior_rows, w_router, w_prior):
    logits = jnp.dot(rounded, w_router, precision=PRECISE) + jnp.dot(
        prior_rows, w_prior, precision=PRECISE
    )
    return jax.nn.softmax(logits, axis=-1)


def picked_of(route_rows, kinds):
    return (
        route_rows[:, :, None] == jnp.arange(kinds, dtype=jnp.int32)[None, None, :]
    ).astype(F32)


def other_terms(normed, router, w_const, const_vector, route_rows, experts):
    mix_one = jax.nn.softmax(jnp.dot(normed, w_const[0], precision=PRECISE), axis=-1)
    mix_two = jax.nn.softmax(jnp.dot(normed, w_const[1], precision=PRECISE), axis=-1)
    constant_one = mix_one[:, :1] * normed + mix_one[:, 1:] * const_vector[0]
    constant_two = mix_two[:, :1] * normed + mix_two[:, 1:] * const_vector[1]

    def weight(kind):
        named = jnp.any(route_rows == kind, axis=1, keepdims=True).astype(F32)
        return router[:, kind : kind + 1] * named

    return (
        weight(experts + 1) * normed
        + weight(experts + 2) * constant_one
        + weight(experts + 3) * constant_two
    )


def two_parts(value):
    high = lax.reduce_precision(value, 8, 7)
    return jnp.concatenate([high, value - high], axis=-1).astype(BF16)


def per_device(
    many,
    inputs,
    cotangent,
    lengths,
    routes,
    drop_order,
    prior_logits,
    attn_gain,
    w_query,
    w_key,
    w_value,
    w_out,
    moe_gain,
    w_router,
    w_prior,
    w_const,
    const_vector,
    w_gate,
    w_up,
    w_down,
):
    tok_rows, width = inputs.shape
    group = tok_rows * 4
    kinds = w_router.shape[1]
    experts, shard_rows, shard_units = w_gate.shape
    capacity = 3 * group // 16
    share = capacity // 2
    local_width = w_query.shape[1]
    heads = local_width // HEAD
    high = lax.axis_index("hi")
    parity = lax.axis_index("y")
    core = lax.axis_index("c")
    place_in_group = parity * 2 + core
    first_mine = place_in_group * tok_rows

    attn_weights = jnp.concatenate([w_query, w_key, w_value, w_out.T], axis=1)
    attn_full = lax.all_gather(attn_weights, ("hi", "lo"), axis=0, tiled=True)
    normed_one = rms_norm(inputs, attn_gain).astype(BF16)
    normed_pieces = gather_pieces(normed_one)
    expert_shards = jnp.stack([w_gate, w_up, w_down.transpose(0, 2, 1)], axis=1)
    expert_part = lax.all_to_all(expert_shards, ("lo", "y"), 0, 0, tiled=True)
    if many == 2:
        expert_rows = jnp.stack([expert_part, swap(expert_part, "hi")])
    else:
        expert_rows = lax.all_gather(expert_part, "hi", axis=0)
    expert_all = jnp.stack([expert_rows, swap(expert_rows, "c")]).reshape(
        2, many, LOW, 2, 3, shard_rows, shard_units
    )
    expert_all = expert_all.transpose(4, 1, 2, 5, 0, 3, 6).reshape(3, width, 4 * shard_units)
    attn_all = lax.all_gather(attn_full, ("y", "c"), axis=0)

    boundary = jnp.cumsum(lengths[0])
    places = jnp.arange(group, dtype=jnp.int32)
    reached = places[:, None] >= boundary[None, :]
    segment = jnp.sum(reached.astype(jnp.int32), axis=1)
    starts = jnp.max(jnp.where(reached, boundary[None, :], 0), axis=1).reshape(1, group)
    valid = segment < lengths.shape[1] - 1
    pair_slots = slots_of(routes, drop_order, valid, capacity, experts, parity, core)
    relative = jnp.arange(4, dtype=jnp.int32) ^ place_in_group
    slots_by_piece = jnp.take(pair_slots.reshape(4, tok_rows, 2), relative, axis=0).reshape(
        group, 2
    )
    slot_ids = jnp.arange(LOW * share, dtype=jnp.int32)[:, None]
    dispatch = (
        (slot_ids == slots_by_piece[None, :, 0]) | (slot_ids == slots_by_piece[None, :, 1])
    ).astype(BF16)
    slot_expert = (slot_ids // share) * 2 + parity
    slot_kind = (slot_expert == jnp.arange(kinds, dtype=jnp.int32)[None, :]).astype(F32)
    valid_mine = lax.dynamic_slice_in_dim(valid, first_mine, tok_rows).astype(F32)[:, None]
    routes_mine = lax.dynamic_slice_in_dim(routes, first_mine, tok_rows)
    prior_mine = lax.dynamic_slice_in_dim(prior_logits, first_mine, tok_rows)
    grad_out = cotangent * valid_mine
    grad_out_pieces = jnp.concatenate(gather_pieces(grad_out.astype(BF16)), axis=0)
    grad_out_slots = jnp.dot(dispatch, grad_out_pieces, preferred_element_type=F32)

    normed_all = natural(normed_pieces, place_in_group).reshape(group, width)
    qkv = lax.dot_general(
        attn_full[:, : 3 * local_width],
        normed_all,
        (((0,), (1,)), ((), ())),
        preferred_element_type=F32,
    ).astype(BF16)
    mixed, lse = attend(qkv, starts, heads)
    mixed_mine = lax.all_to_all(mixed, ("y", "c"), 0, 0, tiled=True)
    out_all = attn_all[:, :, 3 * local_width :]
    hidden = inputs + jnp.einsum(
        "jit,jdi->td", mixed_mine, out_all, preferred_element_type=F32
    )

    normed_two = rms_norm(hidden, moe_gain)
    rounded_two = normed_two.astype(BF16)

    def local_gate(normed, rounded, prior_rows, router_weight, prior_weight, const_weight, const_vec):
        router = router_of(rounded, prior_rows, router_weight, prior_weight)
        return (
            router,
            other_terms(normed, router, const_weight, const_vec, routes_mine, experts),
        )

    (router, other_mine), gate_pull = jax.vjp(
        local_gate,
        normed_two,
        rounded_two.astype(F32),
        prior_mine,
        w_router,
        w_prior,
        w_const,
        const_vector,
    )
    extra = jnp.pad(two_parts(router), ((0, 0), (0, 128 - 2 * kinds)))
    sent_two = jnp.concatenate([rounded_two, extra], axis=1)
    pieces_two = jnp.concatenate(gather_pieces(sent_two), axis=0)
    picked_slots = jnp.dot(dispatch, pieces_two, preferred_element_type=F32)
    slot_router = (
        picked_slots[:, width : width + kinds]
        + picked_slots[:, width + kinds : width + 2 * kinds]
    )
    slot_weight = jnp.sum(slot_router * slot_kind, axis=1, keepdims=True)
    sent_slots = jnp.concatenate(
        [picked_slots[:, :width].astype(BF16), (grad_out_slots * slot_weight).astype(BF16)], axis=1
    ).reshape(LOW, share, 2 * width)
    taken = lax.all_to_all(sent_slots, "lo", 0, 0, tiled=True).reshape(LOW * share, 2, width)
    if many == 2:
        taken = jnp.where(high == 0, taken, jnp.roll(taken, width // 2, axis=2))
    dispatched, grad_expert = taken[:, 0], taken[:, 1]

    gate_w, up_w, down_w = expert_all[0], expert_all[1], expert_all[2]
    contract_last = (((1,), (1,)), ((), ()))
    contract_first = (((0,), (0,)), ((), ()))
    gate_pre = jnp.dot(dispatched, gate_w, preferred_element_type=F32)
    up_pre = jnp.dot(dispatched, up_w, preferred_element_type=F32)
    sigmoid_gate = jax.nn.sigmoid(gate_pre)
    activated = (gate_pre * sigmoid_gate * up_pre).astype(BF16)
    expert_out = lax.dot_general(activated, down_w, contract_last, preferred_element_type=F32)
    grad_act = jnp.dot(grad_expert, down_w, preferred_element_type=F32)
    grad_gate = (
        grad_act * up_pre * sigmoid_gate * (1.0 + gate_pre * (1.0 - sigmoid_gate))
    ).astype(BF16)
    grad_up = (grad_act * gate_pre * sigmoid_gate).astype(BF16)
    grad_slots = lax.dot_general(
        grad_gate, gate_w, contract_last, preferred_element_type=F32
    ) + lax.dot_general(grad_up, up_w, contract_last, preferred_element_type=F32)
    weight_grads = jnp.stack(
        [
            lax.dot_general(dispatched, grad_gate, contract_first, preferred_element_type=F32),
            lax.dot_general(dispatched, grad_up, contract_first, preferred_element_type=F32),
            lax.dot_general(grad_expert, activated, contract_first, preferred_element_type=F32),
        ]
    ).reshape(3, many, LOW, shard_rows, 2, 2, shard_units)
    weight_sum = weight_grads[:, :, :, :, 0] + swap(
        weight_grads[:, :, :, :, 1].astype(BF16), "c"
    ).astype(F32)
    if many == 2:
        weight_part = weight_sum[:, 0] + swap(weight_sum[:, 1].astype(BF16), "hi").astype(F32)
    else:
        weight_part = lax.psum_scatter(weight_sum, "hi", scatter_dimension=1)
    weight_part = weight_part.astype(BF16).transpose(1, 3, 0, 2, 4)
    weight_own = lax.all_to_all(
        weight_part.reshape(2 * LOW, 3, shard_rows, shard_units), ("lo", "y"), 0, 0, tiled=True
    ).astype(F32)
    grad_gate_own = weight_own[:, 0]
    grad_up_own = weight_own[:, 1]
    grad_down_own = weight_own[:, 2].transpose(0, 2, 1)

    returned = jnp.concatenate([expert_out, grad_slots], axis=1).astype(BF16)
    returned = returned.reshape(LOW * share, 2, width)
    if many == 2:
        returned = jnp.where(high == 0, returned, jnp.roll(returned, width // 2, axis=2))
    returned = lax.all_to_all(
        returned.reshape(LOW, share, 2 * width), "lo", 0, 0, tiled=True
    ).reshape(LOW * share, 2 * width)
    out_slots = returned[:, :width].astype(F32)
    pair_slots_grad = jnp.sum(out_slots * grad_out_slots, axis=1, keepdims=True) * slot_kind
    extra_back = jnp.pad(two_parts(pair_slots_grad), ((0, 0), (0, 128 - 2 * kinds)))
    back_slots = jnp.concatenate([returned[:, width:], extra_back], axis=1)
    back_blocks = lax.dot_general(
        dispatch, back_slots, contract_first, preferred_element_type=F32
    ).reshape(4, tok_rows, width + 128)
    back_mine = scatter_sum(back_blocks)
    feed_blocks = lax.dot_general(
        dispatch,
        (out_slots * slot_weight).astype(BF16),
        contract_first,
        preferred_element_type=F32,
    ).reshape(4, tok_rows, width)
    feed_mine = scatter_sum(feed_blocks)
    output = valid_mine * (hidden + feed_mine + other_mine)

    grad_router_rows = (
        back_mine[:, width : width + kinds] + back_mine[:, width + kinds : width + 2 * kinds]
    )
    grad_normed, grad_rounded, grad_prior, grad_router, grad_prior_w, grad_const, grad_vector = (
        gate_pull((grad_router_rows, grad_out))
    )
    _, norm_pull_two = jax.vjp(rms_norm, hidden, moe_gain)
    grad_hidden_part, grad_moe_gain = norm_pull_two(
        grad_normed + grad_rounded + back_mine[:, :width]
    )
    grad_hidden = grad_out + grad_hidden_part

    grad_attn_all = natural(gather_pieces(grad_hidden.astype(BF16)), place_in_group)
    grad_mixed = lax.dot_general(
        attn_full[:, 3 * local_width :],
        grad_attn_all.reshape(group, width),
        (((0,), (1,)), ((), ())),
        preferred_element_type=F32,
    ).astype(BF16)
    grad_out_w = jnp.einsum("jit,jtd->di", mixed, grad_attn_all, preferred_element_type=F32)
    grad_qkv = attend_back(qkv, grad_mixed, starts, lse, heads).reshape(
        4, 3 * local_width, tok_rows
    )
    grad_qkv_w = jnp.einsum(
        "jit,jtd->di",
        grad_qkv,
        normed_all.reshape(4, tok_rows, width),
        preferred_element_type=F32,
    )
    grad_attn_w = jnp.concatenate([grad_qkv_w, grad_out_w], axis=1).astype(BF16)
    fsdp = many * LOW
    grad_attn_own = jnp.sum(
        lax.all_to_all(
            grad_attn_w.reshape(fsdp, width // fsdp, 4 * local_width),
            ("hi", "lo"),
            0,
            0,
            tiled=True,
        ).astype(F32),
        axis=0,
    )
    grad_qkv_mine = lax.all_to_all(grad_qkv, ("y", "c"), 0, 0, tiled=True)
    grad_normed_one = jnp.einsum(
        "jit,jdi->td",
        grad_qkv_mine,
        attn_all[:, :, : 3 * local_width],
        preferred_element_type=F32,
    )
    _, norm_pull_one = jax.vjp(rms_norm, inputs, attn_gain)
    grad_input_part, grad_attn_gain = norm_pull_one(grad_normed_one)
    grad_inputs = grad_hidden + grad_input_part
    summed = lax.psum(
        (grad_attn_gain, grad_moe_gain, grad_router, grad_prior_w, grad_const, grad_vector),
        ("hi", "lo", "y", "c"),
    )
    return (
        output,
        grad_inputs,
        grad_prior,
        summed[0],
        grad_attn_own[:, :local_width],
        grad_attn_own[:, local_width : 2 * local_width],
        grad_attn_own[:, 2 * local_width : 3 * local_width],
        grad_attn_own[:, 3 * local_width :].T,
        summed[1],
        summed[2],
        summed[3],
        summed[4],
        summed[5],
        grad_gate_own,
        grad_up_own,
        grad_down_own,
    )


def solution(mesh):
    many = mesh.shape["fsdp"] // LOW
    fine = Mesh(mesh.devices.reshape(many, LOW, 2, 2), ("hi", "lo", "y", "c"))
    fsdp, tp = ("hi", "lo"), ("y", "c")
    every = fsdp + tp
    return jax.shard_map(
        functools.partial(per_device, many),
        mesh=fine,
        in_specs=(
            P(every, None),
            P(every, None),
            P(fsdp, None),
            P(fsdp, None),
            P(fsdp, None),
            P(fsdp, None),
            P(),
            P(fsdp, tp),
            P(fsdp, tp),
            P(fsdp, tp),
            P(tp, fsdp),
            P(),
            P(),
            P(),
            P(),
            P(),
            P(None, fsdp, tp),
            P(None, fsdp, tp),
            P(None, tp, fsdp),
        ),
        out_specs=(
            P(every, None),
            P(every, None),
            P(every, None),
            P(),
            P(fsdp, tp),
            P(fsdp, tp),
            P(fsdp, tp),
            P(tp, fsdp),
            P(),
            P(),
            P(),
            P(),
            P(),
            P(None, fsdp, tp),
            P(None, fsdp, tp),
            P(None, tp, fsdp),
        ),
        check_vma=False,
    )
```

```python
import functools

import jax
import jax.numpy as jnp
from jax import lax
from jax.experimental import pallas as pl
from jax.experimental.pallas import tpu as pltpu
from jax.sharding import Mesh
from jax.sharding import PartitionSpec as P

HEAD = 64
MAXLEN = 768
LOW = 4
SHARDS = 8
BOUNDS = 4
EPSILON = 1e-06
PRECISE = lax.Precision.HIGHEST
NEGATIVE = -1e30
F32 = jnp.float32
BF16 = jnp.bfloat16


def rms_norm(values, gain):
    return values * lax.rsqrt(jnp.mean(values * values, axis=-1, keepdims=True) + EPSILON) * gain


def swap(value, axis):
    return lax.ppermute(value, axis, [(0, 1), (1, 0)])


def gather_pieces(value):
    other = swap(value, "y")
    return [value, swap(value, "c"), other, swap(other, "c")]


def natural(pieces, index):
    ordered = []
    for j in range(4):
        item = pieces[j]
        for t in range(1, 4):
            item = jnp.where(index == t, pieces[j ^ t], item)
        ordered.append(item)
    return jnp.stack(ordered)


def add_core(near, sent):
    got = swap(sent, "c").astype(F32)
    return near[0] + got[0], (near[1] + got[1]).astype(BF16)


def cost_of(microseconds):
    return pl.CostEstimate(
        flops=int(microseconds * 1.15e9), transcendentals=0, bytes_accessed=2**20
    )


def scores_mask(first_key, first_query, window, block, scalars):
    row = first_query + lax.broadcasted_iota(jnp.int32, (1, block), 1)
    start_row = jnp.zeros_like(row)
    for k in range(BOUNDS, scalars.shape[0]):
        start_row = jnp.where(row >= scalars[k], scalars[k], start_row)
    key_places = first_key + lax.broadcasted_iota(jnp.int32, (window, block), 0)
    query_places = first_query + lax.broadcasted_iota(jnp.int32, (window, block), 1)
    return (key_places >= start_row) & (key_places <= query_places)


def attend_kernel(block, pad, scalars, *refs):
    pieces, refs = refs[:4], refs[4:]
    shards, refs = refs[:SHARDS], refs[SHARDS:]
    out_ref, lse_ref, qkv_ref, weight_ref, last_ref, key_rows, value_pad, full = refs
    group = qkv_ref.shape[1]
    window = pad + block
    quarter = group // 4
    inner = qkv_ref.shape[0] // 3
    head = pl.program_id(0)

    @pl.when(head == 0)
    def _():
        rows = shards[0].shape[0]
        for r in range(SHARDS):
            place = pl.multiple_of((scalars[0] ^ r) * rows, rows)
            full[pl.ds(place, rows), :] = shards[r][...]
        weight_ref[...] = full[:, : 3 * inner]
        last_ref[...] = full[:, 3 * inner :]
        turned = full[:, : 3 * inner].T
        for r in range(4):
            place = pl.multiple_of((scalars[1] ^ r) * quarter, quarter)
            qkv_ref[:, pl.ds(place, quarter)] = lax.dot_general(
                turned, pieces[r][...], (((1,), (1,)), ((), ())), preferred_element_type=F32
            ).astype(BF16)

    first_row = pl.multiple_of(head * HEAD, HEAD)
    key_rows[pl.ds(0, pad), :] = jnp.zeros((pad, HEAD), BF16)
    value_pad[:, pl.ds(0, pad)] = jnp.zeros((HEAD, pad), BF16)
    key_rows[pl.ds(pad, group), :] = qkv_ref[pl.ds(inner + first_row, HEAD), :].T
    value_pad[:, pl.ds(pad, group)] = qkv_ref[pl.ds(2 * inner + first_row, HEAD), :]

    def one(i, carry):
        first = pl.multiple_of(i * block, block)
        scores = jnp.dot(
            key_rows[pl.ds(first, window), :],
            qkv_ref[pl.ds(first_row, HEAD), pl.ds(first, block)],
            preferred_element_type=F32,
        )
        allowed = scores_mask(first - pad, first, window, block, scalars)
        scores = jnp.where(allowed, scores * 0.125, NEGATIVE)
        highest = jnp.max(scores, axis=0, keepdims=True)
        weights = jnp.exp(scores - highest)
        total = jnp.sum(weights, axis=0, keepdims=True)
        mixed = jnp.dot(
            value_pad[:, pl.ds(first, window)], weights.astype(BF16), preferred_element_type=F32
        )
        mixed = (mixed / total).astype(BF16)
        out_ref[first // quarter, :, pl.ds(pl.multiple_of(first % quarter, block), block)] = mixed
        lse_ref[0, :, pl.ds(first, block)] = highest + jnp.log(total)
        return carry

    lax.fori_loop(0, group // block, one, 0)


def attend(pieces, shards, scalars, heads):
    rows, width = pieces[0].shape
    group = 4 * rows
    inner = heads * HEAD
    block = 256

    def whole(shape):
        return pl.BlockSpec(
            shape, lambda i, _: (0,) * len(shape), pipeline_mode=pl.Buffered(1)
        )

    return pl.pallas_call(
        functools.partial(attend_kernel, block, MAXLEN),
        grid_spec=pltpu.PrefetchScalarGridSpec(
            num_scalar_prefetch=1,
            grid=(heads,),
            in_specs=[
                *[whole((rows, width)) for _ in range(4)],
                *[whole(shards[0].shape) for _ in range(SHARDS)],
            ],
            out_specs=[
                pl.BlockSpec((4, HEAD, rows), lambda h, _: (0, h, 0)),
                pl.BlockSpec((1, 1, group), lambda h, _: (h, 0, 0)),
                whole((3 * inner, group)),
                whole((width, 3 * inner)),
                whole((width, inner)),
            ],
            scratch_shapes=[
                pltpu.VMEM((MAXLEN + group, HEAD), BF16),
                pltpu.VMEM((HEAD, MAXLEN + group), BF16),
                pltpu.VMEM((width, 4 * inner), BF16),
            ],
        ),
        out_shape=[
            jax.ShapeDtypeStruct((4, inner, rows), BF16),
            jax.ShapeDtypeStruct((heads, 1, group), F32),
            jax.ShapeDtypeStruct((3 * inner, group), BF16),
            jax.ShapeDtypeStruct((width, 3 * inner), BF16),
            jax.ShapeDtypeStruct((width, inner), BF16),
        ],
        compiler_params=pltpu.CompilerParams(vmem_limit_bytes=48 * 2**20),
        cost_estimate=cost_of(24),
        name="attend",
    )(scalars, *pieces, *shards)


def attn_grads_kernel(scalars, *refs):
    grad_qkv, mixed, refs = refs[0], refs[1], refs[2:]
    tokens, grads, refs = refs[:4], refs[4:8], refs[8:]
    outs, (total,) = refs[:SHARDS], refs[SHARDS:]
    inner3 = grad_qkv.shape[1]
    first, second = 0.0, 0.0
    for r in range(4):
        j = scalars[1] ^ r
        first += jnp.dot(grad_qkv[j], tokens[r][...], preferred_element_type=F32)
        second += jnp.dot(mixed[j], grads[r][...], preferred_element_type=F32)
    total[:, :inner3] = first.T.astype(BF16)
    total[:, inner3:] = second.T.astype(BF16)
    rows = outs[0].shape[0]
    for r in range(SHARDS):
        place = pl.multiple_of((scalars[0] ^ r) * rows, rows)
        outs[r][...] = total[pl.ds(place, rows), :]


def attn_grads(grad_qkv, mixed, tokens, grads, scalars):
    width = tokens[0].shape[1]
    columns = grad_qkv.shape[1] + mixed.shape[1]
    rows = width // SHARDS
    whole = pl.BlockSpec(memory_space=pltpu.VMEM)
    return pl.pallas_call(
        attn_grads_kernel,
        in_specs=[pl.BlockSpec(memory_space=pltpu.SMEM)] + [whole] * 10,
        out_specs=[whole] * SHARDS,
        out_shape=[jax.ShapeDtypeStruct((rows, columns), BF16)] * SHARDS,
        scratch_shapes=[pltpu.VMEM((width, columns), BF16)],
        compiler_params=pltpu.CompilerParams(vmem_limit_bytes=48 * 2**20),
        cost_estimate=cost_of(8),
        name="attn_grads",
    )(scalars, grad_qkv, mixed, *tokens, *grads)


def attend_back_kernel(
    block, pad, scalars, q_ref, k_ref, v_ref, g_ref, lse_ref, out_ref,
    key_rows, value_rows, key_pad, grad_key, grad_value,
):
    group = q_ref.shape[1]
    window = pad + block
    quarter = group // 4
    contract_last = (((1,), (1,)), ((), ()))
    key_rows[pl.ds(0, pad), :] = jnp.zeros((pad, HEAD), BF16)
    value_rows[pl.ds(0, pad), :] = jnp.zeros((pad, HEAD), BF16)
    key_pad[:, pl.ds(0, pad)] = jnp.zeros((HEAD, pad), BF16)
    key_rows[pl.ds(pad, group), :] = k_ref[...].T
    value_rows[pl.ds(pad, group), :] = v_ref[...].T
    key_pad[:, pl.ds(pad, group)] = k_ref[...]
    grad_key[...] = jnp.zeros_like(grad_key)
    grad_value[...] = jnp.zeros_like(grad_value)

    def one(i, carry):
        first = pl.multiple_of(i * block, block)
        query = q_ref[:, pl.ds(first, block)]
        grad = g_ref[:, pl.ds(first, block)]
        scores = jnp.dot(key_rows[pl.ds(first, window), :], query, preferred_element_type=F32)
        allowed = scores_mask(first - pad, first, window, block, scalars)
        exponent = jnp.where(allowed, scores * 0.125 - lse_ref[0, :, pl.ds(first, block)], NEGATIVE)
        probs = jnp.exp(exponent)
        grad_probs = jnp.dot(
            value_rows[pl.ds(first, window), :], grad, preferred_element_type=F32
        )
        inner = jnp.sum(probs * grad_probs, axis=0, keepdims=True)
        raw = (0.125 * (probs * (grad_probs - inner))).astype(BF16)
        grad_query = jnp.dot(key_pad[:, pl.ds(first, window)], raw, preferred_element_type=F32)
        out_ref[
            first // quarter, 0, :, pl.ds(pl.multiple_of(first % quarter, block), block)
        ] = grad_query.astype(BF16)
        grad_value[:, pl.ds(first, window)] += lax.dot_general(
            grad, probs.astype(BF16), contract_last, preferred_element_type=F32
        )
        grad_key[:, pl.ds(first, window)] += lax.dot_general(
            query, raw, contract_last, preferred_element_type=F32
        )
        return carry

    lax.fori_loop(0, group // block, one, 0)
    for j in range(4):
        out_ref[j, 1] = grad_key[:, pl.ds(pad + j * quarter, quarter)].astype(BF16)
        out_ref[j, 2] = grad_value[:, pl.ds(pad + j * quarter, quarter)].astype(BF16)


def attend_back(qkv, grad_mixed, scalars, lse, heads):
    group = qkv.shape[1]
    block = 256
    return pl.pallas_call(
        functools.partial(attend_back_kernel, block, MAXLEN),
        grid_spec=pltpu.PrefetchScalarGridSpec(
            num_scalar_prefetch=1,
            grid=(heads,),
            in_specs=[
                pl.BlockSpec((HEAD, group), lambda h, _: (h, 0)),
                pl.BlockSpec((HEAD, group), lambda h, _: (h + heads, 0)),
                pl.BlockSpec((HEAD, group), lambda h, _: (h + 2 * heads, 0)),
                pl.BlockSpec((HEAD, group), lambda h, _: (h, 0)),
                pl.BlockSpec((1, 1, group), lambda h, _: (h, 0, 0)),
            ],
            out_specs=pl.BlockSpec((4, 3, HEAD, group // 4), lambda h, _: (0, 0, h, 0)),
            scratch_shapes=[
                pltpu.VMEM((MAXLEN + group, HEAD), BF16),
                pltpu.VMEM((MAXLEN + group, HEAD), BF16),
                pltpu.VMEM((HEAD, MAXLEN + group), BF16),
                pltpu.VMEM((HEAD, MAXLEN + group), F32),
                pltpu.VMEM((HEAD, MAXLEN + group), F32),
            ],
        ),
        out_shape=jax.ShapeDtypeStruct((4, 3, heads * HEAD, group // 4), BF16),
        compiler_params=pltpu.CompilerParams(vmem_limit_bytes=48 * 2**20),
        cost_estimate=cost_of(31),
        name="attend_back",
    )(scalars, qkv, qkv, qkv, grad_mixed, lse)


def inputs_back_kernel(scalars, grads, p0, p1, p2, p3, x_ref, gain_ref, hidden_ref, out_ref, sum_ref):
    total = 0.0
    for r, weight in enumerate((p0, p1, p2, p3)):
        total += lax.dot_general(
            grads[scalars[1] ^ r].T, weight[...], (((1,), (1,)), ((), ())),
            preferred_element_type=F32,
        )
    x = x_ref[...]
    scale = lax.rsqrt(jnp.mean(x * x, axis=1, keepdims=True) + EPSILON)
    through = total * gain_ref[...]
    inner = jnp.mean(through * x, axis=1, keepdims=True)
    out_ref[...] = hidden_ref[...] + scale * through - (scale * scale * scale * inner) * x
    sum_ref[...] = jnp.sum(total * x * scale, axis=0, keepdims=True)


def inputs_back(scalars, grads, weights, x, gain, grad_hidden):
    whole = pl.BlockSpec(memory_space=pltpu.VMEM)
    return pl.pallas_call(
        inputs_back_kernel,
        in_specs=[pl.BlockSpec(memory_space=pltpu.SMEM)] + [whole] * 8,
        out_specs=[whole] * 2,
        out_shape=[
            jax.ShapeDtypeStruct(x.shape, F32),
            jax.ShapeDtypeStruct((1, x.shape[1]), F32),
        ],
        compiler_params=pltpu.CompilerParams(vmem_limit_bytes=48 * 2**20),
        cost_estimate=cost_of(6),
        name="inputs_back",
    )(scalars, grads, *weights, x, gain, grad_hidden)


def expert_kernel(
    kinds, scalars, x_own, x_core, g_own, g_core, w_own, *refs
):
    w_far, refs = refs[:LOW], refs[LOW:]
    back_own, back_send, feed_own, feed_send, grads_own, *refs = refs
    grads_far, refs = refs[:LOW], refs[LOW:]
    x_all, g_all, x_t, g_t, weights, hidden, acc_feed, acc_back = refs
    slots, width = g_own.shape
    half = width // 2
    step = pl.program_id(0)
    near = pl.multiple_of(scalars[0] * half, half)
    far = pl.multiple_of((1 - scalars[0]) * half, half)
    contract_last = (((1,), (1,)), ((), ()))
    units = weights.shape[2]

    def weight_column(x_ref):
        extra = x_ref[:, width:].astype(F32)
        lanes = lax.broadcasted_iota(jnp.int32, extra.shape, 1)
        named = (lanes == scalars[1]) | (lanes == scalars[1] + kinds)
        return jnp.sum(jnp.where(named, extra, 0.0), axis=1, keepdims=True)

    @pl.when(step == 0)
    def _():
        for part, (x_ref, g_ref) in enumerate(((x_own, g_own), (x_core, g_core))):
            rows = pl.ds(part * slots, slots)
            x = x_ref[:, :width]
            grad = (g_ref[...].astype(F32) * weight_column(x_ref)).astype(BF16)
            x_all[rows, :] = x
            g_all[rows, :] = grad
            x_t[:, rows] = x.T
            g_t[:, rows] = grad.T
        acc_feed[...] = jnp.zeros_like(acc_feed)
        acc_back[...] = jnp.zeros_like(acc_back)

    for k in range(3):
        weights[k, pl.ds(near, half), :] = w_own[:, 0, k].reshape(half, units)
        for i in range(LOW):
            rows = half // LOW
            weights[k, pl.ds(pl.multiple_of(far + i * rows, rows), rows), :] = w_far[i][0, 0, k]

    for part in range(2):
        rows = pl.ds(part * slots, slots)
        x = x_all[rows, :]
        gate = jnp.dot(x, weights[0], preferred_element_type=F32)
        up = jnp.dot(x, weights[1], preferred_element_type=F32)
        grad_act = jnp.dot(g_all[rows, :], weights[2], preferred_element_type=F32)
        sig = jax.nn.sigmoid(gate)
        silu = gate * sig
        active = (silu * up).astype(BF16)
        grad_gate = (grad_act * up * (sig * (1.0 + gate * (1.0 - sig)))).astype(BF16)
        grad_up = (grad_act * silu).astype(BF16)
        hidden[0, rows, :] = grad_gate
        hidden[1, rows, :] = grad_up
        hidden[2, rows, :] = active
        acc_feed[rows, :] += lax.dot_general(
            active, weights[2], contract_last, preferred_element_type=F32
        )
        acc_back[rows, :] += lax.dot_general(
            grad_gate, weights[0], contract_last, preferred_element_type=F32
        ) + lax.dot_general(grad_up, weights[1], contract_last, preferred_element_type=F32)

    for k in range(3):
        left = (g_t if k == 2 else x_t)
        near_grad = jnp.dot(
            left[pl.ds(near, half), :], hidden[k], preferred_element_type=F32
        )
        far_grad = jnp.dot(left[pl.ds(far, half), :], hidden[k], preferred_element_type=F32)
        grads_own[:, 0, k] = near_grad.reshape(grads_own.shape[0], -1, units)
        for i in range(LOW):
            rows = half // LOW
            grads_far[i][0, 0, k] = far_grad[i * rows : (i + 1) * rows].astype(BF16)

    @pl.when(step == pl.num_programs(0) - 1)
    def _():
        for part, (x_ref, g_ref) in enumerate(((x_own, g_own), (x_core, g_core))):
            rows = pl.ds(part * slots, slots)
            feed = acc_feed[rows, :]
            inner = jnp.sum(feed * g_ref[...].astype(F32), axis=1, keepdims=True)
            feed = feed * weight_column(x_ref)
            lanes = lax.broadcasted_iota(jnp.int32, (slots, 128), 1)
            if part == 0:
                back_own[:, :width] = acc_back[rows, :]
                back_own[:, width:] = jnp.where(lanes == scalars[1], inner, 0.0)
                feed_own[...] = feed
            else:
                high = inner.astype(BF16).astype(F32)
                extra = jnp.where(lanes == scalars[1], high, 0.0)
                extra = jnp.where(lanes == scalars[1] + kinds, inner - high, extra)
                back_send[:, :width] = acc_back[rows, :].astype(BF16)
                back_send[:, width:] = extra.astype(BF16)
                feed_send[...] = feed.astype(BF16)


def expert_pass(kinds, scalars, x_own, x_core, g_own, g_core, w_own, w_far):
    slots, width = g_own.shape
    low, parities, _, shard_rows, shard_units = w_own.shape
    units = 256
    steps = shard_units // units

    def whole(shape):
        return pl.BlockSpec(
            shape, lambda i, _: (0,) * len(shape), pipeline_mode=pl.Buffered(1)
        )

    def weight_spec(count):
        return pl.BlockSpec(
            (count, 1, 3, shard_rows, units), lambda i, _: (0, i // steps, 0, 0, i % steps)
        )

    wide = width + 128
    return pl.pallas_call(
        functools.partial(expert_kernel, kinds),
        grid_spec=pltpu.PrefetchScalarGridSpec(
            num_scalar_prefetch=1,
            grid=(parities * steps,),
            in_specs=[
                whole((slots, wide)),
                whole((slots, wide)),
                whole((slots, width)),
                whole((slots, width)),
                weight_spec(low),
                *[weight_spec(1) for _ in range(low)],
            ],
            out_specs=[
                whole((slots, wide)),
                whole((slots, wide)),
                whole((slots, width)),
                whole((slots, width)),
                weight_spec(low),
                *[weight_spec(1) for _ in range(low)],
            ],
            scratch_shapes=[
                pltpu.VMEM((2 * slots, width), BF16),
                pltpu.VMEM((2 * slots, width), BF16),
                pltpu.VMEM((width, 2 * slots), BF16),
                pltpu.VMEM((width, 2 * slots), BF16),
                pltpu.VMEM((3, width, units), BF16),
                pltpu.VMEM((3, 2 * slots, units), BF16),
                pltpu.VMEM((2 * slots, width), F32),
                pltpu.VMEM((2 * slots, width), F32),
            ],
        ),
        out_shape=[
            jax.ShapeDtypeStruct((slots, wide), F32),
            jax.ShapeDtypeStruct((slots, wide), BF16),
            jax.ShapeDtypeStruct((slots, width), F32),
            jax.ShapeDtypeStruct((slots, width), BF16),
            jax.ShapeDtypeStruct(w_own.shape, F32),
            *[jax.ShapeDtypeStruct(item.shape, BF16) for item in w_far],
        ],
        compiler_params=pltpu.CompilerParams(vmem_limit_bytes=58 * 2**20),
        cost_estimate=cost_of(35),
        name="expert_pass",
    )(scalars, x_own, x_core, g_own, g_core, w_own, *w_far)


def pick_kernel(ids_ref, *refs):
    pieces, out_ref = refs[:4], refs[4]
    block = out_ref.shape[0]
    rows = pieces[0].shape[0]
    first = pl.program_id(0) * block
    total = jnp.zeros(out_ref.shape, F32)
    for r in range(4):
        slot = first + lax.broadcasted_iota(jnp.int32, (block, rows), 0)
        columns = pl.ds(r * rows, rows)
        held = (slot == ids_ref[0:1, columns]) | (slot == ids_ref[1:2, columns])
        held = jnp.where(held, 1.0, 0.0).astype(BF16)
        total = total + jnp.dot(held, pieces[r][...], preferred_element_type=F32)
    out_ref[...] = total.astype(BF16)


def pick(ids, pieces, slots):
    rows, width = pieces[0].shape
    block = 256 if slots % 256 == 0 else slots
    return pl.pallas_call(
        pick_kernel,
        grid=(slots // block,),
        in_specs=[
            pl.BlockSpec((8, 4 * rows), lambda i: (0, 0)),
            *[pl.BlockSpec((rows, width), lambda i: (0, 0)) for _ in range(4)],
        ],
        out_specs=pl.BlockSpec((block, width), lambda i: (i, 0)),
        out_shape=jax.ShapeDtypeStruct((slots, width), BF16),
        compiler_params=pltpu.CompilerParams(vmem_limit_bytes=32 * 2**20),
        cost_estimate=cost_of(5),
        name="pick",
    )(ids, *pieces)


def spread_kernel(ids_ref, slots_ref, near_ref, send_ref):
    rows = near_ref.shape[1]
    slots = slots_ref.shape[0]
    for k, out_ref in enumerate((near_ref, send_ref)):
        slot = lax.broadcasted_iota(jnp.int32, (rows, slots), 1)
        ids = ids_ref[pl.ds(k * rows, rows), :]
        held = (slot == ids[:, 0:1]) | (slot == ids[:, 1:2])
        held = jnp.where(held, 1.0, 0.0).astype(BF16)
        total = jnp.dot(held, slots_ref[...], preferred_element_type=F32)
        out_ref[0] = total.astype(out_ref.dtype)


def spread(ids, values, rows):
    slots, width = values.shape
    return pl.pallas_call(
        spread_kernel,
        grid=(2,),
        in_specs=[
            pl.BlockSpec((2 * rows, 8), lambda i: (i, 0)),
            pl.BlockSpec((slots, width), lambda i: (0, 0)),
        ],
        out_specs=[
            pl.BlockSpec((1, rows, width), lambda i: (i, 0, 0)),
            pl.BlockSpec((1, rows, width), lambda i: (i, 0, 0)),
        ],
        out_shape=[
            jax.ShapeDtypeStruct((2, rows, width), F32),
            jax.ShapeDtypeStruct((2, rows, width), BF16),
        ],
        compiler_params=pltpu.CompilerParams(vmem_limit_bytes=32 * 2**20),
        cost_estimate=cost_of(6),
        name="spread",
    )(ids, values)


def slots_kernel(experts, capacity, scalars, routes_col, order_col, routes_row, order_row,
                 row_ref, col_ref, places_ref):
    group = routes_row.shape[1]
    rows = group // 4
    share = capacity // 2
    span = 2 * group
    bound = scalars[BOUNDS + 2]

    def target_of(routes, axis):
        place = lax.broadcasted_iota(jnp.int32, routes.shape, axis)
        return jnp.where((routes < experts) & (place < bound), routes, experts)

    target = target_of(routes_row[...], 1)
    code = target * span + order_row[...]
    block = 256

    def count(i, carry):
        first = pl.multiple_of(i * block, block)
        routes = routes_col[pl.ds(first, block), :]
        place = first + lax.broadcasted_iota(jnp.int32, routes.shape, 0)
        held = jnp.where((routes < experts) & (place < bound), routes, experts)
        others = held * span + order_col[pl.ds(first, block), :]
        result = []
        for k in range(2):
            total = carry[k]
            for j in range(2):
                smaller = jnp.where(others[:, j : j + 1] < code[k : k + 1, :], 1.0, 0.0)
                total = total + jnp.sum(smaller, axis=0, keepdims=True)
            result.append(total)
        return tuple(result)

    zero = jnp.zeros((1, group), F32)
    counts = lax.fori_loop(0, group // block, count, (zero, zero))
    for k in range(2):
        mine_target = target[k : k + 1, :]
        base = jnp.zeros((1, group), F32)
        for e in range(1, experts):
            earlier = jnp.sum(jnp.where(target < e, 1.0, 0.0))
            base = jnp.where(mine_target == e, earlier, base)
        place = (counts[k] - base).astype(jnp.int32)
        first = scalars[3] * share
        held = (
            (mine_target < experts)
            & (place >= first)
            & (place < first + share)
            & (place < capacity)
            & (jnp.bitwise_and(mine_target, 1) == scalars[2])
        )
        slot = lax.shift_right_logical(mine_target, 1) * share + place - first
        places_ref[k : k + 1, :] = jnp.where(held, slot, -1)
    for r in range(4):
        start = pl.multiple_of((scalars[1] ^ r) * rows, rows)
        piece = places_ref[:, pl.ds(start, rows)]
        row_ref[:, pl.ds(r * rows, rows)] = piece
        col_ref[pl.ds(r * rows, rows), :] = piece.T


def slots_of(scalars, routes, drop_order, experts, capacity):
    group = routes.shape[0]
    whole = pl.BlockSpec(memory_space=pltpu.VMEM)
    return pl.pallas_call(
        functools.partial(slots_kernel, experts, capacity),
        in_specs=[pl.BlockSpec(memory_space=pltpu.SMEM)] + [whole] * 4,
        out_specs=[whole] * 2,
        out_shape=[
            jax.ShapeDtypeStruct((8, group), jnp.int32),
            jax.ShapeDtypeStruct((group, 8), jnp.int32),
        ],
        scratch_shapes=[pltpu.VMEM((8, group), jnp.int32)],
        compiler_params=pltpu.CompilerParams(vmem_limit_bytes=32 * 2**20),
        cost_estimate=cost_of(8),
        name="slots",
    )(scalars, routes, drop_order, routes.T, drop_order.T)


def middle_kernel(kinds, scalars, mixed, p0, p1, p2, p3, x_ref, gain_ref, router_w, prior_ref,
                  prior_w, hidden_ref, sent_ref, router_ref):
    hidden = x_ref[...]
    for r, weight in enumerate((p0, p1, p2, p3)):
        hidden += lax.dot_general(
            mixed[scalars[1] ^ r].T, weight[...], (((1,), (1,)), ((), ())),
            preferred_element_type=F32,
        )
    hidden_ref[...] = hidden
    scale = lax.rsqrt(jnp.mean(hidden * hidden, axis=1, keepdims=True) + EPSILON)
    rounded = (hidden * scale * gain_ref[...]).astype(BF16)
    width = hidden.shape[1]
    sent_ref[:, :width] = rounded
    logits = jnp.dot(
        rounded.astype(F32), router_w[...], precision=PRECISE, preferred_element_type=F32
    ) + jnp.dot(prior_ref[...], prior_w[...], precision=PRECISE, preferred_element_type=F32)
    lanes = lax.broadcasted_iota(jnp.int32, logits.shape, 1)
    logits = jnp.where(lanes < 2 * kinds, logits, NEGATIVE)
    weights = jnp.exp(logits - jnp.max(logits, axis=1, keepdims=True))
    total = jnp.sum(jnp.where(lanes < kinds, weights, 0.0), axis=1, keepdims=True)
    router = weights / total
    router_ref[...] = router
    high = router.astype(BF16).astype(F32)
    sent_ref[:, width:] = jnp.where(lanes < kinds, high, router - high).astype(BF16)


def middle(kinds, scalars, mixed, weights, x, gain, router_w, prior, prior_w):
    rows, width = x.shape
    lanes = router_w.shape[1]

    def whole(shape):
        return pl.BlockSpec(shape, lambda i, _: (0,) * len(shape))

    return pl.pallas_call(
        functools.partial(middle_kernel, kinds),
        grid_spec=pltpu.PrefetchScalarGridSpec(
            num_scalar_prefetch=1,
            grid=(1,),
            in_specs=[
                whole(mixed.shape),
                *[whole(item.shape) for item in weights],
                whole(x.shape),
                whole(gain.shape),
                whole(router_w.shape),
                pl.BlockSpec((rows, kinds), lambda i, scalars: (scalars[1], 0)),
                whole(prior_w.shape),
            ],
            out_specs=[whole((rows, width)), whole((rows, width + lanes)), whole((rows, lanes))],
        ),
        out_shape=[
            jax.ShapeDtypeStruct((rows, width), F32),
            jax.ShapeDtypeStruct((rows, width + lanes), BF16),
            jax.ShapeDtypeStruct((rows, lanes), F32),
        ],
        compiler_params=pltpu.CompilerParams(vmem_limit_bytes=48 * 2**20),
        cost_estimate=cost_of(6),
        name="middle",
    )(scalars, mixed, *weights, x, gain, router_w, prior, prior_w)


def router_back_kernel(kinds, experts, scalars, near_ref, far_ref, hidden_ref, router_ref,
                       routes_ref, cotangent_ref, prior_ref, gain_ref, small_ref, small_t_ref,
                       vector_ref, prior_w_ref,
                       grad_hidden_ref, grad_low_ref, partial_ref, grad_prior_ref, sums_ref):
    step = pl.program_id(0)
    rows, width = hidden_ref.shape
    place = scalars[1] * rows * pl.num_programs(0) + step * rows
    valid = place + lax.broadcasted_iota(jnp.int32, (rows, 1), 0) < scalars[BOUNDS + 2]
    valid = jnp.where(valid, 1.0, 0.0)
    back = near_ref[...] + far_ref[...].astype(F32)
    hidden = hidden_ref[...]
    grad_out = cotangent_ref[...] * valid
    scale = lax.rsqrt(jnp.mean(hidden * hidden, axis=1, keepdims=True) + EPSILON)
    unit = hidden * scale
    normed = unit * gain_ref[...]
    router = router_ref[...]
    lanes = lax.broadcasted_iota(jnp.int32, router.shape, 1)
    routes = routes_ref[...]

    def column(array, k):
        return jnp.sum(jnp.where(lanes == k, array, 0.0), axis=1, keepdims=True)

    def named(kind):
        return jnp.where((routes[:, 0:1] == kind) | (routes[:, 1:2] == kind), 1.0, 0.0)

    copy, first, second = (named(experts + k) for k in (1, 2, 3))
    weight_copy = column(router, experts + 1) * copy
    weight_first = column(router, experts + 2) * first
    weight_second = column(router, experts + 3) * second
    mixlog = jnp.dot(normed, small_ref[...], precision=PRECISE, preferred_element_type=F32)

    def softmax_two(k):
        one, two = column(mixlog, k), column(mixlog, k + 1)
        highest = jnp.maximum(one, two)
        one, two = jnp.exp(one - highest), jnp.exp(two - highest)
        return one / (one + two), two / (one + two)

    mix_one, mix_two = softmax_two(kinds), softmax_two(kinds + 2)
    vector_one, vector_two = vector_ref[0:1, :], vector_ref[1:2, :]
    along = jnp.sum(normed * grad_out, axis=1, keepdims=True)
    along_one = jnp.sum(vector_one * grad_out, axis=1, keepdims=True)
    along_two = jnp.sum(vector_two * grad_out, axis=1, keepdims=True)

    extra = back[:, width:]
    pairs = jnp.where(lanes < kinds, extra, 0.0) + jnp.where(
        lanes < kinds, pltpu.roll(extra, extra.shape[1] - kinds, 1), 0.0
    )
    grad_router = pairs + jnp.where(lanes == experts + 1, copy * along, 0.0)
    grad_router += jnp.where(
        lanes == experts + 2, first * (mix_one[0] * along + mix_one[1] * along_one), 0.0
    )
    grad_router += jnp.where(
        lanes == experts + 3, second * (mix_two[0] * along + mix_two[1] * along_two), 0.0
    )
    held = jnp.where(lanes < kinds, router, 0.0)
    grad_small = held * (grad_router - jnp.sum(held * grad_router, axis=1, keepdims=True))
    grad_prior_ref[...] = jnp.dot(
        grad_small, prior_w_ref[...], precision=PRECISE, preferred_element_type=F32
    )[:, :kinds]
    grad_logits = grad_small

    def mixed_back(weight, mix, other, k):
        one, two = weight * along, weight * other
        inner = mix[0] * one + mix[1] * two
        return jnp.where(lanes == k, mix[0] * (one - inner), 0.0) + jnp.where(
            lanes == k + 1, mix[1] * (two - inner), 0.0
        )

    grad_mixlog = mixed_back(weight_first, mix_one, along_one, kinds) + mixed_back(
        weight_second, mix_two, along_two, kinds + 2
    )
    grad_small = grad_logits + grad_mixlog
    share = weight_copy + weight_first * mix_one[0] + weight_second * mix_two[0]
    grad_normed = (
        back[:, :width]
        + share * grad_out
        + jnp.dot(grad_small, small_t_ref[...], precision=PRECISE, preferred_element_type=F32)
    )
    through = grad_normed * gain_ref[...]
    inner = jnp.mean(through * hidden, axis=1, keepdims=True)
    grad_hidden = grad_out + scale * through - (scale * scale * scale * inner) * hidden
    grad_hidden_ref[...] = grad_hidden
    grad_low_ref[...] = grad_hidden.astype(BF16)
    vector_first, vector_second = weight_first * mix_one[1], weight_second * mix_two[1]
    partial_ref[...] = valid * (
        hidden + share * normed + vector_first * vector_one + vector_second * vector_two
    )

    @pl.when(step == 0)
    def _():
        sums_ref[...] = jnp.zeros_like(sums_ref)

    def turned_dot(left, right):
        return jnp.dot(left.T, right, precision=PRECISE, preferred_element_type=F32)

    rounded = normed.astype(BF16).astype(F32)
    vectors = jnp.where(lanes == kinds + 5, vector_first, 0.0) + jnp.where(
        lanes == kinds + 6, vector_second, 0.0
    )
    total = (
        turned_dot(grad_logits, rounded)
        + turned_dot(grad_mixlog, normed)
        + turned_dot(vectors, grad_out)
    )
    sums_ref[: kinds + 8, :] += total[: kinds + 8, :]
    sums_ref[kinds + 4 : kinds + 5, :] += jnp.sum(grad_normed * unit, axis=0, keepdims=True)
    prior = turned_dot(prior_ref[...], grad_logits)
    sums_ref[pl.ds(kinds + 8, kinds), : lanes.shape[1]] += prior


def router_back(kinds, experts, scalars, near, far, hidden, router, routes, cotangent, prior,
                gain, small, small_t, vector, prior_w):
    rows, width = hidden.shape
    block = rows // 4
    lanes = router.shape[1]

    def whole(shape):
        return pl.BlockSpec(shape, lambda i, _: (0,) * len(shape))

    def part(columns):
        return pl.BlockSpec((block, columns), lambda i, _: (i, 0))

    def mine(columns):
        return pl.BlockSpec((block, columns), lambda i, scalars: (scalars[1] * 4 + i, 0))

    return pl.pallas_call(
        functools.partial(router_back_kernel, kinds, experts),
        grid_spec=pltpu.PrefetchScalarGridSpec(
            num_scalar_prefetch=1,
            grid=(4,),
            in_specs=[
                part(width + lanes),
                part(width + lanes),
                part(width),
                part(lanes),
                mine(2),
                part(width),
                mine(kinds),
                whole(gain.shape),
                whole(small.shape),
                whole(small_t.shape),
                whole(vector.shape),
                whole(prior_w.shape),
            ],
            out_specs=[
                part(width),
                part(width),
                part(width),
                part(kinds),
                whole((32, width)),
            ],
        ),
        out_shape=[
            jax.ShapeDtypeStruct((rows, width), F32),
            jax.ShapeDtypeStruct((rows, width), BF16),
            jax.ShapeDtypeStruct((rows, width), F32),
            jax.ShapeDtypeStruct((rows, kinds), F32),
            jax.ShapeDtypeStruct((32, width), F32),
        ],
        compiler_params=pltpu.CompilerParams(vmem_limit_bytes=48 * 2**20),
        cost_estimate=cost_of(8),
        name="router_back",
    )(scalars, near, far, hidden, router, routes, cotangent, prior, gain, small, small_t,
      vector, prior_w)


def two_parts(value):
    high = lax.reduce_precision(value, 8, 7)
    return jnp.concatenate([high, value - high], axis=-1).astype(BF16)


def after(value, *others):
    return lax.optimization_barrier((value, *others))[0]


def everywhere(value, axes, count):
    copies = jnp.broadcast_to(value[None], (count, *value.shape))
    return lax.all_to_all(copies, axes, 0, 0, tiled=True)


def flip(value, axis, size, bit):
    return lax.ppermute(value, axis, [(i, i ^ bit) for i in range(size)])


def gather_rows(value, many):
    if many != 2:
        full = lax.all_gather(value, ("hi", "lo"), axis=0, tiled=True)
        return list(full.reshape(SHARDS, -1, full.shape[1]))
    return [value] + [flip(value, ("hi", "lo"), SHARDS, bit) for bit in range(1, SHARDS)]


def scatter_rows(pieces, many):
    if many != 2:
        full = jnp.concatenate(pieces).astype(F32)
        return lax.psum_scatter(full, ("hi", "lo"), scatter_dimension=0, tiled=True)
    total = pieces[0].astype(F32)
    for bit in range(1, SHARDS):
        total = total + flip(pieces[bit], ("hi", "lo"), SHARDS, bit).astype(F32)
    return total


def per_device(
    many,
    inputs,
    cotangent,
    lengths,
    routes,
    drop_order,
    prior_logits,
    attn_gain,
    w_query,
    w_key,
    w_value,
    w_out,
    moe_gain,
    w_router,
    w_prior,
    w_const,
    const_vector,
    w_gate,
    w_up,
    w_down,
):
    tok_rows, width = inputs.shape
    group = tok_rows * 4
    kinds = w_router.shape[1]
    experts, shard_rows, shard_units = w_gate.shape
    capacity = 3 * group // 16
    share = capacity // 2
    slots = LOW * share
    local_width = w_query.shape[1]
    heads = local_width // HEAD
    tp_axes = ("y", "c")
    all_axes = ("hi", "lo", "y", "c")
    count = many * LOW * 4
    wide = width + 128
    high = lax.axis_index("hi")
    parity = lax.axis_index("y")
    core = lax.axis_index("c")
    place_in_group = parity * 2 + core
    mine = high * LOW + lax.axis_index("lo") if many == 2 else jnp.zeros_like(high)
    boundary = jnp.cumsum(lengths[0])
    scalars = jnp.concatenate(
        [jnp.stack([mine, place_in_group, parity, core]), boundary[:-1]]
    ).astype(jnp.int32)
    gain_one, gain_two = attn_gain.reshape(1, width), moe_gain.reshape(1, width)

    normed_one = rms_norm(inputs, attn_gain).astype(BF16)
    normed_pieces = gather_pieces(normed_one)
    attn_shard = jnp.concatenate([w_query, w_key, w_value, w_out.T], axis=1)
    attn_shards = gather_rows(attn_shard, many)
    expert_shards = jnp.stack([w_gate, w_up, w_down.transpose(0, 2, 1)], axis=1)
    expert_part = lax.all_to_all(expert_shards, ("lo", "y"), 0, 0, tiled=True)
    expert_part = expert_part.reshape(LOW, 2, 3, shard_rows, shard_units)
    if many == 2:
        expert_near = expert_part
        expert_far = [swap(expert_part[i : i + 1], "hi") for i in range(LOW)]
        high_place = high
    else:
        rows = lax.all_gather(expert_part, "hi", axis=0).transpose(2, 3, 0, 1, 4, 5)
        rows = rows.reshape(2, 3, 2, LOW, width // (2 * LOW), shard_units)
        rows = rows.transpose(2, 3, 0, 1, 4, 5)
        expert_near = rows[0]
        expert_far = [rows[1, i : i + 1] for i in range(LOW)]
        high_place = jnp.zeros_like(high)
    router_lanes = jnp.pad(jnp.concatenate([w_router, w_router], axis=1), ((0, 0), (0, 128 - 2 * kinds)))
    prior_lanes = jnp.pad(jnp.concatenate([w_prior, w_prior], axis=1), ((0, 0), (0, 128 - 2 * kinds)))
    const_flat = w_const.transpose(1, 0, 2).reshape(width, 4)
    small = jnp.pad(jnp.concatenate([w_router, const_flat], axis=1), ((0, 0), (0, 112 - kinds + 12)))
    small_t = small.T
    prior_back = jnp.pad(w_prior.T, ((0, 128 - kinds), (0, 128 - kinds)))

    valid_mine = place_in_group * tok_rows + jnp.arange(tok_rows)[:, None] < boundary[-2]
    valid_mine = valid_mine.astype(F32)
    grad_out_low = (cotangent * valid_mine).astype(BF16)
    grad_out_pieces = gather_pieces(after(grad_out_low, normed_pieces[3]))
    mixed, lse, qkv, qkv_full, out_full = attend(normed_pieces, attn_shards, scalars, heads)
    mixed, expert_far[0], grad_out_pieces = lax.optimization_barrier(
        (mixed, expert_far[0], grad_out_pieces)
    )

    mixed_mine = lax.all_to_all(mixed, tp_axes, 0, 0, tiled=True)
    out_pieces = gather_pieces(out_full)
    ids_rows, ids_cols = slots_of(
        after(scalars, mixed), routes, drop_order, experts, capacity
    )
    grad_out_slots = pick(ids_rows, grad_out_pieces, slots)
    mixed_mine, grad_out_slots, ids_cols, out_pieces = lax.optimization_barrier(
        (mixed_mine, grad_out_slots, ids_cols, out_pieces)
    )

    hidden, sent_two, router = middle(
        kinds, scalars, mixed_mine, out_pieces, inputs, gain_two, router_lanes, prior_logits, prior_lanes
    )
    sent_two, expert_far[1] = lax.optimization_barrier((sent_two, expert_far[1]))

    pieces_two = gather_pieces(sent_two)
    grad_taken = lax.all_to_all(
        grad_out_slots.reshape(LOW, share, width), "lo", 0, 0, tiled=True
    ).reshape(slots, width)
    pieces_two, grad_taken, expert_far[2] = lax.optimization_barrier(
        (pieces_two, grad_taken, expert_far[2])
    )

    grad_core = swap(grad_taken, "c")
    sent_slots = pick(ids_rows, pieces_two, slots)
    taken = lax.all_to_all(sent_slots.reshape(LOW, share, wide), "lo", 0, 0, tiled=True)
    taken = taken.reshape(slots, wide)
    qkv_pieces = gather_pieces(after(qkv_full, sent_slots))
    taken, qkv_pieces, expert_far[3] = lax.optimization_barrier(
        (taken, qkv_pieces, expert_far[3])
    )

    expert = lax.axis_index("lo") * 2 + parity
    back_own, back_send, feed_own, feed_send, grads_own, *grads_far = expert_pass(
        kinds, jnp.stack([high_place, expert]).astype(jnp.int32),
        taken, swap(taken, "c"), grad_taken, grad_core, expert_near, expert_far,
    )

    if many == 2:
        grads_far = [swap(item, "hi") for item in grads_far]
    back_core = swap(back_send, "c").astype(F32)
    inner = (
        back_own[:, width : width + kinds]
        + back_core[:, width : width + kinds]
        + back_core[:, width + kinds : width + 2 * kinds]
    )
    back_slots = jnp.concatenate(
        [
            (back_own[:, :width] + back_core[:, :width]).astype(BF16),
            jnp.pad(two_parts(inner), ((0, 0), (0, 128 - 2 * kinds))),
        ],
        axis=1,
    )
    feed_slots = (feed_own + swap(feed_send, "c").astype(F32)).astype(BF16)
    back_taken = lax.all_to_all(back_slots.reshape(LOW, share, wide), "lo", 0, 0, tiled=True)
    back_taken, feed_slots, grads_far[0] = lax.optimization_barrier(
        (back_taken.reshape(slots, wide), feed_slots, grads_far[0])
    )

    back_near, back_other = add_core(*spread(ids_cols, back_taken, tok_rows))
    back_far = swap(back_other, "y")
    feed_taken = lax.all_to_all(feed_slots.reshape(LOW, share, width), "lo", 0, 0, tiled=True)
    back_far, feed_taken, grads_far[1] = lax.optimization_barrier(
        (back_far, feed_taken.reshape(slots, width), grads_far[1])
    )

    grad_hidden, grad_low, partial, grad_prior, sums = router_back(
        kinds, experts, scalars, back_near, back_far, hidden, router, routes, cotangent,
        prior_logits, gain_two, small, small_t, const_vector, prior_back,
    )
    grad_attn_pieces = gather_pieces(grad_low)
    feed_near, feed_other = add_core(*spread(ids_cols, feed_taken, tok_rows))
    share_sums = lax.all_to_all(sums.reshape(count, 32 * width // count), all_axes, 0, 0, tiled=True)
    share_sums = jnp.sum(share_sums, axis=0)
    grad_attn_pieces, grads_far, feed_near, feed_other, share_sums = lax.optimization_barrier(
        (grad_attn_pieces, grads_far, feed_near, feed_other, share_sums)
    )

    feed_far = swap(feed_other, "y")
    grad_attn_all = natural(grad_attn_pieces, place_in_group)
    grad_mixed = lax.dot_general(
        out_full,
        grad_attn_all.reshape(group, width),
        (((0,), (1,)), ((), ())),
        preferred_element_type=F32,
    ).astype(BF16)
    far_grads = jnp.concatenate(grads_far).reshape(grads_own.shape)
    if many == 2:
        weight_part = (grads_own + far_grads.astype(F32)).astype(BF16)
    else:
        rows = jnp.stack([grads_own, far_grads.astype(F32)])
        rows = rows.transpose(2, 3, 0, 1, 4, 5).reshape(
            2, 3, many, LOW, shard_rows, shard_units
        )
        weight_part = (
            lax.psum_scatter(rows, "hi", scatter_dimension=2).transpose(2, 0, 1, 3, 4).astype(BF16)
        )
    weight_own = lax.all_to_all(
        weight_part.reshape(2 * LOW, 3, shard_rows, shard_units), ("lo", "y"), 0, 0, tiled=True
    )
    grad_qkv = attend_back(qkv, grad_mixed, scalars, lse, heads).reshape(
        4, 3 * local_width, tok_rows
    )
    grad_qkv, weight_own, feed_far = lax.optimization_barrier((grad_qkv, weight_own, feed_far))

    grad_qkv_mine = lax.all_to_all(grad_qkv, tp_axes, 0, 0, tiled=True)
    weight_own = weight_own.astype(F32)
    output = partial + valid_mine * (feed_near + feed_far.astype(F32))
    grad_attn_own = scatter_rows(
        attn_grads(grad_qkv, mixed, normed_pieces, grad_attn_pieces, scalars), many
    )
    grad_inputs, gain_part = inputs_back(
        scalars, grad_qkv_mine, qkv_pieces, inputs, gain_one, grad_hidden
    )
    last = everywhere(
        jnp.concatenate([gain_part.reshape(-1), share_sums]), all_axes, count
    )
    grad_gain = jnp.sum(last[:, :width], axis=0)
    total = last[:, width:].reshape(32, width)
    return (
        output,
        grad_inputs,
        grad_prior,
        grad_gain,
        grad_attn_own[:, :local_width],
        grad_attn_own[:, local_width : 2 * local_width],
        grad_attn_own[:, 2 * local_width : 3 * local_width],
        grad_attn_own[:, 3 * local_width :].T,
        total[kinds + 4],
        total[:kinds].T,
        total[kinds + 8 : 2 * kinds + 8, :kinds],
        total[kinds : kinds + 4].reshape(2, 2, width).transpose(0, 2, 1),
        total[kinds + 5 : kinds + 7],
        weight_own[:, 0],
        weight_own[:, 1],
        weight_own[:, 2].transpose(0, 2, 1),
    )


def solution(mesh):
    many = mesh.shape["fsdp"] // LOW
    fine = Mesh(mesh.devices.reshape(many, LOW, 2, 2), ("hi", "lo", "y", "c"))
    fsdp, tp = ("hi", "lo"), ("y", "c")
    every = fsdp + tp
    return jax.shard_map(
        functools.partial(per_device, many),
        mesh=fine,
        in_specs=(
            P(every, None),
            P(every, None),
            P(fsdp, None),
            P(fsdp, None),
            P(fsdp, None),
            P(fsdp, None),
            P(),
            P(fsdp, tp),
            P(fsdp, tp),
            P(fsdp, tp),
            P(tp, fsdp),
            P(),
            P(),
            P(),
            P(),
            P(),
            P(None, fsdp, tp),
            P(None, fsdp, tp),
            P(None, tp, fsdp),
        ),
        out_specs=(
            P(every, None),
            P(every, None),
            P(every, None),
            P(),
            P(fsdp, tp),
            P(fsdp, tp),
            P(fsdp, tp),
            P(tp, fsdp),
            P(),
            P(),
            P(),
            P(),
            P(),
            P(None, fsdp, tp),
            P(None, fsdp, tp),
            P(None, tp, fsdp),
        ),
        check_vma=False,
    )
```

```python
import functools

import jax
import jax.numpy as jnp
from jax import lax
from jax.experimental import pallas as pl
from jax.experimental.pallas import tpu as pltpu
from jax.sharding import Mesh
from jax.sharding import PartitionSpec as P

HEAD = 64
MAXLEN = 768
LOW = 4
SHARDS = 8
LOW_PLACE = 4
BOUNDS = 5
EPSILON = 1e-06
PRECISE = lax.Precision.HIGHEST
NEGATIVE = -1e30
F32 = jnp.float32
BF16 = jnp.bfloat16


def rms_norm(values, gain):
    return values * lax.rsqrt(jnp.mean(values * values, axis=-1, keepdims=True) + EPSILON) * gain


def swap(value, axis):
    return lax.ppermute(value, axis, [(0, 1), (1, 0)])


def gather_pieces(value):
    other = swap(value, "y")
    return [value, swap(value, "c"), other, swap(other, "c")]


def natural(pieces, index):
    ordered = []
    for j in range(4):
        item = pieces[j]
        for t in range(1, 4):
            item = jnp.where(index == t, pieces[j ^ t], item)
        ordered.append(item)
    return jnp.stack(ordered)


def add_core(near, sent):
    got = swap(sent, "c").astype(F32)
    return near[0] + got[0], (near[1] + got[1]).astype(BF16)


def cost_of(microseconds):
    return pl.CostEstimate(
        flops=int(microseconds * 1.15e9), transcendentals=0, bytes_accessed=2**20
    )


def scores_mask(first_key, first_query, window, block, scalars):
    row = first_query + lax.broadcasted_iota(jnp.int32, (1, block), 1)
    start_row = jnp.zeros_like(row)
    for k in range(BOUNDS, scalars.shape[0]):
        start_row = jnp.where(row >= scalars[k], scalars[k], start_row)
    key_places = first_key + lax.broadcasted_iota(jnp.int32, (window, block), 0)
    query_places = first_query + lax.broadcasted_iota(jnp.int32, (window, block), 1)
    return (key_places >= start_row) & (key_places <= query_places)


def attend_kernel(block, pad, scalars, *refs):
    pieces, refs = refs[:4], refs[4:]
    shards, refs = refs[:LOW], refs[LOW:]
    out_ref, lse_ref, qkv_ref, weight_ref, last_ref, key_rows, value_pad, full = refs
    group = qkv_ref.shape[1]
    window = pad + block
    quarter = group // 4
    inner = qkv_ref.shape[0] // 3
    head = pl.program_id(0)

    @pl.when(head == 0)
    def _():
        rows = shards[0].shape[1]
        for r in range(SHARDS):
            place = pl.multiple_of((scalars[0] ^ r) * rows, rows)
            full[pl.ds(place, rows), :] = shards[r % LOW][r // LOW]
        weight_ref[...] = full[:, : 3 * inner]
        last_ref[...] = full[:, 3 * inner :]
        turned = full[:, : 3 * inner].T
        for r in range(4):
            place = pl.multiple_of((scalars[1] ^ r) * quarter, quarter)
            qkv_ref[:, pl.ds(place, quarter)] = lax.dot_general(
                turned, pieces[r][...], (((1,), (1,)), ((), ())), preferred_element_type=F32
            ).astype(BF16)

    first_row = pl.multiple_of(head * HEAD, HEAD)
    key_rows[pl.ds(0, pad), :] = jnp.zeros((pad, HEAD), BF16)
    value_pad[:, pl.ds(0, pad)] = jnp.zeros((HEAD, pad), BF16)
    key_rows[pl.ds(pad, group), :] = qkv_ref[pl.ds(inner + first_row, HEAD), :].T
    value_pad[:, pl.ds(pad, group)] = qkv_ref[pl.ds(2 * inner + first_row, HEAD), :]

    def one(i, carry):
        first = pl.multiple_of(i * block, block)
        scores = jnp.dot(
            key_rows[pl.ds(first, window), :],
            qkv_ref[pl.ds(first_row, HEAD), pl.ds(first, block)],
            preferred_element_type=F32,
        )
        allowed = scores_mask(first - pad, first, window, block, scalars)
        scores = jnp.where(allowed, scores * 0.125, NEGATIVE)
        highest = jnp.max(scores, axis=0, keepdims=True)
        weights = jnp.exp(scores - highest)
        total = jnp.sum(weights, axis=0, keepdims=True)
        mixed = jnp.dot(
            value_pad[:, pl.ds(first, window)], weights.astype(BF16), preferred_element_type=F32
        )
        mixed = (mixed / total).astype(BF16)
        out_ref[first // quarter, :, pl.ds(pl.multiple_of(first % quarter, block), block)] = mixed
        lse_ref[0, :, pl.ds(first, block)] = highest + jnp.log(total)
        return carry

    lax.fori_loop(0, group // block, one, 0)


def attend(pieces, shards, scalars, heads):
    rows, width = pieces[0].shape
    group = 4 * rows
    inner = heads * HEAD
    block = 256

    def whole(shape):
        return pl.BlockSpec(
            shape, lambda i, _: (0,) * len(shape), pipeline_mode=pl.Buffered(1)
        )

    return pl.pallas_call(
        functools.partial(attend_kernel, block, MAXLEN),
        grid_spec=pltpu.PrefetchScalarGridSpec(
            num_scalar_prefetch=1,
            grid=(heads,),
            in_specs=[
                *[whole((rows, width)) for _ in range(4)],
                *[whole(shards[0].shape) for _ in range(LOW)],
            ],
            out_specs=[
                pl.BlockSpec((4, HEAD, rows), lambda h, _: (0, h, 0)),
                pl.BlockSpec((1, 1, group), lambda h, _: (h, 0, 0)),
                whole((3 * inner, group)),
                whole((width, 3 * inner)),
                whole((width, inner)),
            ],
            scratch_shapes=[
                pltpu.VMEM((MAXLEN + group, HEAD), BF16),
                pltpu.VMEM((HEAD, MAXLEN + group), BF16),
                pltpu.VMEM((width, 4 * inner), BF16),
            ],
        ),
        out_shape=[
            jax.ShapeDtypeStruct((4, inner, rows), BF16),
            jax.ShapeDtypeStruct((heads, 1, group), F32),
            jax.ShapeDtypeStruct((3 * inner, group), BF16),
            jax.ShapeDtypeStruct((width, 3 * inner), BF16),
            jax.ShapeDtypeStruct((width, inner), BF16),
        ],
        compiler_params=pltpu.CompilerParams(vmem_limit_bytes=48 * 2**20),
        cost_estimate=cost_of(24),
        name="attend",
    )(scalars, *pieces, *shards)


def attn_grads_kernel(scalars, *refs):
    grad_qkv, mixed, refs = refs[0], refs[1], refs[2:]
    tokens, grads, refs = refs[:4], refs[4:8], refs[8:]
    outs, (total,) = refs[:2], refs[2:]
    inner3 = grad_qkv.shape[1]
    first, second = 0.0, 0.0
    for r in range(4):
        j = scalars[1] ^ r
        first += jnp.dot(grad_qkv[j], tokens[r][...], preferred_element_type=F32)
        second += jnp.dot(mixed[j], grads[r][...], preferred_element_type=F32)
    total[:, :inner3] = first.T.astype(BF16)
    total[:, inner3:] = second.T.astype(BF16)
    rows = outs[0].shape[1]
    for r in range(SHARDS):
        place = pl.multiple_of((scalars[0] ^ r) * rows, rows)
        outs[r // LOW][r % LOW] = total[pl.ds(place, rows), :]


def attn_grads(grad_qkv, mixed, tokens, grads, scalars):
    width = tokens[0].shape[1]
    columns = grad_qkv.shape[1] + mixed.shape[1]
    rows = width // SHARDS
    whole = pl.BlockSpec(memory_space=pltpu.VMEM)
    return pl.pallas_call(
        attn_grads_kernel,
        in_specs=[pl.BlockSpec(memory_space=pltpu.SMEM)] + [whole] * 10,
        out_specs=[whole] * 2,
        out_shape=[jax.ShapeDtypeStruct((LOW, rows, columns), BF16)] * 2,
        scratch_shapes=[pltpu.VMEM((width, columns), BF16)],
        compiler_params=pltpu.CompilerParams(vmem_limit_bytes=48 * 2**20),
        cost_estimate=cost_of(8),
        name="attn_grads",
    )(scalars, grad_qkv, mixed, *tokens, *grads)


def attend_back_kernel(block, pad, scalars, qkv_ref, lse_ref, last_ref, *refs):
    pieces, refs = refs[:4], refs[4:]
    out_ref, grad_mixed, key_rows, value_rows, key_pad, grad_key, grad_value = refs
    group = qkv_ref.shape[1]
    inner_rows = qkv_ref.shape[0] // 3
    window = pad + block
    quarter = group // 4
    contract_last = (((1,), (1,)), ((), ()))
    head = pl.program_id(0)

    @pl.when(head == 0)
    def _():
        turned = last_ref[...].T
        for r in range(4):
            place = pl.multiple_of((scalars[1] ^ r) * quarter, quarter)
            grad_mixed[:, pl.ds(place, quarter)] = lax.dot_general(
                turned, pieces[r][...], contract_last, preferred_element_type=F32
            ).astype(BF16)

    first_row = pl.multiple_of(head * HEAD, HEAD)
    keys = qkv_ref[pl.ds(inner_rows + first_row, HEAD), :]
    key_rows[pl.ds(0, pad), :] = jnp.zeros((pad, HEAD), BF16)
    value_rows[pl.ds(0, pad), :] = jnp.zeros((pad, HEAD), BF16)
    key_pad[:, pl.ds(0, pad)] = jnp.zeros((HEAD, pad), BF16)
    key_rows[pl.ds(pad, group), :] = keys.T
    value_rows[pl.ds(pad, group), :] = qkv_ref[pl.ds(2 * inner_rows + first_row, HEAD), :].T
    key_pad[:, pl.ds(pad, group)] = keys
    grad_key[...] = jnp.zeros_like(grad_key)
    grad_value[...] = jnp.zeros_like(grad_value)

    def one(i, carry):
        first = pl.multiple_of(i * block, block)
        query = qkv_ref[pl.ds(first_row, HEAD), pl.ds(first, block)]
        grad = grad_mixed[pl.ds(first_row, HEAD), pl.ds(first, block)]
        scores = jnp.dot(key_rows[pl.ds(first, window), :], query, preferred_element_type=F32)
        allowed = scores_mask(first - pad, first, window, block, scalars)
        exponent = jnp.where(allowed, scores * 0.125 - lse_ref[0, :, pl.ds(first, block)], NEGATIVE)
        probs = jnp.exp(exponent)
        grad_probs = jnp.dot(
            value_rows[pl.ds(first, window), :], grad, preferred_element_type=F32
        )
        inner = jnp.sum(probs * grad_probs, axis=0, keepdims=True)
        raw = (0.125 * (probs * (grad_probs - inner))).astype(BF16)
        grad_query = jnp.dot(key_pad[:, pl.ds(first, window)], raw, preferred_element_type=F32)
        out_ref[
            first // quarter, 0, :, pl.ds(pl.multiple_of(first % quarter, block), block)
        ] = grad_query.astype(BF16)
        grad_value[:, pl.ds(first, window)] += lax.dot_general(
            grad, probs.astype(BF16), contract_last, preferred_element_type=F32
        )
        grad_key[:, pl.ds(first, window)] += lax.dot_general(
            query, raw, contract_last, preferred_element_type=F32
        )
        return carry

    lax.fori_loop(0, group // block, one, 0)
    for j in range(4):
        out_ref[j, 1] = grad_key[:, pl.ds(pad + j * quarter, quarter)].astype(BF16)
        out_ref[j, 2] = grad_value[:, pl.ds(pad + j * quarter, quarter)].astype(BF16)


def attend_back(scalars, qkv, lse, last, pieces, heads):
    group = qkv.shape[1]
    block = 256

    def whole(shape):
        return pl.BlockSpec(
            shape, lambda i, _: (0,) * len(shape), pipeline_mode=pl.Buffered(1)
        )

    return pl.pallas_call(
        functools.partial(attend_back_kernel, block, MAXLEN),
        grid_spec=pltpu.PrefetchScalarGridSpec(
            num_scalar_prefetch=1,
            grid=(heads,),
            in_specs=[
                whole(qkv.shape),
                pl.BlockSpec((1, 1, group), lambda h, _: (h, 0, 0)),
                whole(last.shape),
                *[whole(item.shape) for item in pieces],
            ],
            out_specs=pl.BlockSpec((4, 3, HEAD, group // 4), lambda h, _: (0, 0, h, 0)),
            scratch_shapes=[
                pltpu.VMEM((heads * HEAD, group), BF16),
                pltpu.VMEM((MAXLEN + group, HEAD), BF16),
                pltpu.VMEM((MAXLEN + group, HEAD), BF16),
                pltpu.VMEM((HEAD, MAXLEN + group), BF16),
                pltpu.VMEM((HEAD, MAXLEN + group), F32),
                pltpu.VMEM((HEAD, MAXLEN + group), F32),
            ],
        ),
        out_shape=jax.ShapeDtypeStruct((4, 3, heads * HEAD, group // 4), BF16),
        compiler_params=pltpu.CompilerParams(vmem_limit_bytes=48 * 2**20),
        cost_estimate=cost_of(34),
        name="attend_back",
    )(scalars, qkv, lse, last, *pieces)


def inputs_back_kernel(scalars, grads, p0, p1, p2, p3, x_ref, gain_ref, hidden_ref, out_ref, sum_ref):
    total = 0.0
    for r, weight in enumerate((p0, p1, p2, p3)):
        total += lax.dot_general(
            grads[scalars[1] ^ r].T, weight[...], (((1,), (1,)), ((), ())),
            preferred_element_type=F32,
        )
    x = x_ref[...]
    scale = lax.rsqrt(jnp.mean(x * x, axis=1, keepdims=True) + EPSILON)
    through = total * gain_ref[...]
    inner = jnp.mean(through * x, axis=1, keepdims=True)
    out_ref[...] = hidden_ref[...] + scale * through - (scale * scale * scale * inner) * x
    sum_ref[0] = jnp.sum(total * x * scale, axis=0, keepdims=True)


def inputs_back(scalars, grads, weights, x, gain, grad_hidden):
    rows, width = x.shape
    block = rows // 2

    def whole(shape):
        return pl.BlockSpec(shape, lambda i, _: (0,) * len(shape), pipeline_mode=pl.Buffered(1))

    part = pl.BlockSpec((block, width), lambda i, _: (i, 0))
    return pl.pallas_call(
        inputs_back_kernel,
        grid_spec=pltpu.PrefetchScalarGridSpec(
            num_scalar_prefetch=1,
            grid=(2,),
            in_specs=[
                pl.BlockSpec((4, grads.shape[1], block), lambda i, _: (0, 0, i)),
                *[whole(item.shape) for item in weights],
                part,
                whole(gain.shape),
                part,
            ],
            out_specs=[part, pl.BlockSpec((1, 1, width), lambda i, _: (i, 0, 0))],
        ),
        out_shape=[
            jax.ShapeDtypeStruct(x.shape, F32),
            jax.ShapeDtypeStruct((2, 1, width), F32),
        ],
        compiler_params=pltpu.CompilerParams(vmem_limit_bytes=48 * 2**20),
        cost_estimate=cost_of(6),
        name="inputs_back",
    )(scalars, grads, *weights, x, gain, grad_hidden)


def expert_kernel(
    kinds, scalars, w_gate, w_other, *refs
):
    x_blocks, g_blocks, refs = refs[: 2 * LOW], refs[2 * LOW : 4 * LOW], refs[4 * LOW :]
    back_own, back_send, feed_own, feed_send, grads_gate, grads_other, *refs = refs
    x_all, g_all, x_t, g_t, weights, hidden, acc_feed, acc_back, scales, plain = refs
    slots, width = feed_own.shape
    block = slots // LOW
    half = width // 2
    step = pl.program_id(0)
    contract_last = (((1,), (1,)), ((), ()))
    units = weights.shape[2]

    def weight_column(x_ref):
        extra = x_ref[:, width:].astype(F32)
        lanes = lax.broadcasted_iota(jnp.int32, extra.shape, 1)
        named = (lanes == scalars[0]) | (lanes == scalars[0] + kinds)
        return jnp.sum(jnp.where(named, extra, 0.0), axis=1, keepdims=True)

    @pl.when(step == 0)
    def _():
        for i in range(2 * LOW):
            rows = pl.ds(i * block, block)
            scale = weight_column(x_blocks[i])
            scales[rows, :] = jnp.broadcast_to(scale, (block, 128))
            plain[rows, :] = g_blocks[i][...]
            x_all[rows, :] = x_blocks[i][:, :width]
            g_all[rows, :] = (g_blocks[i][...].astype(F32) * scale).astype(BF16)
        x_t[...] = x_all[...].T
        g_t[...] = g_all[...].T
        acc_feed[...] = jnp.zeros_like(acc_feed)
        acc_back[...] = jnp.zeros_like(acc_back)

    for i in range(2):
        rows = pl.ds(i * half, half)
        weights[0, rows, :] = w_gate[i, :, 0].reshape(half, units)
        weights[1, rows, :] = w_other[i, :, 0, 0].reshape(half, units)
        weights[2, rows, :] = w_other[i, :, 0, 1].reshape(half, units)

    for part in range(2):
        rows = pl.ds(part * slots, slots)
        x = x_all[rows, :]
        gate = jnp.dot(x, weights[0], preferred_element_type=F32)
        up = jnp.dot(x, weights[1], preferred_element_type=F32)
        grad_act = jnp.dot(g_all[rows, :], weights[2], preferred_element_type=F32)
        sig = jax.nn.sigmoid(gate)
        silu = gate * sig
        active = (silu * up).astype(BF16)
        grad_gate = (grad_act * up * (sig * (1.0 + gate * (1.0 - sig)))).astype(BF16)
        grad_up = (grad_act * silu).astype(BF16)
        hidden[0, rows, :] = grad_gate
        hidden[1, rows, :] = grad_up
        hidden[2, rows, :] = active
        acc_feed[rows, :] += lax.dot_general(
            active, weights[2], contract_last, preferred_element_type=F32
        )
        acc_back[rows, :] += lax.dot_general(
            grad_gate, weights[0], contract_last, preferred_element_type=F32
        ) + lax.dot_general(grad_up, weights[1], contract_last, preferred_element_type=F32)

    for k in range(3):
        left = (g_t if k == 2 else x_t)
        grad = jnp.dot(left[...], hidden[k], preferred_element_type=F32).astype(BF16)
        for i in range(2):
            part = grad[i * half : (i + 1) * half].reshape(LOW, -1, units)
            if k == 0:
                grads_gate[i, :, 0] = part
            else:
                grads_other[i, :, 0, k - 1] = part

    @pl.when(step == pl.num_programs(0) - 1)
    def _():
        for part in range(2):
            rows = pl.ds(part * slots, slots)
            feed = acc_feed[rows, :]
            inner = jnp.sum(feed * plain[rows, :].astype(F32), axis=1, keepdims=True)
            feed = feed * scales[rows, 0:1]
            lanes = lax.broadcasted_iota(jnp.int32, (slots, 128), 1)
            if part == 0:
                back_own[:, :width] = acc_back[rows, :]
                back_own[:, width:] = jnp.where(lanes == scalars[0], inner, 0.0)
                feed_own[...] = feed
            else:
                high = inner.astype(BF16).astype(F32)
                extra = jnp.where(lanes == scalars[0], high, 0.0)
                extra = jnp.where(lanes == scalars[0] + kinds, inner - high, extra)
                back_send[:, :width] = acc_back[rows, :].astype(BF16)
                back_send[:, width:] = extra.astype(BF16)
                feed_send[...] = feed.astype(BF16)


def expert_pass(kinds, expert, x_blocks, g_blocks, w_gate, w_other):
    block, width = g_blocks[0].shape
    slots = LOW * block
    _, low, parities, _, shard_rows, shard_units = w_other.shape
    units = 256
    steps = shard_units // units

    def whole(shape):
        return pl.BlockSpec(
            shape, lambda i, _: (0,) * len(shape), pipeline_mode=pl.Buffered(1)
        )

    weight_specs = [
        pl.BlockSpec(
            (2, low, 1, shard_rows, units), lambda i, _: (0, 0, i // steps, 0, i % steps)
        ),
        pl.BlockSpec(
            (2, low, 1, 2, shard_rows, units), lambda i, _: (0, 0, i // steps, 0, 0, i % steps)
        ),
    ]
    wide = width + 128
    return pl.pallas_call(
        functools.partial(expert_kernel, kinds),
        grid_spec=pltpu.PrefetchScalarGridSpec(
            num_scalar_prefetch=1,
            grid=(parities * steps,),
            in_specs=[
                *weight_specs,
                *[whole((block, wide)) for _ in range(2 * LOW)],
                *[whole((block, width)) for _ in range(2 * LOW)],
            ],
            out_specs=[
                whole((slots, wide)),
                whole((slots, wide)),
                whole((slots, width)),
                whole((slots, width)),
                *weight_specs,
            ],
            scratch_shapes=[
                pltpu.VMEM((2 * slots, width), BF16),
                pltpu.VMEM((2 * slots, width), BF16),
                pltpu.VMEM((width, 2 * slots), BF16),
                pltpu.VMEM((width, 2 * slots), BF16),
                pltpu.VMEM((3, width, units), BF16),
                pltpu.VMEM((3, 2 * slots, units), BF16),
                pltpu.VMEM((2 * slots, width), F32),
                pltpu.VMEM((2 * slots, width), F32),
                pltpu.VMEM((2 * slots, 128), F32),
                pltpu.VMEM((2 * slots, width), BF16),
            ],
        ),
        out_shape=[
            jax.ShapeDtypeStruct((slots, wide), F32),
            jax.ShapeDtypeStruct((slots, wide), BF16),
            jax.ShapeDtypeStruct((slots, width), F32),
            jax.ShapeDtypeStruct((slots, width), BF16),
            jax.ShapeDtypeStruct(w_gate.shape, BF16),
            jax.ShapeDtypeStruct(w_other.shape, BF16),
        ],
        compiler_params=pltpu.CompilerParams(vmem_limit_bytes=58 * 2**20),
        cost_estimate=cost_of(35),
        name="expert_pass",
    )(expert.reshape(1), w_gate, w_other, *x_blocks, *g_blocks)


def pick_kernel(ids_ref, *refs):
    pieces, outs = refs[:4], refs[4:]
    block = outs[0].shape[0]
    rows = pieces[0].shape[0]
    for i, out_ref in enumerate(outs):
        slot = i * block + lax.broadcasted_iota(jnp.int32, (block, rows), 0)
        total = 0.0
        for r in range(4):
            columns = pl.ds(r * rows, rows)
            held = (slot == ids_ref[0:1, columns]) | (slot == ids_ref[1:2, columns])
            held = jnp.where(held, 1.0, 0.0).astype(BF16)
            total += jnp.dot(held, pieces[r][...], preferred_element_type=F32)
        out_ref[...] = total.astype(BF16)


def pick(ids, pieces, slots):
    rows, width = pieces[0].shape
    block = slots // LOW

    def whole(shape):
        return pl.BlockSpec(shape, lambda i: (0, 0))

    return pl.pallas_call(
        pick_kernel,
        grid=(1,),
        in_specs=[whole((8, 4 * rows)), *[whole((rows, width)) for _ in range(4)]],
        out_specs=[whole((block, width)) for _ in range(LOW)],
        out_shape=[jax.ShapeDtypeStruct((block, width), BF16) for _ in range(LOW)],
        compiler_params=pltpu.CompilerParams(vmem_limit_bytes=32 * 2**20),
        cost_estimate=cost_of(5),
        name="pick",
    )(ids, *pieces)


def to_experts(blocks):
    return [blocks[0]] + [flip(blocks[b], "lo", LOW, b) for b in range(1, LOW)]


def back_sum_kernel(kinds, own_ref, core_ref, *outs):
    width = own_ref.shape[1] - 128
    block = outs[0].shape[0]
    for i, out_ref in enumerate(outs):
        rows = pl.ds(i * block, block)
        out_ref[:, :width] = (
            own_ref[rows, :width] + core_ref[rows, :width].astype(F32)
        ).astype(BF16)
        extra = own_ref[rows, width:] + core_ref[rows, width:].astype(F32)
        lanes = lax.broadcasted_iota(jnp.int32, extra.shape, 1)
        high = jnp.where(lanes < kinds, extra, 0.0).astype(BF16).astype(F32)
        low = jnp.where(lanes < kinds, extra - high, 0.0)
        low = pltpu.roll(low, kinds, 1) + jnp.where(lanes >= kinds, extra, 0.0)
        out_ref[:, width:] = (high + low).astype(BF16)


def back_sum(kinds, own, core):
    slots, wide = own.shape
    block = slots // LOW

    def whole(shape):
        return pl.BlockSpec(shape, lambda i: (0, 0))

    return pl.pallas_call(
        functools.partial(back_sum_kernel, kinds),
        grid=(1,),
        in_specs=[whole(own.shape), whole(core.shape)],
        out_specs=[whole((block, wide)) for _ in range(LOW)],
        out_shape=[jax.ShapeDtypeStruct((block, wide), BF16) for _ in range(LOW)],
        compiler_params=pltpu.CompilerParams(vmem_limit_bytes=32 * 2**20),
        cost_estimate=cost_of(3),
        name="back_sum",
    )(own, core)


def feed_sum_kernel(own_ref, core_ref, *outs):
    block = outs[0].shape[0]
    for i, out_ref in enumerate(outs):
        rows = pl.ds(i * block, block)
        out_ref[...] = (own_ref[rows, :] + core_ref[rows, :].astype(F32)).astype(BF16)


def feed_sum(own, core):
    slots, width = own.shape
    block = slots // LOW

    def whole(shape):
        return pl.BlockSpec(shape, lambda i: (0, 0))

    return pl.pallas_call(
        feed_sum_kernel,
        grid=(1,),
        in_specs=[whole(own.shape), whole(core.shape)],
        out_specs=[whole((block, width)) for _ in range(LOW)],
        out_shape=[jax.ShapeDtypeStruct((block, width), BF16) for _ in range(LOW)],
        compiler_params=pltpu.CompilerParams(vmem_limit_bytes=32 * 2**20),
        cost_estimate=cost_of(3),
        name="feed_sum",
    )(own, core)


def spread_kernel(ids_ref, *refs):
    blocks, (near_ref, send_ref, slots_ref) = refs[:LOW], refs[LOW:]
    rows = near_ref.shape[1]
    slots = slots_ref.shape[0]
    block = slots // LOW

    @pl.when(pl.program_id(0) == 0)
    def _():
        for i in range(LOW):
            slots_ref[pl.ds(i * block, block), :] = blocks[i][...]

    for k, out_ref in enumerate((near_ref, send_ref)):
        slot = lax.broadcasted_iota(jnp.int32, (rows, slots), 1)
        ids = ids_ref[pl.ds(k * rows, rows), :]
        held = (slot == ids[:, 0:1]) | (slot == ids[:, 1:2])
        held = jnp.where(held, 1.0, 0.0).astype(BF16)
        total = jnp.dot(held, slots_ref[...], preferred_element_type=F32)
        out_ref[0] = total.astype(out_ref.dtype)


def spread(ids, values, rows):
    block, width = values[0].shape
    return pl.pallas_call(
        spread_kernel,
        grid=(2,),
        in_specs=[
            pl.BlockSpec((2 * rows, 8), lambda i: (i, 0)),
            *[pl.BlockSpec((block, width), lambda i: (0, 0)) for _ in range(LOW)],
        ],
        out_specs=[
            pl.BlockSpec((1, rows, width), lambda i: (i, 0, 0)),
            pl.BlockSpec((1, rows, width), lambda i: (i, 0, 0)),
        ],
        out_shape=[
            jax.ShapeDtypeStruct((2, rows, width), F32),
            jax.ShapeDtypeStruct((2, rows, width), BF16),
        ],
        scratch_shapes=[pltpu.VMEM((LOW * block, width), BF16)],
        compiler_params=pltpu.CompilerParams(vmem_limit_bytes=32 * 2**20),
        cost_estimate=cost_of(6),
        name="spread",
    )(ids, *values)


def slots_kernel(experts, capacity, scalars, routes_col, order_col, routes_row, order_row,
                 row_ref, col_ref, places_ref):
    group = routes_row.shape[1]
    rows = group // 4
    share = capacity // 2
    span = 2 * group
    bound = scalars[BOUNDS + 2]

    def target_of(routes, axis):
        place = lax.broadcasted_iota(jnp.int32, routes.shape, axis)
        return jnp.where((routes < experts) & (place < bound), routes, experts)

    target = target_of(routes_row[...], 1)
    code = target * span + order_row[...]
    block = 256

    def count(i, carry):
        first = pl.multiple_of(i * block, block)
        routes = routes_col[pl.ds(first, block), :]
        place = first + lax.broadcasted_iota(jnp.int32, routes.shape, 0)
        held = jnp.where((routes < experts) & (place < bound), routes, experts)
        others = held * span + order_col[pl.ds(first, block), :]
        result = []
        for k in range(2):
            total = carry[k]
            for j in range(2):
                smaller = jnp.where(others[:, j : j + 1] < code[k : k + 1, :], 1.0, 0.0)
                total = total + jnp.sum(smaller, axis=0, keepdims=True)
            result.append(total)
        return tuple(result)

    zero = jnp.zeros((1, group), F32)
    counts = lax.fori_loop(0, group // block, count, (zero, zero))
    for k in range(2):
        mine_target = target[k : k + 1, :]
        base = jnp.zeros((1, group), F32)
        for e in range(1, experts):
            earlier = jnp.sum(jnp.where(target < e, 1.0, 0.0))
            base = jnp.where(mine_target == e, earlier, base)
        place = (counts[k] - base).astype(jnp.int32)
        first = scalars[3] * share
        held = (
            (mine_target < experts)
            & (place >= first)
            & (place < first + share)
            & (place < capacity)
            & (jnp.bitwise_and(mine_target, 1) == scalars[2])
        )
        block = jnp.bitwise_xor(lax.shift_right_logical(mine_target, 1), scalars[LOW_PLACE])
        slot = block * share + place - first
        places_ref[k : k + 1, :] = jnp.where(held, slot, -1)
    for r in range(4):
        start = pl.multiple_of((scalars[1] ^ r) * rows, rows)
        piece = places_ref[:, pl.ds(start, rows)]
        row_ref[:, pl.ds(r * rows, rows)] = piece
        col_ref[pl.ds(r * rows, rows), :] = piece.T


def slots_of(scalars, routes, drop_order, experts, capacity):
    group = routes.shape[0]
    whole = pl.BlockSpec(memory_space=pltpu.VMEM)
    return pl.pallas_call(
        functools.partial(slots_kernel, experts, capacity),
        in_specs=[pl.BlockSpec(memory_space=pltpu.SMEM)] + [whole] * 4,
        out_specs=[whole] * 2,
        out_shape=[
            jax.ShapeDtypeStruct((8, group), jnp.int32),
            jax.ShapeDtypeStruct((group, 8), jnp.int32),
        ],
        scratch_shapes=[pltpu.VMEM((8, group), jnp.int32)],
        compiler_params=pltpu.CompilerParams(vmem_limit_bytes=32 * 2**20),
        cost_estimate=cost_of(8),
        name="slots",
    )(scalars, routes, drop_order, routes.T, drop_order.T)


def middle_kernel(kinds, scalars, mixed, p0, p1, p2, p3, x_ref, gain_ref, router_w, prior_ref,
                  prior_w, hidden_ref, sent_ref, router_ref, weight):
    hidden = x_ref[...]
    rows = p0.shape[2]
    for r, shards in enumerate((p0, p1, p2, p3)):
        for k in range(SHARDS):
            place = pl.multiple_of((scalars[0] ^ k) * rows, rows)
            weight[r, pl.ds(place, rows), :] = shards[k % LOW, k // LOW]
        hidden += lax.dot_general(
            mixed[scalars[1] ^ r].T, weight[r], (((1,), (1,)), ((), ())),
            preferred_element_type=F32,
        )
    hidden_ref[...] = hidden
    scale = lax.rsqrt(jnp.mean(hidden * hidden, axis=1, keepdims=True) + EPSILON)
    rounded = (hidden * scale * gain_ref[...]).astype(BF16)
    width = hidden.shape[1]
    sent_ref[:, :width] = rounded
    logits = jnp.dot(
        rounded.astype(F32), router_w[...], precision=PRECISE, preferred_element_type=F32
    ) + jnp.dot(prior_ref[...], prior_w[...], precision=PRECISE, preferred_element_type=F32)
    lanes = lax.broadcasted_iota(jnp.int32, logits.shape, 1)
    logits = jnp.where(lanes < 2 * kinds, logits, NEGATIVE)
    weights = jnp.exp(logits - jnp.max(logits, axis=1, keepdims=True))
    total = jnp.sum(jnp.where(lanes < kinds, weights, 0.0), axis=1, keepdims=True)
    router = weights / total
    router_ref[...] = router
    high = router.astype(BF16).astype(F32)
    sent_ref[:, width:] = jnp.where(lanes < kinds, high, router - high).astype(BF16)


def middle(kinds, scalars, mixed, weights, x, gain, router_w, prior, prior_w):
    rows, width = x.shape
    lanes = router_w.shape[1]

    def whole(shape):
        return pl.BlockSpec(shape, lambda i, _: (0,) * len(shape))

    return pl.pallas_call(
        functools.partial(middle_kernel, kinds),
        grid_spec=pltpu.PrefetchScalarGridSpec(
            num_scalar_prefetch=1,
            grid=(1,),
            in_specs=[
                whole(mixed.shape),
                *[whole(item.shape) for item in weights],
                whole(x.shape),
                whole(gain.shape),
                whole(router_w.shape),
                pl.BlockSpec((rows, kinds), lambda i, scalars: (scalars[1], 0)),
                whole(prior_w.shape),
            ],
            out_specs=[whole((rows, width)), whole((rows, width + lanes)), whole((rows, lanes))],
            scratch_shapes=[pltpu.VMEM((4, width, mixed.shape[1]), BF16)],
        ),
        out_shape=[
            jax.ShapeDtypeStruct((rows, width), F32),
            jax.ShapeDtypeStruct((rows, width + lanes), BF16),
            jax.ShapeDtypeStruct((rows, lanes), F32),
        ],
        compiler_params=pltpu.CompilerParams(vmem_limit_bytes=48 * 2**20),
        cost_estimate=cost_of(6),
        name="middle",
    )(scalars, mixed, *weights, x, gain, router_w, prior, prior_w)


def halves(value):
    high = value.astype(BF16)
    return high, (value - high.astype(F32)).astype(BF16)


def split_dot(left, right):
    (left_high, left_low), (right_high, right_low) = halves(left), halves(right)
    return (
        jnp.dot(left_high, right_high, preferred_element_type=F32)
        + jnp.dot(left_low, right_high, preferred_element_type=F32)
        + jnp.dot(left_high, right_low, preferred_element_type=F32)
    )


def turned_dot(left, right):
    high, low = halves(left.T)
    return jnp.dot(high, right, preferred_element_type=F32) + jnp.dot(
        low, right, preferred_element_type=F32
    )


def router_back_kernel(kinds, experts, scalars, near_ref, far_ref, hidden_ref, router_ref,
                       routes_ref, cotangent_ref, prior_ref, gain_ref, small_ref, small_t_ref,
                       vector_ref, prior_w_ref,
                       grad_hidden_ref, grad_low_ref, partial_ref, grad_prior_ref, sums_ref):
    step = pl.program_id(0)
    rows, width = hidden_ref.shape
    place = scalars[1] * rows * pl.num_programs(0) + step * rows
    valid = place + lax.broadcasted_iota(jnp.int32, (rows, 1), 0) < scalars[BOUNDS + 2]
    valid = jnp.where(valid, 1.0, 0.0)
    back = near_ref[...] + far_ref[...].astype(F32)
    hidden = hidden_ref[...]
    grad_out = cotangent_ref[...] * valid
    scale = lax.rsqrt(jnp.mean(hidden * hidden, axis=1, keepdims=True) + EPSILON)
    unit = hidden * scale
    normed = unit * gain_ref[...]
    router = router_ref[...]
    lanes = lax.broadcasted_iota(jnp.int32, router.shape, 1)
    routes = routes_ref[...]

    def column(array, k):
        return jnp.sum(jnp.where(lanes == k, array, 0.0), axis=1, keepdims=True)

    def named(kind):
        return jnp.where((routes[:, 0:1] == kind) | (routes[:, 1:2] == kind), 1.0, 0.0)

    copy, first, second = (named(experts + k) for k in (1, 2, 3))
    weight_copy = column(router, experts + 1) * copy
    weight_first = column(router, experts + 2) * first
    weight_second = column(router, experts + 3) * second
    mixlog = split_dot(normed, small_ref[...])

    def softmax_two(k):
        one, two = column(mixlog, k), column(mixlog, k + 1)
        highest = jnp.maximum(one, two)
        one, two = jnp.exp(one - highest), jnp.exp(two - highest)
        return one / (one + two), two / (one + two)

    mix_one, mix_two = softmax_two(kinds), softmax_two(kinds + 2)
    vector_one, vector_two = vector_ref[0:1, :], vector_ref[1:2, :]
    along = jnp.sum(normed * grad_out, axis=1, keepdims=True)
    along_one = jnp.sum(vector_one * grad_out, axis=1, keepdims=True)
    along_two = jnp.sum(vector_two * grad_out, axis=1, keepdims=True)

    extra = back[:, width:]
    pairs = jnp.where(lanes < kinds, extra, 0.0) + jnp.where(
        lanes < kinds, pltpu.roll(extra, extra.shape[1] - kinds, 1), 0.0
    )
    grad_router = pairs + jnp.where(lanes == experts + 1, copy * along, 0.0)
    grad_router += jnp.where(
        lanes == experts + 2, first * (mix_one[0] * along + mix_one[1] * along_one), 0.0
    )
    grad_router += jnp.where(
        lanes == experts + 3, second * (mix_two[0] * along + mix_two[1] * along_two), 0.0
    )
    held = jnp.where(lanes < kinds, router, 0.0)
    grad_small = held * (grad_router - jnp.sum(held * grad_router, axis=1, keepdims=True))
    grad_prior_ref[...] = split_dot(grad_small, prior_w_ref[...])[:, :kinds]
    grad_logits = grad_small

    def mixed_back(weight, mix, other, k):
        one, two = weight * along, weight * other
        inner = mix[0] * one + mix[1] * two
        return jnp.where(lanes == k, mix[0] * (one - inner), 0.0) + jnp.where(
            lanes == k + 1, mix[1] * (two - inner), 0.0
        )

    grad_mixlog = mixed_back(weight_first, mix_one, along_one, kinds) + mixed_back(
        weight_second, mix_two, along_two, kinds + 2
    )
    grad_small = grad_logits + grad_mixlog
    share = weight_copy + weight_first * mix_one[0] + weight_second * mix_two[0]
    grad_normed = (
        back[:, :width]
        + share * grad_out
        + split_dot(grad_small, small_t_ref[...])
    )
    through = grad_normed * gain_ref[...]
    inner = jnp.mean(through * hidden, axis=1, keepdims=True)
    grad_hidden = grad_out + scale * through - (scale * scale * scale * inner) * hidden
    grad_hidden_ref[...] = grad_hidden
    grad_low_ref[...] = grad_hidden.astype(BF16)
    vector_first, vector_second = weight_first * mix_one[1], weight_second * mix_two[1]
    partial_ref[...] = valid * (
        hidden + share * normed + vector_first * vector_one + vector_second * vector_two
    )

    @pl.when(step == 0)
    def _():
        sums_ref[...] = jnp.zeros_like(sums_ref)

    vectors = jnp.where(lanes == kinds + 5, vector_first, 0.0) + jnp.where(
        lanes == kinds + 6, vector_second, 0.0
    )
    low = normed.astype(BF16)
    total = turned_dot(grad_small, low) + turned_dot(vectors, grad_out.astype(BF16))
    sums_ref[: kinds + 8, :] += total[: kinds + 8, :]
    sums_ref[kinds + 4 : kinds + 5, :] += jnp.sum(grad_normed * unit, axis=0, keepdims=True)
    prior = split_dot(prior_ref[...].T, grad_logits)
    sums_ref[pl.ds(kinds + 8, kinds), : lanes.shape[1]] += prior


def router_back(kinds, experts, scalars, near, far, hidden, router, routes, cotangent, prior,
                gain, small, small_t, vector, prior_w):
    rows, width = hidden.shape
    block = rows // 2
    lanes = router.shape[1]

    def whole(shape):
        return pl.BlockSpec(shape, lambda i, _: (0,) * len(shape))

    def part(columns):
        return pl.BlockSpec((block, columns), lambda i, _: (i, 0))

    def mine(columns):
        return pl.BlockSpec((block, columns), lambda i, scalars: (scalars[1] * 2 + i, 0))

    return pl.pallas_call(
        functools.partial(router_back_kernel, kinds, experts),
        grid_spec=pltpu.PrefetchScalarGridSpec(
            num_scalar_prefetch=1,
            grid=(2,),
            in_specs=[
                part(width + lanes),
                part(width + lanes),
                part(width),
                part(lanes),
                mine(2),
                part(width),
                mine(kinds),
                whole(gain.shape),
                whole(small.shape),
                whole(small_t.shape),
                whole(vector.shape),
                whole(prior_w.shape),
            ],
            out_specs=[
                part(width),
                part(width),
                part(width),
                part(kinds),
                whole((32, width)),
            ],
        ),
        out_shape=[
            jax.ShapeDtypeStruct((rows, width), F32),
            jax.ShapeDtypeStruct((rows, width), BF16),
            jax.ShapeDtypeStruct((rows, width), F32),
            jax.ShapeDtypeStruct((rows, kinds), F32),
            jax.ShapeDtypeStruct((32, width), F32),
        ],
        compiler_params=pltpu.CompilerParams(vmem_limit_bytes=48 * 2**20),
        cost_estimate=cost_of(8),
        name="router_back",
    )(scalars, near, far, hidden, router, routes, cotangent, prior, gain, small, small_t,
      vector, prior_w)


def two_parts(value):
    high = lax.reduce_precision(value, 8, 7)
    return jnp.concatenate([high, value - high], axis=-1).astype(BF16)


def after(value, *others):
    return lax.optimization_barrier((value, *others))[0]


def everywhere(value, axes, count):
    copies = jnp.broadcast_to(value[None], (count, *value.shape))
    return lax.all_to_all(copies, axes, 0, 0, tiled=True)


def flip(value, axis, size, bit):
    return lax.ppermute(value, axis, [(i, i ^ bit) for i in range(size)])


def by_halves(value):
    if value.shape[0] == 2:
        return value
    rows, units = value.shape[-2:]
    middle_axes = tuple(range(2, value.ndim - 2))
    turned = value.transpose(*middle_axes, 0, 1, value.ndim - 2, value.ndim - 1)
    turned = turned.reshape(*turned.shape[:-4], 2, LOW, value.shape[0] * rows // 2, units)
    axes = turned.ndim
    return turned.transpose(axes - 4, axes - 3, *range(axes - 4), axes - 2, axes - 1)


def scatter_high(value, many):
    if many != 2:
        rows, units = value.shape[-2:]
        middle_axes = tuple(range(2, value.ndim - 2))
        turned = value.transpose(*middle_axes, 0, 1, value.ndim - 2, value.ndim - 1)
        turned = turned.reshape(*turned.shape[:-4], many, LOW, 2 * rows // many, units)
        axes = turned.ndim
        value = turned.transpose(axes - 4, axes - 3, *range(axes - 4), axes - 2, axes - 1)
    return lax.psum_scatter(value, "hi", scatter_dimension=0)


def gather_rows(value, later, many):
    if many != 2:
        full = lax.all_gather(value, ("hi", "lo"), axis=0, tiled=True)
        full = full.reshape(2, LOW, -1, full.shape[1])
        return [full[:, i] for i in range(LOW)], later
    far, later = lax.optimization_barrier((swap(value, "hi"), later))
    both = jnp.stack([value, far])
    return [both] + [flip(both, "lo", LOW, bit) for bit in range(1, LOW)], later


def scatter_rows(near, far, many):
    if many != 2:
        full = jnp.stack([near, far]).astype(F32).reshape(-1, near.shape[2])
        return lax.psum_scatter(full, ("hi", "lo"), scatter_dimension=0, tiled=True)
    both = near.astype(F32) + swap(far, "hi").astype(F32)
    total = both[0]
    for bit in range(1, LOW):
        total = total + flip(both[bit].astype(BF16), "lo", LOW, bit).astype(F32)
    return total


def per_device(
    many,
    inputs,
    cotangent,
    lengths,
    routes,
    drop_order,
    prior_logits,
    attn_gain,
    w_query,
    w_key,
    w_value,
    w_out,
    moe_gain,
    w_router,
    w_prior,
    w_const,
    const_vector,
    w_gate,
    w_up,
    w_down,
):
    tok_rows, width = inputs.shape
    group = tok_rows * 4
    kinds = w_router.shape[1]
    experts, shard_rows, shard_units = w_gate.shape
    capacity = 3 * group // 16
    share = capacity // 2
    slots = LOW * share
    local_width = w_query.shape[1]
    heads = local_width // HEAD
    tp_axes = ("y", "c")
    all_axes = ("hi", "lo", "y", "c")
    count = many * LOW * 4
    wide = width + 128
    high = lax.axis_index("hi")
    parity = lax.axis_index("y")
    core = lax.axis_index("c")
    place_in_group = parity * 2 + core
    mine = high * LOW + lax.axis_index("lo") if many == 2 else jnp.zeros_like(high)
    boundary = jnp.cumsum(lengths[0])
    scalars = jnp.concatenate(
        [jnp.stack([mine, place_in_group, parity, core, lax.axis_index("lo")]), boundary[:-1]]
    ).astype(jnp.int32)
    gain_one, gain_two = attn_gain.reshape(1, width), moe_gain.reshape(1, width)

    normed_one = rms_norm(inputs, attn_gain).astype(BF16)
    normed_other = swap(normed_one, "y")
    attn_shard = jnp.concatenate([w_query, w_key, w_value, w_out.T], axis=1)
    attn_shards, w_gate = gather_rows(attn_shard, w_gate, many)
    other_shards = jnp.stack([w_up, w_down.transpose(0, 2, 1)], axis=1)
    other_part = lax.all_to_all(other_shards, ("lo", "y"), 0, 0, tiled=True)
    other_part = other_part.reshape(LOW, 2, 2, shard_rows, shard_units)
    if many == 2:
        gate_far = swap(w_gate, "hi")
        gate_both = jnp.where(
            high == 0, jnp.stack([w_gate, gate_far], axis=1), jnp.stack([gate_far, w_gate], axis=1)
        )
    else:
        gate_both = lax.all_gather(w_gate, "hi", axis=1)
    gate_part = lax.all_to_all(gate_both, ("lo", "y"), 0, 0, tiled=True)
    gate_part = gate_part.reshape(LOW, 2, many, shard_rows, shard_units).transpose(2, 0, 1, 3, 4)
    ids_rows, ids_cols = slots_of(
        after(scalars, attn_shards[0]), routes, drop_order, experts, capacity
    )
    normed_other, attn_shards, other_part, ids_rows = lax.optimization_barrier(
        (normed_other, attn_shards, other_part, ids_rows)
    )
    w_other = by_halves(lax.all_gather(other_part, "hi"))
    out_mine = jnp.stack([item[:, :, 3 * local_width :] for item in attn_shards])
    out_other = swap(out_mine, "y")
    normed_pieces = [normed_one, swap(normed_one, "c"), normed_other, swap(normed_other, "c")]
    router_lanes = jnp.pad(jnp.concatenate([w_router, w_router], axis=1), ((0, 0), (0, 128 - 2 * kinds)))
    prior_lanes = jnp.pad(jnp.concatenate([w_prior, w_prior], axis=1), ((0, 0), (0, 128 - 2 * kinds)))
    const_flat = w_const.transpose(1, 0, 2).reshape(width, 4)
    small = jnp.pad(jnp.concatenate([w_router, const_flat], axis=1), ((0, 0), (0, 112 - kinds + 12)))
    small_t = small.T
    prior_back = jnp.pad(w_prior.T, ((0, 128 - kinds), (0, 128 - kinds)))
    attn_shards, router_lanes, prior_lanes, small, small_t, prior_back = lax.optimization_barrier(
        (attn_shards, router_lanes, prior_lanes, small, small_t, prior_back)
    )

    valid_mine = place_in_group * tok_rows + jnp.arange(tok_rows)[:, None] < boundary[-2]
    valid_mine = valid_mine.astype(F32)
    grad_out_low = (cotangent * valid_mine).astype(BF16)
    grad_out_other = swap(after(grad_out_low, normed_pieces[3]), "y")
    mixed, lse, qkv, qkv_full, out_full = attend(normed_pieces, attn_shards, scalars, heads)
    mixed, grad_out_other, gate_part, out_other = lax.optimization_barrier(
        (mixed, grad_out_other, gate_part, out_other)
    )
    out_pieces = [out_mine, swap(after(out_mine, mixed), "c"), out_other, swap(out_other, "c")]

    mixed_mine = lax.all_to_all(mixed, tp_axes, 0, 0, tiled=True)
    grad_out_pieces = [
        grad_out_low, swap(after(grad_out_low, mixed), "c"), grad_out_other, swap(grad_out_other, "c"),
    ]
    grad_out_slots = pick(ids_rows, grad_out_pieces, slots)
    mixed_mine, grad_out_slots = lax.optimization_barrier((mixed_mine, grad_out_slots))

    hidden, sent_two, router = middle(
        kinds, scalars, mixed_mine, out_pieces, inputs, gain_two, router_lanes, prior_logits, prior_lanes
    )

    pieces_two = gather_pieces(sent_two)
    grad_taken = to_experts(grad_out_slots)
    pieces_two, grad_taken = lax.optimization_barrier((pieces_two, grad_taken))

    grad_taken += [swap(item, "c") for item in grad_taken]
    sent_slots = pick(ids_rows, pieces_two, slots)
    taken = to_experts(sent_slots)
    taken += [swap(item, "c") for item in taken]
    qkv_pieces = gather_pieces(after(qkv_full, sent_slots[0]))
    taken, qkv_pieces = lax.optimization_barrier((taken, qkv_pieces))

    expert = lax.axis_index("lo") * 2 + parity
    back_own, back_send, feed_own, feed_send, grads_gate, grads_other = expert_pass(
        kinds, expert.astype(jnp.int32), taken, grad_taken, by_halves(gate_part), w_other
    )

    other_sum = scatter_high(grads_other, many)
    gate_sum = scatter_high(grads_gate, many)
    back_taken = to_experts(back_sum(kinds, back_own, swap(back_send, "c")))
    feed_core = swap(feed_send, "c")
    back_taken, feed_core = lax.optimization_barrier((back_taken, feed_core))

    back_near, back_other = add_core(*spread(ids_cols, back_taken, tok_rows))
    back_far = swap(back_other, "y")
    feed_taken = to_experts(feed_sum(feed_own, after(feed_core, back_other)))
    back_far, feed_taken = lax.optimization_barrier((back_far, feed_taken))

    grad_hidden, grad_low, partial, grad_prior, sums = router_back(
        kinds, experts, scalars, back_near, back_far, hidden, router, routes, cotangent,
        prior_logits, gain_two, small, small_t, const_vector, prior_back,
    )
    grad_attn_pieces = gather_pieces(grad_low)
    feed_near, feed_other = add_core(
        *spread(ids_cols, [after(item, grad_attn_pieces[2]) for item in feed_taken], tok_rows)
    )
    sums = after(sums, grad_attn_pieces[2])
    share_sums = lax.all_to_all(sums.reshape(count, 32 * width // count), all_axes, 0, 0, tiled=True)
    share_sums = jnp.sum(share_sums, axis=0)

    feed_far = swap(feed_other, "y")
    other_own = lax.all_to_all(
        other_sum.reshape(2 * LOW, 2, shard_rows, shard_units), ("lo", "y"), 0, 0, tiled=True
    )
    grad_qkv = attend_back(scalars, qkv, lse, out_full, grad_attn_pieces, heads).reshape(
        4, 3 * local_width, tok_rows
    )
    grad_qkv, other_own, feed_far, share_sums, gate_sum = lax.optimization_barrier(
        (grad_qkv, other_own, feed_far, share_sums, gate_sum)
    )

    grad_qkv_mine = lax.all_to_all(grad_qkv, tp_axes, 0, 0, tiled=True)
    gate_own = lax.all_to_all(
        after(gate_sum, grad_qkv_mine).reshape(2 * LOW, shard_rows, shard_units),
        ("lo", "y"), 0, 0, tiled=True,
    )
    output = partial + valid_mine * (feed_near + feed_far.astype(F32))
    grad_attn_own = scatter_rows(
        *attn_grads(grad_qkv, mixed, normed_pieces, grad_attn_pieces, scalars), many
    )
    grad_inputs, gain_part = inputs_back(
        scalars, grad_qkv_mine, qkv_pieces, inputs, gain_one, grad_hidden
    )
    last = everywhere(
        jnp.concatenate([jnp.sum(gain_part, axis=0).reshape(-1), share_sums]), all_axes, count
    )
    grad_gain = jnp.sum(last[:, :width], axis=0)
    total = last[:, width:].reshape(32, width)
    return (
        output,
        grad_inputs,
        grad_prior,
        grad_gain,
        grad_attn_own[:, :local_width],
        grad_attn_own[:, local_width : 2 * local_width],
        grad_attn_own[:, 2 * local_width : 3 * local_width],
        grad_attn_own[:, 3 * local_width :].T,
        total[kinds + 4],
        total[:kinds].T,
        total[kinds + 8 : 2 * kinds + 8, :kinds],
        total[kinds : kinds + 4].reshape(2, 2, width).transpose(0, 2, 1),
        total[kinds + 5 : kinds + 7],
        gate_own.astype(F32),
        other_own[:, 0].astype(F32),
        other_own[:, 1].transpose(0, 2, 1).astype(F32),
    )


def solution(mesh):
    many = mesh.shape["fsdp"] // LOW
    fine = Mesh(mesh.devices.reshape(many, LOW, 2, 2), ("hi", "lo", "y", "c"))
    fsdp, tp = ("hi", "lo"), ("y", "c")
    every = fsdp + tp
    return jax.shard_map(
        functools.partial(per_device, many),
        mesh=fine,
        in_specs=(
            P(every, None),
            P(every, None),
            P(fsdp, None),
            P(fsdp, None),
            P(fsdp, None),
            P(fsdp, None),
            P(),
            P(fsdp, tp),
            P(fsdp, tp),
            P(fsdp, tp),
            P(tp, fsdp),
            P(),
            P(),
            P(),
            P(),
            P(),
            P(None, fsdp, tp),
            P(None, fsdp, tp),
            P(None, tp, fsdp),
        ),
        out_specs=(
            P(every, None),
            P(every, None),
            P(every, None),
            P(),
            P(fsdp, tp),
            P(fsdp, tp),
            P(fsdp, tp),
            P(tp, fsdp),
            P(),
            P(),
            P(),
            P(),
            P(),
            P(None, fsdp, tp),
            P(None, fsdp, tp),
            P(None, tp, fsdp),
        ),
        check_vma=False,
    )
```

```python
import functools

import jax
import jax.numpy as jnp
from jax import lax
from jax.experimental import pallas as pl
from jax.experimental.pallas import tpu as pltpu
from jax.sharding import Mesh
from jax.sharding import PartitionSpec as P

HEAD = 64
MAXLEN = 768
LOW = 4
SHARDS = 8
LOW_PLACE = 4
BOUNDS = 5
EPSILON = 1e-06
PRECISE = lax.Precision.HIGHEST
NEGATIVE = -1e30
F32 = jnp.float32
BF16 = jnp.bfloat16


def rms_norm(values, gain):
    return values * lax.rsqrt(jnp.mean(values * values, axis=-1, keepdims=True) + EPSILON) * gain


def swap(value, axis):
    return lax.ppermute(value, axis, [(0, 1), (1, 0)])


def gather_pieces(value):
    other = swap(value, "y")
    return [value, swap(value, "c"), other, swap(other, "c")]


def natural(pieces, index):
    ordered = []
    for j in range(4):
        item = pieces[j]
        for t in range(1, 4):
            item = jnp.where(index == t, pieces[j ^ t], item)
        ordered.append(item)
    return jnp.stack(ordered)


def add_core(near, sent):
    got = swap(sent, "c")
    return got, (near[1] + got[1].astype(F32)).astype(BF16)


def cost_of(microseconds):
    return pl.CostEstimate(
        flops=int(microseconds * 1.15e9), transcendentals=0, bytes_accessed=2**20
    )


def start_of(row, scalars):
    start_row = jnp.zeros_like(row)
    for k in range(BOUNDS, scalars.shape[0]):
        start_row = jnp.where(row >= scalars[k], scalars[k], start_row)
    return start_row


def for_window(first, block, pad, scalars, body):
    needed = (first - start_of(first, scalars) + block - 1) // block
    most = pad // block
    for blocks in range(most):
        pl.when(needed == blocks)(functools.partial(body, (blocks + 1) * block))
    pl.when(needed >= most)(functools.partial(body, pad + block))


def scores_mask(first_key, first_query, window, block, scalars):
    row = first_query + lax.broadcasted_iota(jnp.int32, (1, block), 1)
    start_row = start_of(row, scalars)
    key_places = first_key + lax.broadcasted_iota(jnp.int32, (window, block), 0)
    query_places = first_query + lax.broadcasted_iota(jnp.int32, (window, block), 1)
    return (key_places >= start_row) & (key_places <= query_places)


def attend_kernel(block, pad, scalars, *refs):
    pieces, refs = refs[:4], refs[4:]
    shards, refs = refs[:LOW], refs[LOW:]
    out_ref, lse_ref, qkv_ref, weight_ref, last_ref, key_rows, value_pad, full = refs
    group = qkv_ref.shape[1]
    quarter = group // 4
    inner = qkv_ref.shape[0] // 3
    head = pl.program_id(0)

    @pl.when(head == 0)
    def _():
        rows = shards[0].shape[1]
        for r in range(SHARDS):
            place = pl.multiple_of((scalars[0] ^ r) * rows, rows)
            full[pl.ds(place, rows), :] = shards[r % LOW][r // LOW]
        last_ref[...] = full[:, 3 * inner :]
        turned = full[:, : 3 * inner].T
        weight_ref[...] = turned
        for r in range(4):
            place = pl.multiple_of((scalars[1] ^ r) * quarter, quarter)
            qkv_ref[:, pl.ds(place, quarter)] = lax.dot_general(
                turned, pieces[r][...], (((1,), (1,)), ((), ())), preferred_element_type=F32
            ).astype(BF16)

    first_row = pl.multiple_of(head * HEAD, HEAD)
    key_rows[pl.ds(0, pad), :] = jnp.zeros((pad, HEAD), BF16)
    value_pad[:, pl.ds(0, pad)] = jnp.zeros((HEAD, pad), BF16)
    key_rows[pl.ds(pad, group), :] = qkv_ref[pl.ds(inner + first_row, HEAD), :].T
    value_pad[:, pl.ds(pad, group)] = qkv_ref[pl.ds(2 * inner + first_row, HEAD), :]

    def one(i, carry):
        first = pl.multiple_of(i * block, block)

        def body(window):
            begin = pl.multiple_of(first + pad + block - window, block)
            scores = jnp.dot(
                key_rows[pl.ds(begin, window), :],
                qkv_ref[pl.ds(first_row, HEAD), pl.ds(first, block)],
                preferred_element_type=F32,
            )
            allowed = scores_mask(begin - pad, first, window, block, scalars)
            scores = jnp.where(allowed, scores * 0.125, NEGATIVE)
            highest = jnp.max(scores, axis=0, keepdims=True)
            weights = jnp.exp(scores - highest)
            total = jnp.sum(weights, axis=0, keepdims=True)
            mixed = jnp.dot(
                value_pad[:, pl.ds(begin, window)],
                weights.astype(BF16),
                preferred_element_type=F32,
            )
            mixed = (mixed / total).astype(BF16)
            column = pl.multiple_of(first % quarter, block)
            out_ref[first // quarter, :, pl.ds(column, block)] = mixed
            lse_ref[0, :, pl.ds(first, block)] = highest + jnp.log(total)

        for_window(first, block, pad, scalars, body)
        return carry

    lax.fori_loop(0, group // block, one, 0)


def attend(pieces, shards, scalars, heads):
    rows, width = pieces[0].shape
    group = 4 * rows
    inner = heads * HEAD
    block = 256

    def whole(shape):
        return pl.BlockSpec(
            shape, lambda i, _: (0,) * len(shape), pipeline_mode=pl.Buffered(1)
        )

    return pl.pallas_call(
        functools.partial(attend_kernel, block, MAXLEN),
        grid_spec=pltpu.PrefetchScalarGridSpec(
            num_scalar_prefetch=1,
            grid=(heads,),
            in_specs=[
                *[whole((rows, width)) for _ in range(4)],
                *[whole(shards[0].shape) for _ in range(LOW)],
            ],
            out_specs=[
                pl.BlockSpec((4, HEAD, rows), lambda h, _: (0, h, 0)),
                pl.BlockSpec((1, 1, group), lambda h, _: (h, 0, 0)),
                whole((3 * inner, group)),
                whole((3 * inner, width)),
                whole((width, inner)),
            ],
            scratch_shapes=[
                pltpu.VMEM((MAXLEN + group, HEAD), BF16),
                pltpu.VMEM((HEAD, MAXLEN + group), BF16),
                pltpu.VMEM((width, 4 * inner), BF16),
            ],
        ),
        out_shape=[
            jax.ShapeDtypeStruct((4, inner, rows), BF16),
            jax.ShapeDtypeStruct((heads, 1, group), F32),
            jax.ShapeDtypeStruct((3 * inner, group), BF16),
            jax.ShapeDtypeStruct((3 * inner, width), BF16),
            jax.ShapeDtypeStruct((width, inner), BF16),
        ],
        compiler_params=pltpu.CompilerParams(vmem_limit_bytes=48 * 2**20),
        cost_estimate=cost_of(24),
        name="attend",
    )(scalars, *pieces, *shards)


def attn_grads_kernel(scalars, *refs):
    grad_qkv, mixed, refs = refs[0], refs[1], refs[2:]
    tokens, grads, refs = refs[:4], refs[4:8], refs[8:]
    outs, (total,) = refs[:2], refs[2:]
    inner3 = grad_qkv.shape[1]
    first, second = 0.0, 0.0
    for r in range(4):
        j = scalars[1] ^ r
        first += jnp.dot(grad_qkv[j], tokens[r][...], preferred_element_type=F32)
        second += jnp.dot(mixed[j], grads[r][...], preferred_element_type=F32)
    total[:, :inner3] = first.T.astype(BF16)
    total[:, inner3:] = second.T.astype(BF16)
    rows = outs[0].shape[1]
    for r in range(SHARDS):
        place = pl.multiple_of((scalars[0] ^ r) * rows, rows)
        outs[r // LOW][r % LOW] = total[pl.ds(place, rows), :]


def attn_grads(grad_qkv, mixed, tokens, grads, scalars):
    width = tokens[0].shape[1]
    columns = grad_qkv.shape[1] + mixed.shape[1]
    rows = width // SHARDS
    whole = pl.BlockSpec(memory_space=pltpu.VMEM)
    return pl.pallas_call(
        attn_grads_kernel,
        in_specs=[pl.BlockSpec(memory_space=pltpu.SMEM)] + [whole] * 10,
        out_specs=[whole] * 2,
        out_shape=[jax.ShapeDtypeStruct((LOW, rows, columns), BF16)] * 2,
        scratch_shapes=[pltpu.VMEM((width, columns), BF16)],
        compiler_params=pltpu.CompilerParams(vmem_limit_bytes=48 * 2**20),
        cost_estimate=cost_of(8),
        name="attn_grads",
    )(scalars, grad_qkv, mixed, *tokens, *grads)


def attend_back_kernel(block, pad, scalars, qkv_ref, lse_ref, last_ref, *refs):
    pieces, refs = refs[:4], refs[4:]
    out_ref, grad_mixed, key_rows, value_rows, key_pad, grad_key, grad_value = refs
    group = qkv_ref.shape[1]
    inner_rows = qkv_ref.shape[0] // 3
    quarter = group // 4
    contract_last = (((1,), (1,)), ((), ()))
    head = pl.program_id(0)

    @pl.when(head == 0)
    def _():
        turned = last_ref[...].T
        for r in range(4):
            place = pl.multiple_of((scalars[1] ^ r) * quarter, quarter)
            grad_mixed[:, pl.ds(place, quarter)] = lax.dot_general(
                turned, pieces[r][...], contract_last, preferred_element_type=F32
            ).astype(BF16)

    first_row = pl.multiple_of(head * HEAD, HEAD)
    keys = qkv_ref[pl.ds(inner_rows + first_row, HEAD), :]
    key_rows[pl.ds(0, pad), :] = jnp.zeros((pad, HEAD), BF16)
    value_rows[pl.ds(0, pad), :] = jnp.zeros((pad, HEAD), BF16)
    key_pad[:, pl.ds(0, pad)] = jnp.zeros((HEAD, pad), BF16)
    key_rows[pl.ds(pad, group), :] = keys.T
    value_rows[pl.ds(pad, group), :] = qkv_ref[pl.ds(2 * inner_rows + first_row, HEAD), :].T
    key_pad[:, pl.ds(pad, group)] = keys
    grad_key[...] = jnp.zeros_like(grad_key)
    grad_value[...] = jnp.zeros_like(grad_value)

    def one(i, carry):
        first = pl.multiple_of(i * block, block)

        def body(window):
            begin = pl.multiple_of(first + pad + block - window, block)
            query = qkv_ref[pl.ds(first_row, HEAD), pl.ds(first, block)]
            grad = grad_mixed[pl.ds(first_row, HEAD), pl.ds(first, block)]
            scores = jnp.dot(key_rows[pl.ds(begin, window), :], query, preferred_element_type=F32)
            allowed = scores_mask(begin - pad, first, window, block, scalars)
            exponent = scores * 0.125 - lse_ref[0, :, pl.ds(first, block)]
            probs = jnp.exp(jnp.where(allowed, exponent, NEGATIVE))
            grad_probs = jnp.dot(
                value_rows[pl.ds(begin, window), :], grad, preferred_element_type=F32
            )
            inner = jnp.sum(probs * grad_probs, axis=0, keepdims=True)
            raw = (0.125 * (probs * (grad_probs - inner))).astype(BF16)
            grad_query = jnp.dot(
                key_pad[:, pl.ds(begin, window)], raw, preferred_element_type=F32
            )
            column = pl.multiple_of(first % quarter, block)
            out_ref[first // quarter, 0, :, pl.ds(column, block)] = grad_query.astype(BF16)
            grad_value[:, pl.ds(begin, window)] += lax.dot_general(
                grad, probs.astype(BF16), contract_last, preferred_element_type=F32
            )
            grad_key[:, pl.ds(begin, window)] += lax.dot_general(
                query, raw, contract_last, preferred_element_type=F32
            )

        for_window(first, block, pad, scalars, body)
        return carry

    lax.fori_loop(0, group // block, one, 0)
    for j in range(4):
        out_ref[j, 1] = grad_key[:, pl.ds(pad + j * quarter, quarter)].astype(BF16)
        out_ref[j, 2] = grad_value[:, pl.ds(pad + j * quarter, quarter)].astype(BF16)


def attend_back(scalars, qkv, lse, last, pieces, heads):
    group = qkv.shape[1]
    block = 256

    def whole(shape):
        return pl.BlockSpec(
            shape, lambda i, _: (0,) * len(shape), pipeline_mode=pl.Buffered(1)
        )

    return pl.pallas_call(
        functools.partial(attend_back_kernel, block, MAXLEN),
        grid_spec=pltpu.PrefetchScalarGridSpec(
            num_scalar_prefetch=1,
            grid=(heads,),
            in_specs=[
                whole(qkv.shape),
                pl.BlockSpec((1, 1, group), lambda h, _: (h, 0, 0)),
                whole(last.shape),
                *[whole(item.shape) for item in pieces],
            ],
            out_specs=pl.BlockSpec((4, 3, HEAD, group // 4), lambda h, _: (0, 0, h, 0)),
            scratch_shapes=[
                pltpu.VMEM((heads * HEAD, group), BF16),
                pltpu.VMEM((MAXLEN + group, HEAD), BF16),
                pltpu.VMEM((MAXLEN + group, HEAD), BF16),
                pltpu.VMEM((HEAD, MAXLEN + group), BF16),
                pltpu.VMEM((HEAD, MAXLEN + group), F32),
                pltpu.VMEM((HEAD, MAXLEN + group), F32),
            ],
        ),
        out_shape=jax.ShapeDtypeStruct((4, 3, heads * HEAD, group // 4), BF16),
        compiler_params=pltpu.CompilerParams(vmem_limit_bytes=48 * 2**20),
        cost_estimate=cost_of(34),
        name="attend_back",
    )(scalars, qkv, lse, last, *pieces)


def inputs_back_kernel(scalars, grads, p0, p1, p2, p3, x_ref, gain_ref, hidden_ref, out_ref, sum_ref):
    total = 0.0
    for r, weight in enumerate((p0, p1, p2, p3)):
        total += jnp.dot(grads[scalars[1] ^ r].T, weight[...], preferred_element_type=F32)
    x = x_ref[...]
    scale = lax.rsqrt(jnp.mean(x * x, axis=1, keepdims=True) + EPSILON)
    through = total * gain_ref[...]
    inner = jnp.mean(through * x, axis=1, keepdims=True)
    out_ref[...] = hidden_ref[...] + scale * through - (scale * scale * scale * inner) * x
    sum_ref[0] = jnp.sum(total * x * scale, axis=0, keepdims=True)


def inputs_back(scalars, grads, weights, x, gain, grad_hidden):
    rows, width = x.shape
    block = rows // 2

    def whole(shape):
        return pl.BlockSpec(shape, lambda i, _: (0,) * len(shape), pipeline_mode=pl.Buffered(1))

    part = pl.BlockSpec((block, width), lambda i, _: (i, 0))
    return pl.pallas_call(
        inputs_back_kernel,
        grid_spec=pltpu.PrefetchScalarGridSpec(
            num_scalar_prefetch=1,
            grid=(2,),
            in_specs=[
                pl.BlockSpec((4, grads.shape[1], block), lambda i, _: (0, 0, i)),
                *[whole(item.shape) for item in weights],
                part,
                whole(gain.shape),
                part,
            ],
            out_specs=[part, pl.BlockSpec((1, 1, width), lambda i, _: (i, 0, 0))],
        ),
        out_shape=[
            jax.ShapeDtypeStruct(x.shape, F32),
            jax.ShapeDtypeStruct((2, 1, width), F32),
        ],
        compiler_params=pltpu.CompilerParams(vmem_limit_bytes=48 * 2**20),
        cost_estimate=cost_of(6),
        name="inputs_back",
    )(scalars, grads, *weights, x, gain, grad_hidden)


def expert_kernel(
    kinds, scalars, w_gate, w_near, *refs
):
    far_pieces, refs = refs[:4], refs[4:]
    x_blocks, g_blocks, refs = refs[: 2 * LOW], refs[2 * LOW : 4 * LOW], refs[4 * LOW :]
    back_own, back_send, feed_own, feed_send, grads_gate, grads_other, *refs = refs
    x_all, g_all, x_t, g_t, weights, hidden, acc_feed, acc_back, scales, plain = refs
    slots, width = feed_own.shape
    block = slots // LOW
    half = width // 2
    step = pl.program_id(0)
    contract_last = (((1,), (1,)), ((), ()))
    units = weights.shape[2]

    def weight_column(x_ref):
        extra = x_ref[:, width:].astype(F32)
        lanes = lax.broadcasted_iota(jnp.int32, extra.shape, 1)
        named = (lanes == scalars[0]) | (lanes == scalars[0] + kinds)
        return jnp.sum(jnp.where(named, extra, 0.0), axis=1, keepdims=True)

    @pl.when(step == 0)
    def _():
        for i in range(2 * LOW):
            rows = pl.ds(i * block, block)
            scale = weight_column(x_blocks[i])
            scales[rows, :] = jnp.broadcast_to(scale, (block, 128))
            plain[rows, :] = g_blocks[i][...]
            x_all[rows, :] = x_blocks[i][:, :width]
            g_all[rows, :] = (g_blocks[i][...].astype(F32) * scale).astype(BF16)
        x_t[...] = x_all[...].T
        g_t[...] = g_all[...].T
        acc_feed[...] = jnp.zeros_like(acc_feed)
        acc_back[...] = jnp.zeros_like(acc_back)

    for i in range(2):
        rows = pl.ds(i * half, half)
        weights[0, rows, :] = w_gate[:, 0, i].reshape(half, units)
    near = pl.multiple_of(scalars[1] * half, half)
    for k in range(2):
        weights[k + 1, pl.ds(near, half), :] = w_near[:, 0, k].reshape(half, units)
        place = (1 - scalars[1]) * half
        for piece in far_pieces[2 * k : 2 * k + 2]:
            rows = piece.shape[0] * half // LOW
            weights[k + 1, pl.ds(pl.multiple_of(place, half // LOW), rows), :] = piece[
                :, 0
            ].reshape(rows, units)
            place += rows

    for part in range(2):
        rows = pl.ds(part * slots, slots)
        x = x_all[rows, :]
        gate = jnp.dot(x, weights[0], preferred_element_type=F32)
        up = jnp.dot(x, weights[1], preferred_element_type=F32)
        grad_act = jnp.dot(g_all[rows, :], weights[2], preferred_element_type=F32)
        sig = jax.nn.sigmoid(gate)
        silu = gate * sig
        active = (silu * up).astype(BF16)
        grad_gate = (grad_act * up * (sig * (1.0 + gate * (1.0 - sig)))).astype(BF16)
        grad_up = (grad_act * silu).astype(BF16)
        hidden[0, rows, :] = grad_gate
        hidden[1, rows, :] = grad_up
        hidden[2, rows, :] = active
        acc_feed[rows, :] += lax.dot_general(
            active, weights[2], contract_last, preferred_element_type=F32
        )
        acc_back[rows, :] += lax.dot_general(
            grad_gate, weights[0], contract_last, preferred_element_type=F32
        ) + lax.dot_general(grad_up, weights[1], contract_last, preferred_element_type=F32)

    for k in range(3):
        left = (g_t if k == 2 else x_t)
        grad = jnp.dot(left[...], hidden[k], preferred_element_type=F32).astype(BF16)
        for i in range(2):
            part = grad[i * half : (i + 1) * half].reshape(LOW, -1, units)
            if k == 0:
                grads_gate[i, :, 0] = part
            else:
                grads_other[i, :, 0, k - 1] = part

    @pl.when(step == pl.num_programs(0) - 1)
    def _():
        for part in range(2):
            rows = pl.ds(part * slots, slots)
            feed = acc_feed[rows, :]
            inner = jnp.sum(feed * plain[rows, :].astype(F32), axis=1, keepdims=True)
            feed = feed * scales[rows, 0:1]
            lanes = lax.broadcasted_iota(jnp.int32, (slots, 128), 1)
            if part == 0:
                back_own[:, :width] = acc_back[rows, :]
                back_own[:, width:] = jnp.where(lanes == scalars[0], inner, 0.0)
                feed_own[...] = feed
            else:
                high = inner.astype(BF16).astype(F32)
                extra = jnp.where(lanes == scalars[0], high, 0.0)
                extra = jnp.where(lanes == scalars[0] + kinds, inner - high, extra)
                back_send[:, :width] = acc_back[rows, :].astype(BF16)
                back_send[:, width:] = extra.astype(BF16)
                feed_send[...] = feed.astype(BF16)


def expert_pass(kinds, scalars, x_blocks, g_blocks, w_gate, w_near, w_far):
    block, width = g_blocks[0].shape
    slots = LOW * block
    low, parities, _, shard_rows, shard_units = w_gate.shape
    units = 256
    steps = shard_units // units

    def whole(shape):
        return pl.BlockSpec(
            shape, lambda i, _: (0,) * len(shape), pipeline_mode=pl.Buffered(1)
        )

    both_spec = pl.BlockSpec(
        (2, low, 1, shard_rows, units), lambda i, _: (0, 0, i // steps, 0, i % steps)
    )
    other_spec = pl.BlockSpec(
        (2, low, 1, 2, shard_rows, units), lambda i, _: (0, 0, i // steps, 0, 0, i % steps)
    )

    gate_spec = pl.BlockSpec(
        (low, 1, 2, shard_rows, units), lambda i, _: (0, i // steps, 0, 0, i % steps)
    )
    def up_spec(count):
        return pl.BlockSpec(
            (count, 1, shard_rows, units), lambda i, _: (0, i // steps, 0, i % steps)
        )

    wide = width + 128
    return pl.pallas_call(
        functools.partial(expert_kernel, kinds),
        grid_spec=pltpu.PrefetchScalarGridSpec(
            num_scalar_prefetch=1,
            grid=(parities * steps,),
            in_specs=[
                gate_spec,
                gate_spec,
                *[up_spec(item.shape[0]) for item in w_far],
                *[whole((block, wide)) for _ in range(2 * LOW)],
                *[whole((block, width)) for _ in range(2 * LOW)],
            ],
            out_specs=[
                whole((slots, wide)),
                whole((slots, wide)),
                whole((slots, width)),
                whole((slots, width)),
                both_spec,
                other_spec,
            ],
            scratch_shapes=[
                pltpu.VMEM((2 * slots, width), BF16),
                pltpu.VMEM((2 * slots, width), BF16),
                pltpu.VMEM((width, 2 * slots), BF16),
                pltpu.VMEM((width, 2 * slots), BF16),
                pltpu.VMEM((3, width, units), BF16),
                pltpu.VMEM((3, 2 * slots, units), BF16),
                pltpu.VMEM((2 * slots, width), F32),
                pltpu.VMEM((2 * slots, width), F32),
                pltpu.VMEM((2 * slots, 128), F32),
                pltpu.VMEM((2 * slots, width), BF16),
            ],
        ),
        out_shape=[
            jax.ShapeDtypeStruct((slots, wide), F32),
            jax.ShapeDtypeStruct((slots, wide), BF16),
            jax.ShapeDtypeStruct((slots, width), F32),
            jax.ShapeDtypeStruct((slots, width), BF16),
            jax.ShapeDtypeStruct((2, low, parities, shard_rows, shard_units), BF16),
            jax.ShapeDtypeStruct((2, low, parities, 2, shard_rows, shard_units), BF16),
        ],
        compiler_params=pltpu.CompilerParams(vmem_limit_bytes=58 * 2**20),
        cost_estimate=cost_of(35),
        name="expert_pass",
    )(scalars, w_gate, w_near, *w_far, *x_blocks, *g_blocks)


def pick_kernel(ids_ref, *refs):
    pieces, outs = refs[:4], refs[4:]
    block = outs[0].shape[0]
    rows = pieces[0].shape[0]
    for i, out_ref in enumerate(outs):
        slot = i * block + lax.broadcasted_iota(jnp.int32, (block, rows), 0)
        total = 0.0
        for r in range(4):
            columns = pl.ds(r * rows, rows)
            held = (slot == ids_ref[0:1, columns]) | (slot == ids_ref[1:2, columns])
            held = jnp.where(held, 1.0, 0.0).astype(BF16)
            total += jnp.dot(held, pieces[r][...], preferred_element_type=F32)
        out_ref[...] = total.astype(BF16)


def pick(ids, pieces, slots):
    rows, width = pieces[0].shape
    block = slots // LOW

    def whole(shape):
        return pl.BlockSpec(shape, lambda i: (0, 0))

    return pl.pallas_call(
        pick_kernel,
        grid=(1,),
        in_specs=[whole((8, 4 * rows)), *[whole((rows, width)) for _ in range(4)]],
        out_specs=[whole((block, width)) for _ in range(LOW)],
        out_shape=[jax.ShapeDtypeStruct((block, width), BF16) for _ in range(LOW)],
        compiler_params=pltpu.CompilerParams(vmem_limit_bytes=32 * 2**20),
        cost_estimate=cost_of(5),
        name="pick",
    )(ids, *pieces)


def to_experts(blocks):
    return [blocks[0]] + [flip(blocks[b], "lo", LOW, b) for b in range(1, LOW)]


def back_sum_kernel(kinds, own_ref, core_ref, *outs):
    width = own_ref.shape[1] - 128
    block = outs[0].shape[0]
    for i, out_ref in enumerate(outs):
        rows = pl.ds(i * block, block)
        out_ref[:, :width] = (
            own_ref[rows, :width] + core_ref[rows, :width].astype(F32)
        ).astype(BF16)
        extra = own_ref[rows, width:] + core_ref[rows, width:].astype(F32)
        lanes = lax.broadcasted_iota(jnp.int32, extra.shape, 1)
        high = jnp.where(lanes < kinds, extra, 0.0).astype(BF16).astype(F32)
        low = jnp.where(lanes < kinds, extra - high, 0.0)
        low = pltpu.roll(low, kinds, 1) + jnp.where(lanes >= kinds, extra, 0.0)
        out_ref[:, width:] = (high + low).astype(BF16)


def back_sum(kinds, own, core):
    slots, wide = own.shape
    block = slots // LOW

    def whole(shape):
        return pl.BlockSpec(shape, lambda i: (0, 0))

    return pl.pallas_call(
        functools.partial(back_sum_kernel, kinds),
        grid=(1,),
        in_specs=[whole(own.shape), whole(core.shape)],
        out_specs=[whole((block, wide)) for _ in range(LOW)],
        out_shape=[jax.ShapeDtypeStruct((block, wide), BF16) for _ in range(LOW)],
        compiler_params=pltpu.CompilerParams(vmem_limit_bytes=32 * 2**20),
        cost_estimate=cost_of(3),
        name="back_sum",
    )(own, core)


def feed_sum_kernel(own_ref, core_ref, *outs):
    block = outs[0].shape[0]
    for i, out_ref in enumerate(outs):
        rows = pl.ds(i * block, block)
        out_ref[...] = (own_ref[rows, :] + core_ref[rows, :].astype(F32)).astype(BF16)


def feed_sum(own, core):
    slots, width = own.shape
    block = slots // LOW

    def whole(shape):
        return pl.BlockSpec(shape, lambda i: (0, 0))

    return pl.pallas_call(
        feed_sum_kernel,
        grid=(1,),
        in_specs=[whole(own.shape), whole(core.shape)],
        out_specs=[whole((block, width)) for _ in range(LOW)],
        out_shape=[jax.ShapeDtypeStruct((block, width), BF16) for _ in range(LOW)],
        compiler_params=pltpu.CompilerParams(vmem_limit_bytes=32 * 2**20),
        cost_estimate=cost_of(3),
        name="feed_sum",
    )(own, core)


def spread_kernel(ids_ref, *refs):
    blocks, (near_ref, send_ref, slots_ref) = refs[:LOW], refs[LOW:]
    rows = near_ref.shape[1]
    slots = slots_ref.shape[0]
    block = slots // LOW

    @pl.when(pl.program_id(0) == 0)
    def _():
        for i in range(LOW):
            slots_ref[pl.ds(i * block, block), :] = blocks[i][...]

    for k, out_ref in enumerate((near_ref, send_ref)):
        slot = lax.broadcasted_iota(jnp.int32, (rows, slots), 1)
        ids = ids_ref[pl.ds(k * rows, rows), :]
        held = (slot == ids[:, 0:1]) | (slot == ids[:, 1:2])
        held = jnp.where(held, 1.0, 0.0).astype(BF16)
        total = jnp.dot(held, slots_ref[...], preferred_element_type=F32)
        out_ref[0] = total.astype(out_ref.dtype)


def spread(ids, values, rows):
    block, width = values[0].shape
    return pl.pallas_call(
        spread_kernel,
        grid=(2,),
        in_specs=[
            pl.BlockSpec((2 * rows, 8), lambda i: (i, 0)),
            *[pl.BlockSpec((block, width), lambda i: (0, 0)) for _ in range(LOW)],
        ],
        out_specs=[
            pl.BlockSpec((1, rows, width), lambda i: (i, 0, 0)),
            pl.BlockSpec((1, rows, width), lambda i: (i, 0, 0)),
        ],
        out_shape=[
            jax.ShapeDtypeStruct((2, rows, width), F32),
            jax.ShapeDtypeStruct((2, rows, width), BF16),
        ],
        scratch_shapes=[pltpu.VMEM((LOW * block, width), BF16)],
        compiler_params=pltpu.CompilerParams(vmem_limit_bytes=32 * 2**20),
        cost_estimate=cost_of(6),
        name="spread",
    )(ids, *values)


def slots_kernel(experts, capacity, scalars, routes_col, order_col, routes_row, order_row,
                 row_ref, col_ref, places_ref):
    group = routes_row.shape[1]
    rows = group // 4
    share = capacity // 2
    span = 2 * group
    bound = scalars[BOUNDS + 2]

    def target_of(routes, axis):
        place = lax.broadcasted_iota(jnp.int32, routes.shape, axis)
        return jnp.where((routes < experts) & (place < bound), routes, experts)

    target = target_of(routes_row[...], 1)
    code = target * span + order_row[...]
    block = 256

    def count(i, carry):
        first = pl.multiple_of(i * block, block)
        routes = routes_col[pl.ds(first, block), :]
        place = first + lax.broadcasted_iota(jnp.int32, routes.shape, 0)
        held = jnp.where((routes < experts) & (place < bound), routes, experts)
        others = held * span + order_col[pl.ds(first, block), :]
        result = []
        for k in range(2):
            total = carry[k]
            for j in range(2):
                smaller = jnp.where(others[:, j : j + 1] < code[k : k + 1, :], 1.0, 0.0)
                total = total + jnp.sum(smaller, axis=0, keepdims=True)
            result.append(total)
        return tuple(result)

    zero = jnp.zeros((1, group), F32)
    counts = lax.fori_loop(0, group // block, count, (zero, zero))
    for k in range(2):
        mine_target = target[k : k + 1, :]
        base = jnp.zeros((1, group), F32)
        for e in range(1, experts):
            earlier = jnp.sum(jnp.where(target < e, 1.0, 0.0))
            base = jnp.where(mine_target == e, earlier, base)
        place = (counts[k] - base).astype(jnp.int32)
        first = scalars[3] * share
        held = (
            (mine_target < experts)
            & (place >= first)
            & (place < first + share)
            & (place < capacity)
            & (jnp.bitwise_and(mine_target, 1) == scalars[2])
        )
        block = jnp.bitwise_xor(lax.shift_right_logical(mine_target, 1), scalars[LOW_PLACE])
        slot = block * share + place - first
        places_ref[k : k + 1, :] = jnp.where(held, slot, -1)
    for r in range(4):
        start = pl.multiple_of((scalars[1] ^ r) * rows, rows)
        piece = places_ref[:, pl.ds(start, rows)]
        row_ref[:, pl.ds(r * rows, rows)] = piece
        col_ref[pl.ds(r * rows, rows), :] = piece.T


def slots_of(scalars, routes, drop_order, experts, capacity):
    group = routes.shape[0]
    whole = pl.BlockSpec(memory_space=pltpu.VMEM)
    return pl.pallas_call(
        functools.partial(slots_kernel, experts, capacity),
        in_specs=[pl.BlockSpec(memory_space=pltpu.SMEM)] + [whole] * 4,
        out_specs=[whole] * 2,
        out_shape=[
            jax.ShapeDtypeStruct((8, group), jnp.int32),
            jax.ShapeDtypeStruct((group, 8), jnp.int32),
        ],
        scratch_shapes=[pltpu.VMEM((8, group), jnp.int32)],
        compiler_params=pltpu.CompilerParams(vmem_limit_bytes=32 * 2**20),
        cost_estimate=cost_of(8),
        name="slots",
    )(scalars, routes, drop_order, routes.T, drop_order.T)


def middle_kernel(kinds, scalars, mixed, p0, p1, p2, p3, x_ref, gain_ref, router_w, prior_ref,
                  prior_w, hidden_ref, sent_ref, router_ref, weight):
    hidden = x_ref[...]
    rows = p0.shape[2]
    for r, shards in enumerate((p0, p1, p2, p3)):
        for k in range(SHARDS):
            place = pl.multiple_of((scalars[0] ^ k) * rows, rows)
            weight[r, pl.ds(place, rows), :] = shards[k % LOW, k // LOW]
        hidden += lax.dot_general(
            mixed[scalars[1] ^ r].T, weight[r], (((1,), (1,)), ((), ())),
            preferred_element_type=F32,
        )
    hidden_ref[...] = hidden
    scale = lax.rsqrt(jnp.mean(hidden * hidden, axis=1, keepdims=True) + EPSILON)
    rounded = (hidden * scale * gain_ref[...]).astype(BF16)
    width = hidden.shape[1]
    sent_ref[:, :width] = rounded
    router_high, router_low = halves(router_w[...])
    logits = (
        jnp.dot(rounded, router_high, preferred_element_type=F32)
        + jnp.dot(rounded, router_low, preferred_element_type=F32)
        + split_dot(prior_ref[...], prior_w[...])
    )
    lanes = lax.broadcasted_iota(jnp.int32, logits.shape, 1)
    logits = jnp.where(lanes < 2 * kinds, logits, NEGATIVE)
    weights = jnp.exp(logits - jnp.max(logits, axis=1, keepdims=True))
    total = jnp.sum(jnp.where(lanes < kinds, weights, 0.0), axis=1, keepdims=True)
    router = weights / total
    router_ref[...] = router
    high = router.astype(BF16).astype(F32)
    sent_ref[:, width:] = jnp.where(lanes < kinds, high, router - high).astype(BF16)


def middle(kinds, scalars, mixed, weights, x, gain, router_w, prior, prior_w):
    rows, width = x.shape
    lanes = router_w.shape[1]

    def whole(shape):
        return pl.BlockSpec(shape, lambda i, _: (0,) * len(shape))

    return pl.pallas_call(
        functools.partial(middle_kernel, kinds),
        grid_spec=pltpu.PrefetchScalarGridSpec(
            num_scalar_prefetch=1,
            grid=(1,),
            in_specs=[
                whole(mixed.shape),
                *[whole(item.shape) for item in weights],
                whole(x.shape),
                whole(gain.shape),
                whole(router_w.shape),
                pl.BlockSpec((rows, kinds), lambda i, scalars: (scalars[1], 0)),
                whole(prior_w.shape),
            ],
            out_specs=[whole((rows, width)), whole((rows, width + lanes)), whole((rows, lanes))],
            scratch_shapes=[pltpu.VMEM((4, width, mixed.shape[1]), BF16)],
        ),
        out_shape=[
            jax.ShapeDtypeStruct((rows, width), F32),
            jax.ShapeDtypeStruct((rows, width + lanes), BF16),
            jax.ShapeDtypeStruct((rows, lanes), F32),
        ],
        compiler_params=pltpu.CompilerParams(vmem_limit_bytes=48 * 2**20),
        cost_estimate=cost_of(6),
        name="middle",
    )(scalars, mixed, *weights, x, gain, router_w, prior, prior_w)


def halves(value):
    high = value.astype(BF16)
    return high, (value - high.astype(F32)).astype(BF16)


def split_dot(left, right):
    (left_high, left_low), (right_high, right_low) = halves(left), halves(right)
    return (
        jnp.dot(left_high, right_high, preferred_element_type=F32)
        + jnp.dot(left_low, right_high, preferred_element_type=F32)
        + jnp.dot(left_high, right_low, preferred_element_type=F32)
    )


def turned_dot(left, right):
    high, low = halves(left.T)
    return jnp.dot(high, right, preferred_element_type=F32) + jnp.dot(
        low, right, preferred_element_type=F32
    )


def router_back_kernel(kinds, experts, scalars, near_ref, got_ref, far_ref, hidden_ref, router_ref,
                       routes_ref, cotangent_ref, prior_ref, gain_ref, small_ref, small_t_ref,
                       vector_ref, prior_w_ref,
                       grad_hidden_ref, grad_low_ref, partial_ref, grad_prior_ref, sums_ref):
    step = pl.program_id(0)
    rows, width = hidden_ref.shape
    place = scalars[1] * rows * pl.num_programs(0) + step * rows
    valid = place + lax.broadcasted_iota(jnp.int32, (rows, 1), 0) < scalars[BOUNDS + 2]
    valid = jnp.where(valid, 1.0, 0.0)
    back = near_ref[0] + got_ref[0].astype(F32) + far_ref[...].astype(F32)
    hidden = hidden_ref[...]
    grad_out = cotangent_ref[...] * valid
    scale = lax.rsqrt(jnp.mean(hidden * hidden, axis=1, keepdims=True) + EPSILON)
    unit = hidden * scale
    normed = unit * gain_ref[...]
    router = router_ref[...]
    lanes = lax.broadcasted_iota(jnp.int32, router.shape, 1)
    routes = routes_ref[...]

    def column(array, k):
        return jnp.sum(jnp.where(lanes == k, array, 0.0), axis=1, keepdims=True)

    def named(kind):
        return jnp.where((routes[:, 0:1] == kind) | (routes[:, 1:2] == kind), 1.0, 0.0)

    copy, first, second = (named(experts + k) for k in (1, 2, 3))
    weight_copy = column(router, experts + 1) * copy
    weight_first = column(router, experts + 2) * first
    weight_second = column(router, experts + 3) * second
    mixlog = split_dot(normed, small_ref[...])

    def softmax_two(k):
        one, two = column(mixlog, k), column(mixlog, k + 1)
        highest = jnp.maximum(one, two)
        one, two = jnp.exp(one - highest), jnp.exp(two - highest)
        return one / (one + two), two / (one + two)

    mix_one, mix_two = softmax_two(kinds), softmax_two(kinds + 2)
    vector_one, vector_two = vector_ref[0:1, :], vector_ref[1:2, :]
    along = jnp.sum(normed * grad_out, axis=1, keepdims=True)
    along_one = jnp.sum(vector_one * grad_out, axis=1, keepdims=True)
    along_two = jnp.sum(vector_two * grad_out, axis=1, keepdims=True)

    extra = back[:, width:]
    pairs = jnp.where(lanes < kinds, extra, 0.0) + jnp.where(
        lanes < kinds, pltpu.roll(extra, extra.shape[1] - kinds, 1), 0.0
    )
    grad_router = pairs + jnp.where(lanes == experts + 1, copy * along, 0.0)
    grad_router += jnp.where(
        lanes == experts + 2, first * (mix_one[0] * along + mix_one[1] * along_one), 0.0
    )
    grad_router += jnp.where(
        lanes == experts + 3, second * (mix_two[0] * along + mix_two[1] * along_two), 0.0
    )
    held = jnp.where(lanes < kinds, router, 0.0)
    grad_small = held * (grad_router - jnp.sum(held * grad_router, axis=1, keepdims=True))
    grad_prior_ref[...] = split_dot(grad_small, prior_w_ref[...])[:, :kinds]
    grad_logits = grad_small

    def mixed_back(weight, mix, other, k):
        one, two = weight * along, weight * other
        inner = mix[0] * one + mix[1] * two
        return jnp.where(lanes == k, mix[0] * (one - inner), 0.0) + jnp.where(
            lanes == k + 1, mix[1] * (two - inner), 0.0
        )

    grad_mixlog = mixed_back(weight_first, mix_one, along_one, kinds) + mixed_back(
        weight_second, mix_two, along_two, kinds + 2
    )
    grad_small = grad_logits + grad_mixlog
    share = weight_copy + weight_first * mix_one[0] + weight_second * mix_two[0]
    grad_normed = (
        back[:, :width]
        + share * grad_out
        + split_dot(grad_small, small_t_ref[...])
    )
    through = grad_normed * gain_ref[...]
    inner = jnp.mean(through * hidden, axis=1, keepdims=True)
    grad_hidden = grad_out + scale * through - (scale * scale * scale * inner) * hidden
    grad_hidden_ref[...] = grad_hidden
    grad_low_ref[...] = grad_hidden.astype(BF16)
    vector_first, vector_second = weight_first * mix_one[1], weight_second * mix_two[1]
    partial_ref[...] = valid * (
        hidden + share * normed + vector_first * vector_one + vector_second * vector_two
    )

    @pl.when(step == 0)
    def _():
        sums_ref[...] = jnp.zeros_like(sums_ref)

    vectors = jnp.where(lanes == kinds + 5, vector_first, 0.0) + jnp.where(
        lanes == kinds + 6, vector_second, 0.0
    )
    low = normed.astype(BF16)
    total = turned_dot(grad_small, low) + turned_dot(vectors, grad_out.astype(BF16))
    sums_ref[: kinds + 8, :] += total[: kinds + 8, :]
    sums_ref[kinds + 4 : kinds + 5, :] += jnp.sum(grad_normed * unit, axis=0, keepdims=True)
    prior = split_dot(prior_ref[...].T, grad_logits)
    sums_ref[pl.ds(kinds + 8, kinds), : lanes.shape[1]] += prior


def router_back(kinds, experts, scalars, near, got, far, hidden, router, routes, cotangent, prior,
                gain, small, small_t, vector, prior_w):
    rows, width = hidden.shape
    block = rows // 2
    lanes = router.shape[1]

    def whole(shape):
        return pl.BlockSpec(shape, lambda i, _: (0,) * len(shape))

    def part(columns):
        return pl.BlockSpec((block, columns), lambda i, _: (i, 0))

    def mine(columns):
        return pl.BlockSpec((block, columns), lambda i, scalars: (scalars[1] * 2 + i, 0))

    return pl.pallas_call(
        functools.partial(router_back_kernel, kinds, experts),
        grid_spec=pltpu.PrefetchScalarGridSpec(
            num_scalar_prefetch=1,
            grid=(2,),
            in_specs=[
                pl.BlockSpec((1, block, width + lanes), lambda i, _: (0, i, 0)),
                pl.BlockSpec((1, block, width + lanes), lambda i, _: (0, i, 0)),
                part(width + lanes),
                part(width),
                part(lanes),
                mine(2),
                part(width),
                mine(kinds),
                whole(gain.shape),
                whole(small.shape),
                whole(small_t.shape),
                whole(vector.shape),
                whole(prior_w.shape),
            ],
            out_specs=[
                part(width),
                part(width),
                part(width),
                part(kinds),
                whole((32, width)),
            ],
        ),
        out_shape=[
            jax.ShapeDtypeStruct((rows, width), F32),
            jax.ShapeDtypeStruct((rows, width), BF16),
            jax.ShapeDtypeStruct((rows, width), F32),
            jax.ShapeDtypeStruct((rows, kinds), F32),
            jax.ShapeDtypeStruct((32, width), F32),
        ],
        compiler_params=pltpu.CompilerParams(vmem_limit_bytes=48 * 2**20),
        cost_estimate=cost_of(8),
        name="router_back",
    )(scalars, near, got, far, hidden, router, routes, cotangent, prior, gain, small, small_t,
      vector, prior_w)


def two_parts(value):
    high = lax.reduce_precision(value, 8, 7)
    return jnp.concatenate([high, value - high], axis=-1).astype(BF16)


def everywhere(value, axes, count):
    copies = jnp.broadcast_to(value[None], (count, *value.shape))
    return lax.all_to_all(copies, axes, 0, 0, tiled=True)


def flip(value, axis, size, bit):
    return lax.ppermute(value, axis, [(i, i ^ bit) for i in range(size)])


def by_halves(value):
    if value.shape[0] == 2:
        return value
    rows, units = value.shape[-2:]
    middle_axes = tuple(range(2, value.ndim - 2))
    turned = value.transpose(*middle_axes, 0, 1, value.ndim - 2, value.ndim - 1)
    turned = turned.reshape(*turned.shape[:-4], 2, LOW, value.shape[0] * rows // 2, units)
    axes = turned.ndim
    return turned.transpose(axes - 4, axes - 3, *range(axes - 4), axes - 2, axes - 1)


def scatter_high(value, many):
    if many != 2:
        rows, units = value.shape[-2:]
        middle_axes = tuple(range(2, value.ndim - 2))
        turned = value.transpose(*middle_axes, 0, 1, value.ndim - 2, value.ndim - 1)
        turned = turned.reshape(*turned.shape[:-4], many, LOW, 2 * rows // many, units)
        axes = turned.ndim
        value = turned.transpose(axes - 4, axes - 3, *range(axes - 4), axes - 2, axes - 1)
    return lax.psum_scatter(value, "hi", scatter_dimension=0)


def gather_rows(value, later, many):
    if many != 2:
        full = lax.all_gather(value, ("hi", "lo"), axis=0, tiled=True)
        full = full.reshape(2, LOW, -1, full.shape[1])
        return [full[:, i] for i in range(LOW)], later
    far, *later = lax.optimization_barrier((swap(value, "hi"), *later))
    both = jnp.stack([value, far])
    return [both] + [flip(both, "lo", LOW, bit) for bit in range(1, LOW)], tuple(later)


def scatter_rows(near, far, many):
    if many != 2:
        full = jnp.stack([near, far]).astype(F32).reshape(-1, near.shape[2])
        return lax.psum_scatter(full, ("hi", "lo"), scatter_dimension=0, tiled=True)
    both = near.astype(F32) + far.astype(F32)
    total = both[0]
    for bit in range(1, LOW):
        total = total + flip(both[bit].astype(BF16), "lo", LOW, bit).astype(F32)
    return total


def per_device(
    many,
    inputs,
    cotangent,
    lengths,
    routes,
    drop_order,
    prior_logits,
    attn_gain,
    w_query,
    w_key,
    w_value,
    w_out,
    moe_gain,
    w_router,
    w_prior,
    w_const,
    const_vector,
    w_gate,
    w_up,
    w_down,
):
    tok_rows, width = inputs.shape
    group = tok_rows * 4
    kinds = w_router.shape[1]
    experts, shard_rows, shard_units = w_gate.shape
    capacity = 3 * group // 16
    share = capacity // 2
    slots = LOW * share
    local_width = w_query.shape[1]
    heads = local_width // HEAD
    tp_axes = ("y", "c")
    all_axes = ("hi", "lo", "y", "c")
    count = many * LOW * 4
    wide = width + 128
    high = lax.axis_index("hi")
    parity = lax.axis_index("y")
    core = lax.axis_index("c")
    place_in_group = parity * 2 + core
    mine = high * LOW + lax.axis_index("lo") if many == 2 else jnp.zeros_like(high)
    boundary = jnp.cumsum(lengths[0])
    scalars = jnp.concatenate(
        [jnp.stack([mine, place_in_group, parity, core, lax.axis_index("lo")]), boundary[:-1]]
    ).astype(jnp.int32)
    gain_one, gain_two = attn_gain.reshape(1, width), moe_gain.reshape(1, width)

    valid_mine = place_in_group * tok_rows + jnp.arange(tok_rows)[:, None] < boundary[-2]
    valid_mine = valid_mine.astype(F32)

    normed_one = rms_norm(inputs, attn_gain).astype(BF16)
    normed_other = swap(normed_one, "y")
    attn_shard = jnp.concatenate([w_query, w_key, w_value, w_out.T], axis=1)
    other_shards = jnp.stack([w_up, w_down.transpose(0, 2, 1)], axis=1)
    attn_shards, (w_gate, other_shards, _) = gather_rows(
        attn_shard, (w_gate, other_shards, normed_one), many
    )
    gate_far = swap(w_gate, "hi") if many == 2 else w_gate
    attn_shards[0], scalars = lax.optimization_barrier((attn_shards[0], scalars))
    ids_rows, ids_cols = slots_of(scalars, routes, drop_order, experts, capacity)
    grad_out_low = (cotangent * valid_mine).astype(BF16)
    grad_out_other = swap(grad_out_low, "y")
    (
        normed_other, attn_shards, ids_rows, prior_logits, other_shards, grad_out_other
    ) = lax.optimization_barrier(
        (normed_other, attn_shards, ids_rows, prior_logits, other_shards, grad_out_other)
    )
    other_part = lax.all_to_all(other_shards, ("lo", "y"), 0, 0, tiled=True)
    other_part = other_part.reshape(LOW, 2, 2, shard_rows, shard_units)
    out_mine = jnp.stack([item[:, :, 3 * local_width :] for item in attn_shards])
    out_other = swap(out_mine, "y")
    normed_pieces = [normed_one, swap(normed_one, "c"), normed_other, swap(normed_other, "c")]
    router_lanes = jnp.pad(jnp.concatenate([w_router, w_router], axis=1), ((0, 0), (0, 128 - 2 * kinds)))
    prior_lanes = jnp.pad(jnp.concatenate([w_prior, w_prior], axis=1), ((0, 0), (0, 128 - 2 * kinds)))
    const_flat = w_const.transpose(1, 0, 2).reshape(width, 4)
    small = jnp.pad(jnp.concatenate([w_router, const_flat], axis=1), ((0, 0), (0, 112 - kinds + 12)))
    small_t = small.T
    prior_back = jnp.pad(w_prior.T, ((0, 128 - kinds), (0, 128 - kinds)))
    attn_shards, router_lanes, prior_lanes, small, small_t, prior_back = lax.optimization_barrier(
        (attn_shards, router_lanes, prior_lanes, small, small_t, prior_back)
    )

    mixed, lse, qkv, qkv_full, out_full = attend(normed_pieces, attn_shards, scalars, heads)
    mixed, out_other, out_mine, gate_far = lax.optimization_barrier(
        (mixed, out_other, out_mine, gate_far)
    )
    if many == 2:
        w_near, high_place = other_part, high
        w_far = [
            swap(other_part[first:last, :, k], "hi")
            for k, first, last in ((0, 0, 1), (0, 1, 4), (1, 0, 1), (1, 1, 4))
        ]
        gate_both = jnp.where(
            high == 0, jnp.stack([w_gate, gate_far], axis=1), jnp.stack([gate_far, w_gate], axis=1)
        )
    else:
        w_all = by_halves(lax.all_gather(other_part, "hi"))
        w_near, high_place = w_all[0], jnp.zeros_like(high)
        w_far = [
            w_all[1, first:last, :, k]
            for k, first, last in ((0, 0, 1), (0, 1, 4), (1, 0, 1), (1, 1, 4))
        ]
        gate_both = lax.all_gather(w_gate, "hi", axis=1)
    out_pieces = [out_mine, swap(out_mine, "c"), out_other, swap(out_other, "c")]

    mixed_mine = lax.all_to_all(mixed, tp_axes, 0, 0, tiled=True)
    grad_out_pieces = [
        grad_out_low, swap(grad_out_low, "c"), grad_out_other, swap(grad_out_other, "c"),
    ]
    grad_out_slots = pick(ids_rows, grad_out_pieces, slots)
    mixed_mine, grad_out_slots, w_far[0], gate_both = lax.optimization_barrier(
        (mixed_mine, grad_out_slots, w_far[0], gate_both)
    )

    hidden, sent_two, router = middle(
        kinds, scalars, mixed_mine, out_pieces, inputs, gain_two, router_lanes, prior_logits, prior_lanes
    )

    gate_part = lax.all_to_all(gate_both, ("lo", "y"), 0, 0, tiled=True)
    gate_part = gate_part.reshape(LOW, 2, many, shard_rows, shard_units)
    if many != 2:
        gate_part = by_halves(gate_part.transpose(2, 0, 1, 3, 4)).transpose(1, 2, 0, 3, 4)
    other_two, grad_taken, gate_part, w_far[1], w_far[2] = lax.optimization_barrier(
        (swap(sent_two, "y"), to_experts(grad_out_slots), gate_part, w_far[1], w_far[2])
    )
    pieces_two = [sent_two, swap(sent_two, "c"), other_two, swap(other_two, "c")]

    grad_taken += [swap(item, "c") for item in grad_taken]
    sent_slots = pick(ids_rows, pieces_two, slots)
    sent_slots, qkv_full = lax.optimization_barrier((sent_slots, qkv_full))
    taken = to_experts(sent_slots)
    taken += [swap(item, "c") for item in taken]
    qkv_pieces = gather_pieces(qkv_full)
    taken, qkv_pieces, w_far[3] = lax.optimization_barrier((taken, qkv_pieces, w_far[3]))

    expert = lax.axis_index("lo") * 2 + parity
    back_own, back_send, feed_own, feed_send, grads_gate, grads_other = expert_pass(
        kinds, jnp.stack([expert, high_place]).astype(jnp.int32), taken, grad_taken,
        gate_part, w_near, w_far,
    )

    other_sum = scatter_high(grads_other, many)
    gate_sum = scatter_high(grads_gate, many)
    back_taken = to_experts(back_sum(kinds, back_own, swap(back_send, "c")))
    feed_core = swap(feed_send, "c")
    back_taken, feed_core = lax.optimization_barrier((back_taken, feed_core))

    back_near, back_sent = spread(ids_cols, back_taken, tok_rows)
    back_got, back_other = add_core(back_near, back_sent)
    back_other, feed_core = lax.optimization_barrier((back_other, feed_core))
    back_far, feed_blocks = lax.optimization_barrier(
        (swap(back_other, "y"), feed_sum(feed_own, feed_core))
    )

    grad_hidden, grad_low, partial, grad_prior, sums = router_back(
        kinds, experts, scalars, back_near, back_got, back_far, hidden, router, routes, cotangent,
        prior_logits, gain_two, small, small_t, const_vector, prior_back,
    )
    feed_taken = to_experts(feed_blocks)
    low_other = swap(grad_low, "y")
    grad_attn_pieces = [grad_low, swap(grad_low, "c"), low_other, swap(low_other, "c")]
    other_own = lax.all_to_all(
        other_sum.reshape(2 * LOW, 2, shard_rows, shard_units), ("lo", "y"), 0, 0, tiled=True
    )
    grad_qkv = attend_back(scalars, qkv, lse, out_full, grad_attn_pieces, heads).reshape(
        4, 3 * local_width, tok_rows
    )
    grad_qkv, other_own, feed_taken = lax.optimization_barrier((grad_qkv, other_own, feed_taken))

    grad_qkv_mine = lax.all_to_all(grad_qkv, tp_axes, 0, 0, tiled=True)
    attn_near, attn_far = attn_grads(grad_qkv, mixed, normed_pieces, grad_attn_pieces, scalars)
    if many == 2:
        attn_far = swap(attn_far, "hi")
    feed_near, feed_sent = spread(ids_cols, feed_taken, tok_rows)
    feed_got, feed_other = add_core(feed_near, feed_sent)
    (
        grad_qkv_mine, sums, gate_sum, attn_near, attn_far, feed_near, feed_got, feed_other
    ) = lax.optimization_barrier(
        (grad_qkv_mine, sums, gate_sum, attn_near, attn_far, feed_near, feed_got, feed_other)
    )
    feed_far = swap(feed_other, "y")
    sums = sums.reshape(count, 32 * width // count)
    share_sums = lax.all_to_all(sums, all_axes, 0, 0, tiled=True)
    share_sums, gate_sum = lax.optimization_barrier((share_sums, gate_sum))
    share_sums = jnp.sum(share_sums, axis=0)
    gate_own = lax.all_to_all(
        gate_sum.reshape(2 * LOW, shard_rows, shard_units), ("lo", "y"), 0, 0, tiled=True
    )
    grad_inputs, gain_part = inputs_back(
        scalars, grad_qkv_mine, qkv_pieces, inputs, gain_one, grad_hidden
    )
    output = partial + valid_mine * (
        feed_near[0] + feed_got[0].astype(F32) + feed_far.astype(F32)
    )
    grad_attn_own = scatter_rows(attn_near, attn_far, many)
    last = jnp.concatenate([jnp.sum(gain_part, axis=0).reshape(-1), share_sums])
    last, gate_own = lax.optimization_barrier((last, gate_own))
    last = everywhere(last, all_axes, count)
    last, grad_attn_own = lax.optimization_barrier((last, grad_attn_own))
    grad_gain = jnp.sum(last[:, :width], axis=0)
    total = last[:, width:].reshape(32, width)
    return (
        output,
        grad_inputs,
        grad_prior,
        grad_gain,
        grad_attn_own[:, :local_width],
        grad_attn_own[:, local_width : 2 * local_width],
        grad_attn_own[:, 2 * local_width : 3 * local_width],
        grad_attn_own[:, 3 * local_width :].T,
        total[kinds + 4],
        total[:kinds].T,
        total[kinds + 8 : 2 * kinds + 8, :kinds],
        total[kinds : kinds + 4].reshape(2, 2, width).transpose(0, 2, 1),
        total[kinds + 5 : kinds + 7],
        gate_own.astype(F32),
        other_own[:, 0].astype(F32),
        other_own[:, 1].transpose(0, 2, 1).astype(F32),
    )


def solution(mesh):
    many = mesh.shape["fsdp"] // LOW
    fine = Mesh(mesh.devices.reshape(many, LOW, 2, 2), ("hi", "lo", "y", "c"))
    fsdp, tp = ("hi", "lo"), ("y", "c")
    every = fsdp + tp
    return jax.shard_map(
        functools.partial(per_device, many),
        mesh=fine,
        in_specs=(
            P(every, None),
            P(every, None),
            P(fsdp, None),
            P(fsdp, None),
            P(fsdp, None),
            P(fsdp, None),
            P(),
            P(fsdp, tp),
            P(fsdp, tp),
            P(fsdp, tp),
            P(tp, fsdp),
            P(),
            P(),
            P(),
            P(),
            P(),
            P(None, fsdp, tp),
            P(None, fsdp, tp),
            P(None, tp, fsdp),
        ),
        out_specs=(
            P(every, None),
            P(every, None),
            P(every, None),
            P(),
            P(fsdp, tp),
            P(fsdp, tp),
            P(fsdp, tp),
            P(tp, fsdp),
            P(),
            P(),
            P(),
            P(),
            P(),
            P(None, fsdp, tp),
            P(None, fsdp, tp),
            P(None, tp, fsdp),
        ),
        check_vma=False,
    )
```

```python
import functools

import jax
import jax.numpy as jnp
from jax import lax
from jax.experimental import pallas as pl
from jax.experimental.pallas import tpu as pltpu
from jax.sharding import Mesh
from jax.sharding import PartitionSpec as P

HEAD = 64
MAXLEN = 768
LOW = 4
SHARDS = 8
LOW_PLACE = 4
BOUNDS = 5
EPSILON = 1e-06
PRECISE = lax.Precision.HIGHEST
NEGATIVE = -1e30
F32 = jnp.float32
BF16 = jnp.bfloat16


def rms_norm(values, gain):
    return values * lax.rsqrt(jnp.mean(values * values, axis=-1, keepdims=True) + EPSILON) * gain


def swap(value, axis):
    return lax.ppermute(value, axis, [(0, 1), (1, 0)])


def gather_pieces(value):
    other = swap(value, "y")
    return [value, swap(value, "c"), other, swap(other, "c")]


def natural(pieces, index):
    ordered = []
    for j in range(4):
        item = pieces[j]
        for t in range(1, 4):
            item = jnp.where(index == t, pieces[j ^ t], item)
        ordered.append(item)
    return jnp.stack(ordered)


def add_core(near, sent):
    got = swap(sent, "c")
    return got, (near[1] + got[1].astype(F32)).astype(BF16)


def cost_of(microseconds):
    return pl.CostEstimate(
        flops=int(microseconds * 1.15e9), transcendentals=0, bytes_accessed=2**16
    )


def start_of(row, scalars):
    start_row = jnp.zeros_like(row)
    for k in range(BOUNDS, scalars.shape[0]):
        start_row = jnp.where(row >= scalars[k], scalars[k], start_row)
    return start_row


def for_window(first, block, pad, scalars, body):
    needed = (first - start_of(first, scalars) + block - 1) // block
    most = pad // block
    for blocks in range(most):
        pl.when(needed == blocks)(functools.partial(body, (blocks + 1) * block))
    pl.when(needed >= most)(functools.partial(body, pad + block))


def scores_mask(first_key, first_query, window, block, scalars):
    row = first_query + lax.broadcasted_iota(jnp.int32, (1, block), 1)
    start_row = start_of(row, scalars)
    key_places = first_key + lax.broadcasted_iota(jnp.int32, (window, block), 0)
    query_places = first_query + lax.broadcasted_iota(jnp.int32, (window, block), 1)
    return (key_places >= start_row) & (key_places <= query_places)


def attend_kernel(block, pad, scalars, *refs):
    pieces, refs = refs[:4], refs[4:]
    shards, refs = refs[:LOW], refs[LOW:]
    out_ref, lse_ref, qkv_ref, weight_ref, key_rows, value_pad, full = refs
    group = qkv_ref.shape[1]
    quarter = group // 4
    inner = qkv_ref.shape[0] // 3
    head = pl.program_id(0)

    @pl.when(head == 0)
    def _():
        rows = shards[0].shape[1]
        for r in range(SHARDS):
            place = pl.multiple_of((scalars[0] ^ r) * rows, rows)
            full[pl.ds(place, rows), :] = shards[r % LOW][r // LOW]
        turned = full[:, : 3 * inner].T
        weight_ref[...] = turned
        for r in range(4):
            place = pl.multiple_of((scalars[1] ^ r) * quarter, quarter)
            qkv_ref[:, pl.ds(place, quarter)] = lax.dot_general(
                turned, pieces[r][...], (((1,), (1,)), ((), ())), preferred_element_type=F32
            ).astype(BF16)

    first_row = pl.multiple_of(head * HEAD, HEAD)
    key_rows[pl.ds(0, pad), :] = jnp.zeros((pad, HEAD), BF16)
    value_pad[:, pl.ds(0, pad)] = jnp.zeros((HEAD, pad), BF16)
    key_rows[pl.ds(pad, group), :] = qkv_ref[pl.ds(inner + first_row, HEAD), :].T
    value_pad[:, pl.ds(pad, group)] = qkv_ref[pl.ds(2 * inner + first_row, HEAD), :]

    def one(i, carry):
        first = pl.multiple_of(i * block, block)

        def body(window):
            begin = pl.multiple_of(first + pad + block - window, block)
            scores = jnp.dot(
                key_rows[pl.ds(begin, window), :],
                qkv_ref[pl.ds(first_row, HEAD), pl.ds(first, block)],
                preferred_element_type=F32,
            )
            allowed = scores_mask(begin - pad, first, window, block, scalars)
            scores = jnp.where(allowed, scores * 0.125, NEGATIVE)
            highest = jnp.max(scores, axis=0, keepdims=True)
            weights = jnp.exp(scores - highest)
            total = jnp.sum(weights, axis=0, keepdims=True)
            mixed = jnp.dot(
                value_pad[:, pl.ds(begin, window)],
                weights.astype(BF16),
                preferred_element_type=F32,
            )
            mixed = (mixed / total).astype(BF16)
            column = pl.multiple_of(first % quarter, block)
            out_ref[first // quarter, :, pl.ds(column, block)] = mixed
            lse_ref[0, :, pl.ds(first, block)] = highest + jnp.log(total)

        for_window(first, block, pad, scalars, body)
        return carry

    lax.fori_loop(0, group // block, one, 0)


def attend(pieces, shards, scalars, heads):
    rows, width = pieces[0].shape
    group = 4 * rows
    inner = heads * HEAD
    block = 256

    def whole(shape):
        return pl.BlockSpec(
            shape, lambda i, _: (0,) * len(shape), pipeline_mode=pl.Buffered(1)
        )

    return pl.pallas_call(
        functools.partial(attend_kernel, block, MAXLEN),
        grid_spec=pltpu.PrefetchScalarGridSpec(
            num_scalar_prefetch=1,
            grid=(heads,),
            in_specs=[
                *[whole((rows, width)) for _ in range(4)],
                *[whole(shards[0].shape) for _ in range(LOW)],
            ],
            out_specs=[
                pl.BlockSpec((4, HEAD, rows), lambda h, _: (0, h, 0)),
                pl.BlockSpec((1, 1, group), lambda h, _: (h, 0, 0)),
                whole((3 * inner, group)),
                whole((3 * inner, width)),
            ],
            scratch_shapes=[
                pltpu.VMEM((MAXLEN + group, HEAD), BF16),
                pltpu.VMEM((HEAD, MAXLEN + group), BF16),
                pltpu.VMEM((width, 4 * inner), BF16),
            ],
        ),
        out_shape=[
            jax.ShapeDtypeStruct((4, inner, rows), BF16),
            jax.ShapeDtypeStruct((heads, 1, group), F32),
            jax.ShapeDtypeStruct((3 * inner, group), BF16),
            jax.ShapeDtypeStruct((3 * inner, width), BF16),
        ],
        compiler_params=pltpu.CompilerParams(vmem_limit_bytes=48 * 2**20),
        cost_estimate=cost_of(24),
        name="attend",
    )(scalars, *pieces, *shards)


def attn_grads_kernel(scalars, *refs):
    grad_qkv, mixed, refs = refs[0], refs[1], refs[2:]
    tokens, grads, refs = refs[:4], refs[4:8], refs[8:]
    outs, (total,) = refs[:2], refs[2:]
    inner3 = grad_qkv.shape[1]
    first, second = 0.0, 0.0
    for r in range(4):
        j = scalars[1] ^ r
        first += jnp.dot(grad_qkv[r], tokens[r][...], preferred_element_type=F32)
        second += jnp.dot(mixed[j], grads[r][...], preferred_element_type=F32)
    total[:, :inner3] = first.T.astype(BF16)
    total[:, inner3:] = second.T.astype(BF16)
    rows = outs[0].shape[1]
    for r in range(SHARDS):
        place = pl.multiple_of((scalars[0] ^ r) * rows, rows)
        outs[r // LOW][r % LOW] = total[pl.ds(place, rows), :]


def attn_grads(grad_qkv, mixed, tokens, grads, scalars):
    width = tokens[0].shape[1]
    columns = grad_qkv.shape[1] + mixed.shape[1]
    rows = width // SHARDS
    whole = pl.BlockSpec(memory_space=pltpu.VMEM)
    return pl.pallas_call(
        attn_grads_kernel,
        in_specs=[pl.BlockSpec(memory_space=pltpu.SMEM)] + [whole] * 10,
        out_specs=[whole] * 2,
        out_shape=[jax.ShapeDtypeStruct((LOW, rows, columns), BF16)] * 2,
        scratch_shapes=[pltpu.VMEM((width, columns), BF16)],
        compiler_params=pltpu.CompilerParams(vmem_limit_bytes=48 * 2**20),
        cost_estimate=cost_of(0.1),
        name="attn_grads",
    )(scalars, grad_qkv, mixed, *tokens, *grads)


def attend_back_kernel(block, pad, scalars, qkv_ref, lse_ref, *refs):
    pieces, refs = refs[:4], refs[4:]
    out_ref, grad_mixed, key_rows, value_rows, key_pad, grad_key, grad_value = refs
    group = qkv_ref.shape[1]
    inner_rows = qkv_ref.shape[0] // 3
    quarter = group // 4
    contract_last = (((1,), (1,)), ((), ()))
    head = pl.program_id(0)

    @pl.when(head == 0)
    def _():
        for r in range(4):
            place = pl.multiple_of((scalars[1] ^ r) * quarter, quarter)
            grad_mixed[:, pl.ds(place, quarter)] = pieces[r][...]

    first_row = pl.multiple_of(head * HEAD, HEAD)
    keys = qkv_ref[pl.ds(inner_rows + first_row, HEAD), :]
    key_rows[pl.ds(0, pad), :] = jnp.zeros((pad, HEAD), BF16)
    value_rows[pl.ds(0, pad), :] = jnp.zeros((pad, HEAD), BF16)
    key_pad[:, pl.ds(0, pad)] = jnp.zeros((HEAD, pad), BF16)
    key_rows[pl.ds(pad, group), :] = keys.T
    value_rows[pl.ds(pad, group), :] = qkv_ref[pl.ds(2 * inner_rows + first_row, HEAD), :].T
    key_pad[:, pl.ds(pad, group)] = keys
    grad_key[...] = jnp.zeros_like(grad_key)
    grad_value[...] = jnp.zeros_like(grad_value)

    def one(i, carry):
        first = pl.multiple_of(i * block, block)

        def body(window):
            begin = pl.multiple_of(first + pad + block - window, block)
            query = qkv_ref[pl.ds(first_row, HEAD), pl.ds(first, block)]
            grad = grad_mixed[pl.ds(first_row, HEAD), pl.ds(first, block)]
            scores = jnp.dot(key_rows[pl.ds(begin, window), :], query, preferred_element_type=F32)
            allowed = scores_mask(begin - pad, first, window, block, scalars)
            exponent = scores * 0.125 - lse_ref[0, :, pl.ds(first, block)]
            probs = jnp.exp(jnp.where(allowed, exponent, NEGATIVE))
            grad_probs = jnp.dot(
                value_rows[pl.ds(begin, window), :], grad, preferred_element_type=F32
            )
            inner = jnp.sum(probs * grad_probs, axis=0, keepdims=True)
            raw = (0.125 * (probs * (grad_probs - inner))).astype(BF16)
            grad_query = jnp.dot(
                key_pad[:, pl.ds(begin, window)], raw, preferred_element_type=F32
            )
            column = pl.multiple_of(first % quarter, block)
            piece = (first // quarter) ^ scalars[1]
            out_ref[piece, 0, :, pl.ds(column, block)] = grad_query.astype(BF16)
            grad_value[:, pl.ds(begin, window)] += lax.dot_general(
                grad, probs.astype(BF16), contract_last, preferred_element_type=F32
            )
            grad_key[:, pl.ds(begin, window)] += lax.dot_general(
                query, raw, contract_last, preferred_element_type=F32
            )

        for_window(first, block, pad, scalars, body)
        return carry

    lax.fori_loop(0, group // block, one, 0)
    for j in range(4):
        piece = scalars[1] ^ j
        out_ref[piece, 1] = grad_key[:, pl.ds(pad + j * quarter, quarter)].astype(BF16)
        out_ref[piece, 2] = grad_value[:, pl.ds(pad + j * quarter, quarter)].astype(BF16)


def attend_back(scalars, qkv, lse, pieces, heads):
    group = qkv.shape[1]
    block = 256

    def whole(shape):
        return pl.BlockSpec(
            shape, lambda i, _: (0,) * len(shape), pipeline_mode=pl.Buffered(1)
        )

    return pl.pallas_call(
        functools.partial(attend_back_kernel, block, MAXLEN),
        grid_spec=pltpu.PrefetchScalarGridSpec(
            num_scalar_prefetch=1,
            grid=(heads,),
            in_specs=[
                whole(qkv.shape),
                pl.BlockSpec((1, 1, group), lambda h, _: (h, 0, 0)),
                *[whole(item.shape) for item in pieces],
            ],
            out_specs=pl.BlockSpec((4, 3, HEAD, group // 4), lambda h, _: (0, 0, h, 0)),
            scratch_shapes=[
                pltpu.VMEM((heads * HEAD, group), BF16),
                pltpu.VMEM((MAXLEN + group, HEAD), BF16),
                pltpu.VMEM((MAXLEN + group, HEAD), BF16),
                pltpu.VMEM((HEAD, MAXLEN + group), BF16),
                pltpu.VMEM((HEAD, MAXLEN + group), F32),
                pltpu.VMEM((HEAD, MAXLEN + group), F32),
            ],
        ),
        out_shape=jax.ShapeDtypeStruct((4, 3, heads * HEAD, group // 4), BF16),
        compiler_params=pltpu.CompilerParams(vmem_limit_bytes=48 * 2**20),
        cost_estimate=cost_of(34),
        name="attend_back",
    )(scalars, qkv, lse, *pieces)


def mixed_back_kernel(scalars, grad_ref, p0, p1, p2, p3, *refs):
    outs, weight = refs[:4], refs[4]
    rows = p0.shape[2]
    for r, shards in enumerate((p0, p1, p2, p3)):
        for k in range(SHARDS):
            place = pl.multiple_of((scalars[0] ^ k) * rows, rows)
            weight[pl.ds(place, rows), :] = shards[k % LOW, k // LOW]
        outs[r][...] = lax.dot_general(
            weight[...].T, grad_ref[...], (((1,), (1,)), ((), ())), preferred_element_type=F32
        ).astype(BF16)


def mixed_back(scalars, grad, weights):
    rows, width = grad.shape
    inner = weights[0].shape[3]

    def whole(shape):
        return pl.BlockSpec(shape, lambda i, _: (0,) * len(shape))

    return pl.pallas_call(
        mixed_back_kernel,
        grid_spec=pltpu.PrefetchScalarGridSpec(
            num_scalar_prefetch=1,
            grid=(1,),
            in_specs=[whole(grad.shape), *[whole(item.shape) for item in weights]],
            out_specs=[whole((inner, rows)) for _ in range(4)],
            scratch_shapes=[pltpu.VMEM((width, inner), BF16)],
        ),
        out_shape=[jax.ShapeDtypeStruct((inner, rows), BF16) for _ in range(4)],
        compiler_params=pltpu.CompilerParams(vmem_limit_bytes=32 * 2**20),
        cost_estimate=cost_of(4),
        name="mixed_back",
    )(scalars, grad, *weights)


def inputs_back_kernel(g0, g1, g2, g3, p0, p1, p2, p3, x_ref, gain_ref, hidden_ref, out_ref, sum_ref):
    total = 0.0
    for grad, weight in zip((g0, g1, g2, g3), (p0, p1, p2, p3)):
        total += jnp.dot(grad[...].T, weight[...], preferred_element_type=F32)
    x = x_ref[...]
    scale = lax.rsqrt(jnp.mean(x * x, axis=1, keepdims=True) + EPSILON)
    through = total * gain_ref[...]
    inner = jnp.mean(through * x, axis=1, keepdims=True)
    out_ref[...] = hidden_ref[...] + scale * through - (scale * scale * scale * inner) * x
    sum_ref[0] = jnp.sum(total * x * scale, axis=0, keepdims=True)


def inputs_back(grads, weights, x, gain, grad_hidden):
    rows, width = x.shape
    block = rows // 2

    def whole(shape):
        return pl.BlockSpec(shape, lambda i: (0,) * len(shape), pipeline_mode=pl.Buffered(1))

    part = pl.BlockSpec((block, width), lambda i: (i, 0))
    return pl.pallas_call(
        inputs_back_kernel,
        grid=(2,),
        in_specs=[
            *[pl.BlockSpec((item.shape[0], block), lambda i: (0, i)) for item in grads],
            *[whole(item.shape) for item in weights],
            part,
            whole(gain.shape),
            part,
        ],
        out_specs=[part, pl.BlockSpec((1, 1, width), lambda i: (i, 0, 0))],
        out_shape=[
            jax.ShapeDtypeStruct(x.shape, F32),
            jax.ShapeDtypeStruct((2, 1, width), F32),
        ],
        compiler_params=pltpu.CompilerParams(vmem_limit_bytes=48 * 2**20),
        cost_estimate=cost_of(6),
        name="inputs_back",
    )(*grads, *weights, x, gain, grad_hidden)


def expert_kernel(
    kinds, scalars, w_gate, *refs
):
    near_pieces, far_pieces, refs = refs[:2], refs[2:6], refs[6:]
    x_blocks, g_blocks, refs = refs[: 2 * LOW], refs[2 * LOW : 4 * LOW], refs[4 * LOW :]
    back_own, back_send, feed_own, feed_send, grads_out, *refs = refs
    x_all, g_all, x_t, g_t, weights, hidden, acc_feed, acc_back, scales, plain = refs
    slots, width = feed_own.shape
    block = slots // LOW
    half = width // 2
    step = pl.program_id(0)
    contract_last = (((1,), (1,)), ((), ()))
    units = weights.shape[2]

    def weight_column(x_ref):
        extra = x_ref[:, width:].astype(F32)
        lanes = lax.broadcasted_iota(jnp.int32, extra.shape, 1)
        named = (lanes == scalars[0]) | (lanes == scalars[0] + kinds)
        return jnp.sum(jnp.where(named, extra, 0.0), axis=1, keepdims=True)

    @pl.when(step == 0)
    def _():
        for i in range(2 * LOW):
            rows = pl.ds(i * block, block)
            scale = weight_column(x_blocks[i])
            scales[rows, :] = jnp.broadcast_to(scale, (block, 128))
            plain[rows, :] = g_blocks[i][...]
            x_all[rows, :] = x_blocks[i][:, :width]
            g_all[rows, :] = (g_blocks[i][...].astype(F32) * scale).astype(BF16)
        x_t[...] = x_all[...].T
        g_t[...] = g_all[...].T
        acc_feed[...] = jnp.zeros_like(acc_feed)
        acc_back[...] = jnp.zeros_like(acc_back)

    for i in range(2):
        rows = pl.ds(i * half, half)
        weights[0, rows, :] = w_gate[:, 0, i].reshape(half, units)
    near = pl.multiple_of(scalars[1] * half, half)
    for k in range(2):
        weights[k + 1, pl.ds(near, half), :] = near_pieces[k][:, 0].reshape(half, units)
        place = (1 - scalars[1]) * half
        for piece in far_pieces[2 * k : 2 * k + 2]:
            rows = piece.shape[0] * half // LOW
            weights[k + 1, pl.ds(pl.multiple_of(place, half // LOW), rows), :] = piece[
                :, 0
            ].reshape(rows, units)
            place += rows

    for part in range(2):
        rows = pl.ds(part * slots, slots)
        x = x_all[rows, :]
        gate = jnp.dot(x, weights[0], preferred_element_type=F32)
        up = jnp.dot(x, weights[1], preferred_element_type=F32)
        grad_act = jnp.dot(g_all[rows, :], weights[2], preferred_element_type=F32)
        sig = jax.nn.sigmoid(gate)
        silu = gate * sig
        active = (silu * up).astype(BF16)
        grad_gate = (grad_act * up * (sig * (1.0 + gate * (1.0 - sig)))).astype(BF16)
        grad_up = (grad_act * silu).astype(BF16)
        hidden[0, rows, :] = grad_gate
        hidden[1, rows, :] = grad_up
        hidden[2, rows, :] = active
        acc_feed[rows, :] += lax.dot_general(
            active, weights[2], contract_last, preferred_element_type=F32
        )
        acc_back[rows, :] += lax.dot_general(
            grad_gate, weights[0], contract_last, preferred_element_type=F32
        ) + lax.dot_general(grad_up, weights[1], contract_last, preferred_element_type=F32)

    for k in range(3):
        left = (g_t if k == 2 else x_t)
        grad = jnp.dot(left[...], hidden[k], preferred_element_type=F32).astype(BF16)
        for i in range(2):
            part = grad[i * half : (i + 1) * half].reshape(LOW, -1, units)
            grads_out[i, :, 0, k] = part

    @pl.when(step == pl.num_programs(0) - 1)
    def _():
        for part in range(2):
            rows = pl.ds(part * slots, slots)
            feed = acc_feed[rows, :]
            inner = jnp.sum(feed * plain[rows, :].astype(F32), axis=1, keepdims=True)
            feed = feed * scales[rows, 0:1]
            lanes = lax.broadcasted_iota(jnp.int32, (slots, 128), 1)
            if part == 0:
                back_own[:, :width] = acc_back[rows, :]
                back_own[:, width:] = jnp.where(lanes == scalars[0], inner, 0.0)
                feed_own[...] = feed
            else:
                high = inner.astype(BF16).astype(F32)
                extra = jnp.where(lanes == scalars[0], high, 0.0)
                extra = jnp.where(lanes == scalars[0] + kinds, inner - high, extra)
                back_send[:, :width] = acc_back[rows, :].astype(BF16)
                back_send[:, width:] = extra.astype(BF16)
                feed_send[...] = feed.astype(BF16)


def expert_pass(kinds, scalars, x_blocks, g_blocks, w_gate, w_near, w_far):
    block, width = g_blocks[0].shape
    slots = LOW * block
    low, parities, _, shard_rows, shard_units = w_gate.shape
    units = 256
    steps = shard_units // units

    def whole(shape):
        return pl.BlockSpec(
            shape, lambda i, _: (0,) * len(shape), pipeline_mode=pl.Buffered(1)
        )

    grads_spec = pl.BlockSpec(
        (2, low, 1, 3, shard_rows, units), lambda i, _: (0, 0, i // steps, 0, 0, i % steps)
    )
    gate_spec = pl.BlockSpec(
        (low, 1, 2, shard_rows, units), lambda i, _: (0, i // steps, 0, 0, i % steps)
    )
    def up_spec(count):
        return pl.BlockSpec(
            (count, 1, shard_rows, units), lambda i, _: (0, i // steps, 0, i % steps)
        )

    wide = width + 128
    return pl.pallas_call(
        functools.partial(expert_kernel, kinds),
        grid_spec=pltpu.PrefetchScalarGridSpec(
            num_scalar_prefetch=1,
            grid=(parities * steps,),
            in_specs=[
                gate_spec,
                *[up_spec(item.shape[0]) for item in (*w_near, *w_far)],
                *[whole((block, wide)) for _ in range(2 * LOW)],
                *[whole((block, width)) for _ in range(2 * LOW)],
            ],
            out_specs=[
                whole((slots, wide)),
                whole((slots, wide)),
                whole((slots, width)),
                whole((slots, width)),
                grads_spec,
            ],
            scratch_shapes=[
                pltpu.VMEM((2 * slots, width), BF16),
                pltpu.VMEM((2 * slots, width), BF16),
                pltpu.VMEM((width, 2 * slots), BF16),
                pltpu.VMEM((width, 2 * slots), BF16),
                pltpu.VMEM((3, width, units), BF16),
                pltpu.VMEM((3, 2 * slots, units), BF16),
                pltpu.VMEM((2 * slots, width), F32),
                pltpu.VMEM((2 * slots, width), F32),
                pltpu.VMEM((2 * slots, 128), F32),
                pltpu.VMEM((2 * slots, width), BF16),
            ],
        ),
        out_shape=[
            jax.ShapeDtypeStruct((slots, wide), F32),
            jax.ShapeDtypeStruct((slots, wide), BF16),
            jax.ShapeDtypeStruct((slots, width), F32),
            jax.ShapeDtypeStruct((slots, width), BF16),
            jax.ShapeDtypeStruct((2, low, parities, 3, shard_rows, shard_units), BF16),
        ],
        compiler_params=pltpu.CompilerParams(vmem_limit_bytes=58 * 2**20),
        cost_estimate=cost_of(35),
        name="expert_pass",
    )(scalars, w_gate, *w_near, *w_far, *x_blocks, *g_blocks)


def pick_kernel(ids_ref, *refs):
    pieces, outs = refs[:4], refs[4:]
    block = outs[0].shape[0]
    rows = pieces[0].shape[0]
    for i, out_ref in enumerate(outs):
        slot = i * block + lax.broadcasted_iota(jnp.int32, (block, rows), 0)
        total = 0.0
        for r in range(4):
            columns = pl.ds(r * rows, rows)
            held = (slot == ids_ref[0:1, columns]) | (slot == ids_ref[1:2, columns])
            held = jnp.where(held, 1.0, 0.0).astype(BF16)
            total += jnp.dot(held, pieces[r][...], preferred_element_type=F32)
        out_ref[...] = total.astype(BF16)


def pick(ids, pieces, slots):
    rows, width = pieces[0].shape
    block = slots // LOW

    def whole(shape):
        return pl.BlockSpec(shape, lambda i: (0, 0))

    return pl.pallas_call(
        pick_kernel,
        grid=(1,),
        in_specs=[whole((8, 4 * rows)), *[whole((rows, width)) for _ in range(4)]],
        out_specs=[whole((block, width)) for _ in range(LOW)],
        out_shape=[jax.ShapeDtypeStruct((block, width), BF16) for _ in range(LOW)],
        compiler_params=pltpu.CompilerParams(vmem_limit_bytes=32 * 2**20),
        cost_estimate=cost_of(5),
        name="pick",
    )(ids, *pieces)


def to_experts(blocks):
    return [blocks[0]] + [flip(blocks[b], "lo", LOW, b) for b in range(1, LOW)]


def to_heads(blocks):
    return [blocks[0]] + [
        lax.ppermute(blocks[r], ("y", "c"), [(i, i ^ r) for i in range(4)]) for r in range(1, 4)
    ]


def back_sum_kernel(kinds, own_ref, core_ref, *outs):
    width = own_ref.shape[1] - 128
    block = outs[0].shape[0]
    for i, out_ref in enumerate(outs):
        rows = pl.ds(i * block, block)
        out_ref[:, :width] = (
            own_ref[rows, :width] + core_ref[rows, :width].astype(F32)
        ).astype(BF16)
        extra = own_ref[rows, width:] + core_ref[rows, width:].astype(F32)
        lanes = lax.broadcasted_iota(jnp.int32, extra.shape, 1)
        high = jnp.where(lanes < kinds, extra, 0.0).astype(BF16).astype(F32)
        low = jnp.where(lanes < kinds, extra - high, 0.0)
        low = pltpu.roll(low, kinds, 1) + jnp.where(lanes >= kinds, extra, 0.0)
        out_ref[:, width:] = (high + low).astype(BF16)


def back_sum(kinds, own, core):
    slots, wide = own.shape
    block = slots // LOW

    def whole(shape):
        return pl.BlockSpec(shape, lambda i: (0, 0))

    return pl.pallas_call(
        functools.partial(back_sum_kernel, kinds),
        grid=(1,),
        in_specs=[whole(own.shape), whole(core.shape)],
        out_specs=[whole((block, wide)) for _ in range(LOW)],
        out_shape=[jax.ShapeDtypeStruct((block, wide), BF16) for _ in range(LOW)],
        compiler_params=pltpu.CompilerParams(vmem_limit_bytes=32 * 2**20),
        cost_estimate=cost_of(3),
        name="back_sum",
    )(own, core)


def feed_sum_kernel(own_ref, core_ref, *outs):
    block = outs[0].shape[0]
    for i, out_ref in enumerate(outs):
        rows = pl.ds(i * block, block)
        out_ref[...] = (own_ref[rows, :] + core_ref[rows, :].astype(F32)).astype(BF16)


def feed_sum(own, core):
    slots, width = own.shape
    block = slots // LOW

    def whole(shape):
        return pl.BlockSpec(shape, lambda i: (0, 0))

    return pl.pallas_call(
        feed_sum_kernel,
        grid=(1,),
        in_specs=[whole(own.shape), whole(core.shape)],
        out_specs=[whole((block, width)) for _ in range(LOW)],
        out_shape=[jax.ShapeDtypeStruct((block, width), BF16) for _ in range(LOW)],
        compiler_params=pltpu.CompilerParams(vmem_limit_bytes=32 * 2**20),
        cost_estimate=cost_of(3),
        name="feed_sum",
    )(own, core)


def spread_kernel(ids_ref, *refs):
    blocks, (near_ref, send_ref, slots_ref) = refs[:LOW], refs[LOW:]
    rows = near_ref.shape[1]
    slots = slots_ref.shape[0]
    block = slots // LOW

    @pl.when(pl.program_id(0) == 0)
    def _():
        for i in range(LOW):
            slots_ref[pl.ds(i * block, block), :] = blocks[i][...]

    for k, out_ref in enumerate((near_ref, send_ref)):
        slot = lax.broadcasted_iota(jnp.int32, (rows, slots), 1)
        ids = ids_ref[pl.ds(k * rows, rows), :]
        held = (slot == ids[:, 0:1]) | (slot == ids[:, 1:2])
        held = jnp.where(held, 1.0, 0.0).astype(BF16)
        total = jnp.dot(held, slots_ref[...], preferred_element_type=F32)
        out_ref[0] = total.astype(out_ref.dtype)


def spread(ids, values, rows):
    block, width = values[0].shape
    return pl.pallas_call(
        spread_kernel,
        grid=(2,),
        in_specs=[
            pl.BlockSpec((2 * rows, 8), lambda i: (i, 0)),
            *[pl.BlockSpec((block, width), lambda i: (0, 0)) for _ in range(LOW)],
        ],
        out_specs=[
            pl.BlockSpec((1, rows, width), lambda i: (i, 0, 0)),
            pl.BlockSpec((1, rows, width), lambda i: (i, 0, 0)),
        ],
        out_shape=[
            jax.ShapeDtypeStruct((2, rows, width), F32),
            jax.ShapeDtypeStruct((2, rows, width), BF16),
        ],
        scratch_shapes=[pltpu.VMEM((LOW * block, width), BF16)],
        compiler_params=pltpu.CompilerParams(vmem_limit_bytes=32 * 2**20),
        cost_estimate=cost_of(0.1),
        name="spread",
    )(ids, *values)


def slots_kernel(experts, capacity, scalars, routes_col, order_col, routes_row, order_row,
                 row_ref, col_ref, places_ref):
    group = routes_row.shape[1]
    rows = group // 4
    share = capacity // 2
    span = 2 * group
    bound = scalars[BOUNDS + 2]

    def target_of(routes, axis):
        place = lax.broadcasted_iota(jnp.int32, routes.shape, axis)
        return jnp.where((routes < experts) & (place < bound), routes, experts)

    target = target_of(routes_row[...], 1)
    code = target * span + order_row[...]
    block = 256

    def count(i, carry):
        first = pl.multiple_of(i * block, block)
        routes = routes_col[pl.ds(first, block), :]
        place = first + lax.broadcasted_iota(jnp.int32, routes.shape, 0)
        held = jnp.where((routes < experts) & (place < bound), routes, experts)
        others = held * span + order_col[pl.ds(first, block), :]
        result = []
        for k in range(2):
            total = carry[k]
            for j in range(2):
                smaller = jnp.where(others[:, j : j + 1] < code[k : k + 1, :], 1.0, 0.0)
                total = total + jnp.sum(smaller, axis=0, keepdims=True)
            result.append(total)
        return tuple(result)

    zero = jnp.zeros((1, group), F32)
    counts = lax.fori_loop(0, group // block, count, (zero, zero))
    for k in range(2):
        mine_target = target[k : k + 1, :]
        base = jnp.zeros((1, group), F32)
        for e in range(1, experts):
            earlier = jnp.sum(jnp.where(target < e, 1.0, 0.0))
            base = jnp.where(mine_target == e, earlier, base)
        place = (counts[k] - base).astype(jnp.int32)
        first = scalars[3] * share
        held = (
            (mine_target < experts)
            & (place >= first)
            & (place < first + share)
            & (place < capacity)
            & (jnp.bitwise_and(mine_target, 1) == scalars[2])
        )
        block = jnp.bitwise_xor(lax.shift_right_logical(mine_target, 1), scalars[LOW_PLACE])
        slot = block * share + place - first
        places_ref[k : k + 1, :] = jnp.where(held, slot, -1)
    for r in range(4):
        start = pl.multiple_of((scalars[1] ^ r) * rows, rows)
        piece = places_ref[:, pl.ds(start, rows)]
        row_ref[:, pl.ds(r * rows, rows)] = piece
        col_ref[pl.ds(r * rows, rows), :] = piece.T


def slots_of(scalars, routes, drop_order, experts, capacity):
    group = routes.shape[0]
    whole = pl.BlockSpec(memory_space=pltpu.VMEM)
    return pl.pallas_call(
        functools.partial(slots_kernel, experts, capacity),
        in_specs=[pl.BlockSpec(memory_space=pltpu.SMEM)] + [whole] * 4,
        out_specs=[whole] * 2,
        out_shape=[
            jax.ShapeDtypeStruct((8, group), jnp.int32),
            jax.ShapeDtypeStruct((group, 8), jnp.int32),
        ],
        scratch_shapes=[pltpu.VMEM((8, group), jnp.int32)],
        compiler_params=pltpu.CompilerParams(vmem_limit_bytes=32 * 2**20),
        cost_estimate=cost_of(8),
        name="slots",
    )(scalars, routes, drop_order, routes.T, drop_order.T)


def middle_kernel(kinds, scalars, mixed, p0, p1, p2, p3, x_ref, gain_ref, router_w, prior_ref,
                  prior_w, hidden_ref, sent_ref, router_ref, weight):
    hidden = x_ref[...]
    rows = p0.shape[2]
    for r, shards in enumerate((p0, p1, p2, p3)):
        for k in range(SHARDS):
            place = pl.multiple_of((scalars[0] ^ k) * rows, rows)
            weight[r, pl.ds(place, rows), :] = shards[k % LOW, k // LOW]
        hidden += lax.dot_general(
            mixed[scalars[1] ^ r].T, weight[r], (((1,), (1,)), ((), ())),
            preferred_element_type=F32,
        )
    hidden_ref[...] = hidden
    scale = lax.rsqrt(jnp.mean(hidden * hidden, axis=1, keepdims=True) + EPSILON)
    rounded = (hidden * scale * gain_ref[...]).astype(BF16)
    width = hidden.shape[1]
    sent_ref[:, :width] = rounded
    router_high, router_low = halves(router_w[...])
    logits = (
        jnp.dot(rounded, router_high, preferred_element_type=F32)
        + jnp.dot(rounded, router_low, preferred_element_type=F32)
        + split_dot(prior_ref[...], prior_w[...])
    )
    lanes = lax.broadcasted_iota(jnp.int32, logits.shape, 1)
    logits = jnp.where(lanes < 2 * kinds, logits, NEGATIVE)
    weights = jnp.exp(logits - jnp.max(logits, axis=1, keepdims=True))
    total = jnp.sum(jnp.where(lanes < kinds, weights, 0.0), axis=1, keepdims=True)
    router = weights / total
    router_ref[...] = router
    high = router.astype(BF16).astype(F32)
    sent_ref[:, width:] = jnp.where(lanes < kinds, high, router - high).astype(BF16)


def middle(kinds, scalars, mixed, weights, x, gain, router_w, prior, prior_w):
    rows, width = x.shape
    lanes = router_w.shape[1]

    def whole(shape):
        return pl.BlockSpec(shape, lambda i, _: (0,) * len(shape))

    return pl.pallas_call(
        functools.partial(middle_kernel, kinds),
        grid_spec=pltpu.PrefetchScalarGridSpec(
            num_scalar_prefetch=1,
            grid=(1,),
            in_specs=[
                whole(mixed.shape),
                *[whole(item.shape) for item in weights],
                whole(x.shape),
                whole(gain.shape),
                whole(router_w.shape),
                pl.BlockSpec((rows, kinds), lambda i, scalars: (scalars[1], 0)),
                whole(prior_w.shape),
            ],
            out_specs=[whole((rows, width)), whole((rows, width + lanes)), whole((rows, lanes))],
            scratch_shapes=[pltpu.VMEM((4, width, mixed.shape[1]), BF16)],
        ),
        out_shape=[
            jax.ShapeDtypeStruct((rows, width), F32),
            jax.ShapeDtypeStruct((rows, width + lanes), BF16),
            jax.ShapeDtypeStruct((rows, lanes), F32),
        ],
        compiler_params=pltpu.CompilerParams(vmem_limit_bytes=48 * 2**20),
        cost_estimate=cost_of(6),
        name="middle",
    )(scalars, mixed, *weights, x, gain, router_w, prior, prior_w)


def halves(value):
    high = value.astype(BF16)
    return high, (value - high.astype(F32)).astype(BF16)


def split_dot(left, right):
    (left_high, left_low), (right_high, right_low) = halves(left), halves(right)
    return (
        jnp.dot(left_high, right_high, preferred_element_type=F32)
        + jnp.dot(left_low, right_high, preferred_element_type=F32)
        + jnp.dot(left_high, right_low, preferred_element_type=F32)
    )


def turned_dot(left, right):
    high, low = halves(left.T)
    return jnp.dot(high, right, preferred_element_type=F32) + jnp.dot(
        low, right, preferred_element_type=F32
    )


def router_back_kernel(kinds, experts, scalars, near_ref, got_ref, far_ref, hidden_ref, router_ref,
                       routes_ref, cotangent_ref, prior_ref, gain_ref, small_ref, small_t_ref,
                       vector_ref, prior_w_ref,
                       grad_hidden_ref, grad_low_ref, partial_ref, grad_prior_ref, sums_ref):
    step = pl.program_id(0)
    rows, width = hidden_ref.shape
    place = scalars[1] * rows * pl.num_programs(0) + step * rows
    valid = place + lax.broadcasted_iota(jnp.int32, (rows, 1), 0) < scalars[BOUNDS + 2]
    valid = jnp.where(valid, 1.0, 0.0)
    back = near_ref[0] + got_ref[0].astype(F32) + far_ref[...].astype(F32)
    hidden = hidden_ref[...]
    grad_out = cotangent_ref[...] * valid
    scale = lax.rsqrt(jnp.mean(hidden * hidden, axis=1, keepdims=True) + EPSILON)
    unit = hidden * scale
    normed = unit * gain_ref[...]
    router = router_ref[...]
    lanes = lax.broadcasted_iota(jnp.int32, router.shape, 1)
    routes = routes_ref[...]

    def column(array, k):
        return jnp.sum(jnp.where(lanes == k, array, 0.0), axis=1, keepdims=True)

    def named(kind):
        return jnp.where((routes[:, 0:1] == kind) | (routes[:, 1:2] == kind), 1.0, 0.0)

    copy, first, second = (named(experts + k) for k in (1, 2, 3))
    weight_copy = column(router, experts + 1) * copy
    weight_first = column(router, experts + 2) * first
    weight_second = column(router, experts + 3) * second
    mixlog = split_dot(normed, small_ref[...])

    def softmax_two(k):
        one, two = column(mixlog, k), column(mixlog, k + 1)
        highest = jnp.maximum(one, two)
        one, two = jnp.exp(one - highest), jnp.exp(two - highest)
        return one / (one + two), two / (one + two)

    mix_one, mix_two = softmax_two(kinds), softmax_two(kinds + 2)
    vector_one, vector_two = vector_ref[0:1, :], vector_ref[1:2, :]
    along = jnp.sum(normed * grad_out, axis=1, keepdims=True)
    along_one = jnp.sum(vector_one * grad_out, axis=1, keepdims=True)
    along_two = jnp.sum(vector_two * grad_out, axis=1, keepdims=True)

    extra = back[:, width:]
    pairs = jnp.where(lanes < kinds, extra, 0.0) + jnp.where(
        lanes < kinds, pltpu.roll(extra, extra.shape[1] - kinds, 1), 0.0
    )
    grad_router = pairs + jnp.where(lanes == experts + 1, copy * along, 0.0)
    grad_router += jnp.where(
        lanes == experts + 2, first * (mix_one[0] * along + mix_one[1] * along_one), 0.0
    )
    grad_router += jnp.where(
        lanes == experts + 3, second * (mix_two[0] * along + mix_two[1] * along_two), 0.0
    )
    held = jnp.where(lanes < kinds, router, 0.0)
    grad_small = held * (grad_router - jnp.sum(held * grad_router, axis=1, keepdims=True))
    grad_prior_ref[...] = split_dot(grad_small, prior_w_ref[...])[:, :kinds]
    grad_logits = grad_small

    def mixed_back(weight, mix, other, k):
        one, two = weight * along, weight * other
        inner = mix[0] * one + mix[1] * two
        return jnp.where(lanes == k, mix[0] * (one - inner), 0.0) + jnp.where(
            lanes == k + 1, mix[1] * (two - inner), 0.0
        )

    grad_mixlog = mixed_back(weight_first, mix_one, along_one, kinds) + mixed_back(
        weight_second, mix_two, along_two, kinds + 2
    )
    grad_small = grad_logits + grad_mixlog
    share = weight_copy + weight_first * mix_one[0] + weight_second * mix_two[0]
    grad_normed = (
        back[:, :width]
        + share * grad_out
        + split_dot(grad_small, small_t_ref[...])
    )
    through = grad_normed * gain_ref[...]
    inner = jnp.mean(through * hidden, axis=1, keepdims=True)
    grad_hidden = grad_out + scale * through - (scale * scale * scale * inner) * hidden
    grad_hidden_ref[...] = grad_hidden
    grad_low_ref[...] = grad_hidden.astype(BF16)
    vector_first, vector_second = weight_first * mix_one[1], weight_second * mix_two[1]
    partial_ref[...] = valid * (
        hidden + share * normed + vector_first * vector_one + vector_second * vector_two
    )

    @pl.when(step == 0)
    def _():
        sums_ref[...] = jnp.zeros_like(sums_ref)

    vectors = jnp.where(lanes == kinds + 5, vector_first, 0.0) + jnp.where(
        lanes == kinds + 6, vector_second, 0.0
    )
    low = normed.astype(BF16)
    total = turned_dot(grad_small, low) + turned_dot(vectors, grad_out.astype(BF16))
    sums_ref[: kinds + 8, :] += total[: kinds + 8, :]
    sums_ref[kinds + 4 : kinds + 5, :] += jnp.sum(grad_normed * unit, axis=0, keepdims=True)
    prior = split_dot(prior_ref[...].T, grad_logits)
    sums_ref[pl.ds(kinds + 8, kinds), : lanes.shape[1]] += prior


def router_back(kinds, experts, scalars, near, got, far, hidden, router, routes, cotangent, prior,
                gain, small, small_t, vector, prior_w):
    rows, width = hidden.shape
    block = rows // 2
    lanes = router.shape[1]

    def whole(shape):
        return pl.BlockSpec(shape, lambda i, _: (0,) * len(shape))

    def part(columns):
        return pl.BlockSpec((block, columns), lambda i, _: (i, 0))

    def mine(columns):
        return pl.BlockSpec((block, columns), lambda i, scalars: (scalars[1] * 2 + i, 0))

    return pl.pallas_call(
        functools.partial(router_back_kernel, kinds, experts),
        grid_spec=pltpu.PrefetchScalarGridSpec(
            num_scalar_prefetch=1,
            grid=(2,),
            in_specs=[
                pl.BlockSpec((1, block, width + lanes), lambda i, _: (0, i, 0)),
                pl.BlockSpec((1, block, width + lanes), lambda i, _: (0, i, 0)),
                part(width + lanes),
                part(width),
                part(lanes),
                mine(2),
                part(width),
                mine(kinds),
                whole(gain.shape),
                whole(small.shape),
                whole(small_t.shape),
                whole(vector.shape),
                whole(prior_w.shape),
            ],
            out_specs=[
                part(width),
                part(width),
                part(width),
                part(kinds),
                whole((32, width)),
            ],
        ),
        out_shape=[
            jax.ShapeDtypeStruct((rows, width), F32),
            jax.ShapeDtypeStruct((rows, width), BF16),
            jax.ShapeDtypeStruct((rows, width), F32),
            jax.ShapeDtypeStruct((rows, kinds), F32),
            jax.ShapeDtypeStruct((32, width), F32),
        ],
        compiler_params=pltpu.CompilerParams(vmem_limit_bytes=48 * 2**20),
        cost_estimate=cost_of(8),
        name="router_back",
    )(scalars, near, got, far, hidden, router, routes, cotangent, prior, gain, small, small_t,
      vector, prior_w)


def two_parts(value):
    high = lax.reduce_precision(value, 8, 7)
    return jnp.concatenate([high, value - high], axis=-1).astype(BF16)


def everywhere(value, axes, count):
    copies = jnp.broadcast_to(value[None], (count, *value.shape))
    return lax.all_to_all(copies, axes, 0, 0, tiled=True)


def flip(value, axis, size, bit):
    return lax.ppermute(value, axis, [(i, i ^ bit) for i in range(size)])


def by_halves(value):
    if value.shape[0] == 2:
        return value
    rows, units = value.shape[-2:]
    middle_axes = tuple(range(2, value.ndim - 2))
    turned = value.transpose(*middle_axes, 0, 1, value.ndim - 2, value.ndim - 1)
    turned = turned.reshape(*turned.shape[:-4], 2, LOW, value.shape[0] * rows // 2, units)
    axes = turned.ndim
    return turned.transpose(axes - 4, axes - 3, *range(axes - 4), axes - 2, axes - 1)


def scatter_high(value, many):
    if many != 2:
        rows, units = value.shape[-2:]
        middle_axes = tuple(range(2, value.ndim - 2))
        turned = value.transpose(*middle_axes, 0, 1, value.ndim - 2, value.ndim - 1)
        turned = turned.reshape(*turned.shape[:-4], many, LOW, 2 * rows // many, units)
        axes = turned.ndim
        value = turned.transpose(axes - 4, axes - 3, *range(axes - 4), axes - 2, axes - 1)
    return lax.psum_scatter(value, "hi", scatter_dimension=0)


def gather_rows(value, later, many):
    if many != 2:
        full = lax.all_gather(value, ("hi", "lo"), axis=0, tiled=True)
        full = full.reshape(2, LOW, -1, full.shape[1])
        return [full[:, i] for i in range(LOW)], later
    far, *later = lax.optimization_barrier((swap(value, "hi"), *later))
    both = jnp.stack([value, far])
    return [both] + [flip(both, "lo", LOW, bit) for bit in range(1, LOW)], tuple(later)


def scatter_rows(near, far, many):
    if many != 2:
        full = jnp.stack([near, far]).astype(F32).reshape(-1, near.shape[2])
        return lax.psum_scatter(full, ("hi", "lo"), scatter_dimension=0, tiled=True)
    both = near.astype(F32) + far.astype(F32)
    total = both[0]
    for bit in range(1, LOW):
        total = total + flip(both[bit].astype(BF16), "lo", LOW, bit).astype(F32)
    return total


def per_device(
    many,
    inputs,
    cotangent,
    lengths,
    routes,
    drop_order,
    prior_logits,
    attn_gain,
    w_query,
    w_key,
    w_value,
    w_out,
    moe_gain,
    w_router,
    w_prior,
    w_const,
    const_vector,
    w_gate,
    w_up,
    w_down,
):
    tok_rows, width = inputs.shape
    group = tok_rows * 4
    kinds = w_router.shape[1]
    experts, shard_rows, shard_units = w_gate.shape
    capacity = 3 * group // 16
    share = capacity // 2
    slots = LOW * share
    local_width = w_query.shape[1]
    heads = local_width // HEAD
    tp_axes = ("y", "c")
    all_axes = ("hi", "lo", "y", "c")
    count = many * LOW * 4
    wide = width + 128
    high = lax.axis_index("hi")
    parity = lax.axis_index("y")
    core = lax.axis_index("c")
    place_in_group = parity * 2 + core
    mine = high * LOW + lax.axis_index("lo") if many == 2 else jnp.zeros_like(high)
    boundary = jnp.cumsum(lengths[0])
    scalars = jnp.concatenate(
        [jnp.stack([mine, place_in_group, parity, core, lax.axis_index("lo")]), boundary[:-1]]
    ).astype(jnp.int32)
    gain_one, gain_two = attn_gain.reshape(1, width), moe_gain.reshape(1, width)

    valid_mine = place_in_group * tok_rows + jnp.arange(tok_rows)[:, None] < boundary[-2]
    valid_mine = valid_mine.astype(F32)

    normed_one = rms_norm(inputs, attn_gain).astype(BF16)
    normed_other = swap(normed_one, "y")
    attn_shard = jnp.concatenate([w_query, w_key, w_value, w_out.T], axis=1)
    up_part = lax.all_to_all(w_up, ("lo", "y"), 0, 0, tiled=True)
    up_part = up_part.reshape(LOW, 2, shard_rows, shard_units)
    down_shard = w_down.transpose(0, 2, 1)
    attn_shards, (w_gate,) = gather_rows(attn_shard, (w_gate,), many)
    gate_far = swap(w_gate, "hi") if many == 2 else w_gate
    router_lanes = jnp.pad(
        jnp.concatenate([w_router, w_router], axis=1), ((0, 0), (0, 128 - 2 * kinds))
    )
    prior_lanes = jnp.pad(
        jnp.concatenate([w_prior, w_prior], axis=1), ((0, 0), (0, 128 - 2 * kinds))
    )
    const_flat = w_const.transpose(1, 0, 2).reshape(width, 4)
    small = jnp.pad(
        jnp.concatenate([w_router, const_flat], axis=1), ((0, 0), (0, 128 - kinds - 4))
    )
    small_t = small.T
    prior_back = jnp.pad(w_prior.T, ((0, 128 - kinds), (0, 128 - kinds)))
    (
        attn_shards[0], scalars, router_lanes, prior_lanes, small, small_t, prior_back, prior_logits
    ) = lax.optimization_barrier(
        (attn_shards[0], scalars, router_lanes, prior_lanes, small, small_t, prior_back, prior_logits)
    )
    ids_rows, ids_cols = slots_of(scalars, routes, drop_order, experts, capacity)
    grad_out_low = (cotangent * valid_mine).astype(BF16)
    grad_out_other = swap(grad_out_low, "y")
    (
        normed_other, attn_shards, ids_rows, down_shard, grad_out_other, up_part, gate_far
    ) = lax.optimization_barrier(
        (normed_other, attn_shards, ids_rows, down_shard, grad_out_other, up_part, gate_far)
    )
    down_part = lax.all_to_all(down_shard, ("lo", "y"), 0, 0, tiled=True)
    down_part = down_part.reshape(LOW, 2, shard_rows, shard_units)
    if many == 2:
        up_far = [swap(up_part[:2], "hi"), swap(up_part[2:], "hi")]
    else:
        up_all = by_halves(lax.all_gather(up_part, "hi"))
        up_part, up_far = up_all[0], [up_all[1, :2], up_all[1, 2:]]
    out_mine = jnp.stack([item[:, :, 3 * local_width :] for item in attn_shards])
    out_other = swap(out_mine, "y")
    normed_pieces = [normed_one, swap(normed_one, "c"), normed_other, swap(normed_other, "c")]
    mixed, lse, qkv, qkv_full = attend(normed_pieces, attn_shards, scalars, heads)
    mixed, out_other, out_mine, up_far[0], down_part = lax.optimization_barrier(
        (mixed, out_other, out_mine, up_far[0], down_part)
    )
    if many == 2:
        high_place = high
        down_far = [swap(down_part[:3], "hi"), swap(down_part[3:], "hi")]
        gate_both = jnp.where(
            high == 0, jnp.stack([w_gate, gate_far], axis=1), jnp.stack([gate_far, w_gate], axis=1)
        )
    else:
        high_place = jnp.zeros_like(high)
        down_all = by_halves(lax.all_gather(down_part, "hi"))
        down_part, down_far = down_all[0], [down_all[1, :3], down_all[1, 3:]]
        gate_both = lax.all_gather(w_gate, "hi", axis=1)
    out_pieces = [out_mine, swap(out_mine, "c"), out_other, swap(out_other, "c")]

    mixed_mine = lax.all_to_all(mixed, tp_axes, 0, 0, tiled=True)
    grad_out_pieces = [
        grad_out_low, swap(grad_out_low, "c"), grad_out_other, swap(grad_out_other, "c"),
    ]
    grad_out_slots = pick(ids_rows, grad_out_pieces, slots)
    mixed_mine, grad_out_slots, up_far[1], gate_both = lax.optimization_barrier(
        (mixed_mine, grad_out_slots, up_far[1], gate_both)
    )

    hidden, sent_two, router = middle(
        kinds, scalars, mixed_mine, out_pieces, inputs, gain_two, router_lanes, prior_logits, prior_lanes
    )

    gate_part = lax.all_to_all(gate_both, ("lo", "y"), 0, 0, tiled=True)
    gate_part = gate_part.reshape(LOW, 2, many, shard_rows, shard_units)
    if many != 2:
        gate_part = by_halves(gate_part.transpose(2, 0, 1, 3, 4)).transpose(1, 2, 0, 3, 4)
    other_two, grad_taken, gate_part, down_far[0] = lax.optimization_barrier(
        (swap(sent_two, "y"), to_experts(grad_out_slots), gate_part, down_far[0])
    )
    pieces_two = [sent_two, swap(sent_two, "c"), other_two, swap(other_two, "c")]

    grad_taken += [swap(item, "c") for item in grad_taken]
    sent_slots = pick(ids_rows, pieces_two, slots)
    sent_slots, qkv_full = lax.optimization_barrier((sent_slots, qkv_full))
    taken = to_experts(sent_slots)
    taken += [swap(item, "c") for item in taken]
    qkv_pieces = gather_pieces(qkv_full)
    taken, qkv_pieces, down_far[1] = lax.optimization_barrier((taken, qkv_pieces, down_far[1]))

    expert = lax.axis_index("lo") * 2 + parity
    back_own, back_send, feed_own, feed_send, grads_out = expert_pass(
        kinds, jnp.stack([expert, high_place]).astype(jnp.int32), taken, grad_taken,
        gate_part, [up_part, down_part], up_far + down_far,
    )

    weight_sum = scatter_high(grads_out, many)
    back_taken = to_experts(back_sum(kinds, back_own, swap(back_send, "c")))
    feed_core = swap(feed_send, "c")
    back_taken, feed_core = lax.optimization_barrier((back_taken, feed_core))

    back_near, back_sent = spread(ids_cols, back_taken, tok_rows)
    back_got, back_other = add_core(back_near, back_sent)
    back_other, feed_core = lax.optimization_barrier((back_other, feed_core))
    back_far, feed_blocks = lax.optimization_barrier(
        (swap(back_other, "y"), feed_sum(feed_own, feed_core))
    )

    grad_hidden, grad_low, partial, grad_prior, sums = router_back(
        kinds, experts, scalars, back_near, back_got, back_far, hidden, router, routes, cotangent,
        prior_logits, gain_two, small, small_t, const_vector, prior_back,
    )
    feed_taken = to_experts(feed_blocks)
    grad_mixed = to_heads(mixed_back(scalars, grad_low, out_pieces))
    grad_mixed, grad_low = lax.optimization_barrier((grad_mixed, grad_low))
    low_other = swap(grad_low, "y")
    share_sums = lax.all_to_all(sums.reshape(count, 32 * width // count), all_axes, 0, 0, tiled=True)
    grad_qkv = attend_back(scalars, qkv, lse, grad_mixed, heads).reshape(
        4, 3 * local_width, tok_rows
    )
    grad_qkv, feed_taken, weight_sum, low_other = lax.optimization_barrier(
        (grad_qkv, feed_taken, weight_sum, low_other)
    )
    grad_attn_pieces = [grad_low, swap(grad_low, "c"), low_other, swap(low_other, "c")]

    weight_own = lax.all_to_all(
        weight_sum.reshape(2 * LOW, 3, shard_rows, shard_units), ("lo", "y"), 0, 0, tiled=True
    )
    grad_qkv_mine = to_heads(grad_qkv)
    attn_near, attn_far = attn_grads(grad_qkv, mixed, normed_pieces, grad_attn_pieces, scalars)
    if many == 2:
        attn_far = swap(attn_far, "hi")
    feed_near, feed_sent = spread(ids_cols, feed_taken, tok_rows)
    feed_got, feed_other = add_core(feed_near, feed_sent)
    (
        grad_qkv_mine, share_sums, attn_near, attn_far, feed_near, feed_got, feed_other
    ) = lax.optimization_barrier(
        (grad_qkv_mine, share_sums, attn_near, attn_far, feed_near, feed_got, feed_other)
    )
    feed_far = swap(feed_other, "y")
    share_sums = jnp.sum(share_sums, axis=0)
    grad_inputs, gain_part = inputs_back(
        grad_qkv_mine, qkv_pieces, inputs, gain_one, grad_hidden
    )
    output = partial + valid_mine * (
        feed_near[0] + feed_got[0].astype(F32) + feed_far.astype(F32)
    )
    grad_attn_own = scatter_rows(attn_near, attn_far, many)
    last = jnp.concatenate([jnp.sum(gain_part, axis=0).reshape(-1), share_sums])
    last, weight_own = lax.optimization_barrier((last, weight_own))
    last = everywhere(last, all_axes, count)
    last, grad_attn_own = lax.optimization_barrier((last, grad_attn_own))
    grad_gain = jnp.sum(last[:, :width], axis=0)
    total = last[:, width:].reshape(32, width)
    return (
        output,
        grad_inputs,
        grad_prior,
        grad_gain,
        grad_attn_own[:, :local_width],
        grad_attn_own[:, local_width : 2 * local_width],
        grad_attn_own[:, 2 * local_width : 3 * local_width],
        grad_attn_own[:, 3 * local_width :].T,
        total[kinds + 4],
        total[:kinds].T,
        total[kinds + 8 : 2 * kinds + 8, :kinds],
        total[kinds : kinds + 4].reshape(2, 2, width).transpose(0, 2, 1),
        total[kinds + 5 : kinds + 7],
        weight_own[:, 0].astype(F32),
        weight_own[:, 1].astype(F32),
        weight_own[:, 2].transpose(0, 2, 1).astype(F32),
    )


def solution(mesh):
    many = mesh.shape["fsdp"] // LOW
    fine = Mesh(mesh.devices.reshape(many, LOW, 2, 2), ("hi", "lo", "y", "c"))
    fsdp, tp = ("hi", "lo"), ("y", "c")
    every = fsdp + tp
    return jax.shard_map(
        functools.partial(per_device, many),
        mesh=fine,
        in_specs=(
            P(every, None),
            P(every, None),
            P(fsdp, None),
            P(fsdp, None),
            P(fsdp, None),
            P(fsdp, None),
            P(),
            P(fsdp, tp),
            P(fsdp, tp),
            P(fsdp, tp),
            P(tp, fsdp),
            P(),
            P(),
            P(),
            P(),
            P(),
            P(None, fsdp, tp),
            P(None, fsdp, tp),
            P(None, tp, fsdp),
        ),
        out_specs=(
            P(every, None),
            P(every, None),
            P(every, None),
            P(),
            P(fsdp, tp),
            P(fsdp, tp),
            P(fsdp, tp),
            P(tp, fsdp),
            P(),
            P(),
            P(),
            P(),
            P(),
            P(None, fsdp, tp),
            P(None, fsdp, tp),
            P(None, tp, fsdp),
        ),
        check_vma=False,
    )
```

```python
import functools

import jax
import jax.numpy as jnp
from jax import lax
from jax.experimental import pallas as pl
from jax.experimental.pallas import tpu as pltpu
from jax.sharding import Mesh
from jax.sharding import PartitionSpec as P

HEAD = 64
MAXLEN = 768
LOW = 4
SHARDS = 8
LOW_PLACE = 4
BOUNDS = 5
EPSILON = 1e-06
PRECISE = lax.Precision.HIGHEST
NEGATIVE = -1e30
F32 = jnp.float32
BF16 = jnp.bfloat16


def rms_norm(values, gain):
    return values * lax.rsqrt(jnp.mean(values * values, axis=-1, keepdims=True) + EPSILON) * gain


def swap(value, axis):
    return lax.ppermute(value, axis, [(0, 1), (1, 0)])


def gather_pieces(value):
    other = swap(value, "y")
    return [value, swap(value, "c"), other, swap(other, "c")]


def natural(pieces, index):
    ordered = []
    for j in range(4):
        item = pieces[j]
        for t in range(1, 4):
            item = jnp.where(index == t, pieces[j ^ t], item)
        ordered.append(item)
    return jnp.stack(ordered)


def add_core(near, sent):
    got = swap(sent, "c")
    return got, (near[1] + got[1].astype(F32)).astype(BF16)


def cost_of(microseconds):
    return pl.CostEstimate(
        flops=int(microseconds * 1.15e9), transcendentals=0, bytes_accessed=2**16
    )


def start_of(row, scalars):
    start_row = jnp.zeros_like(row)
    for k in range(BOUNDS, scalars.shape[0]):
        start_row = jnp.where(row >= scalars[k], scalars[k], start_row)
    return start_row


def for_window(first, block, pad, scalars, body):
    needed = (first - start_of(first, scalars) + block - 1) // block
    most = pad // block
    for blocks in range(most):
        pl.when(needed == blocks)(functools.partial(body, (blocks + 1) * block))
    pl.when(needed >= most)(functools.partial(body, pad + block))


def scores_mask(first_key, first_query, window, block, scalars):
    row = first_query + lax.broadcasted_iota(jnp.int32, (1, block), 1)
    start_row = start_of(row, scalars)
    key_places = first_key + lax.broadcasted_iota(jnp.int32, (window, block), 0)
    query_places = first_query + lax.broadcasted_iota(jnp.int32, (window, block), 1)
    return (key_places >= start_row) & (key_places <= query_places)


def attend_kernel(block, pad, scalars, *refs):
    pieces, refs = refs[:4], refs[4:]
    shards, refs = refs[:LOW], refs[LOW:]
    out_ref, lse_ref, qkv_ref, weight_ref, key_rows, value_pad, full = refs
    group = qkv_ref.shape[1]
    quarter = group // 4
    inner = qkv_ref.shape[0] // 3
    head = pl.program_id(0)

    @pl.when(head == 0)
    def _():
        rows = shards[0].shape[1]
        for r in range(SHARDS):
            place = pl.multiple_of((scalars[0] ^ r) * rows, rows)
            full[pl.ds(place, rows), :] = shards[r % LOW][r // LOW]
        turned = full[:, : 3 * inner].T
        weight_ref[...] = turned
        for r in range(4):
            place = pl.multiple_of((scalars[1] ^ r) * quarter, quarter)
            qkv_ref[:, pl.ds(place, quarter)] = lax.dot_general(
                turned, pieces[r][...], (((1,), (1,)), ((), ())), preferred_element_type=F32
            ).astype(BF16)

    first_row = pl.multiple_of(head * HEAD, HEAD)
    key_rows[pl.ds(0, pad), :] = jnp.zeros((pad, HEAD), BF16)
    value_pad[:, pl.ds(0, pad)] = jnp.zeros((HEAD, pad), BF16)
    key_rows[pl.ds(pad, group), :] = qkv_ref[pl.ds(inner + first_row, HEAD), :].T
    value_pad[:, pl.ds(pad, group)] = qkv_ref[pl.ds(2 * inner + first_row, HEAD), :]

    def one(i, carry):
        first = pl.multiple_of(i * block, block)

        def body(window):
            begin = pl.multiple_of(first + pad + block - window, block)
            scores = jnp.dot(
                key_rows[pl.ds(begin, window), :],
                qkv_ref[pl.ds(first_row, HEAD), pl.ds(first, block)],
                preferred_element_type=F32,
            )
            allowed = scores_mask(begin - pad, first, window, block, scalars)
            scores = jnp.where(allowed, scores * 0.125, NEGATIVE)
            highest = jnp.max(scores, axis=0, keepdims=True)
            weights = jnp.exp(scores - highest)
            total = jnp.sum(weights, axis=0, keepdims=True)
            mixed = jnp.dot(
                value_pad[:, pl.ds(begin, window)],
                weights.astype(BF16),
                preferred_element_type=F32,
            )
            mixed = (mixed / total).astype(BF16)
            column = pl.multiple_of(first % quarter, block)
            out_ref[first // quarter, :, pl.ds(column, block)] = mixed
            lse_ref[0, :, pl.ds(first, block)] = highest + jnp.log(total)

        for_window(first, block, pad, scalars, body)
        return carry

    lax.fori_loop(0, group // block, one, 0)


def attend(pieces, shards, scalars, heads):
    rows, width = pieces[0].shape
    group = 4 * rows
    inner = heads * HEAD
    block = 256

    def whole(shape):
        return pl.BlockSpec(
            shape, lambda i, _: (0,) * len(shape), pipeline_mode=pl.Buffered(1)
        )

    return pl.pallas_call(
        functools.partial(attend_kernel, block, MAXLEN),
        grid_spec=pltpu.PrefetchScalarGridSpec(
            num_scalar_prefetch=1,
            grid=(heads,),
            in_specs=[
                *[whole((rows, width)) for _ in range(4)],
                *[whole(shards[0].shape) for _ in range(LOW)],
            ],
            out_specs=[
                pl.BlockSpec((4, HEAD, rows), lambda h, _: (0, h, 0)),
                pl.BlockSpec((1, 1, group), lambda h, _: (h, 0, 0)),
                whole((3 * inner, group)),
                whole((3 * inner, width)),
            ],
            scratch_shapes=[
                pltpu.VMEM((MAXLEN + group, HEAD), BF16),
                pltpu.VMEM((HEAD, MAXLEN + group), BF16),
                pltpu.VMEM((width, 4 * inner), BF16),
            ],
        ),
        out_shape=[
            jax.ShapeDtypeStruct((4, inner, rows), BF16),
            jax.ShapeDtypeStruct((heads, 1, group), F32),
            jax.ShapeDtypeStruct((3 * inner, group), BF16),
            jax.ShapeDtypeStruct((3 * inner, width), BF16),
        ],
        compiler_params=pltpu.CompilerParams(vmem_limit_bytes=48 * 2**20),
        cost_estimate=cost_of(24),
        name="attend",
    )(scalars, *pieces, *shards)


def attn_grads_kernel(scalars, *refs):
    grad_qkv, mixed, refs = refs[0], refs[1], refs[2:]
    tokens, grads, refs = refs[:4], refs[4:8], refs[8:]
    outs, (total,) = refs[:2], refs[2:]
    inner3 = grad_qkv.shape[1]
    first, second = 0.0, 0.0
    for r in range(4):
        j = scalars[1] ^ r
        first += jnp.dot(grad_qkv[r], tokens[r][...], preferred_element_type=F32)
        second += jnp.dot(mixed[j], grads[r][...], preferred_element_type=F32)
    total[:, :inner3] = first.T.astype(BF16)
    total[:, inner3:] = second.T.astype(BF16)
    rows = outs[0].shape[1]
    for r in range(SHARDS):
        place = pl.multiple_of((scalars[0] ^ r) * rows, rows)
        outs[r // LOW][r % LOW] = total[pl.ds(place, rows), :]


def attn_grads(grad_qkv, mixed, tokens, grads, scalars):
    width = tokens[0].shape[1]
    columns = grad_qkv.shape[1] + mixed.shape[1]
    rows = width // SHARDS
    whole = pl.BlockSpec(memory_space=pltpu.VMEM)
    return pl.pallas_call(
        attn_grads_kernel,
        in_specs=[pl.BlockSpec(memory_space=pltpu.SMEM)] + [whole] * 10,
        out_specs=[whole] * 2,
        out_shape=[jax.ShapeDtypeStruct((LOW, rows, columns), BF16)] * 2,
        scratch_shapes=[pltpu.VMEM((width, columns), BF16)],
        compiler_params=pltpu.CompilerParams(vmem_limit_bytes=48 * 2**20),
        cost_estimate=cost_of(30),
        name="attn_grads",
    )(scalars, grad_qkv, mixed, *tokens, *grads)


def attend_back_kernel(block, pad, scalars, qkv_ref, lse_ref, *refs):
    pieces, refs = refs[:4], refs[4:]
    out_ref, grad_mixed, key_rows, value_rows, key_pad, grad_key, grad_value = refs
    group = qkv_ref.shape[1]
    inner_rows = qkv_ref.shape[0] // 3
    quarter = group // 4
    contract_last = (((1,), (1,)), ((), ()))
    head = pl.program_id(0)

    @pl.when(head == 0)
    def _():
        for r in range(4):
            place = pl.multiple_of((scalars[1] ^ r) * quarter, quarter)
            grad_mixed[:, pl.ds(place, quarter)] = pieces[r][...]

    first_row = pl.multiple_of(head * HEAD, HEAD)
    keys = qkv_ref[pl.ds(inner_rows + first_row, HEAD), :]
    key_rows[pl.ds(0, pad), :] = jnp.zeros((pad, HEAD), BF16)
    value_rows[pl.ds(0, pad), :] = jnp.zeros((pad, HEAD), BF16)
    key_pad[:, pl.ds(0, pad)] = jnp.zeros((HEAD, pad), BF16)
    key_rows[pl.ds(pad, group), :] = keys.T
    value_rows[pl.ds(pad, group), :] = qkv_ref[pl.ds(2 * inner_rows + first_row, HEAD), :].T
    key_pad[:, pl.ds(pad, group)] = keys
    grad_key[...] = jnp.zeros_like(grad_key)
    grad_value[...] = jnp.zeros_like(grad_value)

    def one(i, carry):
        first = pl.multiple_of(i * block, block)

        def body(window):
            begin = pl.multiple_of(first + pad + block - window, block)
            query = qkv_ref[pl.ds(first_row, HEAD), pl.ds(first, block)]
            grad = grad_mixed[pl.ds(first_row, HEAD), pl.ds(first, block)]
            scores = jnp.dot(key_rows[pl.ds(begin, window), :], query, preferred_element_type=F32)
            allowed = scores_mask(begin - pad, first, window, block, scalars)
            exponent = scores * 0.125 - lse_ref[0, :, pl.ds(first, block)]
            probs = jnp.exp(jnp.where(allowed, exponent, NEGATIVE))
            grad_probs = jnp.dot(
                value_rows[pl.ds(begin, window), :], grad, preferred_element_type=F32
            )
            inner = jnp.sum(probs * grad_probs, axis=0, keepdims=True)
            raw = (0.125 * (probs * (grad_probs - inner))).astype(BF16)
            grad_query = jnp.dot(
                key_pad[:, pl.ds(begin, window)], raw, preferred_element_type=F32
            )
            column = pl.multiple_of(first % quarter, block)
            piece = (first // quarter) ^ scalars[1]
            out_ref[piece, 0, :, pl.ds(column, block)] = grad_query.astype(BF16)
            grad_value[:, pl.ds(begin, window)] += lax.dot_general(
                grad, probs.astype(BF16), contract_last, preferred_element_type=F32
            )
            grad_key[:, pl.ds(begin, window)] += lax.dot_general(
                query, raw, contract_last, preferred_element_type=F32
            )

        for_window(first, block, pad, scalars, body)
        return carry

    lax.fori_loop(0, group // block, one, 0)
    for j in range(4):
        piece = scalars[1] ^ j
        out_ref[piece, 1] = grad_key[:, pl.ds(pad + j * quarter, quarter)].astype(BF16)
        out_ref[piece, 2] = grad_value[:, pl.ds(pad + j * quarter, quarter)].astype(BF16)


def attend_back(scalars, qkv, lse, pieces, heads):
    group = qkv.shape[1]
    block = 256

    def whole(shape):
        return pl.BlockSpec(
            shape, lambda i, _: (0,) * len(shape), pipeline_mode=pl.Buffered(1)
        )

    return pl.pallas_call(
        functools.partial(attend_back_kernel, block, MAXLEN),
        grid_spec=pltpu.PrefetchScalarGridSpec(
            num_scalar_prefetch=1,
            grid=(heads,),
            in_specs=[
                whole(qkv.shape),
                pl.BlockSpec((1, 1, group), lambda h, _: (h, 0, 0)),
                *[whole(item.shape) for item in pieces],
            ],
            out_specs=pl.BlockSpec((4, 3, HEAD, group // 4), lambda h, _: (0, 0, h, 0)),
            scratch_shapes=[
                pltpu.VMEM((heads * HEAD, group), BF16),
                pltpu.VMEM((MAXLEN + group, HEAD), BF16),
                pltpu.VMEM((MAXLEN + group, HEAD), BF16),
                pltpu.VMEM((HEAD, MAXLEN + group), BF16),
                pltpu.VMEM((HEAD, MAXLEN + group), F32),
                pltpu.VMEM((HEAD, MAXLEN + group), F32),
            ],
        ),
        out_shape=jax.ShapeDtypeStruct((4, 3, heads * HEAD, group // 4), BF16),
        compiler_params=pltpu.CompilerParams(vmem_limit_bytes=48 * 2**20),
        cost_estimate=cost_of(34),
        name="attend_back",
    )(scalars, qkv, lse, *pieces)


def mixed_back_kernel(scalars, grad_ref, p0, p1, p2, p3, *refs):
    outs, weight = refs[:4], refs[4]
    rows = p0.shape[2]
    for r, shards in enumerate((p0, p1, p2, p3)):
        for k in range(SHARDS):
            place = pl.multiple_of((scalars[0] ^ k) * rows, rows)
            weight[pl.ds(place, rows), :] = shards[k % LOW, k // LOW]
        outs[r][...] = lax.dot_general(
            weight[...].T, grad_ref[...], (((1,), (1,)), ((), ())), preferred_element_type=F32
        ).astype(BF16)


def mixed_back(scalars, grad, weights):
    rows, width = grad.shape
    inner = weights[0].shape[3]

    def whole(shape):
        return pl.BlockSpec(shape, lambda i, _: (0,) * len(shape))

    return pl.pallas_call(
        mixed_back_kernel,
        grid_spec=pltpu.PrefetchScalarGridSpec(
            num_scalar_prefetch=1,
            grid=(1,),
            in_specs=[whole(grad.shape), *[whole(item.shape) for item in weights]],
            out_specs=[whole((inner, rows)) for _ in range(4)],
            scratch_shapes=[pltpu.VMEM((width, inner), BF16)],
        ),
        out_shape=[jax.ShapeDtypeStruct((inner, rows), BF16) for _ in range(4)],
        compiler_params=pltpu.CompilerParams(vmem_limit_bytes=32 * 2**20),
        cost_estimate=cost_of(4),
        name="mixed_back",
    )(scalars, grad, *weights)


def inputs_back_kernel(g0, g1, g2, g3, p0, p1, p2, p3, x_ref, gain_ref, hidden_ref, out_ref, sum_ref):
    total = 0.0
    for grad, weight in zip((g0, g1, g2, g3), (p0, p1, p2, p3)):
        total += jnp.dot(grad[...].T, weight[...], preferred_element_type=F32)
    x = x_ref[...]
    scale = lax.rsqrt(jnp.mean(x * x, axis=1, keepdims=True) + EPSILON)
    through = total * gain_ref[...]
    inner = jnp.mean(through * x, axis=1, keepdims=True)
    out_ref[...] = hidden_ref[...] + scale * through - (scale * scale * scale * inner) * x
    sum_ref[0] = jnp.sum(total * x * scale, axis=0, keepdims=True)


def inputs_back(grads, weights, x, gain, grad_hidden):
    rows, width = x.shape
    block = rows // 2

    def whole(shape):
        return pl.BlockSpec(shape, lambda i: (0,) * len(shape), pipeline_mode=pl.Buffered(1))

    part = pl.BlockSpec((block, width), lambda i: (i, 0))
    return pl.pallas_call(
        inputs_back_kernel,
        grid=(2,),
        in_specs=[
            *[pl.BlockSpec((item.shape[0], block), lambda i: (0, i)) for item in grads],
            *[whole(item.shape) for item in weights],
            part,
            whole(gain.shape),
            part,
        ],
        out_specs=[part, pl.BlockSpec((1, 1, width), lambda i: (i, 0, 0))],
        out_shape=[
            jax.ShapeDtypeStruct(x.shape, F32),
            jax.ShapeDtypeStruct((2, 1, width), F32),
        ],
        compiler_params=pltpu.CompilerParams(vmem_limit_bytes=48 * 2**20),
        cost_estimate=cost_of(6),
        name="inputs_back",
    )(*grads, *weights, x, gain, grad_hidden)


def expert_kernel(
    kinds, scalars, w_gate, *refs
):
    near_pieces, far_pieces, refs = refs[:2], refs[2:6], refs[6:]
    x_blocks, g_blocks, refs = refs[: 2 * LOW], refs[2 * LOW : 4 * LOW], refs[4 * LOW :]
    back_own, back_send, feed_own, feed_send, grads_out, *refs = refs
    x_all, g_all, x_t, g_t, weights, hidden, acc_feed, acc_back, scales, plain = refs
    slots, width = feed_own.shape
    block = slots // LOW
    half = width // 2
    step = pl.program_id(0)
    contract_last = (((1,), (1,)), ((), ()))
    units = weights.shape[2]

    def weight_column(x_ref):
        extra = x_ref[:, width:].astype(F32)
        lanes = lax.broadcasted_iota(jnp.int32, extra.shape, 1)
        named = (lanes == scalars[0]) | (lanes == scalars[0] + kinds)
        return jnp.sum(jnp.where(named, extra, 0.0), axis=1, keepdims=True)

    @pl.when(step == 0)
    def _():
        for i in range(2 * LOW):
            rows = pl.ds(i * block, block)
            scale = weight_column(x_blocks[i])
            scales[rows, :] = jnp.broadcast_to(scale, (block, 128))
            plain[rows, :] = g_blocks[i][...]
            x_all[rows, :] = x_blocks[i][:, :width]
            g_all[rows, :] = (g_blocks[i][...].astype(F32) * scale).astype(BF16)
        x_t[...] = x_all[...].T
        g_t[...] = g_all[...].T
        acc_feed[...] = jnp.zeros_like(acc_feed)
        acc_back[...] = jnp.zeros_like(acc_back)

    for i in range(2):
        rows = pl.ds(i * half, half)
        weights[0, rows, :] = w_gate[:, 0, i].reshape(half, units)
    near = pl.multiple_of(scalars[1] * half, half)
    for k in range(2):
        weights[k + 1, pl.ds(near, half), :] = near_pieces[k][:, 0].reshape(half, units)
        place = (1 - scalars[1]) * half
        for piece in far_pieces[2 * k : 2 * k + 2]:
            rows = piece.shape[0] * half // LOW
            weights[k + 1, pl.ds(pl.multiple_of(place, half // LOW), rows), :] = piece[
                :, 0
            ].reshape(rows, units)
            place += rows

    for part in range(2):
        rows = pl.ds(part * slots, slots)
        x = x_all[rows, :]
        gate = jnp.dot(x, weights[0], preferred_element_type=F32)
        up = jnp.dot(x, weights[1], preferred_element_type=F32)
        grad_act = jnp.dot(g_all[rows, :], weights[2], preferred_element_type=F32)
        sig = jax.nn.sigmoid(gate)
        silu = gate * sig
        active = (silu * up).astype(BF16)
        grad_gate = (grad_act * up * (sig * (1.0 + gate * (1.0 - sig)))).astype(BF16)
        grad_up = (grad_act * silu).astype(BF16)
        hidden[0, rows, :] = grad_gate
        hidden[1, rows, :] = grad_up
        hidden[2, rows, :] = active
        acc_feed[rows, :] += lax.dot_general(
            active, weights[2], contract_last, preferred_element_type=F32
        )
        acc_back[rows, :] += lax.dot_general(
            grad_gate, weights[0], contract_last, preferred_element_type=F32
        ) + lax.dot_general(grad_up, weights[1], contract_last, preferred_element_type=F32)

    for k in range(3):
        left = (g_t if k == 2 else x_t)
        grad = jnp.dot(left[...], hidden[k], preferred_element_type=F32).astype(BF16)
        for i in range(2):
            part = grad[i * half : (i + 1) * half].reshape(LOW, -1, units)
            grads_out[i, :, 0, k] = part

    @pl.when(step == pl.num_programs(0) - 1)
    def _():
        for part in range(2):
            rows = pl.ds(part * slots, slots)
            feed = acc_feed[rows, :]
            inner = jnp.sum(feed * plain[rows, :].astype(F32), axis=1, keepdims=True)
            feed = feed * scales[rows, 0:1]
            lanes = lax.broadcasted_iota(jnp.int32, (slots, 128), 1)
            if part == 0:
                back_own[:, :width] = acc_back[rows, :]
                back_own[:, width:] = jnp.where(lanes == scalars[0], inner, 0.0)
                feed_own[...] = feed
            else:
                high = inner.astype(BF16).astype(F32)
                extra = jnp.where(lanes == scalars[0], high, 0.0)
                extra = jnp.where(lanes == scalars[0] + kinds, inner - high, extra)
                back_send[:, :width] = acc_back[rows, :].astype(BF16)
                back_send[:, width:] = extra.astype(BF16)
                feed_send[...] = feed.astype(BF16)


def expert_pass(kinds, scalars, x_blocks, g_blocks, w_gate, w_near, w_far):
    block, width = g_blocks[0].shape
    slots = LOW * block
    low, parities, _, shard_rows, shard_units = w_gate.shape
    units = 512
    steps = shard_units // units

    def whole(shape):
        return pl.BlockSpec(
            shape, lambda i, _: (0,) * len(shape), pipeline_mode=pl.Buffered(1)
        )

    grads_spec = pl.BlockSpec(
        (2, low, 1, 3, shard_rows, units), lambda i, _: (0, 0, i // steps, 0, 0, i % steps)
    )
    gate_spec = pl.BlockSpec(
        (low, 1, 2, shard_rows, units), lambda i, _: (0, i // steps, 0, 0, i % steps)
    )
    def up_spec(count):
        return pl.BlockSpec(
            (count, 1, shard_rows, units), lambda i, _: (0, i // steps, 0, i % steps)
        )

    wide = width + 128
    return pl.pallas_call(
        functools.partial(expert_kernel, kinds),
        grid_spec=pltpu.PrefetchScalarGridSpec(
            num_scalar_prefetch=1,
            grid=(parities * steps,),
            in_specs=[
                gate_spec,
                *[up_spec(item.shape[0]) for item in (*w_near, *w_far)],
                *[whole((block, wide)) for _ in range(2 * LOW)],
                *[whole((block, width)) for _ in range(2 * LOW)],
            ],
            out_specs=[
                whole((slots, wide)),
                whole((slots, wide)),
                whole((slots, width)),
                whole((slots, width)),
                grads_spec,
            ],
            scratch_shapes=[
                pltpu.VMEM((2 * slots, width), BF16),
                pltpu.VMEM((2 * slots, width), BF16),
                pltpu.VMEM((width, 2 * slots), BF16),
                pltpu.VMEM((width, 2 * slots), BF16),
                pltpu.VMEM((3, width, units), BF16),
                pltpu.VMEM((3, 2 * slots, units), BF16),
                pltpu.VMEM((2 * slots, width), F32),
                pltpu.VMEM((2 * slots, width), F32),
                pltpu.VMEM((2 * slots, 128), F32),
                pltpu.VMEM((2 * slots, width), BF16),
            ],
        ),
        out_shape=[
            jax.ShapeDtypeStruct((slots, wide), F32),
            jax.ShapeDtypeStruct((slots, wide), BF16),
            jax.ShapeDtypeStruct((slots, width), F32),
            jax.ShapeDtypeStruct((slots, width), BF16),
            jax.ShapeDtypeStruct((2, low, parities, 3, shard_rows, shard_units), BF16),
        ],
        compiler_params=pltpu.CompilerParams(vmem_limit_bytes=58 * 2**20),
        cost_estimate=cost_of(35),
        name="expert_pass",
    )(scalars, w_gate, *w_near, *w_far, *x_blocks, *g_blocks)


def pick_kernel(ids_ref, *refs):
    pieces, outs = refs[:4], refs[4:]
    block = outs[0].shape[0]
    rows = pieces[0].shape[0]
    for i, out_ref in enumerate(outs):
        slot = i * block + lax.broadcasted_iota(jnp.int32, (block, rows), 0)
        total = 0.0
        for r in range(4):
            columns = pl.ds(r * rows, rows)
            held = (slot == ids_ref[0:1, columns]) | (slot == ids_ref[1:2, columns])
            held = jnp.where(held, 1.0, 0.0).astype(BF16)
            total += jnp.dot(held, pieces[r][...], preferred_element_type=F32)
        out_ref[...] = total.astype(BF16)


def pick(ids, pieces, slots):
    rows, width = pieces[0].shape
    block = slots // LOW

    def whole(shape):
        return pl.BlockSpec(shape, lambda i: (0, 0))

    return pl.pallas_call(
        pick_kernel,
        grid=(1,),
        in_specs=[whole((8, 4 * rows)), *[whole((rows, width)) for _ in range(4)]],
        out_specs=[whole((block, width)) for _ in range(LOW)],
        out_shape=[jax.ShapeDtypeStruct((block, width), BF16) for _ in range(LOW)],
        compiler_params=pltpu.CompilerParams(vmem_limit_bytes=32 * 2**20),
        cost_estimate=cost_of(5),
        name="pick",
    )(ids, *pieces)


def to_experts(blocks):
    return [blocks[0]] + [flip(blocks[b], "lo", LOW, b) for b in range(1, LOW)]


def to_heads(blocks):
    return [blocks[0]] + [
        lax.ppermute(blocks[r], ("y", "c"), [(i, i ^ r) for i in range(4)]) for r in range(1, 4)
    ]


def back_sum_kernel(kinds, own_ref, core_ref, *outs):
    width = own_ref.shape[1] - 128
    block = outs[0].shape[0]
    for i, out_ref in enumerate(outs):
        rows = pl.ds(i * block, block)
        out_ref[:, :width] = (
            own_ref[rows, :width] + core_ref[rows, :width].astype(F32)
        ).astype(BF16)
        extra = own_ref[rows, width:] + core_ref[rows, width:].astype(F32)
        lanes = lax.broadcasted_iota(jnp.int32, extra.shape, 1)
        high = jnp.where(lanes < kinds, extra, 0.0).astype(BF16).astype(F32)
        low = jnp.where(lanes < kinds, extra - high, 0.0)
        low = pltpu.roll(low, kinds, 1) + jnp.where(lanes >= kinds, extra, 0.0)
        out_ref[:, width:] = (high + low).astype(BF16)


def back_sum(kinds, own, core):
    slots, wide = own.shape
    block = slots // LOW

    def whole(shape):
        return pl.BlockSpec(shape, lambda i: (0, 0))

    return pl.pallas_call(
        functools.partial(back_sum_kernel, kinds),
        grid=(1,),
        in_specs=[whole(own.shape), whole(core.shape)],
        out_specs=[whole((block, wide)) for _ in range(LOW)],
        out_shape=[jax.ShapeDtypeStruct((block, wide), BF16) for _ in range(LOW)],
        compiler_params=pltpu.CompilerParams(vmem_limit_bytes=32 * 2**20),
        cost_estimate=cost_of(3),
        name="back_sum",
    )(own, core)


def feed_sum_kernel(own_ref, core_ref, *outs):
    block = outs[0].shape[0]
    for i, out_ref in enumerate(outs):
        rows = pl.ds(i * block, block)
        out_ref[...] = (own_ref[rows, :] + core_ref[rows, :].astype(F32)).astype(BF16)


def feed_sum(own, core):
    slots, width = own.shape
    block = slots // LOW

    def whole(shape):
        return pl.BlockSpec(shape, lambda i: (0, 0))

    return pl.pallas_call(
        feed_sum_kernel,
        grid=(1,),
        in_specs=[whole(own.shape), whole(core.shape)],
        out_specs=[whole((block, width)) for _ in range(LOW)],
        out_shape=[jax.ShapeDtypeStruct((block, width), BF16) for _ in range(LOW)],
        compiler_params=pltpu.CompilerParams(vmem_limit_bytes=32 * 2**20),
        cost_estimate=cost_of(3),
        name="feed_sum",
    )(own, core)


def spread_kernel(ids_ref, *refs):
    blocks, (near_ref, send_ref, slots_ref) = refs[:LOW], refs[LOW:]
    rows = near_ref.shape[1]
    slots = slots_ref.shape[0]
    block = slots // LOW

    @pl.when(pl.program_id(0) == 0)
    def _():
        for i in range(LOW):
            slots_ref[pl.ds(i * block, block), :] = blocks[i][...]

    for k, out_ref in enumerate((near_ref, send_ref)):
        slot = lax.broadcasted_iota(jnp.int32, (rows, slots), 1)
        ids = ids_ref[pl.ds(k * rows, rows), :]
        held = (slot == ids[:, 0:1]) | (slot == ids[:, 1:2])
        held = jnp.where(held, 1.0, 0.0).astype(BF16)
        total = jnp.dot(held, slots_ref[...], preferred_element_type=F32)
        out_ref[0] = total.astype(out_ref.dtype)


def spread(ids, values, rows):
    block, width = values[0].shape
    return pl.pallas_call(
        spread_kernel,
        grid=(2,),
        in_specs=[
            pl.BlockSpec((2 * rows, 8), lambda i: (i, 0)),
            *[pl.BlockSpec((block, width), lambda i: (0, 0)) for _ in range(LOW)],
        ],
        out_specs=[
            pl.BlockSpec((1, rows, width), lambda i: (i, 0, 0)),
            pl.BlockSpec((1, rows, width), lambda i: (i, 0, 0)),
        ],
        out_shape=[
            jax.ShapeDtypeStruct((2, rows, width), F32),
            jax.ShapeDtypeStruct((2, rows, width), BF16),
        ],
        scratch_shapes=[pltpu.VMEM((LOW * block, width), BF16)],
        compiler_params=pltpu.CompilerParams(vmem_limit_bytes=32 * 2**20),
        cost_estimate=cost_of(30),
        name="spread",
    )(ids, *values)


def slots_kernel(experts, capacity, scalars, routes_col, order_col, routes_row, order_row,
                 row_ref, col_ref, places_ref):
    group = routes_row.shape[1]
    rows = group // 4
    share = capacity // 2
    span = 2 * group
    bound = scalars[BOUNDS + 2]

    def target_of(routes, axis):
        place = lax.broadcasted_iota(jnp.int32, routes.shape, axis)
        return jnp.where((routes < experts) & (place < bound), routes, experts)

    target = target_of(routes_row[...], 1)
    code = target * span + order_row[...]
    block = 256

    def count(i, carry):
        first = pl.multiple_of(i * block, block)
        routes = routes_col[pl.ds(first, block), :]
        place = first + lax.broadcasted_iota(jnp.int32, routes.shape, 0)
        held = jnp.where((routes < experts) & (place < bound), routes, experts)
        others = held * span + order_col[pl.ds(first, block), :]
        result = []
        for k in range(2):
            total = carry[k]
            for j in range(2):
                smaller = jnp.where(others[:, j : j + 1] < code[k : k + 1, :], 1.0, 0.0)
                total = total + jnp.sum(smaller, axis=0, keepdims=True)
            result.append(total)
        return tuple(result)

    zero = jnp.zeros((1, group), F32)
    counts = lax.fori_loop(0, group // block, count, (zero, zero))
    for k in range(2):
        mine_target = target[k : k + 1, :]
        base = jnp.zeros((1, group), F32)
        for e in range(1, experts):
            earlier = jnp.sum(jnp.where(target < e, 1.0, 0.0))
            base = jnp.where(mine_target == e, earlier, base)
        place = (counts[k] - base).astype(jnp.int32)
        first = scalars[3] * share
        held = (
            (mine_target < experts)
            & (place >= first)
            & (place < first + share)
            & (place < capacity)
            & (jnp.bitwise_and(mine_target, 1) == scalars[2])
        )
        block = jnp.bitwise_xor(lax.shift_right_logical(mine_target, 1), scalars[LOW_PLACE])
        slot = block * share + place - first
        places_ref[k : k + 1, :] = jnp.where(held, slot, -1)
    for r in range(4):
        start = pl.multiple_of((scalars[1] ^ r) * rows, rows)
        piece = places_ref[:, pl.ds(start, rows)]
        row_ref[:, pl.ds(r * rows, rows)] = piece
        col_ref[pl.ds(r * rows, rows), :] = piece.T


def slots_of(scalars, routes, drop_order, experts, capacity):
    group = routes.shape[0]
    whole = pl.BlockSpec(memory_space=pltpu.VMEM)
    return pl.pallas_call(
        functools.partial(slots_kernel, experts, capacity),
        in_specs=[pl.BlockSpec(memory_space=pltpu.SMEM)] + [whole] * 4,
        out_specs=[whole] * 2,
        out_shape=[
            jax.ShapeDtypeStruct((8, group), jnp.int32),
            jax.ShapeDtypeStruct((group, 8), jnp.int32),
        ],
        scratch_shapes=[pltpu.VMEM((8, group), jnp.int32)],
        compiler_params=pltpu.CompilerParams(vmem_limit_bytes=32 * 2**20),
        cost_estimate=cost_of(8),
        name="slots",
    )(scalars, routes, drop_order, routes.T, drop_order.T)


def middle_kernel(kinds, scalars, mixed, p0, p1, p2, p3, x_ref, gain_ref, router_w, prior_ref,
                  prior_w, hidden_ref, sent_ref, router_ref, weight):
    hidden = x_ref[...]
    rows = p0.shape[2]
    for r, shards in enumerate((p0, p1, p2, p3)):
        for k in range(SHARDS):
            place = pl.multiple_of((scalars[0] ^ k) * rows, rows)
            weight[r, pl.ds(place, rows), :] = shards[k % LOW, k // LOW]
        hidden += lax.dot_general(
            mixed[scalars[1] ^ r].T, weight[r], (((1,), (1,)), ((), ())),
            preferred_element_type=F32,
        )
    hidden_ref[...] = hidden
    scale = lax.rsqrt(jnp.mean(hidden * hidden, axis=1, keepdims=True) + EPSILON)
    rounded = (hidden * scale * gain_ref[...]).astype(BF16)
    width = hidden.shape[1]
    sent_ref[:, :width] = rounded
    router_high, router_low = halves(router_w[...])
    logits = (
        jnp.dot(rounded, router_high, preferred_element_type=F32)
        + jnp.dot(rounded, router_low, preferred_element_type=F32)
        + split_dot(prior_ref[...], prior_w[...])
    )
    lanes = lax.broadcasted_iota(jnp.int32, logits.shape, 1)
    logits = jnp.where(lanes < 2 * kinds, logits, NEGATIVE)
    weights = jnp.exp(logits - jnp.max(logits, axis=1, keepdims=True))
    total = jnp.sum(jnp.where(lanes < kinds, weights, 0.0), axis=1, keepdims=True)
    router = weights / total
    router_ref[...] = router
    high = router.astype(BF16).astype(F32)
    sent_ref[:, width:] = jnp.where(lanes < kinds, high, router - high).astype(BF16)


def middle(kinds, scalars, mixed, weights, x, gain, router_w, prior, prior_w):
    rows, width = x.shape
    lanes = router_w.shape[1]

    def whole(shape):
        return pl.BlockSpec(shape, lambda i, _: (0,) * len(shape))

    return pl.pallas_call(
        functools.partial(middle_kernel, kinds),
        grid_spec=pltpu.PrefetchScalarGridSpec(
            num_scalar_prefetch=1,
            grid=(1,),
            in_specs=[
                whole(mixed.shape),
                *[whole(item.shape) for item in weights],
                whole(x.shape),
                whole(gain.shape),
                whole(router_w.shape),
                pl.BlockSpec((rows, kinds), lambda i, scalars: (scalars[1], 0)),
                whole(prior_w.shape),
            ],
            out_specs=[whole((rows, width)), whole((rows, width + lanes)), whole((rows, lanes))],
            scratch_shapes=[pltpu.VMEM((4, width, mixed.shape[1]), BF16)],
        ),
        out_shape=[
            jax.ShapeDtypeStruct((rows, width), F32),
            jax.ShapeDtypeStruct((rows, width + lanes), BF16),
            jax.ShapeDtypeStruct((rows, lanes), F32),
        ],
        compiler_params=pltpu.CompilerParams(vmem_limit_bytes=48 * 2**20),
        cost_estimate=cost_of(6),
        name="middle",
    )(scalars, mixed, *weights, x, gain, router_w, prior, prior_w)


def halves(value):
    high = value.astype(BF16)
    return high, (value - high.astype(F32)).astype(BF16)


def split_dot(left, right):
    (left_high, left_low), (right_high, right_low) = halves(left), halves(right)
    return (
        jnp.dot(left_high, right_high, preferred_element_type=F32)
        + jnp.dot(left_low, right_high, preferred_element_type=F32)
        + jnp.dot(left_high, right_low, preferred_element_type=F32)
    )


def turned_dot(left, right):
    high, low = halves(left.T)
    return jnp.dot(high, right, preferred_element_type=F32) + jnp.dot(
        low, right, preferred_element_type=F32
    )


def router_back_kernel(kinds, experts, scalars, near_ref, got_ref, far_ref, hidden_ref, router_ref,
                       routes_ref, cotangent_ref, prior_ref, gain_ref, small_ref, small_t_ref,
                       vector_ref, prior_w_ref,
                       grad_hidden_ref, grad_low_ref, partial_ref, grad_prior_ref, sums_ref):
    step = pl.program_id(0)
    rows, width = hidden_ref.shape
    place = scalars[1] * rows * pl.num_programs(0) + step * rows
    valid = place + lax.broadcasted_iota(jnp.int32, (rows, 1), 0) < scalars[BOUNDS + 2]
    valid = jnp.where(valid, 1.0, 0.0)
    back = near_ref[0] + got_ref[0].astype(F32) + far_ref[...].astype(F32)
    hidden = hidden_ref[...]
    grad_out = cotangent_ref[...] * valid
    scale = lax.rsqrt(jnp.mean(hidden * hidden, axis=1, keepdims=True) + EPSILON)
    unit = hidden * scale
    normed = unit * gain_ref[...]
    router = router_ref[...]
    lanes = lax.broadcasted_iota(jnp.int32, router.shape, 1)
    routes = routes_ref[...]

    def column(array, k):
        return jnp.sum(jnp.where(lanes == k, array, 0.0), axis=1, keepdims=True)

    def named(kind):
        return jnp.where((routes[:, 0:1] == kind) | (routes[:, 1:2] == kind), 1.0, 0.0)

    copy, first, second = (named(experts + k) for k in (1, 2, 3))
    weight_copy = column(router, experts + 1) * copy
    weight_first = column(router, experts + 2) * first
    weight_second = column(router, experts + 3) * second
    mixlog = split_dot(normed, small_ref[...])

    def softmax_two(k):
        one, two = column(mixlog, k), column(mixlog, k + 1)
        highest = jnp.maximum(one, two)
        one, two = jnp.exp(one - highest), jnp.exp(two - highest)
        return one / (one + two), two / (one + two)

    mix_one, mix_two = softmax_two(kinds), softmax_two(kinds + 2)
    vector_one, vector_two = vector_ref[0:1, :], vector_ref[1:2, :]
    along = jnp.sum(normed * grad_out, axis=1, keepdims=True)
    along_one = jnp.sum(vector_one * grad_out, axis=1, keepdims=True)
    along_two = jnp.sum(vector_two * grad_out, axis=1, keepdims=True)

    extra = back[:, width:]
    pairs = jnp.where(lanes < kinds, extra, 0.0) + jnp.where(
        lanes < kinds, pltpu.roll(extra, extra.shape[1] - kinds, 1), 0.0
    )
    grad_router = pairs + jnp.where(lanes == experts + 1, copy * along, 0.0)
    grad_router += jnp.where(
        lanes == experts + 2, first * (mix_one[0] * along + mix_one[1] * along_one), 0.0
    )
    grad_router += jnp.where(
        lanes == experts + 3, second * (mix_two[0] * along + mix_two[1] * along_two), 0.0
    )
    held = jnp.where(lanes < kinds, router, 0.0)
    grad_small = held * (grad_router - jnp.sum(held * grad_router, axis=1, keepdims=True))
    grad_prior_ref[...] = split_dot(grad_small, prior_w_ref[...])[:, :kinds]
    grad_logits = grad_small

    def mixed_back(weight, mix, other, k):
        one, two = weight * along, weight * other
        inner = mix[0] * one + mix[1] * two
        return jnp.where(lanes == k, mix[0] * (one - inner), 0.0) + jnp.where(
            lanes == k + 1, mix[1] * (two - inner), 0.0
        )

    grad_mixlog = mixed_back(weight_first, mix_one, along_one, kinds) + mixed_back(
        weight_second, mix_two, along_two, kinds + 2
    )
    grad_small = grad_logits + grad_mixlog
    share = weight_copy + weight_first * mix_one[0] + weight_second * mix_two[0]
    grad_normed = (
        back[:, :width]
        + share * grad_out
        + split_dot(grad_small, small_t_ref[...])
    )
    through = grad_normed * gain_ref[...]
    inner = jnp.mean(through * hidden, axis=1, keepdims=True)
    grad_hidden = grad_out + scale * through - (scale * scale * scale * inner) * hidden
    grad_hidden_ref[...] = grad_hidden
    grad_low_ref[...] = grad_hidden.astype(BF16)
    vector_first, vector_second = weight_first * mix_one[1], weight_second * mix_two[1]
    partial_ref[...] = valid * (
        hidden + share * normed + vector_first * vector_one + vector_second * vector_two
    )

    @pl.when(step == 0)
    def _():
        sums_ref[...] = jnp.zeros_like(sums_ref)

    vectors = jnp.where(lanes == kinds + 5, vector_first, 0.0) + jnp.where(
        lanes == kinds + 6, vector_second, 0.0
    )
    low = normed.astype(BF16)
    total = turned_dot(grad_small, low) + turned_dot(vectors, grad_out.astype(BF16))
    sums_ref[: kinds + 8, :] += total[: kinds + 8, :]
    sums_ref[kinds + 4 : kinds + 5, :] += jnp.sum(grad_normed * unit, axis=0, keepdims=True)
    prior = split_dot(prior_ref[...].T, grad_logits)
    sums_ref[pl.ds(kinds + 8, kinds), : lanes.shape[1]] += prior


def router_back(kinds, experts, scalars, near, got, far, hidden, router, routes, cotangent, prior,
                gain, small, small_t, vector, prior_w):
    rows, width = hidden.shape
    block = rows // 2
    lanes = router.shape[1]

    def whole(shape):
        return pl.BlockSpec(shape, lambda i, _: (0,) * len(shape))

    def part(columns):
        return pl.BlockSpec((block, columns), lambda i, _: (i, 0))

    def mine(columns):
        return pl.BlockSpec((block, columns), lambda i, scalars: (scalars[1] * 2 + i, 0))

    return pl.pallas_call(
        functools.partial(router_back_kernel, kinds, experts),
        grid_spec=pltpu.PrefetchScalarGridSpec(
            num_scalar_prefetch=1,
            grid=(2,),
            in_specs=[
                pl.BlockSpec((1, block, width + lanes), lambda i, _: (0, i, 0)),
                pl.BlockSpec((1, block, width + lanes), lambda i, _: (0, i, 0)),
                part(width + lanes),
                part(width),
                part(lanes),
                mine(2),
                part(width),
                mine(kinds),
                whole(gain.shape),
                whole(small.shape),
                whole(small_t.shape),
                whole(vector.shape),
                whole(prior_w.shape),
            ],
            out_specs=[
                part(width),
                part(width),
                part(width),
                part(kinds),
                whole((32, width)),
            ],
        ),
        out_shape=[
            jax.ShapeDtypeStruct((rows, width), F32),
            jax.ShapeDtypeStruct((rows, width), BF16),
            jax.ShapeDtypeStruct((rows, width), F32),
            jax.ShapeDtypeStruct((rows, kinds), F32),
            jax.ShapeDtypeStruct((32, width), F32),
        ],
        compiler_params=pltpu.CompilerParams(vmem_limit_bytes=48 * 2**20),
        cost_estimate=cost_of(8),
        name="router_back",
    )(scalars, near, got, far, hidden, router, routes, cotangent, prior, gain, small, small_t,
      vector, prior_w)


def two_parts(value):
    high = lax.reduce_precision(value, 8, 7)
    return jnp.concatenate([high, value - high], axis=-1).astype(BF16)


def everywhere(value, axes, count):
    copies = jnp.broadcast_to(value[None], (count, *value.shape))
    return lax.all_to_all(copies, axes, 0, 0, tiled=True)


def flip(value, axis, size, bit):
    return lax.ppermute(value, axis, [(i, i ^ bit) for i in range(size)])


def by_halves(value):
    if value.shape[0] == 2:
        return value
    rows, units = value.shape[-2:]
    middle_axes = tuple(range(2, value.ndim - 2))
    turned = value.transpose(*middle_axes, 0, 1, value.ndim - 2, value.ndim - 1)
    turned = turned.reshape(*turned.shape[:-4], 2, LOW, value.shape[0] * rows // 2, units)
    axes = turned.ndim
    return turned.transpose(axes - 4, axes - 3, *range(axes - 4), axes - 2, axes - 1)


def scatter_high(value, many):
    if many != 2:
        rows, units = value.shape[-2:]
        middle_axes = tuple(range(2, value.ndim - 2))
        turned = value.transpose(*middle_axes, 0, 1, value.ndim - 2, value.ndim - 1)
        turned = turned.reshape(*turned.shape[:-4], many, LOW, 2 * rows // many, units)
        axes = turned.ndim
        value = turned.transpose(axes - 4, axes - 3, *range(axes - 4), axes - 2, axes - 1)
    return lax.psum_scatter(value, "hi", scatter_dimension=0)


def gather_rows(value, later, many):
    if many != 2:
        full = lax.all_gather(value, ("hi", "lo"), axis=0, tiled=True)
        full = full.reshape(2, LOW, -1, full.shape[1])
        return [full[:, i] for i in range(LOW)], later
    far, *later = lax.optimization_barrier((swap(value, "hi"), *later))
    both = jnp.stack([value, far])
    return [both] + [flip(both, "lo", LOW, bit) for bit in range(1, LOW)], tuple(later)


def scatter_rows(near, far, many):
    if many != 2:
        full = jnp.stack([near, far]).astype(F32).reshape(-1, near.shape[2])
        return lax.psum_scatter(full, ("hi", "lo"), scatter_dimension=0, tiled=True)
    both = near.astype(F32) + far.astype(F32)
    total = both[0]
    for bit in range(1, LOW):
        total = total + flip(both[bit].astype(BF16), "lo", LOW, bit).astype(F32)
    return total


def per_device(
    many,
    inputs,
    cotangent,
    lengths,
    routes,
    drop_order,
    prior_logits,
    attn_gain,
    w_query,
    w_key,
    w_value,
    w_out,
    moe_gain,
    w_router,
    w_prior,
    w_const,
    const_vector,
    w_gate,
    w_up,
    w_down,
):
    tok_rows, width = inputs.shape
    group = tok_rows * 4
    kinds = w_router.shape[1]
    experts, shard_rows, shard_units = w_gate.shape
    capacity = 3 * group // 16
    share = capacity // 2
    slots = LOW * share
    local_width = w_query.shape[1]
    heads = local_width // HEAD
    tp_axes = ("y", "c")
    all_axes = ("hi", "lo", "y", "c")
    count = many * LOW * 4
    wide = width + 128
    high = lax.axis_index("hi")
    parity = lax.axis_index("y")
    core = lax.axis_index("c")
    place_in_group = parity * 2 + core
    mine = high * LOW + lax.axis_index("lo") if many == 2 else jnp.zeros_like(high)
    boundary = jnp.cumsum(lengths[0])
    scalars = jnp.concatenate(
        [jnp.stack([mine, place_in_group, parity, core, lax.axis_index("lo")]), boundary[:-1]]
    ).astype(jnp.int32)
    gain_one, gain_two = attn_gain.reshape(1, width), moe_gain.reshape(1, width)

    valid_mine = place_in_group * tok_rows + jnp.arange(tok_rows)[:, None] < boundary[-2]
    valid_mine = valid_mine.astype(F32)

    normed_one = rms_norm(inputs, attn_gain).astype(BF16)
    normed_other = swap(normed_one, "y")
    attn_shard = jnp.concatenate([w_query, w_key, w_value, w_out.T], axis=1)
    up_part = lax.all_to_all(w_up, ("lo", "y"), 0, 0, tiled=True)
    up_part = up_part.reshape(LOW, 2, shard_rows, shard_units)
    down_shard = w_down.transpose(0, 2, 1)
    attn_shards, (w_gate,) = gather_rows(attn_shard, (w_gate,), many)
    gate_far = swap(w_gate, "hi") if many == 2 else w_gate
    router_lanes = jnp.pad(
        jnp.concatenate([w_router, w_router], axis=1), ((0, 0), (0, 128 - 2 * kinds))
    )
    prior_lanes = jnp.pad(
        jnp.concatenate([w_prior, w_prior], axis=1), ((0, 0), (0, 128 - 2 * kinds))
    )
    const_flat = w_const.transpose(1, 0, 2).reshape(width, 4)
    small = jnp.pad(
        jnp.concatenate([w_router, const_flat], axis=1), ((0, 0), (0, 128 - kinds - 4))
    )
    small_t = small.T
    prior_back = jnp.pad(w_prior.T, ((0, 128 - kinds), (0, 128 - kinds)))
    (
        attn_shards[0], scalars, router_lanes, prior_lanes, small, small_t, prior_back, prior_logits
    ) = lax.optimization_barrier(
        (attn_shards[0], scalars, router_lanes, prior_lanes, small, small_t, prior_back, prior_logits)
    )
    ids_rows, ids_cols = slots_of(scalars, routes, drop_order, experts, capacity)
    grad_out_low = (cotangent * valid_mine).astype(BF16)
    grad_out_other = swap(grad_out_low, "y")
    (
        normed_other, attn_shards, ids_rows, down_shard, grad_out_other, up_part, gate_far
    ) = lax.optimization_barrier(
        (normed_other, attn_shards, ids_rows, down_shard, grad_out_other, up_part, gate_far)
    )
    down_part = lax.all_to_all(down_shard, ("lo", "y"), 0, 0, tiled=True)
    down_part = down_part.reshape(LOW, 2, shard_rows, shard_units)
    if many == 2:
        up_far = [swap(up_part[:2], "hi"), swap(up_part[2:], "hi")]
    else:
        up_all = by_halves(lax.all_gather(up_part, "hi"))
        up_part, up_far = up_all[0], [up_all[1, :2], up_all[1, 2:]]
    out_mine = jnp.stack([item[:, :, 3 * local_width :] for item in attn_shards])
    out_other = swap(out_mine, "y")
    normed_pieces = [normed_one, swap(normed_one, "c"), normed_other, swap(normed_other, "c")]
    mixed, lse, qkv, qkv_full = attend(normed_pieces, attn_shards, scalars, heads)
    mixed, out_other, out_mine, up_far[0], down_part = lax.optimization_barrier(
        (mixed, out_other, out_mine, up_far[0], down_part)
    )
    if many == 2:
        high_place = high
        down_far = [swap(down_part[:3], "hi"), swap(down_part[3:], "hi")]
        gate_both = jnp.where(
            high == 0, jnp.stack([w_gate, gate_far], axis=1), jnp.stack([gate_far, w_gate], axis=1)
        )
    else:
        high_place = jnp.zeros_like(high)
        down_all = by_halves(lax.all_gather(down_part, "hi"))
        down_part, down_far = down_all[0], [down_all[1, :3], down_all[1, 3:]]
        gate_both = lax.all_gather(w_gate, "hi", axis=1)
    out_pieces = [out_mine, swap(out_mine, "c"), out_other, swap(out_other, "c")]

    mixed_mine = lax.all_to_all(mixed, tp_axes, 0, 0, tiled=True)
    grad_out_pieces = [
        grad_out_low, swap(grad_out_low, "c"), grad_out_other, swap(grad_out_other, "c"),
    ]
    grad_out_slots = pick(ids_rows, grad_out_pieces, slots)
    mixed_mine, grad_out_slots, up_far[1], gate_both = lax.optimization_barrier(
        (mixed_mine, grad_out_slots, up_far[1], gate_both)
    )

    hidden, sent_two, router = middle(
        kinds, scalars, mixed_mine, out_pieces, inputs, gain_two, router_lanes, prior_logits, prior_lanes
    )

    gate_part = lax.all_to_all(gate_both, ("lo", "y"), 0, 0, tiled=True)
    gate_part = gate_part.reshape(LOW, 2, many, shard_rows, shard_units)
    if many != 2:
        gate_part = by_halves(gate_part.transpose(2, 0, 1, 3, 4)).transpose(1, 2, 0, 3, 4)
    other_two, grad_taken, gate_part, down_far[0] = lax.optimization_barrier(
        (swap(sent_two, "y"), to_experts(grad_out_slots), gate_part, down_far[0])
    )
    pieces_two = [sent_two, swap(sent_two, "c"), other_two, swap(other_two, "c")]

    grad_taken += [swap(item, "c") for item in grad_taken]
    sent_slots = pick(ids_rows, pieces_two, slots)
    sent_slots, qkv_full = lax.optimization_barrier((sent_slots, qkv_full))
    taken = to_experts(sent_slots)
    taken += [swap(item, "c") for item in taken]
    qkv_pieces = gather_pieces(qkv_full)
    taken, qkv_pieces, down_far[1] = lax.optimization_barrier((taken, qkv_pieces, down_far[1]))

    expert = lax.axis_index("lo") * 2 + parity
    back_own, back_send, feed_own, feed_send, grads_out = expert_pass(
        kinds, jnp.stack([expert, high_place]).astype(jnp.int32), taken, grad_taken,
        gate_part, [up_part, down_part], up_far + down_far,
    )

    weight_sum = scatter_high(grads_out, many)
    back_taken = to_experts(back_sum(kinds, back_own, swap(back_send, "c")))
    feed_core = swap(feed_send, "c")
    back_taken, feed_core = lax.optimization_barrier((back_taken, feed_core))

    back_near, back_sent = spread(ids_cols, back_taken, tok_rows)
    back_got, back_other = add_core(back_near, back_sent)
    back_other, feed_core = lax.optimization_barrier((back_other, feed_core))
    back_far, feed_blocks = lax.optimization_barrier(
        (swap(back_other, "y"), feed_sum(feed_own, feed_core))
    )

    grad_hidden, grad_low, partial, grad_prior, sums = router_back(
        kinds, experts, scalars, back_near, back_got, back_far, hidden, router, routes, cotangent,
        prior_logits, gain_two, small, small_t, const_vector, prior_back,
    )
    feed_taken = to_experts(feed_blocks)
    grad_mixed = to_heads(mixed_back(scalars, grad_low, out_pieces))
    grad_mixed, grad_low = lax.optimization_barrier((grad_mixed, grad_low))
    low_other = swap(grad_low, "y")
    share_sums = lax.all_to_all(sums.reshape(count, 32 * width // count), all_axes, 0, 0, tiled=True)
    grad_qkv = attend_back(scalars, qkv, lse, grad_mixed, heads).reshape(
        4, 3 * local_width, tok_rows
    )
    grad_qkv, feed_taken, weight_sum, low_other = lax.optimization_barrier(
        (grad_qkv, feed_taken, weight_sum, low_other)
    )
    grad_attn_pieces = [grad_low, swap(grad_low, "c"), low_other, swap(low_other, "c")]

    weight_own = lax.all_to_all(
        weight_sum.reshape(2 * LOW, 3, shard_rows, shard_units), ("lo", "y"), 0, 0, tiled=True
    )
    grad_qkv_mine = to_heads(grad_qkv)
    attn_near, attn_far = attn_grads(grad_qkv, mixed, normed_pieces, grad_attn_pieces, scalars)
    if many == 2:
        attn_far = swap(attn_far, "hi")
    feed_near, feed_sent = spread(ids_cols, feed_taken, tok_rows)
    feed_got, feed_other = add_core(feed_near, feed_sent)
    (
        grad_qkv_mine, share_sums, attn_near, attn_far, feed_near, feed_got, feed_other
    ) = lax.optimization_barrier(
        (grad_qkv_mine, share_sums, attn_near, attn_far, feed_near, feed_got, feed_other)
    )
    feed_far = swap(feed_other, "y")
    share_sums = jnp.sum(share_sums, axis=0)
    grad_inputs, gain_part = inputs_back(
        grad_qkv_mine, qkv_pieces, inputs, gain_one, grad_hidden
    )
    output = partial + valid_mine * (
        feed_near[0] + feed_got[0].astype(F32) + feed_far.astype(F32)
    )
    grad_attn_own = scatter_rows(attn_near, attn_far, many)
    last = jnp.concatenate([jnp.sum(gain_part, axis=0).reshape(-1), share_sums])
    last, weight_own = lax.optimization_barrier((last, weight_own))
    last = everywhere(last, all_axes, count)
    last, grad_attn_own = lax.optimization_barrier((last, grad_attn_own))
    grad_gain = jnp.sum(last[:, :width], axis=0)
    total = last[:, width:].reshape(32, width)
    return (
        output,
        grad_inputs,
        grad_prior,
        grad_gain,
        grad_attn_own[:, :local_width],
        grad_attn_own[:, local_width : 2 * local_width],
        grad_attn_own[:, 2 * local_width : 3 * local_width],
        grad_attn_own[:, 3 * local_width :].T,
        total[kinds + 4],
        total[:kinds].T,
        total[kinds + 8 : 2 * kinds + 8, :kinds],
        total[kinds : kinds + 4].reshape(2, 2, width).transpose(0, 2, 1),
        total[kinds + 5 : kinds + 7],
        weight_own[:, 0].astype(F32),
        weight_own[:, 1].astype(F32),
        weight_own[:, 2].transpose(0, 2, 1).astype(F32),
    )


def solution(mesh):
    many = mesh.shape["fsdp"] // LOW
    fine = Mesh(mesh.devices.reshape(many, LOW, 2, 2), ("hi", "lo", "y", "c"))
    fsdp, tp = ("hi", "lo"), ("y", "c")
    every = fsdp + tp
    return jax.shard_map(
        functools.partial(per_device, many),
        mesh=fine,
        in_specs=(
            P(every, None),
            P(every, None),
            P(fsdp, None),
            P(fsdp, None),
            P(fsdp, None),
            P(fsdp, None),
            P(),
            P(fsdp, tp),
            P(fsdp, tp),
            P(fsdp, tp),
            P(tp, fsdp),
            P(),
            P(),
            P(),
            P(),
            P(),
            P(None, fsdp, tp),
            P(None, fsdp, tp),
            P(None, tp, fsdp),
        ),
        out_specs=(
            P(every, None),
            P(every, None),
            P(every, None),
            P(),
            P(fsdp, tp),
            P(fsdp, tp),
            P(fsdp, tp),
            P(tp, fsdp),
            P(),
            P(),
            P(),
            P(),
            P(),
            P(None, fsdp, tp),
            P(None, fsdp, tp),
            P(None, tp, fsdp),
        ),
        check_vma=False,
    )
```

```python
import functools

import jax
import jax.numpy as jnp
from jax import lax
from jax.experimental import pallas as pl
from jax.experimental.pallas import tpu as pltpu
from jax.sharding import Mesh
from jax.sharding import PartitionSpec as P

HEAD = 64
MAXLEN = 768
LOW = 4
SHARDS = 8
LOW_PLACE = 4
BOUNDS = 5
EPSILON = 1e-06
PRECISE = lax.Precision.HIGHEST
NEGATIVE = -1e30
F32 = jnp.float32
BF16 = jnp.bfloat16


def rms_norm(values, gain):
    return values * lax.rsqrt(jnp.mean(values * values, axis=-1, keepdims=True) + EPSILON) * gain


def swap(value, axis):
    return lax.ppermute(value, axis, [(0, 1), (1, 0)])


def gather_pieces(value):
    other = swap(value, "y")
    return [value, swap(value, "c"), other, swap(other, "c")]


def natural(pieces, index):
    ordered = []
    for j in range(4):
        item = pieces[j]
        for t in range(1, 4):
            item = jnp.where(index == t, pieces[j ^ t], item)
        ordered.append(item)
    return jnp.stack(ordered)


def add_core(near, sent):
    got = swap(sent, "c")
    return got, (near[1] + got[1].astype(F32)).astype(BF16)


def cost_of(microseconds):
    return pl.CostEstimate(
        flops=int(microseconds * 1.15e9), transcendentals=0, bytes_accessed=2**16
    )


def start_of(row, scalars):
    start_row = jnp.zeros_like(row)
    for k in range(BOUNDS, scalars.shape[0]):
        start_row = jnp.where(row >= scalars[k], scalars[k], start_row)
    return start_row


def for_window(first, block, pad, scalars, body):
    needed = (first - start_of(first, scalars) + block - 1) // block
    most = pad // block
    for blocks in range(most):
        pl.when(needed == blocks)(functools.partial(body, (blocks + 1) * block))
    pl.when(needed >= most)(functools.partial(body, pad + block))


def scores_mask(first_key, first_query, window, block, scalars):
    row = first_query + lax.broadcasted_iota(jnp.int32, (1, block), 1)
    start_row = start_of(row, scalars)
    key_places = first_key + lax.broadcasted_iota(jnp.int32, (window, block), 0)
    query_places = first_query + lax.broadcasted_iota(jnp.int32, (window, block), 1)
    return (key_places >= start_row) & (key_places <= query_places)


def attend_kernel(block, pad, scalars, *refs):
    pieces, refs = refs[:4], refs[4:]
    shards, refs = refs[:LOW], refs[LOW:]
    out_ref, lse_ref, qkv_ref, weight_ref, key_rows, value_pad, full = refs
    group = qkv_ref.shape[1]
    quarter = group // 4
    inner = qkv_ref.shape[0] // 3
    head = pl.program_id(0)

    @pl.when(head == 0)
    def _():
        rows = shards[0].shape[1]
        for r in range(SHARDS):
            place = pl.multiple_of((scalars[0] ^ r) * rows, rows)
            full[pl.ds(place, rows), :] = shards[r % LOW][r // LOW]
        turned = full[:, : 3 * inner].T
        weight_ref[...] = turned
        for r in range(4):
            place = pl.multiple_of((scalars[1] ^ r) * quarter, quarter)
            qkv_ref[:, pl.ds(place, quarter)] = lax.dot_general(
                turned, pieces[r][...], (((1,), (1,)), ((), ())), preferred_element_type=F32
            ).astype(BF16)

    first_row = pl.multiple_of(head * HEAD, HEAD)
    key_rows[pl.ds(0, pad), :] = jnp.zeros((pad, HEAD), BF16)
    value_pad[:, pl.ds(0, pad)] = jnp.zeros((HEAD, pad), BF16)
    key_rows[pl.ds(pad, group), :] = qkv_ref[pl.ds(inner + first_row, HEAD), :].T
    value_pad[:, pl.ds(pad, group)] = qkv_ref[pl.ds(2 * inner + first_row, HEAD), :]

    def one(i, carry):
        first = pl.multiple_of(i * block, block)

        def body(window):
            begin = pl.multiple_of(first + pad + block - window, block)
            scores = jnp.dot(
                key_rows[pl.ds(begin, window), :],
                qkv_ref[pl.ds(first_row, HEAD), pl.ds(first, block)],
                preferred_element_type=F32,
            )
            allowed = scores_mask(begin - pad, first, window, block, scalars)
            scores = jnp.where(allowed, scores * 0.125, NEGATIVE)
            highest = jnp.max(scores, axis=0, keepdims=True)
            weights = jnp.exp(scores - highest)
            total = jnp.sum(weights, axis=0, keepdims=True)
            mixed = jnp.dot(
                value_pad[:, pl.ds(begin, window)],
                weights.astype(BF16),
                preferred_element_type=F32,
            )
            mixed = (mixed / total).astype(BF16)
            column = pl.multiple_of(first % quarter, block)
            out_ref[first // quarter, :, pl.ds(column, block)] = mixed
            lse_ref[0, :, pl.ds(first, block)] = highest + jnp.log(total)

        for_window(first, block, pad, scalars, body)
        return carry

    lax.fori_loop(0, group // block, one, 0)


def attend(pieces, shards, scalars, heads):
    rows, width = pieces[0].shape
    group = 4 * rows
    inner = heads * HEAD
    block = 256

    def whole(shape):
        return pl.BlockSpec(
            shape, lambda i, _: (0,) * len(shape), pipeline_mode=pl.Buffered(1)
        )

    return pl.pallas_call(
        functools.partial(attend_kernel, block, MAXLEN),
        grid_spec=pltpu.PrefetchScalarGridSpec(
            num_scalar_prefetch=1,
            grid=(heads,),
            in_specs=[
                *[whole((rows, width)) for _ in range(4)],
                *[whole(shards[0].shape) for _ in range(LOW)],
            ],
            out_specs=[
                pl.BlockSpec((4, HEAD, rows), lambda h, _: (0, h, 0)),
                pl.BlockSpec((1, 1, group), lambda h, _: (h, 0, 0)),
                whole((3 * inner, group)),
                whole((3 * inner, width)),
            ],
            scratch_shapes=[
                pltpu.VMEM((MAXLEN + group, HEAD), BF16),
                pltpu.VMEM((HEAD, MAXLEN + group), BF16),
                pltpu.VMEM((width, 4 * inner), BF16),
            ],
        ),
        out_shape=[
            jax.ShapeDtypeStruct((4, inner, rows), BF16),
            jax.ShapeDtypeStruct((heads, 1, group), F32),
            jax.ShapeDtypeStruct((3 * inner, group), BF16),
            jax.ShapeDtypeStruct((3 * inner, width), BF16),
        ],
        compiler_params=pltpu.CompilerParams(vmem_limit_bytes=48 * 2**20),
        cost_estimate=cost_of(24),
        name="attend",
    )(scalars, *pieces, *shards)


def attn_grads_kernel(scalars, *refs):
    grad_qkv, mixed, refs = refs[0], refs[1], refs[2:]
    tokens, grads, refs = refs[:4], refs[4:8], refs[8:]
    outs, (total,) = refs[:2], refs[2:]
    inner3 = grad_qkv.shape[1]
    first, second = 0.0, 0.0
    for r in range(4):
        j = scalars[1] ^ r
        first += jnp.dot(grad_qkv[r], tokens[r][...], preferred_element_type=F32)
        second += jnp.dot(mixed[j], grads[r][...], preferred_element_type=F32)
    total[:, :inner3] = first.T.astype(BF16)
    total[:, inner3:] = second.T.astype(BF16)
    rows = outs[0].shape[1]
    for r in range(SHARDS):
        place = pl.multiple_of((scalars[0] ^ r) * rows, rows)
        outs[r // LOW][r % LOW] = total[pl.ds(place, rows), :]


def attn_grads(grad_qkv, mixed, tokens, grads, scalars):
    width = tokens[0].shape[1]
    columns = grad_qkv.shape[1] + mixed.shape[1]
    rows = width // SHARDS
    whole = pl.BlockSpec(memory_space=pltpu.VMEM)
    return pl.pallas_call(
        attn_grads_kernel,
        in_specs=[pl.BlockSpec(memory_space=pltpu.SMEM)] + [whole] * 10,
        out_specs=[whole] * 2,
        out_shape=[jax.ShapeDtypeStruct((LOW, rows, columns), BF16)] * 2,
        scratch_shapes=[pltpu.VMEM((width, columns), BF16)],
        compiler_params=pltpu.CompilerParams(vmem_limit_bytes=48 * 2**20),
        cost_estimate=cost_of(30),
        name="attn_grads",
    )(scalars, grad_qkv, mixed, *tokens, *grads)


def attend_back_kernel(block, pad, scalars, qkv_ref, lse_ref, *refs):
    pieces, refs = refs[:4], refs[4:]
    out_ref, grad_mixed, key_rows, value_rows, key_pad, grad_key, grad_value = refs
    group = qkv_ref.shape[1]
    inner_rows = qkv_ref.shape[0] // 3
    quarter = group // 4
    contract_last = (((1,), (1,)), ((), ()))
    head = pl.program_id(0)

    @pl.when(head == 0)
    def _():
        for r in range(4):
            place = pl.multiple_of((scalars[1] ^ r) * quarter, quarter)
            grad_mixed[:, pl.ds(place, quarter)] = pieces[r][...]

    first_row = pl.multiple_of(head * HEAD, HEAD)
    keys = qkv_ref[pl.ds(inner_rows + first_row, HEAD), :]
    key_rows[pl.ds(0, pad), :] = jnp.zeros((pad, HEAD), BF16)
    value_rows[pl.ds(0, pad), :] = jnp.zeros((pad, HEAD), BF16)
    key_pad[:, pl.ds(0, pad)] = jnp.zeros((HEAD, pad), BF16)
    key_rows[pl.ds(pad, group), :] = keys.T
    value_rows[pl.ds(pad, group), :] = qkv_ref[pl.ds(2 * inner_rows + first_row, HEAD), :].T
    key_pad[:, pl.ds(pad, group)] = keys
    grad_key[...] = jnp.zeros_like(grad_key)
    grad_value[...] = jnp.zeros_like(grad_value)

    def one(i, carry):
        first = pl.multiple_of(i * block, block)

        def body(window):
            begin = pl.multiple_of(first + pad + block - window, block)
            query = qkv_ref[pl.ds(first_row, HEAD), pl.ds(first, block)]
            grad = grad_mixed[pl.ds(first_row, HEAD), pl.ds(first, block)]
            scores = jnp.dot(key_rows[pl.ds(begin, window), :], query, preferred_element_type=F32)
            allowed = scores_mask(begin - pad, first, window, block, scalars)
            exponent = scores * 0.125 - lse_ref[0, :, pl.ds(first, block)]
            probs = jnp.exp(jnp.where(allowed, exponent, NEGATIVE))
            grad_probs = jnp.dot(
                value_rows[pl.ds(begin, window), :], grad, preferred_element_type=F32
            )
            inner = jnp.sum(probs * grad_probs, axis=0, keepdims=True)
            raw = (0.125 * (probs * (grad_probs - inner))).astype(BF16)
            grad_query = jnp.dot(
                key_pad[:, pl.ds(begin, window)], raw, preferred_element_type=F32
            )
            column = pl.multiple_of(first % quarter, block)
            piece = (first // quarter) ^ scalars[1]
            out_ref[piece, 0, :, pl.ds(column, block)] = grad_query.astype(BF16)
            grad_value[:, pl.ds(begin, window)] += lax.dot_general(
                grad, probs.astype(BF16), contract_last, preferred_element_type=F32
            )
            grad_key[:, pl.ds(begin, window)] += lax.dot_general(
                query, raw, contract_last, preferred_element_type=F32
            )

        for_window(first, block, pad, scalars, body)
        return carry

    lax.fori_loop(0, group // block, one, 0)
    for j in range(4):
        piece = scalars[1] ^ j
        out_ref[piece, 1] = grad_key[:, pl.ds(pad + j * quarter, quarter)].astype(BF16)
        out_ref[piece, 2] = grad_value[:, pl.ds(pad + j * quarter, quarter)].astype(BF16)


def attend_back(scalars, qkv, lse, pieces, heads):
    group = qkv.shape[1]
    block = 256

    def whole(shape):
        return pl.BlockSpec(
            shape, lambda i, _: (0,) * len(shape), pipeline_mode=pl.Buffered(1)
        )

    return pl.pallas_call(
        functools.partial(attend_back_kernel, block, MAXLEN),
        grid_spec=pltpu.PrefetchScalarGridSpec(
            num_scalar_prefetch=1,
            grid=(heads,),
            in_specs=[
                whole(qkv.shape),
                pl.BlockSpec((1, 1, group), lambda h, _: (h, 0, 0)),
                *[whole(item.shape) for item in pieces],
            ],
            out_specs=pl.BlockSpec((4, 3, HEAD, group // 4), lambda h, _: (0, 0, h, 0)),
            scratch_shapes=[
                pltpu.VMEM((heads * HEAD, group), BF16),
                pltpu.VMEM((MAXLEN + group, HEAD), BF16),
                pltpu.VMEM((MAXLEN + group, HEAD), BF16),
                pltpu.VMEM((HEAD, MAXLEN + group), BF16),
                pltpu.VMEM((HEAD, MAXLEN + group), F32),
                pltpu.VMEM((HEAD, MAXLEN + group), F32),
            ],
        ),
        out_shape=jax.ShapeDtypeStruct((4, 3, heads * HEAD, group // 4), BF16),
        compiler_params=pltpu.CompilerParams(vmem_limit_bytes=48 * 2**20),
        cost_estimate=cost_of(34),
        name="attend_back",
    )(scalars, qkv, lse, *pieces)


def mixed_back_kernel(scalars, grad_ref, p0, p1, p2, p3, *refs):
    outs, weight = refs[:4], refs[4]
    rows = p0.shape[2]
    for r, shards in enumerate((p0, p1, p2, p3)):
        for k in range(SHARDS):
            place = pl.multiple_of((scalars[0] ^ k) * rows, rows)
            weight[pl.ds(place, rows), :] = shards[k % LOW, k // LOW]
        outs[r][...] = lax.dot_general(
            weight[...].T, grad_ref[...], (((1,), (1,)), ((), ())), preferred_element_type=F32
        ).astype(BF16)


def mixed_back(scalars, grad, weights):
    rows, width = grad.shape
    inner = weights[0].shape[3]

    def whole(shape):
        return pl.BlockSpec(shape, lambda i, _: (0,) * len(shape))

    return pl.pallas_call(
        mixed_back_kernel,
        grid_spec=pltpu.PrefetchScalarGridSpec(
            num_scalar_prefetch=1,
            grid=(1,),
            in_specs=[whole(grad.shape), *[whole(item.shape) for item in weights]],
            out_specs=[whole((inner, rows)) for _ in range(4)],
            scratch_shapes=[pltpu.VMEM((width, inner), BF16)],
        ),
        out_shape=[jax.ShapeDtypeStruct((inner, rows), BF16) for _ in range(4)],
        compiler_params=pltpu.CompilerParams(vmem_limit_bytes=32 * 2**20),
        cost_estimate=cost_of(4),
        name="mixed_back",
    )(scalars, grad, *weights)


def inputs_back_kernel(g0, g1, g2, g3, p0, p1, p2, p3, x_ref, gain_ref, hidden_ref, out_ref, sum_ref):
    total = 0.0
    for grad, weight in zip((g0, g1, g2, g3), (p0, p1, p2, p3)):
        total += jnp.dot(grad[...].T, weight[...], preferred_element_type=F32)
    x = x_ref[...]
    scale = lax.rsqrt(jnp.mean(x * x, axis=1, keepdims=True) + EPSILON)
    through = total * gain_ref[...]
    inner = jnp.mean(through * x, axis=1, keepdims=True)
    out_ref[...] = hidden_ref[...] + scale * through - (scale * scale * scale * inner) * x
    sum_ref[0] = jnp.sum(total * x * scale, axis=0, keepdims=True)


def inputs_back(grads, weights, x, gain, grad_hidden):
    rows, width = x.shape
    block = rows // 2

    def whole(shape):
        return pl.BlockSpec(shape, lambda i: (0,) * len(shape), pipeline_mode=pl.Buffered(1))

    part = pl.BlockSpec((block, width), lambda i: (i, 0))
    return pl.pallas_call(
        inputs_back_kernel,
        grid=(2,),
        in_specs=[
            *[pl.BlockSpec((item.shape[0], block), lambda i: (0, i)) for item in grads],
            *[whole(item.shape) for item in weights],
            part,
            whole(gain.shape),
            part,
        ],
        out_specs=[part, pl.BlockSpec((1, 1, width), lambda i: (i, 0, 0))],
        out_shape=[
            jax.ShapeDtypeStruct(x.shape, F32),
            jax.ShapeDtypeStruct((2, 1, width), F32),
        ],
        compiler_params=pltpu.CompilerParams(vmem_limit_bytes=48 * 2**20),
        cost_estimate=cost_of(6),
        name="inputs_back",
    )(*grads, *weights, x, gain, grad_hidden)


def expert_kernel(
    kinds, scalars, w_gate, *refs
):
    near_pieces, far_pieces, refs = refs[:2], refs[2:6], refs[6:]
    x_blocks, g_blocks, g_core = refs[: 2 * LOW], refs[2 * LOW : 3 * LOW], refs[3 * LOW]
    refs = refs[3 * LOW + 1 :]
    back_own, back_send, feed_own, feed_send, grads_out, *refs = refs
    x_all, g_all, x_t, g_t, weights, hidden, acc_feed, acc_back, scales, plain = refs
    slots, width = feed_own.shape
    block = slots // LOW
    half = width // 2
    step = pl.program_id(0)
    contract_last = (((1,), (1,)), ((), ()))
    units = weights.shape[2]

    def weight_column(x_ref):
        extra = x_ref[:, width:].astype(F32)
        lanes = lax.broadcasted_iota(jnp.int32, extra.shape, 1)
        named = (lanes == scalars[0]) | (lanes == scalars[0] + kinds)
        return jnp.sum(jnp.where(named, extra, 0.0), axis=1, keepdims=True)

    @pl.when(step == 0)
    def _():
        for i in range(2 * LOW):
            rows = pl.ds(i * block, block)
            scale = weight_column(x_blocks[i])
            scales[rows, :] = jnp.broadcast_to(scale, (block, 128))
            if i < LOW:
                plain[rows, :] = g_blocks[i][...]
            else:
                plain[rows, :] = g_core[pl.ds((i - LOW) * block, block), :]
            x_all[rows, :] = x_blocks[i][:, :width]
            g_all[rows, :] = (plain[rows, :].astype(F32) * scale).astype(BF16)
        x_t[...] = x_all[...].T
        g_t[...] = g_all[...].T
        acc_feed[...] = jnp.zeros_like(acc_feed)
        acc_back[...] = jnp.zeros_like(acc_back)

    for i in range(2):
        rows = pl.ds(i * half, half)
        weights[0, rows, :] = w_gate[:, 0, i].reshape(half, units)
    near = pl.multiple_of(scalars[1] * half, half)
    for k in range(2):
        weights[k + 1, pl.ds(near, half), :] = near_pieces[k][:, 0].reshape(half, units)
        place = (1 - scalars[1]) * half
        for piece in far_pieces[2 * k : 2 * k + 2]:
            rows = piece.shape[0] * half // LOW
            weights[k + 1, pl.ds(pl.multiple_of(place, half // LOW), rows), :] = piece[
                :, 0
            ].reshape(rows, units)
            place += rows

    for part in range(2):
        rows = pl.ds(part * slots, slots)
        x = x_all[rows, :]
        gate = jnp.dot(x, weights[0], preferred_element_type=F32)
        up = jnp.dot(x, weights[1], preferred_element_type=F32)
        grad_act = jnp.dot(g_all[rows, :], weights[2], preferred_element_type=F32)
        sig = jax.nn.sigmoid(gate)
        silu = gate * sig
        active = (silu * up).astype(BF16)
        grad_gate = (grad_act * up * (sig * (1.0 + gate * (1.0 - sig)))).astype(BF16)
        grad_up = (grad_act * silu).astype(BF16)
        hidden[0, rows, :] = grad_gate
        hidden[1, rows, :] = grad_up
        hidden[2, rows, :] = active
        acc_feed[rows, :] += lax.dot_general(
            active, weights[2], contract_last, preferred_element_type=F32
        )
        acc_back[rows, :] += lax.dot_general(
            grad_gate, weights[0], contract_last, preferred_element_type=F32
        ) + lax.dot_general(grad_up, weights[1], contract_last, preferred_element_type=F32)

    for k in range(3):
        left = (g_t if k == 2 else x_t)
        grad = jnp.dot(left[...], hidden[k], preferred_element_type=F32).astype(BF16)
        for i in range(2):
            part = grad[i * half : (i + 1) * half].reshape(LOW, -1, units)
            grads_out[i, :, 0, k] = part

    @pl.when(step == pl.num_programs(0) - 1)
    def _():
        for part in range(2):
            rows = pl.ds(part * slots, slots)
            feed = acc_feed[rows, :]
            inner = jnp.sum(feed * plain[rows, :].astype(F32), axis=1, keepdims=True)
            feed = feed * scales[rows, 0:1]
            lanes = lax.broadcasted_iota(jnp.int32, (slots, 128), 1)
            if part == 0:
                back_own[:, :width] = acc_back[rows, :]
                back_own[:, width:] = jnp.where(lanes == scalars[0], inner, 0.0)
                feed_own[...] = feed
            else:
                high = inner.astype(BF16).astype(F32)
                extra = jnp.where(lanes == scalars[0], high, 0.0)
                extra = jnp.where(lanes == scalars[0] + kinds, inner - high, extra)
                back_send[:, :width] = acc_back[rows, :].astype(BF16)
                back_send[:, width:] = extra.astype(BF16)
                feed_send[...] = feed.astype(BF16)


def expert_pass(kinds, scalars, x_blocks, g_blocks, w_gate, w_near, w_far):
    block, width = g_blocks[0].shape
    slots = LOW * block
    low, parities, _, shard_rows, shard_units = w_gate.shape
    units = 512
    steps = shard_units // units

    def whole(shape):
        return pl.BlockSpec(
            shape, lambda i, _: (0,) * len(shape), pipeline_mode=pl.Buffered(1)
        )

    grads_spec = pl.BlockSpec(
        (2, low, 1, 3, shard_rows, units), lambda i, _: (0, 0, i // steps, 0, 0, i % steps)
    )
    gate_spec = pl.BlockSpec(
        (low, 1, 2, shard_rows, units), lambda i, _: (0, i // steps, 0, 0, i % steps)
    )
    def up_spec(count):
        return pl.BlockSpec(
            (count, 1, shard_rows, units), lambda i, _: (0, i // steps, 0, i % steps)
        )

    wide = width + 128
    return pl.pallas_call(
        functools.partial(expert_kernel, kinds),
        grid_spec=pltpu.PrefetchScalarGridSpec(
            num_scalar_prefetch=1,
            grid=(parities * steps,),
            in_specs=[
                gate_spec,
                *[up_spec(item.shape[0]) for item in (*w_near, *w_far)],
                *[whole((block, wide)) for _ in range(2 * LOW)],
                *[whole(item.shape) for item in g_blocks],
            ],
            out_specs=[
                whole((slots, wide)),
                whole((slots, wide)),
                whole((slots, width)),
                whole((slots, width)),
                grads_spec,
            ],
            scratch_shapes=[
                pltpu.VMEM((2 * slots, width), BF16),
                pltpu.VMEM((2 * slots, width), BF16),
                pltpu.VMEM((width, 2 * slots), BF16),
                pltpu.VMEM((width, 2 * slots), BF16),
                pltpu.VMEM((3, width, units), BF16),
                pltpu.VMEM((3, 2 * slots, units), BF16),
                pltpu.VMEM((2 * slots, width), F32),
                pltpu.VMEM((2 * slots, width), F32),
                pltpu.VMEM((2 * slots, 128), F32),
                pltpu.VMEM((2 * slots, width), BF16),
            ],
        ),
        out_shape=[
            jax.ShapeDtypeStruct((slots, wide), F32),
            jax.ShapeDtypeStruct((slots, wide), BF16),
            jax.ShapeDtypeStruct((slots, width), F32),
            jax.ShapeDtypeStruct((slots, width), BF16),
            jax.ShapeDtypeStruct((2, low, parities, 3, shard_rows, shard_units), BF16),
        ],
        compiler_params=pltpu.CompilerParams(vmem_limit_bytes=58 * 2**20),
        cost_estimate=cost_of(35),
        name="expert_pass",
    )(scalars, w_gate, *w_near, *w_far, *x_blocks, *g_blocks)


def pick_kernel(ids_ref, *refs):
    pieces, outs = refs[:4], refs[4:]
    block = outs[0].shape[0]
    rows = pieces[0].shape[0]
    for i, out_ref in enumerate(outs):
        slot = i * block + lax.broadcasted_iota(jnp.int32, (block, rows), 0)
        total = 0.0
        for r in range(4):
            columns = pl.ds(r * rows, rows)
            held = (slot == ids_ref[0:1, columns]) | (slot == ids_ref[1:2, columns])
            held = jnp.where(held, 1.0, 0.0).astype(BF16)
            total += jnp.dot(held, pieces[r][...], preferred_element_type=F32)
        out_ref[...] = total.astype(BF16)


def pick(ids, pieces, slots):
    rows, width = pieces[0].shape
    block = slots // LOW

    def whole(shape):
        return pl.BlockSpec(shape, lambda i: (0, 0))

    return pl.pallas_call(
        pick_kernel,
        grid=(1,),
        in_specs=[whole((8, 4 * rows)), *[whole((rows, width)) for _ in range(4)]],
        out_specs=[whole((block, width)) for _ in range(LOW)],
        out_shape=[jax.ShapeDtypeStruct((block, width), BF16) for _ in range(LOW)],
        compiler_params=pltpu.CompilerParams(vmem_limit_bytes=32 * 2**20),
        cost_estimate=cost_of(5),
        name="pick",
    )(ids, *pieces)


def to_experts(blocks):
    return [blocks[0]] + [flip(blocks[b], "lo", LOW, b) for b in range(1, LOW)]


def to_heads(blocks):
    return [blocks[0]] + [
        lax.ppermute(blocks[r], ("y", "c"), [(i, i ^ r) for i in range(4)]) for r in range(1, 4)
    ]


def back_sum_kernel(kinds, own_ref, core_ref, *outs):
    width = own_ref.shape[1] - 128
    block = outs[0].shape[0]
    for i, out_ref in enumerate(outs):
        rows = pl.ds(i * block, block)
        out_ref[:, :width] = (
            own_ref[rows, :width] + core_ref[rows, :width].astype(F32)
        ).astype(BF16)
        extra = own_ref[rows, width:] + core_ref[rows, width:].astype(F32)
        lanes = lax.broadcasted_iota(jnp.int32, extra.shape, 1)
        high = jnp.where(lanes < kinds, extra, 0.0).astype(BF16).astype(F32)
        low = jnp.where(lanes < kinds, extra - high, 0.0)
        low = pltpu.roll(low, kinds, 1) + jnp.where(lanes >= kinds, extra, 0.0)
        out_ref[:, width:] = (high + low).astype(BF16)


def back_sum(kinds, own, core):
    slots, wide = own.shape
    block = slots // LOW

    def whole(shape):
        return pl.BlockSpec(shape, lambda i: (0, 0))

    return pl.pallas_call(
        functools.partial(back_sum_kernel, kinds),
        grid=(1,),
        in_specs=[whole(own.shape), whole(core.shape)],
        out_specs=[whole((block, wide)) for _ in range(LOW)],
        out_shape=[jax.ShapeDtypeStruct((block, wide), BF16) for _ in range(LOW)],
        compiler_params=pltpu.CompilerParams(vmem_limit_bytes=32 * 2**20),
        cost_estimate=cost_of(3),
        name="back_sum",
    )(own, core)


def feed_sum_kernel(own_ref, core_ref, *outs):
    block = outs[0].shape[0]
    for i, out_ref in enumerate(outs):
        rows = pl.ds(i * block, block)
        out_ref[...] = (own_ref[rows, :] + core_ref[rows, :].astype(F32)).astype(BF16)


def feed_sum(own, core):
    slots, width = own.shape
    block = slots // LOW

    def whole(shape):
        return pl.BlockSpec(shape, lambda i: (0, 0))

    return pl.pallas_call(
        feed_sum_kernel,
        grid=(1,),
        in_specs=[whole(own.shape), whole(core.shape)],
        out_specs=[whole((block, width)) for _ in range(LOW)],
        out_shape=[jax.ShapeDtypeStruct((block, width), BF16) for _ in range(LOW)],
        compiler_params=pltpu.CompilerParams(vmem_limit_bytes=32 * 2**20),
        cost_estimate=cost_of(3),
        name="feed_sum",
    )(own, core)


def spread_kernel(ids_ref, *refs):
    blocks, (near_ref, send_ref, slots_ref) = refs[:LOW], refs[LOW:]
    rows = near_ref.shape[1]
    slots = slots_ref.shape[0]
    block = slots // LOW

    @pl.when(pl.program_id(0) == 0)
    def _():
        for i in range(LOW):
            slots_ref[pl.ds(i * block, block), :] = blocks[i][...]

    for k, out_ref in enumerate((near_ref, send_ref)):
        slot = lax.broadcasted_iota(jnp.int32, (rows, slots), 1)
        ids = ids_ref[pl.ds(k * rows, rows), :]
        held = (slot == ids[:, 0:1]) | (slot == ids[:, 1:2])
        held = jnp.where(held, 1.0, 0.0).astype(BF16)
        total = jnp.dot(held, slots_ref[...], preferred_element_type=F32)
        out_ref[0] = total.astype(out_ref.dtype)


def spread(ids, values, rows):
    block, width = values[0].shape
    return pl.pallas_call(
        spread_kernel,
        grid=(2,),
        in_specs=[
            pl.BlockSpec((2 * rows, 8), lambda i: (i, 0)),
            *[pl.BlockSpec((block, width), lambda i: (0, 0)) for _ in range(LOW)],
        ],
        out_specs=[
            pl.BlockSpec((1, rows, width), lambda i: (i, 0, 0)),
            pl.BlockSpec((1, rows, width), lambda i: (i, 0, 0)),
        ],
        out_shape=[
            jax.ShapeDtypeStruct((2, rows, width), F32),
            jax.ShapeDtypeStruct((2, rows, width), BF16),
        ],
        scratch_shapes=[pltpu.VMEM((LOW * block, width), BF16)],
        compiler_params=pltpu.CompilerParams(vmem_limit_bytes=32 * 2**20),
        cost_estimate=cost_of(30),
        name="spread",
    )(ids, *values)


def slots_kernel(experts, capacity, scalars, routes_col, order_col, routes_row, order_row,
                 row_ref, col_ref, places_ref):
    group = routes_row.shape[1]
    rows = group // 4
    share = capacity // 2
    span = 2 * group
    bound = scalars[BOUNDS + 2]

    def target_of(routes, axis):
        place = lax.broadcasted_iota(jnp.int32, routes.shape, axis)
        return jnp.where((routes < experts) & (place < bound), routes, experts)

    target = target_of(routes_row[...], 1)
    code = target * span + order_row[...]
    block = 256

    def count(i, carry):
        first = pl.multiple_of(i * block, block)
        routes = routes_col[pl.ds(first, block), :]
        place = first + lax.broadcasted_iota(jnp.int32, routes.shape, 0)
        held = jnp.where((routes < experts) & (place < bound), routes, experts)
        others = held * span + order_col[pl.ds(first, block), :]
        result = []
        for k in range(2):
            total = carry[k]
            for j in range(2):
                smaller = jnp.where(others[:, j : j + 1] < code[k : k + 1, :], 1.0, 0.0)
                total = total + jnp.sum(smaller, axis=0, keepdims=True)
            result.append(total)
        return tuple(result)

    zero = jnp.zeros((1, group), F32)
    counts = lax.fori_loop(0, group // block, count, (zero, zero))
    for k in range(2):
        mine_target = target[k : k + 1, :]
        base = jnp.zeros((1, group), F32)
        for e in range(1, experts):
            earlier = jnp.sum(jnp.where(target < e, 1.0, 0.0))
            base = jnp.where(mine_target == e, earlier, base)
        place = (counts[k] - base).astype(jnp.int32)
        first = scalars[3] * share
        held = (
            (mine_target < experts)
            & (place >= first)
            & (place < first + share)
            & (place < capacity)
            & (jnp.bitwise_and(mine_target, 1) == scalars[2])
        )
        block = jnp.bitwise_xor(lax.shift_right_logical(mine_target, 1), scalars[LOW_PLACE])
        slot = block * share + place - first
        places_ref[k : k + 1, :] = jnp.where(held, slot, -1)
    for r in range(4):
        start = pl.multiple_of((scalars[1] ^ r) * rows, rows)
        piece = places_ref[:, pl.ds(start, rows)]
        row_ref[:, pl.ds(r * rows, rows)] = piece
        col_ref[pl.ds(r * rows, rows), :] = piece.T


def slots_of(scalars, routes, drop_order, experts, capacity):
    group = routes.shape[0]
    whole = pl.BlockSpec(memory_space=pltpu.VMEM)
    return pl.pallas_call(
        functools.partial(slots_kernel, experts, capacity),
        in_specs=[pl.BlockSpec(memory_space=pltpu.SMEM)] + [whole] * 4,
        out_specs=[whole] * 2,
        out_shape=[
            jax.ShapeDtypeStruct((8, group), jnp.int32),
            jax.ShapeDtypeStruct((group, 8), jnp.int32),
        ],
        scratch_shapes=[pltpu.VMEM((8, group), jnp.int32)],
        compiler_params=pltpu.CompilerParams(vmem_limit_bytes=32 * 2**20),
        cost_estimate=cost_of(8),
        name="slots",
    )(scalars, routes, drop_order, routes.T, drop_order.T)


def middle_kernel(kinds, scalars, mixed, p0, p1, p2, p3, x_ref, gain_ref, router_w, prior_ref,
                  prior_w, hidden_ref, sent_ref, router_ref, weight):
    hidden = x_ref[...]
    rows = p0.shape[2]
    for r, shards in enumerate((p0, p1, p2, p3)):
        for k in range(SHARDS):
            place = pl.multiple_of((scalars[0] ^ k) * rows, rows)
            weight[r, pl.ds(place, rows), :] = shards[k % LOW, k // LOW]
        hidden += lax.dot_general(
            mixed[scalars[1] ^ r].T, weight[r], (((1,), (1,)), ((), ())),
            preferred_element_type=F32,
        )
    hidden_ref[...] = hidden
    scale = lax.rsqrt(jnp.mean(hidden * hidden, axis=1, keepdims=True) + EPSILON)
    rounded = (hidden * scale * gain_ref[...]).astype(BF16)
    width = hidden.shape[1]
    sent_ref[:, :width] = rounded
    router_high, router_low = halves(router_w[...])
    logits = (
        jnp.dot(rounded, router_high, preferred_element_type=F32)
        + jnp.dot(rounded, router_low, preferred_element_type=F32)
        + split_dot(prior_ref[...], prior_w[...])
    )
    lanes = lax.broadcasted_iota(jnp.int32, logits.shape, 1)
    logits = jnp.where(lanes < 2 * kinds, logits, NEGATIVE)
    weights = jnp.exp(logits - jnp.max(logits, axis=1, keepdims=True))
    total = jnp.sum(jnp.where(lanes < kinds, weights, 0.0), axis=1, keepdims=True)
    router = weights / total
    router_ref[...] = router
    high = router.astype(BF16).astype(F32)
    sent_ref[:, width:] = jnp.where(lanes < kinds, high, router - high).astype(BF16)


def middle(kinds, scalars, mixed, weights, x, gain, router_w, prior, prior_w):
    rows, width = x.shape
    lanes = router_w.shape[1]

    def whole(shape):
        return pl.BlockSpec(shape, lambda i, _: (0,) * len(shape))

    return pl.pallas_call(
        functools.partial(middle_kernel, kinds),
        grid_spec=pltpu.PrefetchScalarGridSpec(
            num_scalar_prefetch=1,
            grid=(1,),
            in_specs=[
                whole(mixed.shape),
                *[whole(item.shape) for item in weights],
                whole(x.shape),
                whole(gain.shape),
                whole(router_w.shape),
                pl.BlockSpec((rows, kinds), lambda i, scalars: (scalars[1], 0)),
                whole(prior_w.shape),
            ],
            out_specs=[whole((rows, width)), whole((rows, width + lanes)), whole((rows, lanes))],
            scratch_shapes=[pltpu.VMEM((4, width, mixed.shape[1]), BF16)],
        ),
        out_shape=[
            jax.ShapeDtypeStruct((rows, width), F32),
            jax.ShapeDtypeStruct((rows, width + lanes), BF16),
            jax.ShapeDtypeStruct((rows, lanes), F32),
        ],
        compiler_params=pltpu.CompilerParams(vmem_limit_bytes=48 * 2**20),
        cost_estimate=cost_of(6),
        name="middle",
    )(scalars, mixed, *weights, x, gain, router_w, prior, prior_w)


def halves(value):
    high = value.astype(BF16)
    return high, (value - high.astype(F32)).astype(BF16)


def split_dot(left, right):
    (left_high, left_low), (right_high, right_low) = halves(left), halves(right)
    return (
        jnp.dot(left_high, right_high, preferred_element_type=F32)
        + jnp.dot(left_low, right_high, preferred_element_type=F32)
        + jnp.dot(left_high, right_low, preferred_element_type=F32)
    )


def turned_dot(left, right):
    high, low = halves(left.T)
    return jnp.dot(high, right, preferred_element_type=F32) + jnp.dot(
        low, right, preferred_element_type=F32
    )


def router_back_kernel(kinds, experts, scalars, near_ref, got_ref, far_ref, hidden_ref, router_ref,
                       routes_ref, cotangent_ref, prior_ref, gain_ref, small_ref, small_t_ref,
                       vector_ref, prior_w_ref,
                       grad_hidden_ref, grad_low_ref, partial_ref, grad_prior_ref, sums_ref):
    step = pl.program_id(0)
    rows, width = hidden_ref.shape
    place = scalars[1] * rows * pl.num_programs(0) + step * rows
    valid = place + lax.broadcasted_iota(jnp.int32, (rows, 1), 0) < scalars[BOUNDS + 2]
    valid = jnp.where(valid, 1.0, 0.0)
    back = near_ref[0] + got_ref[0].astype(F32) + far_ref[...].astype(F32)
    hidden = hidden_ref[...]
    grad_out = cotangent_ref[...] * valid
    scale = lax.rsqrt(jnp.mean(hidden * hidden, axis=1, keepdims=True) + EPSILON)
    unit = hidden * scale
    normed = unit * gain_ref[...]
    router = router_ref[...]
    lanes = lax.broadcasted_iota(jnp.int32, router.shape, 1)
    routes = routes_ref[...]

    def column(array, k):
        return jnp.sum(jnp.where(lanes == k, array, 0.0), axis=1, keepdims=True)

    def named(kind):
        return jnp.where((routes[:, 0:1] == kind) | (routes[:, 1:2] == kind), 1.0, 0.0)

    copy, first, second = (named(experts + k) for k in (1, 2, 3))
    weight_copy = column(router, experts + 1) * copy
    weight_first = column(router, experts + 2) * first
    weight_second = column(router, experts + 3) * second
    mixlog = split_dot(normed, small_ref[...])

    def softmax_two(k):
        one, two = column(mixlog, k), column(mixlog, k + 1)
        highest = jnp.maximum(one, two)
        one, two = jnp.exp(one - highest), jnp.exp(two - highest)
        return one / (one + two), two / (one + two)

    mix_one, mix_two = softmax_two(kinds), softmax_two(kinds + 2)
    vector_one, vector_two = vector_ref[0:1, :], vector_ref[1:2, :]
    along = jnp.sum(normed * grad_out, axis=1, keepdims=True)
    along_one = jnp.sum(vector_one * grad_out, axis=1, keepdims=True)
    along_two = jnp.sum(vector_two * grad_out, axis=1, keepdims=True)

    extra = back[:, width:]
    pairs = jnp.where(lanes < kinds, extra, 0.0) + jnp.where(
        lanes < kinds, pltpu.roll(extra, extra.shape[1] - kinds, 1), 0.0
    )
    grad_router = pairs + jnp.where(lanes == experts + 1, copy * along, 0.0)
    grad_router += jnp.where(
        lanes == experts + 2, first * (mix_one[0] * along + mix_one[1] * along_one), 0.0
    )
    grad_router += jnp.where(
        lanes == experts + 3, second * (mix_two[0] * along + mix_two[1] * along_two), 0.0
    )
    held = jnp.where(lanes < kinds, router, 0.0)
    grad_small = held * (grad_router - jnp.sum(held * grad_router, axis=1, keepdims=True))
    grad_prior_ref[...] = split_dot(grad_small, prior_w_ref[...])[:, :kinds]
    grad_logits = grad_small

    def mixed_back(weight, mix, other, k):
        one, two = weight * along, weight * other
        inner = mix[0] * one + mix[1] * two
        return jnp.where(lanes == k, mix[0] * (one - inner), 0.0) + jnp.where(
            lanes == k + 1, mix[1] * (two - inner), 0.0
        )

    grad_mixlog = mixed_back(weight_first, mix_one, along_one, kinds) + mixed_back(
        weight_second, mix_two, along_two, kinds + 2
    )
    grad_small = grad_logits + grad_mixlog
    share = weight_copy + weight_first * mix_one[0] + weight_second * mix_two[0]
    grad_normed = (
        back[:, :width]
        + share * grad_out
        + split_dot(grad_small, small_t_ref[...])
    )
    through = grad_normed * gain_ref[...]
    inner = jnp.mean(through * hidden, axis=1, keepdims=True)
    grad_hidden = grad_out + scale * through - (scale * scale * scale * inner) * hidden
    grad_hidden_ref[...] = grad_hidden
    grad_low_ref[...] = grad_hidden.astype(BF16)
    vector_first, vector_second = weight_first * mix_one[1], weight_second * mix_two[1]
    partial_ref[...] = valid * (
        hidden + share * normed + vector_first * vector_one + vector_second * vector_two
    )

    @pl.when(step == 0)
    def _():
        sums_ref[...] = jnp.zeros_like(sums_ref)

    vectors = jnp.where(lanes == kinds + 5, vector_first, 0.0) + jnp.where(
        lanes == kinds + 6, vector_second, 0.0
    )
    low = normed.astype(BF16)
    total = turned_dot(grad_small, low) + turned_dot(vectors, grad_out.astype(BF16))
    sums_ref[: kinds + 8, :] += total[: kinds + 8, :]
    sums_ref[kinds + 4 : kinds + 5, :] += jnp.sum(grad_normed * unit, axis=0, keepdims=True)
    prior = split_dot(prior_ref[...].T, grad_logits)
    sums_ref[pl.ds(kinds + 8, kinds), : lanes.shape[1]] += prior


def router_back(kinds, experts, scalars, near, got, far, hidden, router, routes, cotangent, prior,
                gain, small, small_t, vector, prior_w):
    rows, width = hidden.shape
    block = rows // 2
    lanes = router.shape[1]

    def whole(shape):
        return pl.BlockSpec(shape, lambda i, _: (0,) * len(shape))

    def part(columns):
        return pl.BlockSpec((block, columns), lambda i, _: (i, 0))

    def mine(columns):
        return pl.BlockSpec((block, columns), lambda i, scalars: (scalars[1] * 2 + i, 0))

    return pl.pallas_call(
        functools.partial(router_back_kernel, kinds, experts),
        grid_spec=pltpu.PrefetchScalarGridSpec(
            num_scalar_prefetch=1,
            grid=(2,),
            in_specs=[
                pl.BlockSpec((1, block, width + lanes), lambda i, _: (0, i, 0)),
                pl.BlockSpec((1, block, width + lanes), lambda i, _: (0, i, 0)),
                part(width + lanes),
                part(width),
                part(lanes),
                mine(2),
                part(width),
                mine(kinds),
                whole(gain.shape),
                whole(small.shape),
                whole(small_t.shape),
                whole(vector.shape),
                whole(prior_w.shape),
            ],
            out_specs=[
                part(width),
                part(width),
                part(width),
                part(kinds),
                whole((32, width)),
            ],
        ),
        out_shape=[
            jax.ShapeDtypeStruct((rows, width), F32),
            jax.ShapeDtypeStruct((rows, width), BF16),
            jax.ShapeDtypeStruct((rows, width), F32),
            jax.ShapeDtypeStruct((rows, kinds), F32),
            jax.ShapeDtypeStruct((32, width), F32),
        ],
        compiler_params=pltpu.CompilerParams(vmem_limit_bytes=48 * 2**20),
        cost_estimate=cost_of(8),
        name="router_back",
    )(scalars, near, got, far, hidden, router, routes, cotangent, prior, gain, small, small_t,
      vector, prior_w)


def two_parts(value):
    high = lax.reduce_precision(value, 8, 7)
    return jnp.concatenate([high, value - high], axis=-1).astype(BF16)


def everywhere(value, axes, count):
    copies = jnp.broadcast_to(value[None], (count, *value.shape))
    return lax.all_to_all(copies, axes, 0, 0, tiled=True)


def flip(value, axis, size, bit):
    return lax.ppermute(value, axis, [(i, i ^ bit) for i in range(size)])


def by_halves(value):
    if value.shape[0] == 2:
        return value
    rows, units = value.shape[-2:]
    middle_axes = tuple(range(2, value.ndim - 2))
    turned = value.transpose(*middle_axes, 0, 1, value.ndim - 2, value.ndim - 1)
    turned = turned.reshape(*turned.shape[:-4], 2, LOW, value.shape[0] * rows // 2, units)
    axes = turned.ndim
    return turned.transpose(axes - 4, axes - 3, *range(axes - 4), axes - 2, axes - 1)


def scatter_high(value, many):
    if many != 2:
        rows, units = value.shape[-2:]
        middle_axes = tuple(range(2, value.ndim - 2))
        turned = value.transpose(*middle_axes, 0, 1, value.ndim - 2, value.ndim - 1)
        turned = turned.reshape(*turned.shape[:-4], many, LOW, 2 * rows // many, units)
        axes = turned.ndim
        value = turned.transpose(axes - 4, axes - 3, *range(axes - 4), axes - 2, axes - 1)
    return lax.psum_scatter(value, "hi", scatter_dimension=0)


def gather_rows(value, later, many):
    if many != 2:
        full = lax.all_gather(value, ("hi", "lo"), axis=0, tiled=True)
        full = full.reshape(2, LOW, -1, full.shape[1])
        return [full[:, i] for i in range(LOW)], later
    far, *later = lax.optimization_barrier((swap(value, "hi"), *later))
    both = jnp.stack([value, far])
    return [both] + [flip(both, "lo", LOW, bit) for bit in range(1, LOW)], tuple(later)


def scatter_rows(near, far, many):
    if many != 2:
        full = jnp.stack([near, far]).astype(F32).reshape(-1, near.shape[2])
        return lax.psum_scatter(full, ("hi", "lo"), scatter_dimension=0, tiled=True)
    both = near.astype(F32) + far.astype(F32)
    total = both[0]
    for bit in range(1, LOW):
        total = total + flip(both[bit].astype(BF16), "lo", LOW, bit).astype(F32)
    return total


def per_device(
    many,
    inputs,
    cotangent,
    lengths,
    routes,
    drop_order,
    prior_logits,
    attn_gain,
    w_query,
    w_key,
    w_value,
    w_out,
    moe_gain,
    w_router,
    w_prior,
    w_const,
    const_vector,
    w_gate,
    w_up,
    w_down,
):
    tok_rows, width = inputs.shape
    group = tok_rows * 4
    kinds = w_router.shape[1]
    experts, shard_rows, shard_units = w_gate.shape
    capacity = 3 * group // 16
    share = capacity // 2
    slots = LOW * share
    local_width = w_query.shape[1]
    heads = local_width // HEAD
    tp_axes = ("y", "c")
    all_axes = ("hi", "lo", "y", "c")
    count = many * LOW * 4
    wide = width + 128
    high = lax.axis_index("hi")
    parity = lax.axis_index("y")
    core = lax.axis_index("c")
    place_in_group = parity * 2 + core
    mine = high * LOW + lax.axis_index("lo") if many == 2 else jnp.zeros_like(high)
    boundary = jnp.cumsum(lengths[0])
    scalars = jnp.concatenate(
        [jnp.stack([mine, place_in_group, parity, core, lax.axis_index("lo")]), boundary[:-1]]
    ).astype(jnp.int32)
    gain_one, gain_two = attn_gain.reshape(1, width), moe_gain.reshape(1, width)

    valid_mine = place_in_group * tok_rows + jnp.arange(tok_rows)[:, None] < boundary[-2]
    valid_mine = valid_mine.astype(F32)

    normed_one = rms_norm(inputs, attn_gain).astype(BF16)
    normed_other = swap(normed_one, "y")
    attn_shard = jnp.concatenate([w_query, w_key, w_value, w_out.T], axis=1)
    up_part = lax.all_to_all(w_up, ("lo", "y"), 0, 0, tiled=True)
    up_part = up_part.reshape(LOW, 2, shard_rows, shard_units)
    down_shard = w_down.transpose(0, 2, 1)
    attn_shards, (w_gate,) = gather_rows(attn_shard, (w_gate,), many)
    gate_far = swap(w_gate, "hi") if many == 2 else w_gate
    router_lanes = jnp.pad(
        jnp.concatenate([w_router, w_router], axis=1), ((0, 0), (0, 128 - 2 * kinds))
    )
    prior_lanes = jnp.pad(
        jnp.concatenate([w_prior, w_prior], axis=1), ((0, 0), (0, 128 - 2 * kinds))
    )
    const_flat = w_const.transpose(1, 0, 2).reshape(width, 4)
    small = jnp.pad(
        jnp.concatenate([w_router, const_flat], axis=1), ((0, 0), (0, 128 - kinds - 4))
    )
    small_t = small.T
    prior_back = jnp.pad(w_prior.T, ((0, 128 - kinds), (0, 128 - kinds)))
    (
        attn_shards[0], scalars, router_lanes, prior_lanes, small, small_t, prior_back, prior_logits
    ) = lax.optimization_barrier(
        (attn_shards[0], scalars, router_lanes, prior_lanes, small, small_t, prior_back, prior_logits)
    )
    ids_rows, ids_cols = slots_of(scalars, routes, drop_order, experts, capacity)
    grad_out_low = (cotangent * valid_mine).astype(BF16)
    (
        normed_other, attn_shards, ids_rows, down_shard, grad_out_low, up_part, gate_far
    ) = lax.optimization_barrier(
        (normed_other, attn_shards, ids_rows, down_shard, grad_out_low, up_part, gate_far)
    )
    grad_out_other = swap(grad_out_low, "y")
    down_part = lax.all_to_all(down_shard, ("lo", "y"), 0, 0, tiled=True)
    down_part = down_part.reshape(LOW, 2, shard_rows, shard_units)
    if many == 2:
        up_far = [swap(up_part[:2], "hi"), swap(up_part[2:], "hi")]
    else:
        up_all = by_halves(lax.all_gather(up_part, "hi"))
        up_part, up_far = up_all[0], [up_all[1, :2], up_all[1, 2:]]
    out_mine = jnp.stack([item[:, :, 3 * local_width :] for item in attn_shards])
    out_other = swap(out_mine, "y")
    normed_pieces = [normed_one, swap(normed_one, "c"), normed_other, swap(normed_other, "c")]
    mixed, lse, qkv, qkv_full = attend(normed_pieces, attn_shards, scalars, heads)
    mixed, out_other, out_mine, up_far[0], down_part, grad_out_other = lax.optimization_barrier(
        (mixed, out_other, out_mine, up_far[0], down_part, grad_out_other)
    )
    if many == 2:
        high_place = high
        down_far = [swap(down_part[:3], "hi"), swap(down_part[3:], "hi")]
        gate_both = jnp.where(
            high == 0, jnp.stack([w_gate, gate_far], axis=1), jnp.stack([gate_far, w_gate], axis=1)
        )
    else:
        high_place = jnp.zeros_like(high)
        down_all = by_halves(lax.all_gather(down_part, "hi"))
        down_part, down_far = down_all[0], [down_all[1, :3], down_all[1, 3:]]
        gate_both = lax.all_gather(w_gate, "hi", axis=1)
    out_pieces = [out_mine, swap(out_mine, "c"), out_other, swap(out_other, "c")]

    mixed_mine = lax.all_to_all(mixed, tp_axes, 0, 0, tiled=True)
    grad_out_pieces = [
        grad_out_low, swap(grad_out_low, "c"), grad_out_other, swap(grad_out_other, "c"),
    ]
    grad_out_slots = pick(ids_rows, grad_out_pieces, slots)
    mixed_mine, grad_out_slots, up_far[1], gate_both = lax.optimization_barrier(
        (mixed_mine, grad_out_slots, up_far[1], gate_both)
    )

    hidden, sent_two, router = middle(
        kinds, scalars, mixed_mine, out_pieces, inputs, gain_two, router_lanes, prior_logits, prior_lanes
    )

    gate_part = lax.all_to_all(gate_both, ("lo", "y"), 0, 0, tiled=True)
    gate_part = gate_part.reshape(LOW, 2, many, shard_rows, shard_units)
    if many != 2:
        gate_part = by_halves(gate_part.transpose(2, 0, 1, 3, 4)).transpose(1, 2, 0, 3, 4)
    other_two, grad_taken, gate_part, down_far[0] = lax.optimization_barrier(
        (swap(sent_two, "y"), to_experts(grad_out_slots), gate_part, down_far[0])
    )
    pieces_two = [sent_two, swap(sent_two, "c"), other_two, swap(other_two, "c")]

    grad_taken = [*grad_taken, swap(jnp.concatenate(grad_taken), "c")]
    sent_slots = pick(ids_rows, pieces_two, slots)
    sent_slots, qkv_full = lax.optimization_barrier((sent_slots, qkv_full))
    taken = to_experts(sent_slots)
    taken += [swap(item, "c") for item in taken]
    qkv_pieces = gather_pieces(qkv_full)
    taken, qkv_pieces, down_far[1] = lax.optimization_barrier((taken, qkv_pieces, down_far[1]))

    expert = lax.axis_index("lo") * 2 + parity
    back_own, back_send, feed_own, feed_send, grads_out = expert_pass(
        kinds, jnp.stack([expert, high_place]).astype(jnp.int32), taken, grad_taken,
        gate_part, [up_part, down_part], up_far + down_far,
    )

    weight_sum = scatter_high(grads_out, many)
    back_taken = to_experts(back_sum(kinds, back_own, swap(back_send, "c")))
    feed_core = swap(feed_send, "c")
    back_taken, feed_core = lax.optimization_barrier((back_taken, feed_core))

    back_near, back_sent = spread(ids_cols, back_taken, tok_rows)
    back_got, back_other = add_core(back_near, back_sent)
    back_other, feed_core = lax.optimization_barrier((back_other, feed_core))
    back_far, feed_blocks = lax.optimization_barrier(
        (swap(back_other, "y"), feed_sum(feed_own, feed_core))
    )

    grad_hidden, grad_low, partial, grad_prior, sums = router_back(
        kinds, experts, scalars, back_near, back_got, back_far, hidden, router, routes, cotangent,
        prior_logits, gain_two, small, small_t, const_vector, prior_back,
    )
    feed_taken = to_experts(feed_blocks)
    grad_mixed = to_heads(mixed_back(scalars, grad_low, out_pieces))
    grad_mixed, grad_low = lax.optimization_barrier((grad_mixed, grad_low))
    low_other = swap(grad_low, "y")
    share_sums = lax.all_to_all(sums.reshape(count, 32 * width // count), all_axes, 0, 0, tiled=True)
    grad_qkv = attend_back(scalars, qkv, lse, grad_mixed, heads).reshape(
        4, 3 * local_width, tok_rows
    )
    grad_qkv, feed_taken, weight_sum, low_other = lax.optimization_barrier(
        (grad_qkv, feed_taken, weight_sum, low_other)
    )
    grad_attn_pieces = [grad_low, swap(grad_low, "c"), low_other, swap(low_other, "c")]

    weight_own = lax.all_to_all(
        weight_sum.reshape(2 * LOW, 3, shard_rows, shard_units), ("lo", "y"), 0, 0, tiled=True
    )
    grad_qkv_mine = to_heads(grad_qkv)
    attn_near, attn_far = attn_grads(grad_qkv, mixed, normed_pieces, grad_attn_pieces, scalars)
    if many == 2:
        attn_far = swap(attn_far, "hi")
    feed_near, feed_sent = spread(ids_cols, feed_taken, tok_rows)
    feed_got, feed_other = add_core(feed_near, feed_sent)
    (
        grad_qkv_mine, share_sums, attn_near, attn_far, feed_near, feed_got, feed_other
    ) = lax.optimization_barrier(
        (grad_qkv_mine, share_sums, attn_near, attn_far, feed_near, feed_got, feed_other)
    )
    feed_far = swap(feed_other, "y")
    share_sums = jnp.sum(share_sums, axis=0)
    grad_inputs, gain_part = inputs_back(
        grad_qkv_mine, qkv_pieces, inputs, gain_one, grad_hidden
    )
    output = partial + valid_mine * (
        feed_near[0] + feed_got[0].astype(F32) + feed_far.astype(F32)
    )
    grad_attn_own = scatter_rows(attn_near, attn_far, many)
    last = jnp.concatenate([jnp.sum(gain_part, axis=0).reshape(-1), share_sums])
    last, weight_own = lax.optimization_barrier((last, weight_own))
    last = everywhere(last, all_axes, count)
    last, grad_attn_own = lax.optimization_barrier((last, grad_attn_own))
    grad_gain = jnp.sum(last[:, :width], axis=0)
    total = last[:, width:].reshape(32, width)
    return (
        output,
        grad_inputs,
        grad_prior,
        grad_gain,
        grad_attn_own[:, :local_width],
        grad_attn_own[:, local_width : 2 * local_width],
        grad_attn_own[:, 2 * local_width : 3 * local_width],
        grad_attn_own[:, 3 * local_width :].T,
        total[kinds + 4],
        total[:kinds].T,
        total[kinds + 8 : 2 * kinds + 8, :kinds],
        total[kinds : kinds + 4].reshape(2, 2, width).transpose(0, 2, 1),
        total[kinds + 5 : kinds + 7],
        weight_own[:, 0].astype(F32),
        weight_own[:, 1].astype(F32),
        weight_own[:, 2].transpose(0, 2, 1).astype(F32),
    )


def solution(mesh):
    many = mesh.shape["fsdp"] // LOW
    fine = Mesh(mesh.devices.reshape(many, LOW, 2, 2), ("hi", "lo", "y", "c"))
    fsdp, tp = ("hi", "lo"), ("y", "c")
    every = fsdp + tp
    return jax.shard_map(
        functools.partial(per_device, many),
        mesh=fine,
        in_specs=(
            P(every, None),
            P(every, None),
            P(fsdp, None),
            P(fsdp, None),
            P(fsdp, None),
            P(fsdp, None),
            P(),
            P(fsdp, tp),
            P(fsdp, tp),
            P(fsdp, tp),
            P(tp, fsdp),
            P(),
            P(),
            P(),
            P(),
            P(),
            P(None, fsdp, tp),
            P(None, fsdp, tp),
            P(None, tp, fsdp),
        ),
        out_specs=(
            P(every, None),
            P(every, None),
            P(every, None),
            P(),
            P(fsdp, tp),
            P(fsdp, tp),
            P(fsdp, tp),
            P(tp, fsdp),
            P(),
            P(),
            P(),
            P(),
            P(),
            P(None, fsdp, tp),
            P(None, fsdp, tp),
            P(None, tp, fsdp),
        ),
        check_vma=False,
    )
```

```python
import functools

import jax
import jax.numpy as jnp
from jax import lax
from jax.experimental import pallas as pl
from jax.experimental.pallas import tpu as pltpu
from jax.sharding import Mesh
from jax.sharding import PartitionSpec as P

HEAD = 64
MAXLEN = 768
LOW = 4
SHARDS = 8
LOW_PLACE = 4
BOUNDS = 5
EPSILON = 1e-06
PRECISE = lax.Precision.HIGHEST
NEGATIVE = -1e30
F32 = jnp.float32
BF16 = jnp.bfloat16


def rms_norm(values, gain):
    return values * lax.rsqrt(jnp.mean(values * values, axis=-1, keepdims=True) + EPSILON) * gain


def swap(value, axis):
    return lax.ppermute(value, axis, [(0, 1), (1, 0)])


def gather_pieces(value):
    other = swap(value, "y")
    return [value, swap(value, "c"), other, swap(other, "c")]


def natural(pieces, index):
    ordered = []
    for j in range(4):
        item = pieces[j]
        for t in range(1, 4):
            item = jnp.where(index == t, pieces[j ^ t], item)
        ordered.append(item)
    return jnp.stack(ordered)


def add_core(near, sent):
    got = swap(sent, "c")
    return got, (near[1] + got[1].astype(F32)).astype(BF16)


def cost_of(microseconds):
    return pl.CostEstimate(
        flops=int(microseconds * 1.15e9), transcendentals=0, bytes_accessed=2**16
    )


def start_of(row, scalars):
    start_row = jnp.zeros_like(row)
    for k in range(BOUNDS, scalars.shape[0]):
        start_row = jnp.where(row >= scalars[k], scalars[k], start_row)
    return start_row


def for_window(first, block, pad, scalars, body):
    needed = (first - start_of(first, scalars) + block - 1) // block
    most = pad // block
    for blocks in range(most):
        pl.when(needed == blocks)(functools.partial(body, (blocks + 1) * block))
    pl.when(needed >= most)(functools.partial(body, pad + block))


def scores_mask(first_key, first_query, window, block, scalars):
    row = first_query + lax.broadcasted_iota(jnp.int32, (1, block), 1)
    start_row = start_of(row, scalars)
    key_places = first_key + lax.broadcasted_iota(jnp.int32, (window, block), 0)
    query_places = first_query + lax.broadcasted_iota(jnp.int32, (window, block), 1)
    return (key_places >= start_row) & (key_places <= query_places)


def attend_kernel(block, pad, scalars, *refs):
    pieces, refs = refs[:4], refs[4:]
    shards, refs = refs[:LOW], refs[LOW:]
    out_ref, lse_ref, qkv_ref, weight_ref, key_rows, value_pad, full = refs
    group = qkv_ref.shape[1]
    quarter = group // 4
    inner = qkv_ref.shape[0] // 3
    head = pl.program_id(0)

    @pl.when(head == 0)
    def _():
        rows = shards[0].shape[1]
        for r in range(SHARDS):
            place = pl.multiple_of((scalars[0] ^ r) * rows, rows)
            full[pl.ds(place, rows), :] = shards[r % LOW][r // LOW]
        turned = full[:, : 3 * inner].T
        weight_ref[...] = turned
        for r in range(4):
            place = pl.multiple_of((scalars[1] ^ r) * quarter, quarter)
            qkv_ref[:, pl.ds(place, quarter)] = lax.dot_general(
                turned, pieces[r][...], (((1,), (1,)), ((), ())), preferred_element_type=F32
            ).astype(BF16)

    first_row = pl.multiple_of(head * HEAD, HEAD)
    key_rows[pl.ds(0, pad), :] = jnp.zeros((pad, HEAD), BF16)
    value_pad[:, pl.ds(0, pad)] = jnp.zeros((HEAD, pad), BF16)
    key_rows[pl.ds(pad, group), :] = qkv_ref[pl.ds(inner + first_row, HEAD), :].T
    value_pad[:, pl.ds(pad, group)] = qkv_ref[pl.ds(2 * inner + first_row, HEAD), :]

    def one(i, carry):
        first = pl.multiple_of(i * block, block)

        def body(window):
            begin = pl.multiple_of(first + pad + block - window, block)
            scores = jnp.dot(
                key_rows[pl.ds(begin, window), :],
                qkv_ref[pl.ds(first_row, HEAD), pl.ds(first, block)],
                preferred_element_type=F32,
            )
            allowed = scores_mask(begin - pad, first, window, block, scalars)
            scores = jnp.where(allowed, scores * 0.125, NEGATIVE)
            highest = jnp.max(scores, axis=0, keepdims=True)
            weights = jnp.exp(scores - highest)
            total = jnp.sum(weights, axis=0, keepdims=True)
            mixed = jnp.dot(
                value_pad[:, pl.ds(begin, window)],
                weights.astype(BF16),
                preferred_element_type=F32,
            )
            mixed = (mixed / total).astype(BF16)
            column = pl.multiple_of(first % quarter, block)
            out_ref[first // quarter, :, pl.ds(column, block)] = mixed
            lse_ref[0, :, pl.ds(first, block)] = highest + jnp.log(total)

        for_window(first, block, pad, scalars, body)
        return carry

    lax.fori_loop(0, group // block, one, 0)


def attend(pieces, shards, scalars, heads):
    rows, width = pieces[0].shape
    group = 4 * rows
    inner = heads * HEAD
    block = 256

    def whole(shape):
        return pl.BlockSpec(
            shape, lambda i, _: (0,) * len(shape), pipeline_mode=pl.Buffered(1)
        )

    return pl.pallas_call(
        functools.partial(attend_kernel, block, MAXLEN),
        grid_spec=pltpu.PrefetchScalarGridSpec(
            num_scalar_prefetch=1,
            grid=(heads,),
            in_specs=[
                *[whole((rows, width)) for _ in range(4)],
                *[whole(shards[0].shape) for _ in range(LOW)],
            ],
            out_specs=[
                pl.BlockSpec((4, HEAD, rows), lambda h, _: (0, h, 0)),
                pl.BlockSpec((1, 1, group), lambda h, _: (h, 0, 0)),
                whole((3 * inner, group)),
                whole((3 * inner, width)),
            ],
            scratch_shapes=[
                pltpu.VMEM((MAXLEN + group, HEAD), BF16),
                pltpu.VMEM((HEAD, MAXLEN + group), BF16),
                pltpu.VMEM((width, 4 * inner), BF16),
            ],
        ),
        out_shape=[
            jax.ShapeDtypeStruct((4, inner, rows), BF16),
            jax.ShapeDtypeStruct((heads, 1, group), F32),
            jax.ShapeDtypeStruct((3 * inner, group), BF16),
            jax.ShapeDtypeStruct((3 * inner, width), BF16),
        ],
        compiler_params=pltpu.CompilerParams(vmem_limit_bytes=48 * 2**20),
        cost_estimate=cost_of(24),
        name="attend",
    )(scalars, *pieces, *shards)


def attn_grads_kernel(scalars, *refs):
    grad_qkv, mixed, refs = refs[0], refs[1], refs[2:]
    tokens, grads, refs = refs[:4], refs[4:8], refs[8:]
    outs, (total,) = refs[:2], refs[2:]
    inner3 = grad_qkv.shape[1]
    first, second = 0.0, 0.0
    for r in range(4):
        j = scalars[1] ^ r
        first += jnp.dot(grad_qkv[r], tokens[r][...], preferred_element_type=F32)
        second += jnp.dot(mixed[j], grads[r][...], preferred_element_type=F32)
    total[:, :inner3] = first.T.astype(BF16)
    total[:, inner3:] = second.T.astype(BF16)
    rows = outs[0].shape[1]
    for r in range(SHARDS):
        place = pl.multiple_of((scalars[0] ^ r) * rows, rows)
        outs[r // LOW][r % LOW] = total[pl.ds(place, rows), :]


def attn_grads(grad_qkv, mixed, tokens, grads, scalars):
    width = tokens[0].shape[1]
    columns = grad_qkv.shape[1] + mixed.shape[1]
    rows = width // SHARDS
    whole = pl.BlockSpec(memory_space=pltpu.VMEM)
    return pl.pallas_call(
        attn_grads_kernel,
        in_specs=[pl.BlockSpec(memory_space=pltpu.SMEM)] + [whole] * 10,
        out_specs=[whole] * 2,
        out_shape=[jax.ShapeDtypeStruct((LOW, rows, columns), BF16)] * 2,
        scratch_shapes=[pltpu.VMEM((width, columns), BF16)],
        compiler_params=pltpu.CompilerParams(vmem_limit_bytes=48 * 2**20),
        cost_estimate=cost_of(30),
        name="attn_grads",
    )(scalars, grad_qkv, mixed, *tokens, *grads)


def attend_back_kernel(block, pad, scalars, qkv_ref, lse_ref, *refs):
    pieces, refs = refs[:4], refs[4:]
    out_ref, grad_mixed, key_rows, value_rows, key_pad, grad_key, grad_value = refs
    group = qkv_ref.shape[1]
    inner_rows = qkv_ref.shape[0] // 3
    quarter = group // 4
    contract_last = (((1,), (1,)), ((), ()))
    head = pl.program_id(0)

    @pl.when(head == 0)
    def _():
        for r in range(4):
            place = pl.multiple_of((scalars[1] ^ r) * quarter, quarter)
            grad_mixed[:, pl.ds(place, quarter)] = pieces[r][...]

    first_row = pl.multiple_of(head * HEAD, HEAD)
    keys = qkv_ref[pl.ds(inner_rows + first_row, HEAD), :]
    key_rows[pl.ds(0, pad), :] = jnp.zeros((pad, HEAD), BF16)
    value_rows[pl.ds(0, pad), :] = jnp.zeros((pad, HEAD), BF16)
    key_pad[:, pl.ds(0, pad)] = jnp.zeros((HEAD, pad), BF16)
    key_rows[pl.ds(pad, group), :] = keys.T
    value_rows[pl.ds(pad, group), :] = qkv_ref[pl.ds(2 * inner_rows + first_row, HEAD), :].T
    key_pad[:, pl.ds(pad, group)] = keys
    grad_key[...] = jnp.zeros_like(grad_key)
    grad_value[...] = jnp.zeros_like(grad_value)

    def one(i, carry):
        first = pl.multiple_of(i * block, block)

        def body(window):
            begin = pl.multiple_of(first + pad + block - window, block)
            query = qkv_ref[pl.ds(first_row, HEAD), pl.ds(first, block)]
            grad = grad_mixed[pl.ds(first_row, HEAD), pl.ds(first, block)]
            scores = jnp.dot(key_rows[pl.ds(begin, window), :], query, preferred_element_type=F32)
            allowed = scores_mask(begin - pad, first, window, block, scalars)
            exponent = scores * 0.125 - lse_ref[0, :, pl.ds(first, block)]
            probs = jnp.exp(jnp.where(allowed, exponent, NEGATIVE))
            grad_probs = jnp.dot(
                value_rows[pl.ds(begin, window), :], grad, preferred_element_type=F32
            )
            inner = jnp.sum(probs * grad_probs, axis=0, keepdims=True)
            raw = (0.125 * (probs * (grad_probs - inner))).astype(BF16)
            grad_query = jnp.dot(
                key_pad[:, pl.ds(begin, window)], raw, preferred_element_type=F32
            )
            column = pl.multiple_of(first % quarter, block)
            piece = (first // quarter) ^ scalars[1]
            out_ref[piece, 0, :, pl.ds(column, block)] = grad_query.astype(BF16)
            grad_value[:, pl.ds(begin, window)] += lax.dot_general(
                grad, probs.astype(BF16), contract_last, preferred_element_type=F32
            )
            grad_key[:, pl.ds(begin, window)] += lax.dot_general(
                query, raw, contract_last, preferred_element_type=F32
            )

        for_window(first, block, pad, scalars, body)
        return carry

    lax.fori_loop(0, group // block, one, 0)
    for j in range(4):
        piece = scalars[1] ^ j
        out_ref[piece, 1] = grad_key[:, pl.ds(pad + j * quarter, quarter)].astype(BF16)
        out_ref[piece, 2] = grad_value[:, pl.ds(pad + j * quarter, quarter)].astype(BF16)


def attend_back(scalars, qkv, lse, pieces, heads):
    group = qkv.shape[1]
    block = 256

    def whole(shape):
        return pl.BlockSpec(
            shape, lambda i, _: (0,) * len(shape), pipeline_mode=pl.Buffered(1)
        )

    return pl.pallas_call(
        functools.partial(attend_back_kernel, block, MAXLEN),
        grid_spec=pltpu.PrefetchScalarGridSpec(
            num_scalar_prefetch=1,
            grid=(heads,),
            in_specs=[
                whole(qkv.shape),
                pl.BlockSpec((1, 1, group), lambda h, _: (h, 0, 0)),
                *[whole(item.shape) for item in pieces],
            ],
            out_specs=pl.BlockSpec((4, 3, HEAD, group // 4), lambda h, _: (0, 0, h, 0)),
            scratch_shapes=[
                pltpu.VMEM((heads * HEAD, group), BF16),
                pltpu.VMEM((MAXLEN + group, HEAD), BF16),
                pltpu.VMEM((MAXLEN + group, HEAD), BF16),
                pltpu.VMEM((HEAD, MAXLEN + group), BF16),
                pltpu.VMEM((HEAD, MAXLEN + group), F32),
                pltpu.VMEM((HEAD, MAXLEN + group), F32),
            ],
        ),
        out_shape=jax.ShapeDtypeStruct((4, 3, heads * HEAD, group // 4), BF16),
        compiler_params=pltpu.CompilerParams(vmem_limit_bytes=48 * 2**20),
        cost_estimate=cost_of(34),
        name="attend_back",
    )(scalars, qkv, lse, *pieces)


def mixed_back_kernel(scalars, grad_ref, p0, p1, p2, p3, *refs):
    outs, weight = refs[:4], refs[4]
    rows = p0.shape[2]
    for r, shards in enumerate((p0, p1, p2, p3)):
        for k in range(SHARDS):
            place = pl.multiple_of((scalars[0] ^ k) * rows, rows)
            weight[pl.ds(place, rows), :] = shards[k % LOW, k // LOW]
        outs[r][...] = lax.dot_general(
            weight[...].T, grad_ref[...], (((1,), (1,)), ((), ())), preferred_element_type=F32
        ).astype(BF16)


def mixed_back(scalars, grad, weights):
    rows, width = grad.shape
    inner = weights[0].shape[3]

    def whole(shape):
        return pl.BlockSpec(shape, lambda i, _: (0,) * len(shape))

    return pl.pallas_call(
        mixed_back_kernel,
        grid_spec=pltpu.PrefetchScalarGridSpec(
            num_scalar_prefetch=1,
            grid=(1,),
            in_specs=[whole(grad.shape), *[whole(item.shape) for item in weights]],
            out_specs=[whole((inner, rows)) for _ in range(4)],
            scratch_shapes=[pltpu.VMEM((width, inner), BF16)],
        ),
        out_shape=[jax.ShapeDtypeStruct((inner, rows), BF16) for _ in range(4)],
        compiler_params=pltpu.CompilerParams(vmem_limit_bytes=32 * 2**20),
        cost_estimate=cost_of(4),
        name="mixed_back",
    )(scalars, grad, *weights)


def inputs_back_kernel(g0, g1, g2, g3, p0, p1, p2, p3, x_ref, gain_ref, hidden_ref, out_ref, sum_ref):
    total = 0.0
    for grad, weight in zip((g0, g1, g2, g3), (p0, p1, p2, p3)):
        total += jnp.dot(grad[...].T, weight[...], preferred_element_type=F32)
    x = x_ref[...]
    scale = lax.rsqrt(jnp.mean(x * x, axis=1, keepdims=True) + EPSILON)
    through = total * gain_ref[...]
    inner = jnp.mean(through * x, axis=1, keepdims=True)
    out_ref[...] = hidden_ref[...] + scale * through - (scale * scale * scale * inner) * x
    sum_ref[0] = jnp.sum(total * x * scale, axis=0, keepdims=True)


def inputs_back(grads, weights, x, gain, grad_hidden):
    rows, width = x.shape
    block = rows // 2

    def whole(shape):
        return pl.BlockSpec(shape, lambda i: (0,) * len(shape), pipeline_mode=pl.Buffered(1))

    part = pl.BlockSpec((block, width), lambda i: (i, 0))
    return pl.pallas_call(
        inputs_back_kernel,
        grid=(2,),
        in_specs=[
            *[pl.BlockSpec((item.shape[0], block), lambda i: (0, i)) for item in grads],
            *[whole(item.shape) for item in weights],
            part,
            whole(gain.shape),
            part,
        ],
        out_specs=[part, pl.BlockSpec((1, 1, width), lambda i: (i, 0, 0))],
        out_shape=[
            jax.ShapeDtypeStruct(x.shape, F32),
            jax.ShapeDtypeStruct((2, 1, width), F32),
        ],
        compiler_params=pltpu.CompilerParams(vmem_limit_bytes=48 * 2**20),
        cost_estimate=cost_of(6),
        name="inputs_back",
    )(*grads, *weights, x, gain, grad_hidden)


def expert_kernel(
    kinds, scalars, w_gate, *refs
):
    near_pieces, far_pieces, refs = refs[:2], refs[2:6], refs[6:]
    x_blocks, g_blocks, g_core = refs[: 2 * LOW], refs[2 * LOW : 3 * LOW], refs[3 * LOW]
    refs = refs[3 * LOW + 1 :]
    back_own, back_send, feed_own, feed_send, grads_out, *refs = refs
    x_all, g_all, x_t, g_t, weights, hidden, acc_feed, acc_back, scales, plain = refs
    slots, width = feed_own.shape
    block = slots // LOW
    half = width // 2
    step = pl.program_id(0)
    contract_last = (((1,), (1,)), ((), ()))
    units = weights.shape[2]

    def weight_column(x_ref):
        extra = x_ref[:, width:].astype(F32)
        lanes = lax.broadcasted_iota(jnp.int32, extra.shape, 1)
        named = (lanes == scalars[0]) | (lanes == scalars[0] + kinds)
        return jnp.sum(jnp.where(named, extra, 0.0), axis=1, keepdims=True)

    @pl.when(step == 0)
    def _():
        for i in range(2 * LOW):
            rows = pl.ds(i * block, block)
            scale = weight_column(x_blocks[i])
            scales[rows, :] = jnp.broadcast_to(scale, (block, 128))
            if i < LOW:
                plain[rows, :] = g_blocks[i][...]
            else:
                plain[rows, :] = g_core[pl.ds((i - LOW) * block, block), :]
            x_all[rows, :] = x_blocks[i][:, :width]
            g_all[rows, :] = (plain[rows, :].astype(F32) * scale).astype(BF16)
        x_t[...] = x_all[...].T
        g_t[...] = g_all[...].T
        acc_feed[...] = jnp.zeros_like(acc_feed)
        acc_back[...] = jnp.zeros_like(acc_back)

    for i in range(2):
        rows = pl.ds(i * half, half)
        weights[0, rows, :] = w_gate[:, 0, i].reshape(half, units)
    near = pl.multiple_of(scalars[1] * half, half)
    for k in range(2):
        weights[k + 1, pl.ds(near, half), :] = near_pieces[k][:, 0].reshape(half, units)
        place = (1 - scalars[1]) * half
        for piece in far_pieces[2 * k : 2 * k + 2]:
            rows = piece.shape[0] * half // LOW
            weights[k + 1, pl.ds(pl.multiple_of(place, half // LOW), rows), :] = piece[
                :, 0
            ].reshape(rows, units)
            place += rows

    for part in range(2):
        rows = pl.ds(part * slots, slots)
        x = x_all[rows, :]
        gate = jnp.dot(x, weights[0], preferred_element_type=F32)
        up = jnp.dot(x, weights[1], preferred_element_type=F32)
        grad_act = jnp.dot(g_all[rows, :], weights[2], preferred_element_type=F32)
        sig = jax.nn.sigmoid(gate)
        silu = gate * sig
        active = (silu * up).astype(BF16)
        grad_gate = (grad_act * up * (sig * (1.0 + gate * (1.0 - sig)))).astype(BF16)
        grad_up = (grad_act * silu).astype(BF16)
        hidden[0, rows, :] = grad_gate
        hidden[1, rows, :] = grad_up
        hidden[2, rows, :] = active
        acc_feed[rows, :] += lax.dot_general(
            active, weights[2], contract_last, preferred_element_type=F32
        )
        acc_back[rows, :] += lax.dot_general(
            grad_gate, weights[0], contract_last, preferred_element_type=F32
        ) + lax.dot_general(grad_up, weights[1], contract_last, preferred_element_type=F32)

    for k in range(3):
        left = (g_t if k == 2 else x_t)
        grad = jnp.dot(left[...], hidden[k], preferred_element_type=F32).astype(BF16)
        for i in range(2):
            part = grad[i * half : (i + 1) * half].reshape(LOW, -1, units)
            grads_out[i, :, 0, k] = part

    @pl.when(step == pl.num_programs(0) - 1)
    def _():
        for part in range(2):
            rows = pl.ds(part * slots, slots)
            feed = acc_feed[rows, :]
            inner = jnp.sum(feed * plain[rows, :].astype(F32), axis=1, keepdims=True)
            feed = feed * scales[rows, 0:1]
            lanes = lax.broadcasted_iota(jnp.int32, (slots, 128), 1)
            if part == 0:
                back_own[:, :width] = acc_back[rows, :]
                back_own[:, width:] = jnp.where(lanes == scalars[0], inner, 0.0)
                feed_own[...] = feed
            else:
                high = inner.astype(BF16).astype(F32)
                extra = jnp.where(lanes == scalars[0], high, 0.0)
                extra = jnp.where(lanes == scalars[0] + kinds, inner - high, extra)
                back_send[:, :width] = acc_back[rows, :].astype(BF16)
                back_send[:, width:] = extra.astype(BF16)
                feed_send[...] = feed.astype(BF16)


def expert_pass(kinds, scalars, x_blocks, g_blocks, w_gate, w_near, w_far):
    block, width = g_blocks[0].shape
    slots = LOW * block
    low, parities, _, shard_rows, shard_units = w_gate.shape
    units = 512
    steps = shard_units // units

    def whole(shape):
        return pl.BlockSpec(
            shape, lambda i, _: (0,) * len(shape), pipeline_mode=pl.Buffered(1)
        )

    grads_spec = pl.BlockSpec(
        (2, low, 1, 3, shard_rows, units), lambda i, _: (0, 0, i // steps, 0, 0, i % steps)
    )
    gate_spec = pl.BlockSpec(
        (low, 1, 2, shard_rows, units), lambda i, _: (0, i // steps, 0, 0, i % steps)
    )
    def up_spec(count):
        return pl.BlockSpec(
            (count, 1, shard_rows, units), lambda i, _: (0, i // steps, 0, i % steps)
        )

    wide = width + 128
    return pl.pallas_call(
        functools.partial(expert_kernel, kinds),
        grid_spec=pltpu.PrefetchScalarGridSpec(
            num_scalar_prefetch=1,
            grid=(parities * steps,),
            in_specs=[
                gate_spec,
                *[up_spec(item.shape[0]) for item in (*w_near, *w_far)],
                *[whole((block, wide)) for _ in range(2 * LOW)],
                *[whole(item.shape) for item in g_blocks],
            ],
            out_specs=[
                whole((slots, wide)),
                whole((slots, wide)),
                whole((slots, width)),
                whole((slots, width)),
                grads_spec,
            ],
            scratch_shapes=[
                pltpu.VMEM((2 * slots, width), BF16),
                pltpu.VMEM((2 * slots, width), BF16),
                pltpu.VMEM((width, 2 * slots), BF16),
                pltpu.VMEM((width, 2 * slots), BF16),
                pltpu.VMEM((3, width, units), BF16),
                pltpu.VMEM((3, 2 * slots, units), BF16),
                pltpu.VMEM((2 * slots, width), F32),
                pltpu.VMEM((2 * slots, width), F32),
                pltpu.VMEM((2 * slots, 128), F32),
                pltpu.VMEM((2 * slots, width), BF16),
            ],
        ),
        out_shape=[
            jax.ShapeDtypeStruct((slots, wide), F32),
            jax.ShapeDtypeStruct((slots, wide), BF16),
            jax.ShapeDtypeStruct((slots, width), F32),
            jax.ShapeDtypeStruct((slots, width), BF16),
            jax.ShapeDtypeStruct((2, low, parities, 3, shard_rows, shard_units), BF16),
        ],
        compiler_params=pltpu.CompilerParams(vmem_limit_bytes=58 * 2**20),
        cost_estimate=cost_of(35),
        name="expert_pass",
    )(scalars, w_gate, *w_near, *w_far, *x_blocks, *g_blocks)


def pick_kernel(ids_ref, *refs):
    pieces, outs = refs[:4], refs[4:]
    block = outs[0].shape[0]
    rows = pieces[0].shape[0]
    for i, out_ref in enumerate(outs):
        slot = i * block + lax.broadcasted_iota(jnp.int32, (block, rows), 0)
        total = 0.0
        for r in range(4):
            columns = pl.ds(r * rows, rows)
            held = (slot == ids_ref[0:1, columns]) | (slot == ids_ref[1:2, columns])
            held = jnp.where(held, 1.0, 0.0).astype(BF16)
            total += jnp.dot(held, pieces[r][...], preferred_element_type=F32)
        out_ref[...] = total.astype(BF16)


def pick(ids, pieces, slots):
    rows, width = pieces[0].shape
    block = slots // LOW

    def whole(shape):
        return pl.BlockSpec(shape, lambda i: (0, 0))

    return pl.pallas_call(
        pick_kernel,
        grid=(1,),
        in_specs=[whole((8, 4 * rows)), *[whole((rows, width)) for _ in range(4)]],
        out_specs=[whole((block, width)) for _ in range(LOW)],
        out_shape=[jax.ShapeDtypeStruct((block, width), BF16) for _ in range(LOW)],
        compiler_params=pltpu.CompilerParams(vmem_limit_bytes=32 * 2**20),
        cost_estimate=cost_of(5),
        name="pick",
    )(ids, *pieces)


def to_experts(blocks):
    return [blocks[0]] + [flip(blocks[b], "lo", LOW, b) for b in range(1, LOW)]


def to_heads(blocks):
    return [blocks[0]] + [
        lax.ppermute(blocks[r], ("y", "c"), [(i, i ^ r) for i in range(4)]) for r in range(1, 4)
    ]


def back_sum_kernel(kinds, own_ref, core_ref, *outs):
    width = own_ref.shape[1] - 128
    block = outs[0].shape[0]
    for i, out_ref in enumerate(outs):
        rows = pl.ds(i * block, block)
        out_ref[:, :width] = (
            own_ref[rows, :width] + core_ref[rows, :width].astype(F32)
        ).astype(BF16)
        extra = own_ref[rows, width:] + core_ref[rows, width:].astype(F32)
        lanes = lax.broadcasted_iota(jnp.int32, extra.shape, 1)
        high = jnp.where(lanes < kinds, extra, 0.0).astype(BF16).astype(F32)
        low = jnp.where(lanes < kinds, extra - high, 0.0)
        low = pltpu.roll(low, kinds, 1) + jnp.where(lanes >= kinds, extra, 0.0)
        out_ref[:, width:] = (high + low).astype(BF16)


def back_sum(kinds, own, core):
    slots, wide = own.shape
    block = slots // LOW

    def whole(shape):
        return pl.BlockSpec(shape, lambda i: (0, 0))

    return pl.pallas_call(
        functools.partial(back_sum_kernel, kinds),
        grid=(1,),
        in_specs=[whole(own.shape), whole(core.shape)],
        out_specs=[whole((block, wide)) for _ in range(LOW)],
        out_shape=[jax.ShapeDtypeStruct((block, wide), BF16) for _ in range(LOW)],
        compiler_params=pltpu.CompilerParams(vmem_limit_bytes=32 * 2**20),
        cost_estimate=cost_of(3),
        name="back_sum",
    )(own, core)


def feed_sum_kernel(own_ref, core_ref, *outs):
    block = outs[0].shape[0]
    for i, out_ref in enumerate(outs):
        rows = pl.ds(i * block, block)
        out_ref[...] = (own_ref[rows, :] + core_ref[rows, :].astype(F32)).astype(BF16)


def feed_sum(own, core):
    slots, width = own.shape
    block = slots // LOW

    def whole(shape):
        return pl.BlockSpec(shape, lambda i: (0, 0))

    return pl.pallas_call(
        feed_sum_kernel,
        grid=(1,),
        in_specs=[whole(own.shape), whole(core.shape)],
        out_specs=[whole((block, width)) for _ in range(LOW)],
        out_shape=[jax.ShapeDtypeStruct((block, width), BF16) for _ in range(LOW)],
        compiler_params=pltpu.CompilerParams(vmem_limit_bytes=32 * 2**20),
        cost_estimate=cost_of(3),
        name="feed_sum",
    )(own, core)


def spread_kernel(ids_ref, *refs):
    blocks, (near_ref, send_ref, slots_ref) = refs[:LOW], refs[LOW:]
    rows = near_ref.shape[1]
    slots = slots_ref.shape[0]
    block = slots // LOW

    @pl.when(pl.program_id(0) == 0)
    def _():
        for i in range(LOW):
            slots_ref[pl.ds(i * block, block), :] = blocks[i][...]

    for k, out_ref in enumerate((near_ref, send_ref)):
        slot = lax.broadcasted_iota(jnp.int32, (rows, slots), 1)
        ids = ids_ref[pl.ds(k * rows, rows), :]
        held = (slot == ids[:, 0:1]) | (slot == ids[:, 1:2])
        held = jnp.where(held, 1.0, 0.0).astype(BF16)
        total = jnp.dot(held, slots_ref[...], preferred_element_type=F32)
        out_ref[0] = total.astype(out_ref.dtype)


def spread(ids, values, rows):
    block, width = values[0].shape
    return pl.pallas_call(
        spread_kernel,
        grid=(2,),
        in_specs=[
            pl.BlockSpec((2 * rows, 8), lambda i: (i, 0)),
            *[pl.BlockSpec((block, width), lambda i: (0, 0)) for _ in range(LOW)],
        ],
        out_specs=[
            pl.BlockSpec((1, rows, width), lambda i: (i, 0, 0)),
            pl.BlockSpec((1, rows, width), lambda i: (i, 0, 0)),
        ],
        out_shape=[
            jax.ShapeDtypeStruct((2, rows, width), F32),
            jax.ShapeDtypeStruct((2, rows, width), BF16),
        ],
        scratch_shapes=[pltpu.VMEM((LOW * block, width), BF16)],
        compiler_params=pltpu.CompilerParams(vmem_limit_bytes=32 * 2**20),
        cost_estimate=cost_of(30),
        name="spread",
    )(ids, *values)


def slots_kernel(experts, capacity, scalars, routes_col, order_col, routes_row, order_row,
                 row_ref, col_ref, places_ref):
    group = routes_row.shape[1]
    rows = group // 4
    share = capacity // 2
    span = 2 * group
    bound = scalars[BOUNDS + 2]

    def target_of(routes, axis):
        place = lax.broadcasted_iota(jnp.int32, routes.shape, axis)
        return jnp.where((routes < experts) & (place < bound), routes, experts)

    target = target_of(routes_row[...], 1)
    code = target * span + order_row[...]
    block = 256

    def count(i, carry):
        first = pl.multiple_of(i * block, block)
        routes = routes_col[pl.ds(first, block), :]
        place = first + lax.broadcasted_iota(jnp.int32, routes.shape, 0)
        held = jnp.where((routes < experts) & (place < bound), routes, experts)
        others = held * span + order_col[pl.ds(first, block), :]
        result = []
        for k in range(2):
            total = carry[k]
            for j in range(2):
                smaller = jnp.where(others[:, j : j + 1] < code[k : k + 1, :], 1.0, 0.0)
                total = total + jnp.sum(smaller, axis=0, keepdims=True)
            result.append(total)
        return tuple(result)

    zero = jnp.zeros((1, group), F32)
    counts = lax.fori_loop(0, group // block, count, (zero, zero))
    for k in range(2):
        mine_target = target[k : k + 1, :]
        base = jnp.zeros((1, group), F32)
        for e in range(1, experts):
            earlier = jnp.sum(jnp.where(target < e, 1.0, 0.0))
            base = jnp.where(mine_target == e, earlier, base)
        place = (counts[k] - base).astype(jnp.int32)
        first = scalars[3] * share
        held = (
            (mine_target < experts)
            & (place >= first)
            & (place < first + share)
            & (place < capacity)
            & (jnp.bitwise_and(mine_target, 1) == scalars[2])
        )
        block = jnp.bitwise_xor(lax.shift_right_logical(mine_target, 1), scalars[LOW_PLACE])
        slot = block * share + place - first
        places_ref[k : k + 1, :] = jnp.where(held, slot, -1)
    for r in range(4):
        start = pl.multiple_of((scalars[1] ^ r) * rows, rows)
        piece = places_ref[:, pl.ds(start, rows)]
        row_ref[:, pl.ds(r * rows, rows)] = piece
        col_ref[pl.ds(r * rows, rows), :] = piece.T


def slots_of(scalars, routes, drop_order, experts, capacity):
    group = routes.shape[0]
    whole = pl.BlockSpec(memory_space=pltpu.VMEM)
    return pl.pallas_call(
        functools.partial(slots_kernel, experts, capacity),
        in_specs=[pl.BlockSpec(memory_space=pltpu.SMEM)] + [whole] * 4,
        out_specs=[whole] * 2,
        out_shape=[
            jax.ShapeDtypeStruct((8, group), jnp.int32),
            jax.ShapeDtypeStruct((group, 8), jnp.int32),
        ],
        scratch_shapes=[pltpu.VMEM((8, group), jnp.int32)],
        compiler_params=pltpu.CompilerParams(vmem_limit_bytes=32 * 2**20),
        cost_estimate=cost_of(8),
        name="slots",
    )(scalars, routes, drop_order, routes.T, drop_order.T)


def middle_kernel(kinds, scalars, mixed, p0, p1, p2, p3, x_ref, gain_ref, router_w, prior_ref,
                  prior_w, hidden_ref, sent_ref, router_ref, weight):
    hidden = x_ref[...]
    rows = p0.shape[2]
    for r, shards in enumerate((p0, p1, p2, p3)):
        for k in range(SHARDS):
            place = pl.multiple_of((scalars[0] ^ k) * rows, rows)
            weight[r, pl.ds(place, rows), :] = shards[k % LOW, k // LOW]
        hidden += lax.dot_general(
            mixed[scalars[1] ^ r].T, weight[r], (((1,), (1,)), ((), ())),
            preferred_element_type=F32,
        )
    hidden_ref[...] = hidden
    scale = lax.rsqrt(jnp.mean(hidden * hidden, axis=1, keepdims=True) + EPSILON)
    rounded = (hidden * scale * gain_ref[...]).astype(BF16)
    width = hidden.shape[1]
    sent_ref[:, :width] = rounded
    router_high, router_low = halves(router_w[...])
    logits = (
        jnp.dot(rounded, router_high, preferred_element_type=F32)
        + jnp.dot(rounded, router_low, preferred_element_type=F32)
        + split_dot(prior_ref[...], prior_w[...])
    )
    lanes = lax.broadcasted_iota(jnp.int32, logits.shape, 1)
    logits = jnp.where(lanes < 2 * kinds, logits, NEGATIVE)
    weights = jnp.exp(logits - jnp.max(logits, axis=1, keepdims=True))
    total = jnp.sum(jnp.where(lanes < kinds, weights, 0.0), axis=1, keepdims=True)
    router = weights / total
    router_ref[...] = router
    high = router.astype(BF16).astype(F32)
    sent_ref[:, width:] = jnp.where(lanes < kinds, high, router - high).astype(BF16)


def middle(kinds, scalars, mixed, weights, x, gain, router_w, prior, prior_w):
    rows, width = x.shape
    lanes = router_w.shape[1]

    def whole(shape):
        return pl.BlockSpec(shape, lambda i, _: (0,) * len(shape))

    return pl.pallas_call(
        functools.partial(middle_kernel, kinds),
        grid_spec=pltpu.PrefetchScalarGridSpec(
            num_scalar_prefetch=1,
            grid=(1,),
            in_specs=[
                whole(mixed.shape),
                *[whole(item.shape) for item in weights],
                whole(x.shape),
                whole(gain.shape),
                whole(router_w.shape),
                pl.BlockSpec((rows, kinds), lambda i, scalars: (scalars[1], 0)),
                whole(prior_w.shape),
            ],
            out_specs=[whole((rows, width)), whole((rows, width + lanes)), whole((rows, lanes))],
            scratch_shapes=[pltpu.VMEM((4, width, mixed.shape[1]), BF16)],
        ),
        out_shape=[
            jax.ShapeDtypeStruct((rows, width), F32),
            jax.ShapeDtypeStruct((rows, width + lanes), BF16),
            jax.ShapeDtypeStruct((rows, lanes), F32),
        ],
        compiler_params=pltpu.CompilerParams(vmem_limit_bytes=48 * 2**20),
        cost_estimate=cost_of(6),
        name="middle",
    )(scalars, mixed, *weights, x, gain, router_w, prior, prior_w)


def halves(value):
    high = value.astype(BF16)
    return high, (value - high.astype(F32)).astype(BF16)


def split_dot(left, right):
    (left_high, left_low), (right_high, right_low) = halves(left), halves(right)
    return (
        jnp.dot(left_high, right_high, preferred_element_type=F32)
        + jnp.dot(left_low, right_high, preferred_element_type=F32)
        + jnp.dot(left_high, right_low, preferred_element_type=F32)
    )


def turned_dot(left, right):
    high, low = halves(left.T)
    return jnp.dot(high, right, preferred_element_type=F32) + jnp.dot(
        low, right, preferred_element_type=F32
    )


def router_back_kernel(kinds, experts, scalars, near_ref, got_ref, far_ref, hidden_ref, router_ref,
                       routes_ref, cotangent_ref, prior_ref, gain_ref, small_ref, small_t_ref,
                       vector_ref, prior_w_ref,
                       grad_hidden_ref, grad_low_ref, partial_ref, grad_prior_ref, sums_ref):
    step = pl.program_id(0)
    rows, width = hidden_ref.shape
    place = scalars[1] * rows * pl.num_programs(0) + step * rows
    valid = place + lax.broadcasted_iota(jnp.int32, (rows, 1), 0) < scalars[BOUNDS + 2]
    valid = jnp.where(valid, 1.0, 0.0)
    back = near_ref[0] + got_ref[0].astype(F32) + far_ref[...].astype(F32)
    hidden = hidden_ref[...]
    grad_out = cotangent_ref[...] * valid
    scale = lax.rsqrt(jnp.mean(hidden * hidden, axis=1, keepdims=True) + EPSILON)
    unit = hidden * scale
    normed = unit * gain_ref[...]
    router = router_ref[...]
    lanes = lax.broadcasted_iota(jnp.int32, router.shape, 1)
    routes = routes_ref[...]

    def column(array, k):
        return jnp.sum(jnp.where(lanes == k, array, 0.0), axis=1, keepdims=True)

    def named(kind):
        return jnp.where((routes[:, 0:1] == kind) | (routes[:, 1:2] == kind), 1.0, 0.0)

    copy, first, second = (named(experts + k) for k in (1, 2, 3))
    weight_copy = column(router, experts + 1) * copy
    weight_first = column(router, experts + 2) * first
    weight_second = column(router, experts + 3) * second
    mixlog = split_dot(normed, small_ref[...])

    def softmax_two(k):
        one, two = column(mixlog, k), column(mixlog, k + 1)
        highest = jnp.maximum(one, two)
        one, two = jnp.exp(one - highest), jnp.exp(two - highest)
        return one / (one + two), two / (one + two)

    mix_one, mix_two = softmax_two(kinds), softmax_two(kinds + 2)
    vector_one, vector_two = vector_ref[0:1, :], vector_ref[1:2, :]
    along = jnp.sum(normed * grad_out, axis=1, keepdims=True)
    along_one = jnp.sum(vector_one * grad_out, axis=1, keepdims=True)
    along_two = jnp.sum(vector_two * grad_out, axis=1, keepdims=True)

    extra = back[:, width:]
    pairs = jnp.where(lanes < kinds, extra, 0.0) + jnp.where(
        lanes < kinds, pltpu.roll(extra, extra.shape[1] - kinds, 1), 0.0
    )
    grad_router = pairs + jnp.where(lanes == experts + 1, copy * along, 0.0)
    grad_router += jnp.where(
        lanes == experts + 2, first * (mix_one[0] * along + mix_one[1] * along_one), 0.0
    )
    grad_router += jnp.where(
        lanes == experts + 3, second * (mix_two[0] * along + mix_two[1] * along_two), 0.0
    )
    held = jnp.where(lanes < kinds, router, 0.0)
    grad_small = held * (grad_router - jnp.sum(held * grad_router, axis=1, keepdims=True))
    grad_prior_ref[...] = split_dot(grad_small, prior_w_ref[...])[:, :kinds]
    grad_logits = grad_small

    def mixed_back(weight, mix, other, k):
        one, two = weight * along, weight * other
        inner = mix[0] * one + mix[1] * two
        return jnp.where(lanes == k, mix[0] * (one - inner), 0.0) + jnp.where(
            lanes == k + 1, mix[1] * (two - inner), 0.0
        )

    grad_mixlog = mixed_back(weight_first, mix_one, along_one, kinds) + mixed_back(
        weight_second, mix_two, along_two, kinds + 2
    )
    grad_small = grad_logits + grad_mixlog
    share = weight_copy + weight_first * mix_one[0] + weight_second * mix_two[0]
    grad_normed = (
        back[:, :width]
        + share * grad_out
        + split_dot(grad_small, small_t_ref[...])
    )
    through = grad_normed * gain_ref[...]
    inner = jnp.mean(through * hidden, axis=1, keepdims=True)
    grad_hidden = grad_out + scale * through - (scale * scale * scale * inner) * hidden
    grad_hidden_ref[...] = grad_hidden
    grad_low_ref[...] = grad_hidden.astype(BF16)
    vector_first, vector_second = weight_first * mix_one[1], weight_second * mix_two[1]
    partial_ref[...] = valid * (
        hidden + share * normed + vector_first * vector_one + vector_second * vector_two
    )

    @pl.when(step == 0)
    def _():
        sums_ref[...] = jnp.zeros_like(sums_ref)

    vectors = jnp.where(lanes == kinds + 5, vector_first, 0.0) + jnp.where(
        lanes == kinds + 6, vector_second, 0.0
    )
    low = normed.astype(BF16)
    total = turned_dot(grad_small, low) + turned_dot(vectors, grad_out.astype(BF16))
    sums_ref[: kinds + 8, :] += total[: kinds + 8, :]
    sums_ref[kinds + 4 : kinds + 5, :] += jnp.sum(grad_normed * unit, axis=0, keepdims=True)
    prior = split_dot(prior_ref[...].T, grad_logits)
    sums_ref[pl.ds(kinds + 8, kinds), : lanes.shape[1]] += prior


def router_back(kinds, experts, scalars, near, got, far, hidden, router, routes, cotangent, prior,
                gain, small, small_t, vector, prior_w):
    rows, width = hidden.shape
    block = rows // 2
    lanes = router.shape[1]

    def whole(shape):
        return pl.BlockSpec(shape, lambda i, _: (0,) * len(shape))

    def part(columns):
        return pl.BlockSpec((block, columns), lambda i, _: (i, 0))

    def mine(columns):
        return pl.BlockSpec((block, columns), lambda i, scalars: (scalars[1] * 2 + i, 0))

    return pl.pallas_call(
        functools.partial(router_back_kernel, kinds, experts),
        grid_spec=pltpu.PrefetchScalarGridSpec(
            num_scalar_prefetch=1,
            grid=(2,),
            in_specs=[
                pl.BlockSpec((1, block, width + lanes), lambda i, _: (0, i, 0)),
                pl.BlockSpec((1, block, width + lanes), lambda i, _: (0, i, 0)),
                part(width + lanes),
                part(width),
                part(lanes),
                mine(2),
                part(width),
                mine(kinds),
                whole(gain.shape),
                whole(small.shape),
                whole(small_t.shape),
                whole(vector.shape),
                whole(prior_w.shape),
            ],
            out_specs=[
                part(width),
                part(width),
                part(width),
                part(kinds),
                whole((32, width)),
            ],
        ),
        out_shape=[
            jax.ShapeDtypeStruct((rows, width), F32),
            jax.ShapeDtypeStruct((rows, width), BF16),
            jax.ShapeDtypeStruct((rows, width), F32),
            jax.ShapeDtypeStruct((rows, kinds), F32),
            jax.ShapeDtypeStruct((32, width), F32),
        ],
        compiler_params=pltpu.CompilerParams(vmem_limit_bytes=48 * 2**20),
        cost_estimate=cost_of(8),
        name="router_back",
    )(scalars, near, got, far, hidden, router, routes, cotangent, prior, gain, small, small_t,
      vector, prior_w)


def two_parts(value):
    high = lax.reduce_precision(value, 8, 7)
    return jnp.concatenate([high, value - high], axis=-1).astype(BF16)


def everywhere(value, axes, count):
    copies = jnp.broadcast_to(value[None], (count, *value.shape))
    return lax.all_to_all(copies, axes, 0, 0, tiled=True)


def flip(value, axis, size, bit):
    return lax.ppermute(value, axis, [(i, i ^ bit) for i in range(size)])


def by_halves(value):
    if value.shape[0] == 2:
        return value
    rows, units = value.shape[-2:]
    middle_axes = tuple(range(2, value.ndim - 2))
    turned = value.transpose(*middle_axes, 0, 1, value.ndim - 2, value.ndim - 1)
    turned = turned.reshape(*turned.shape[:-4], 2, LOW, value.shape[0] * rows // 2, units)
    axes = turned.ndim
    return turned.transpose(axes - 4, axes - 3, *range(axes - 4), axes - 2, axes - 1)


def scatter_high(value, many):
    if many != 2:
        rows, units = value.shape[-2:]
        middle_axes = tuple(range(2, value.ndim - 2))
        turned = value.transpose(*middle_axes, 0, 1, value.ndim - 2, value.ndim - 1)
        turned = turned.reshape(*turned.shape[:-4], many, LOW, 2 * rows // many, units)
        axes = turned.ndim
        value = turned.transpose(axes - 4, axes - 3, *range(axes - 4), axes - 2, axes - 1)
    return lax.psum_scatter(value, "hi", scatter_dimension=0)


def gather_rows(value, later, many):
    if many != 2:
        full = lax.all_gather(value, ("hi", "lo"), axis=0, tiled=True)
        full = full.reshape(2, LOW, -1, full.shape[1])
        return [full[:, i] for i in range(LOW)], later
    far, *later = lax.optimization_barrier((swap(value, "hi"), *later))
    both = jnp.stack([value, far])
    return [both] + [flip(both, "lo", LOW, bit) for bit in range(1, LOW)], tuple(later)


def scatter_rows(near, far, many):
    if many != 2:
        full = jnp.stack([near, far]).astype(F32).reshape(-1, near.shape[2])
        return lax.psum_scatter(full, ("hi", "lo"), scatter_dimension=0, tiled=True)
    both = near.astype(F32) + far.astype(F32)
    total = both[0]
    for bit in range(1, LOW):
        total = total + flip(both[bit].astype(BF16), "lo", LOW, bit).astype(F32)
    return total


def per_device(
    many,
    inputs,
    cotangent,
    lengths,
    routes,
    drop_order,
    prior_logits,
    attn_gain,
    w_query,
    w_key,
    w_value,
    w_out,
    moe_gain,
    w_router,
    w_prior,
    w_const,
    const_vector,
    w_gate,
    w_up,
    w_down,
):
    tok_rows, width = inputs.shape
    group = tok_rows * 4
    kinds = w_router.shape[1]
    experts, shard_rows, shard_units = w_gate.shape
    capacity = 3 * group // 16
    share = capacity // 2
    slots = LOW * share
    local_width = w_query.shape[1]
    heads = local_width // HEAD
    tp_axes = ("y", "c")
    all_axes = ("hi", "lo", "y", "c")
    count = many * LOW * 4
    wide = width + 128
    high = lax.axis_index("hi")
    parity = lax.axis_index("y")
    core = lax.axis_index("c")
    place_in_group = parity * 2 + core
    mine = high * LOW + lax.axis_index("lo") if many == 2 else jnp.zeros_like(high)
    boundary = jnp.cumsum(lengths[0])
    scalars = jnp.concatenate(
        [jnp.stack([mine, place_in_group, parity, core, lax.axis_index("lo")]), boundary[:-1]]
    ).astype(jnp.int32)
    gain_one, gain_two = attn_gain.reshape(1, width), moe_gain.reshape(1, width)

    valid_mine = place_in_group * tok_rows + jnp.arange(tok_rows)[:, None] < boundary[-2]
    valid_mine = valid_mine.astype(F32)

    normed_one = rms_norm(inputs, attn_gain).astype(BF16)
    normed_other = swap(normed_one, "y")
    attn_shard = jnp.concatenate([w_query, w_key, w_value, w_out.T], axis=1)
    up_part = lax.all_to_all(w_up, ("lo", "y"), 0, 0, tiled=True)
    up_part = up_part.reshape(LOW, 2, shard_rows, shard_units)
    down_shard = w_down.transpose(0, 2, 1)
    attn_shards, (w_gate,) = gather_rows(attn_shard, (w_gate,), many)
    gate_far = swap(w_gate, "hi") if many == 2 else w_gate
    router_lanes = jnp.pad(
        jnp.concatenate([w_router, w_router], axis=1), ((0, 0), (0, 128 - 2 * kinds))
    )
    prior_lanes = jnp.pad(
        jnp.concatenate([w_prior, w_prior], axis=1), ((0, 0), (0, 128 - 2 * kinds))
    )
    const_flat = w_const.transpose(1, 0, 2).reshape(width, 4)
    small = jnp.pad(
        jnp.concatenate([w_router, const_flat], axis=1), ((0, 0), (0, 128 - kinds - 4))
    )
    small_t = small.T
    prior_back = jnp.pad(w_prior.T, ((0, 128 - kinds), (0, 128 - kinds)))
    (
        attn_shards[0], scalars, router_lanes, prior_lanes, small, small_t, prior_back, prior_logits
    ) = lax.optimization_barrier(
        (attn_shards[0], scalars, router_lanes, prior_lanes, small, small_t, prior_back, prior_logits)
    )
    ids_rows, ids_cols = slots_of(scalars, routes, drop_order, experts, capacity)
    grad_out_low = (cotangent * valid_mine).astype(BF16)
    (
        normed_other, attn_shards, ids_rows, down_shard, grad_out_low, up_part, gate_far
    ) = lax.optimization_barrier(
        (normed_other, attn_shards, ids_rows, down_shard, grad_out_low, up_part, gate_far)
    )
    grad_out_other = swap(grad_out_low, "y")
    down_part = lax.all_to_all(down_shard, ("lo", "y"), 0, 0, tiled=True)
    down_part = down_part.reshape(LOW, 2, shard_rows, shard_units)
    if many == 2:
        up_far = [swap(up_part[:2], "hi"), swap(up_part[2:], "hi")]
    else:
        up_all = by_halves(lax.all_gather(up_part, "hi"))
        up_part, up_far = up_all[0], [up_all[1, :2], up_all[1, 2:]]
    out_mine = jnp.stack([item[:, :, 3 * local_width :] for item in attn_shards])
    out_other = swap(out_mine, "y")
    normed_pieces = [normed_one, swap(normed_one, "c"), normed_other, swap(normed_other, "c")]
    mixed, lse, qkv, qkv_full = attend(normed_pieces, attn_shards, scalars, heads)
    mixed, out_other, out_mine, up_far[0], down_part, grad_out_other = lax.optimization_barrier(
        (mixed, out_other, out_mine, up_far[0], down_part, grad_out_other)
    )
    if many == 2:
        high_place = high
        down_far = [swap(down_part[:2], "hi"), swap(down_part[2:], "hi")]
        gate_both = jnp.where(
            high == 0, jnp.stack([w_gate, gate_far], axis=1), jnp.stack([gate_far, w_gate], axis=1)
        )
    else:
        high_place = jnp.zeros_like(high)
        down_all = by_halves(lax.all_gather(down_part, "hi"))
        down_part, down_far = down_all[0], [down_all[1, :2], down_all[1, 2:]]
        gate_both = lax.all_gather(w_gate, "hi", axis=1)
    out_pieces = [out_mine, swap(out_mine, "c"), out_other, swap(out_other, "c")]

    mixed_mine = lax.all_to_all(mixed, tp_axes, 0, 0, tiled=True)
    grad_out_pieces = [
        grad_out_low, swap(grad_out_low, "c"), grad_out_other, swap(grad_out_other, "c"),
    ]
    grad_out_slots = pick(ids_rows, grad_out_pieces, slots)
    mixed_mine, grad_out_slots, up_far[1], gate_both = lax.optimization_barrier(
        (mixed_mine, grad_out_slots, up_far[1], gate_both)
    )

    hidden, sent_two, router = middle(
        kinds, scalars, mixed_mine, out_pieces, inputs, gain_two, router_lanes, prior_logits, prior_lanes
    )

    gate_part = lax.all_to_all(gate_both, ("lo", "y"), 0, 0, tiled=True)
    gate_part = gate_part.reshape(LOW, 2, many, shard_rows, shard_units)
    if many != 2:
        gate_part = by_halves(gate_part.transpose(2, 0, 1, 3, 4)).transpose(1, 2, 0, 3, 4)
    other_two, grad_taken, gate_part, down_far[0] = lax.optimization_barrier(
        (swap(sent_two, "y"), to_experts(grad_out_slots), gate_part, down_far[0])
    )
    pieces_two = [sent_two, swap(sent_two, "c"), other_two, swap(other_two, "c")]

    grad_taken = [*grad_taken, swap(jnp.concatenate(grad_taken), "c")]
    sent_slots = pick(ids_rows, pieces_two, slots)
    sent_slots, qkv_full = lax.optimization_barrier((sent_slots, qkv_full))
    taken = to_experts(sent_slots)
    taken += [swap(item, "c") for item in taken]
    qkv_pieces = gather_pieces(qkv_full)
    taken, qkv_pieces, down_far[1] = lax.optimization_barrier((taken, qkv_pieces, down_far[1]))

    expert = lax.axis_index("lo") * 2 + parity
    back_own, back_send, feed_own, feed_send, grads_out = expert_pass(
        kinds, jnp.stack([expert, high_place]).astype(jnp.int32), taken, grad_taken,
        gate_part, [up_part, down_part], up_far + down_far,
    )

    weight_sum = scatter_high(grads_out, many)
    back_taken = to_experts(back_sum(kinds, back_own, swap(back_send, "c")))
    feed_core = swap(feed_send, "c")
    back_taken, feed_core = lax.optimization_barrier((back_taken, feed_core))

    back_near, back_sent = spread(ids_cols, back_taken, tok_rows)
    back_got, back_other = add_core(back_near, back_sent)
    back_other, feed_core = lax.optimization_barrier((back_other, feed_core))
    back_far, feed_blocks = lax.optimization_barrier(
        (swap(back_other, "y"), feed_sum(feed_own, feed_core))
    )

    grad_hidden, grad_low, partial, grad_prior, sums = router_back(
        kinds, experts, scalars, back_near, back_got, back_far, hidden, router, routes, cotangent,
        prior_logits, gain_two, small, small_t, const_vector, prior_back,
    )
    feed_taken = to_experts(feed_blocks)
    grad_mixed = to_heads(mixed_back(scalars, grad_low, out_pieces))
    grad_mixed, grad_low = lax.optimization_barrier((grad_mixed, grad_low))
    low_other = swap(grad_low, "y")
    share_sums = lax.all_to_all(sums.reshape(count, 32 * width // count), all_axes, 0, 0, tiled=True)
    grad_qkv = attend_back(scalars, qkv, lse, grad_mixed, heads).reshape(
        4, 3 * local_width, tok_rows
    )
    grad_qkv, feed_taken, weight_sum, low_other = lax.optimization_barrier(
        (grad_qkv, feed_taken, weight_sum, low_other)
    )
    grad_attn_pieces = [grad_low, swap(grad_low, "c"), low_other, swap(low_other, "c")]

    weight_own = lax.all_to_all(
        weight_sum.reshape(2 * LOW, 3, shard_rows, shard_units), ("lo", "y"), 0, 0, tiled=True
    )
    grad_qkv_mine = to_heads(grad_qkv)
    attn_near, attn_far = attn_grads(grad_qkv, mixed, normed_pieces, grad_attn_pieces, scalars)
    if many == 2:
        attn_far = swap(attn_far, "hi")
    feed_near, feed_sent = spread(ids_cols, feed_taken, tok_rows)
    feed_got, feed_other = add_core(feed_near, feed_sent)
    (
        grad_qkv_mine, share_sums, attn_near, attn_far, feed_near, feed_got, feed_other
    ) = lax.optimization_barrier(
        (grad_qkv_mine, share_sums, attn_near, attn_far, feed_near, feed_got, feed_other)
    )
    feed_far = swap(feed_other, "y")
    share_sums = jnp.sum(share_sums, axis=0)
    grad_inputs, gain_part = inputs_back(
        grad_qkv_mine, qkv_pieces, inputs, gain_one, grad_hidden
    )
    output = partial + valid_mine * (
        feed_near[0] + feed_got[0].astype(F32) + feed_far.astype(F32)
    )
    grad_attn_own = scatter_rows(attn_near, attn_far, many)
    last = jnp.concatenate([jnp.sum(gain_part, axis=0).reshape(-1), share_sums])
    last, weight_own = lax.optimization_barrier((last, weight_own))
    last = everywhere(last, all_axes, count)
    last, grad_attn_own = lax.optimization_barrier((last, grad_attn_own))
    grad_gain = jnp.sum(last[:, :width], axis=0)
    total = last[:, width:].reshape(32, width)
    return (
        output,
        grad_inputs,
        grad_prior,
        grad_gain,
        grad_attn_own[:, :local_width],
        grad_attn_own[:, local_width : 2 * local_width],
        grad_attn_own[:, 2 * local_width : 3 * local_width],
        grad_attn_own[:, 3 * local_width :].T,
        total[kinds + 4],
        total[:kinds].T,
        total[kinds + 8 : 2 * kinds + 8, :kinds],
        total[kinds : kinds + 4].reshape(2, 2, width).transpose(0, 2, 1),
        total[kinds + 5 : kinds + 7],
        weight_own[:, 0].astype(F32),
        weight_own[:, 1].astype(F32),
        weight_own[:, 2].transpose(0, 2, 1).astype(F32),
    )


def solution(mesh):
    many = mesh.shape["fsdp"] // LOW
    fine = Mesh(mesh.devices.reshape(many, LOW, 2, 2), ("hi", "lo", "y", "c"))
    fsdp, tp = ("hi", "lo"), ("y", "c")
    every = fsdp + tp
    return jax.shard_map(
        functools.partial(per_device, many),
        mesh=fine,
        in_specs=(
            P(every, None),
            P(every, None),
            P(fsdp, None),
            P(fsdp, None),
            P(fsdp, None),
            P(fsdp, None),
            P(),
            P(fsdp, tp),
            P(fsdp, tp),
            P(fsdp, tp),
            P(tp, fsdp),
            P(),
            P(),
            P(),
            P(),
            P(),
            P(None, fsdp, tp),
            P(None, fsdp, tp),
            P(None, tp, fsdp),
        ),
        out_specs=(
            P(every, None),
            P(every, None),
            P(every, None),
            P(),
            P(fsdp, tp),
            P(fsdp, tp),
            P(fsdp, tp),
            P(tp, fsdp),
            P(),
            P(),
            P(),
            P(),
            P(),
            P(None, fsdp, tp),
            P(None, fsdp, tp),
            P(None, tp, fsdp),
        ),
        check_vma=False,
    )
```

```python
import functools

import jax
import jax.numpy as jnp
from jax import lax
from jax.experimental import pallas as pl
from jax.experimental.pallas import tpu as pltpu
from jax.sharding import Mesh
from jax.sharding import PartitionSpec as P

HEAD = 64
MAXLEN = 768
LOW = 4
SHARDS = 8
LOW_PLACE = 4
BOUNDS = 5
EPSILON = 1e-06
PRECISE = lax.Precision.HIGHEST
NEGATIVE = -1e30
F32 = jnp.float32
BF16 = jnp.bfloat16


def rms_norm(values, gain):
    return values * lax.rsqrt(jnp.mean(values * values, axis=-1, keepdims=True) + EPSILON) * gain


def swap(value, axis):
    return lax.ppermute(value, axis, [(0, 1), (1, 0)])


def gather_pieces(value):
    other = swap(value, "y")
    return [value, swap(value, "c"), other, swap(other, "c")]


def natural(pieces, index):
    ordered = []
    for j in range(4):
        item = pieces[j]
        for t in range(1, 4):
            item = jnp.where(index == t, pieces[j ^ t], item)
        ordered.append(item)
    return jnp.stack(ordered)


def add_core(near, sent):
    got = swap(sent, "c")
    return got, (near[1] + got[1].astype(F32)).astype(BF16)


def cost_of(microseconds):
    return pl.CostEstimate(
        flops=int(microseconds * 1.15e9), transcendentals=0, bytes_accessed=2**16
    )


def start_of(row, scalars):
    start_row = jnp.zeros_like(row)
    for k in range(BOUNDS, scalars.shape[0]):
        start_row = jnp.where(row >= scalars[k], scalars[k], start_row)
    return start_row


def for_window(first, block, pad, scalars, body):
    needed = (first - start_of(first, scalars) + block - 1) // block
    most = pad // block
    for blocks in range(most):
        pl.when(needed == blocks)(functools.partial(body, (blocks + 1) * block))
    pl.when(needed >= most)(functools.partial(body, pad + block))


def scores_mask(first_key, first_query, window, block, scalars):
    row = first_query + lax.broadcasted_iota(jnp.int32, (1, block), 1)
    start_row = start_of(row, scalars)
    key_places = first_key + lax.broadcasted_iota(jnp.int32, (window, block), 0)
    query_places = first_query + lax.broadcasted_iota(jnp.int32, (window, block), 1)
    return (key_places >= start_row) & (key_places <= query_places)


def attend_kernel(block, pad, scalars, *refs):
    pieces, refs = refs[:4], refs[4:]
    shards, refs = refs[:LOW], refs[LOW:]
    out_ref, lse_ref, qkv_ref, weight_ref, key_rows, value_pad, full = refs
    group = qkv_ref.shape[1]
    quarter = group // 4
    inner = qkv_ref.shape[0] // 3
    head = pl.program_id(0)

    @pl.when(head == 0)
    def _():
        rows = shards[0].shape[1]
        for r in range(SHARDS):
            place = pl.multiple_of((scalars[0] ^ r) * rows, rows)
            full[pl.ds(place, rows), :] = shards[r % LOW][r // LOW]
        turned = full[:, : 3 * inner].T
        weight_ref[...] = turned
        for r in range(4):
            place = pl.multiple_of((scalars[1] ^ r) * quarter, quarter)
            qkv_ref[:, pl.ds(place, quarter)] = lax.dot_general(
                turned, pieces[r][...], (((1,), (1,)), ((), ())), preferred_element_type=F32
            ).astype(BF16)

    first_row = pl.multiple_of(head * HEAD, HEAD)
    key_rows[pl.ds(0, pad), :] = jnp.zeros((pad, HEAD), BF16)
    value_pad[:, pl.ds(0, pad)] = jnp.zeros((HEAD, pad), BF16)
    key_rows[pl.ds(pad, group), :] = qkv_ref[pl.ds(inner + first_row, HEAD), :].T
    value_pad[:, pl.ds(pad, group)] = qkv_ref[pl.ds(2 * inner + first_row, HEAD), :]

    def one(i, carry):
        first = pl.multiple_of(i * block, block)

        def body(window):
            begin = pl.multiple_of(first + pad + block - window, block)
            scores = jnp.dot(
                key_rows[pl.ds(begin, window), :],
                qkv_ref[pl.ds(first_row, HEAD), pl.ds(first, block)],
                preferred_element_type=F32,
            )
            allowed = scores_mask(begin - pad, first, window, block, scalars)
            scores = jnp.where(allowed, scores * 0.125, NEGATIVE)
            highest = jnp.max(scores, axis=0, keepdims=True)
            weights = jnp.exp(scores - highest)
            total = jnp.sum(weights, axis=0, keepdims=True)
            mixed = jnp.dot(
                value_pad[:, pl.ds(begin, window)],
                weights.astype(BF16),
                preferred_element_type=F32,
            )
            mixed = (mixed / total).astype(BF16)
            column = pl.multiple_of(first % quarter, block)
            out_ref[first // quarter, :, pl.ds(column, block)] = mixed
            lse_ref[0, :, pl.ds(first, block)] = highest + jnp.log(total)

        for_window(first, block, pad, scalars, body)
        return carry

    lax.fori_loop(0, group // block, one, 0)


def attend(pieces, shards, scalars, heads):
    rows, width = pieces[0].shape
    group = 4 * rows
    inner = heads * HEAD
    block = 256

    def whole(shape):
        return pl.BlockSpec(
            shape, lambda i, _: (0,) * len(shape), pipeline_mode=pl.Buffered(1)
        )

    return pl.pallas_call(
        functools.partial(attend_kernel, block, MAXLEN),
        grid_spec=pltpu.PrefetchScalarGridSpec(
            num_scalar_prefetch=1,
            grid=(heads,),
            in_specs=[
                *[whole((rows, width)) for _ in range(4)],
                *[whole(shards[0].shape) for _ in range(LOW)],
            ],
            out_specs=[
                pl.BlockSpec((4, HEAD, rows), lambda h, _: (0, h, 0)),
                pl.BlockSpec((1, 1, group), lambda h, _: (h, 0, 0)),
                whole((3 * inner, group)),
                whole((3 * inner, width)),
            ],
            scratch_shapes=[
                pltpu.VMEM((MAXLEN + group, HEAD), BF16),
                pltpu.VMEM((HEAD, MAXLEN + group), BF16),
                pltpu.VMEM((width, 4 * inner), BF16),
            ],
        ),
        out_shape=[
            jax.ShapeDtypeStruct((4, inner, rows), BF16),
            jax.ShapeDtypeStruct((heads, 1, group), F32),
            jax.ShapeDtypeStruct((3 * inner, group), BF16),
            jax.ShapeDtypeStruct((3 * inner, width), BF16),
        ],
        compiler_params=pltpu.CompilerParams(vmem_limit_bytes=48 * 2**20),
        cost_estimate=cost_of(24),
        name="attend",
    )(scalars, *pieces, *shards)


def attn_grads_kernel(scalars, *refs):
    grad_qkv, mixed, refs = refs[0], refs[1], refs[2:]
    tokens, grads, refs = refs[:4], refs[4:8], refs[8:]
    outs, (total,) = refs[:2], refs[2:]
    inner3 = grad_qkv.shape[1]
    first, second = 0.0, 0.0
    for r in range(4):
        j = scalars[1] ^ r
        first += jnp.dot(grad_qkv[r], tokens[r][...], preferred_element_type=F32)
        second += jnp.dot(mixed[j], grads[r][...], preferred_element_type=F32)
    total[:, :inner3] = first.T.astype(BF16)
    total[:, inner3:] = second.T.astype(BF16)
    rows = outs[0].shape[1]
    for r in range(SHARDS):
        place = pl.multiple_of((scalars[0] ^ r) * rows, rows)
        outs[r // LOW][r % LOW] = total[pl.ds(place, rows), :]


def attn_grads(grad_qkv, mixed, tokens, grads, scalars):
    width = tokens[0].shape[1]
    columns = grad_qkv.shape[1] + mixed.shape[1]
    rows = width // SHARDS
    whole = pl.BlockSpec(memory_space=pltpu.VMEM)
    return pl.pallas_call(
        attn_grads_kernel,
        in_specs=[pl.BlockSpec(memory_space=pltpu.SMEM)] + [whole] * 10,
        out_specs=[whole] * 2,
        out_shape=[jax.ShapeDtypeStruct((LOW, rows, columns), BF16)] * 2,
        scratch_shapes=[pltpu.VMEM((width, columns), BF16)],
        compiler_params=pltpu.CompilerParams(vmem_limit_bytes=48 * 2**20),
        cost_estimate=cost_of(30),
        name="attn_grads",
    )(scalars, grad_qkv, mixed, *tokens, *grads)


def attend_back_kernel(block, pad, scalars, qkv_ref, lse_ref, *refs):
    pieces, refs = refs[:4], refs[4:]
    out_ref, grad_mixed, key_rows, value_rows, key_pad, grad_key, grad_value = refs
    group = qkv_ref.shape[1]
    inner_rows = qkv_ref.shape[0] // 3
    quarter = group // 4
    contract_last = (((1,), (1,)), ((), ()))
    head = pl.program_id(0)

    @pl.when(head == 0)
    def _():
        for r in range(4):
            place = pl.multiple_of((scalars[1] ^ r) * quarter, quarter)
            grad_mixed[:, pl.ds(place, quarter)] = pieces[r][...]

    first_row = pl.multiple_of(head * HEAD, HEAD)
    keys = qkv_ref[pl.ds(inner_rows + first_row, HEAD), :]
    key_rows[pl.ds(0, pad), :] = jnp.zeros((pad, HEAD), BF16)
    value_rows[pl.ds(0, pad), :] = jnp.zeros((pad, HEAD), BF16)
    key_pad[:, pl.ds(0, pad)] = jnp.zeros((HEAD, pad), BF16)
    key_rows[pl.ds(pad, group), :] = keys.T
    value_rows[pl.ds(pad, group), :] = qkv_ref[pl.ds(2 * inner_rows + first_row, HEAD), :].T
    key_pad[:, pl.ds(pad, group)] = keys
    grad_key[...] = jnp.zeros_like(grad_key)
    grad_value[...] = jnp.zeros_like(grad_value)

    def one(i, carry):
        first = pl.multiple_of(i * block, block)

        def body(window):
            begin = pl.multiple_of(first + pad + block - window, block)
            query = qkv_ref[pl.ds(first_row, HEAD), pl.ds(first, block)]
            grad = grad_mixed[pl.ds(first_row, HEAD), pl.ds(first, block)]
            scores = jnp.dot(key_rows[pl.ds(begin, window), :], query, preferred_element_type=F32)
            allowed = scores_mask(begin - pad, first, window, block, scalars)
            exponent = scores * 0.125 - lse_ref[0, :, pl.ds(first, block)]
            probs = jnp.exp(jnp.where(allowed, exponent, NEGATIVE))
            grad_probs = jnp.dot(
                value_rows[pl.ds(begin, window), :], grad, preferred_element_type=F32
            )
            inner = jnp.sum(probs * grad_probs, axis=0, keepdims=True)
            raw = (0.125 * (probs * (grad_probs - inner))).astype(BF16)
            grad_query = jnp.dot(
                key_pad[:, pl.ds(begin, window)], raw, preferred_element_type=F32
            )
            column = pl.multiple_of(first % quarter, block)
            piece = (first // quarter) ^ scalars[1]
            out_ref[piece, 0, :, pl.ds(column, block)] = grad_query.astype(BF16)
            grad_value[:, pl.ds(begin, window)] += lax.dot_general(
                grad, probs.astype(BF16), contract_last, preferred_element_type=F32
            )
            grad_key[:, pl.ds(begin, window)] += lax.dot_general(
                query, raw, contract_last, preferred_element_type=F32
            )

        for_window(first, block, pad, scalars, body)
        return carry

    lax.fori_loop(0, group // block, one, 0)
    for j in range(4):
        piece = scalars[1] ^ j
        out_ref[piece, 1] = grad_key[:, pl.ds(pad + j * quarter, quarter)].astype(BF16)
        out_ref[piece, 2] = grad_value[:, pl.ds(pad + j * quarter, quarter)].astype(BF16)


def attend_back(scalars, qkv, lse, pieces, heads):
    group = qkv.shape[1]
    block = 256

    def whole(shape):
        return pl.BlockSpec(
            shape, lambda i, _: (0,) * len(shape), pipeline_mode=pl.Buffered(1)
        )

    return pl.pallas_call(
        functools.partial(attend_back_kernel, block, MAXLEN),
        grid_spec=pltpu.PrefetchScalarGridSpec(
            num_scalar_prefetch=1,
            grid=(heads,),
            in_specs=[
                whole(qkv.shape),
                pl.BlockSpec((1, 1, group), lambda h, _: (h, 0, 0)),
                *[whole(item.shape) for item in pieces],
            ],
            out_specs=pl.BlockSpec((4, 3, HEAD, group // 4), lambda h, _: (0, 0, h, 0)),
            scratch_shapes=[
                pltpu.VMEM((heads * HEAD, group), BF16),
                pltpu.VMEM((MAXLEN + group, HEAD), BF16),
                pltpu.VMEM((MAXLEN + group, HEAD), BF16),
                pltpu.VMEM((HEAD, MAXLEN + group), BF16),
                pltpu.VMEM((HEAD, MAXLEN + group), F32),
                pltpu.VMEM((HEAD, MAXLEN + group), F32),
            ],
        ),
        out_shape=jax.ShapeDtypeStruct((4, 3, heads * HEAD, group // 4), BF16),
        compiler_params=pltpu.CompilerParams(vmem_limit_bytes=48 * 2**20),
        cost_estimate=cost_of(34),
        name="attend_back",
    )(scalars, qkv, lse, *pieces)


def mixed_back_kernel(scalars, grad_ref, p0, p1, p2, p3, *refs):
    outs, weight = refs[:4], refs[4]
    rows = p0.shape[2]
    for r, shards in enumerate((p0, p1, p2, p3)):
        for k in range(SHARDS):
            place = pl.multiple_of((scalars[0] ^ k) * rows, rows)
            weight[pl.ds(place, rows), :] = shards[k % LOW, k // LOW]
        outs[r][...] = lax.dot_general(
            weight[...].T, grad_ref[...], (((1,), (1,)), ((), ())), preferred_element_type=F32
        ).astype(BF16)


def mixed_back(scalars, grad, weights):
    rows, width = grad.shape
    inner = weights[0].shape[3]

    def whole(shape):
        return pl.BlockSpec(shape, lambda i, _: (0,) * len(shape))

    return pl.pallas_call(
        mixed_back_kernel,
        grid_spec=pltpu.PrefetchScalarGridSpec(
            num_scalar_prefetch=1,
            grid=(1,),
            in_specs=[whole(grad.shape), *[whole(item.shape) for item in weights]],
            out_specs=[whole((inner, rows)) for _ in range(4)],
            scratch_shapes=[pltpu.VMEM((width, inner), BF16)],
        ),
        out_shape=[jax.ShapeDtypeStruct((inner, rows), BF16) for _ in range(4)],
        compiler_params=pltpu.CompilerParams(vmem_limit_bytes=32 * 2**20),
        cost_estimate=cost_of(4),
        name="mixed_back",
    )(scalars, grad, *weights)


def inputs_back_kernel(g0, g1, g2, g3, p0, p1, p2, p3, x_ref, gain_ref, hidden_ref, out_ref, sum_ref):
    total = 0.0
    for grad, weight in zip((g0, g1, g2, g3), (p0, p1, p2, p3)):
        total += jnp.dot(grad[...].T, weight[...], preferred_element_type=F32)
    x = x_ref[...]
    scale = lax.rsqrt(jnp.mean(x * x, axis=1, keepdims=True) + EPSILON)
    through = total * gain_ref[...]
    inner = jnp.mean(through * x, axis=1, keepdims=True)
    out_ref[...] = hidden_ref[...] + scale * through - (scale * scale * scale * inner) * x
    sum_ref[0] = jnp.sum(total * x * scale, axis=0, keepdims=True)


def inputs_back(grads, weights, x, gain, grad_hidden):
    rows, width = x.shape
    block = rows // 2

    def whole(shape):
        return pl.BlockSpec(shape, lambda i: (0,) * len(shape), pipeline_mode=pl.Buffered(1))

    part = pl.BlockSpec((block, width), lambda i: (i, 0))
    return pl.pallas_call(
        inputs_back_kernel,
        grid=(2,),
        in_specs=[
            *[pl.BlockSpec((item.shape[0], block), lambda i: (0, i)) for item in grads],
            *[whole(item.shape) for item in weights],
            part,
            whole(gain.shape),
            part,
        ],
        out_specs=[part, pl.BlockSpec((1, 1, width), lambda i: (i, 0, 0))],
        out_shape=[
            jax.ShapeDtypeStruct(x.shape, F32),
            jax.ShapeDtypeStruct((2, 1, width), F32),
        ],
        compiler_params=pltpu.CompilerParams(vmem_limit_bytes=48 * 2**20),
        cost_estimate=cost_of(6),
        name="inputs_back",
    )(*grads, *weights, x, gain, grad_hidden)


def expert_kernel(
    kinds, scalars, w_gate, *refs
):
    near_pieces, far_pieces, refs = refs[:2], refs[2:6], refs[6:]
    x_blocks, g_blocks, g_core = refs[: 2 * LOW], refs[2 * LOW : 3 * LOW], refs[3 * LOW]
    refs = refs[3 * LOW + 1 :]
    back_own, back_send, feed_own, feed_send, grads_out, *refs = refs
    x_all, g_all, x_t, g_t, weights, hidden, acc_feed, acc_back, scales, plain = refs
    slots, width = feed_own.shape
    block = slots // LOW
    half = width // 2
    step = pl.program_id(0)
    contract_last = (((1,), (1,)), ((), ()))
    units = weights.shape[2]

    def weight_column(x_ref):
        extra = x_ref[:, width:].astype(F32)
        lanes = lax.broadcasted_iota(jnp.int32, extra.shape, 1)
        named = (lanes == scalars[0]) | (lanes == scalars[0] + kinds)
        return jnp.sum(jnp.where(named, extra, 0.0), axis=1, keepdims=True)

    @pl.when(step == 0)
    def _():
        for i in range(2 * LOW):
            rows = pl.ds(i * block, block)
            scale = weight_column(x_blocks[i])
            scales[rows, :] = jnp.broadcast_to(scale, (block, 128))
            if i < LOW:
                plain[rows, :] = g_blocks[i][...]
            else:
                plain[rows, :] = g_core[pl.ds((i - LOW) * block, block), :]
            x_all[rows, :] = x_blocks[i][:, :width]
            g_all[rows, :] = (plain[rows, :].astype(F32) * scale).astype(BF16)
        x_t[...] = x_all[...].T
        g_t[...] = g_all[...].T
        acc_feed[...] = jnp.zeros_like(acc_feed)
        acc_back[...] = jnp.zeros_like(acc_back)

    for i in range(2):
        rows = pl.ds(i * half, half)
        weights[0, rows, :] = w_gate[:, 0, i].reshape(half, units)
    near = pl.multiple_of(scalars[1] * half, half)
    for k in range(2):
        weights[k + 1, pl.ds(near, half), :] = near_pieces[k][:, 0].reshape(half, units)
        place = (1 - scalars[1]) * half
        for piece in far_pieces[2 * k : 2 * k + 2]:
            rows = piece.shape[0] * half // LOW
            weights[k + 1, pl.ds(pl.multiple_of(place, half // LOW), rows), :] = piece[
                :, 0
            ].reshape(rows, units)
            place += rows

    for part in range(2):
        rows = pl.ds(part * slots, slots)
        x = x_all[rows, :]
        gate = jnp.dot(x, weights[0], preferred_element_type=F32)
        up = jnp.dot(x, weights[1], preferred_element_type=F32)
        grad_act = jnp.dot(g_all[rows, :], weights[2], preferred_element_type=F32)
        sig = jax.nn.sigmoid(gate)
        silu = gate * sig
        active = (silu * up).astype(BF16)
        grad_gate = (grad_act * up * (sig * (1.0 + gate * (1.0 - sig)))).astype(BF16)
        grad_up = (grad_act * silu).astype(BF16)
        hidden[0, rows, :] = grad_gate
        hidden[1, rows, :] = grad_up
        hidden[2, rows, :] = active
        acc_feed[rows, :] += lax.dot_general(
            active, weights[2], contract_last, preferred_element_type=F32
        )
        acc_back[rows, :] += lax.dot_general(
            grad_gate, weights[0], contract_last, preferred_element_type=F32
        ) + lax.dot_general(grad_up, weights[1], contract_last, preferred_element_type=F32)

    for k in range(3):
        left = (g_t if k == 2 else x_t)
        grad = jnp.dot(left[...], hidden[k], preferred_element_type=F32).astype(BF16)
        for i in range(2):
            part = grad[i * half : (i + 1) * half].reshape(LOW, -1, units)
            grads_out[i, :, 0, k] = part

    @pl.when(step == pl.num_programs(0) - 1)
    def _():
        for part in range(2):
            rows = pl.ds(part * slots, slots)
            feed = acc_feed[rows, :]
            inner = jnp.sum(feed * plain[rows, :].astype(F32), axis=1, keepdims=True)
            feed = feed * scales[rows, 0:1]
            lanes = lax.broadcasted_iota(jnp.int32, (slots, 128), 1)
            if part == 0:
                back_own[:, :width] = acc_back[rows, :]
                back_own[:, width:] = jnp.where(lanes == scalars[0], inner, 0.0)
                feed_own[...] = feed
            else:
                high = inner.astype(BF16).astype(F32)
                extra = jnp.where(lanes == scalars[0], high, 0.0)
                extra = jnp.where(lanes == scalars[0] + kinds, inner - high, extra)
                back_send[:, :width] = acc_back[rows, :].astype(BF16)
                back_send[:, width:] = extra.astype(BF16)
                feed_send[...] = feed.astype(BF16)


def expert_pass(kinds, scalars, x_blocks, g_blocks, w_gate, w_near, w_far):
    block, width = g_blocks[0].shape
    slots = LOW * block
    low, parities, _, shard_rows, shard_units = w_gate.shape
    units = 512
    steps = shard_units // units

    def whole(shape):
        return pl.BlockSpec(
            shape, lambda i, _: (0,) * len(shape), pipeline_mode=pl.Buffered(1)
        )

    grads_spec = pl.BlockSpec(
        (2, low, 1, 3, shard_rows, units), lambda i, _: (0, 0, i // steps, 0, 0, i % steps)
    )
    gate_spec = pl.BlockSpec(
        (low, 1, 2, shard_rows, units), lambda i, _: (0, i // steps, 0, 0, i % steps)
    )
    def up_spec(count):
        return pl.BlockSpec(
            (count, 1, shard_rows, units), lambda i, _: (0, i // steps, 0, i % steps)
        )

    wide = width + 128
    return pl.pallas_call(
        functools.partial(expert_kernel, kinds),
        grid_spec=pltpu.PrefetchScalarGridSpec(
            num_scalar_prefetch=1,
            grid=(parities * steps,),
            in_specs=[
                gate_spec,
                *[up_spec(item.shape[0]) for item in (*w_near, *w_far)],
                *[whole((block, wide)) for _ in range(2 * LOW)],
                *[whole(item.shape) for item in g_blocks],
            ],
            out_specs=[
                whole((slots, wide)),
                whole((slots, wide)),
                whole((slots, width)),
                whole((slots, width)),
                grads_spec,
            ],
            scratch_shapes=[
                pltpu.VMEM((2 * slots, width), BF16),
                pltpu.VMEM((2 * slots, width), BF16),
                pltpu.VMEM((width, 2 * slots), BF16),
                pltpu.VMEM((width, 2 * slots), BF16),
                pltpu.VMEM((3, width, units), BF16),
                pltpu.VMEM((3, 2 * slots, units), BF16),
                pltpu.VMEM((2 * slots, width), F32),
                pltpu.VMEM((2 * slots, width), F32),
                pltpu.VMEM((2 * slots, 128), F32),
                pltpu.VMEM((2 * slots, width), BF16),
            ],
        ),
        out_shape=[
            jax.ShapeDtypeStruct((slots, wide), F32),
            jax.ShapeDtypeStruct((slots, wide), BF16),
            jax.ShapeDtypeStruct((slots, width), F32),
            jax.ShapeDtypeStruct((slots, width), BF16),
            jax.ShapeDtypeStruct((2, low, parities, 3, shard_rows, shard_units), BF16),
        ],
        compiler_params=pltpu.CompilerParams(vmem_limit_bytes=58 * 2**20),
        cost_estimate=cost_of(35),
        name="expert_pass",
    )(scalars, w_gate, *w_near, *w_far, *x_blocks, *g_blocks)


def pick_kernel(ids_ref, *refs):
    pieces, outs = refs[:4], refs[4:]
    block = outs[0].shape[0]
    rows = pieces[0].shape[0]
    for i, out_ref in enumerate(outs):
        slot = i * block + lax.broadcasted_iota(jnp.int32, (block, rows), 0)
        total = 0.0
        for r in range(4):
            columns = pl.ds(r * rows, rows)
            held = (slot == ids_ref[0:1, columns]) | (slot == ids_ref[1:2, columns])
            held = jnp.where(held, 1.0, 0.0).astype(BF16)
            total += jnp.dot(held, pieces[r][...], preferred_element_type=F32)
        out_ref[...] = total.astype(BF16)


def pick(ids, pieces, slots):
    rows, width = pieces[0].shape
    block = slots // LOW

    def whole(shape):
        return pl.BlockSpec(shape, lambda i: (0, 0))

    return pl.pallas_call(
        pick_kernel,
        grid=(1,),
        in_specs=[whole((8, 4 * rows)), *[whole((rows, width)) for _ in range(4)]],
        out_specs=[whole((block, width)) for _ in range(LOW)],
        out_shape=[jax.ShapeDtypeStruct((block, width), BF16) for _ in range(LOW)],
        compiler_params=pltpu.CompilerParams(vmem_limit_bytes=32 * 2**20),
        cost_estimate=cost_of(5),
        name="pick",
    )(ids, *pieces)


def to_experts(blocks):
    return [blocks[0]] + [flip(blocks[b], "lo", LOW, b) for b in range(1, LOW)]


def to_heads(blocks):
    return [blocks[0]] + [
        lax.ppermute(blocks[r], ("y", "c"), [(i, i ^ r) for i in range(4)]) for r in range(1, 4)
    ]


def back_sum_kernel(kinds, own_ref, core_ref, *outs):
    width = own_ref.shape[1] - 128
    block = outs[0].shape[0]
    for i, out_ref in enumerate(outs):
        rows = pl.ds(i * block, block)
        out_ref[:, :width] = (
            own_ref[rows, :width] + core_ref[rows, :width].astype(F32)
        ).astype(BF16)
        extra = own_ref[rows, width:] + core_ref[rows, width:].astype(F32)
        lanes = lax.broadcasted_iota(jnp.int32, extra.shape, 1)
        high = jnp.where(lanes < kinds, extra, 0.0).astype(BF16).astype(F32)
        low = jnp.where(lanes < kinds, extra - high, 0.0)
        low = pltpu.roll(low, kinds, 1) + jnp.where(lanes >= kinds, extra, 0.0)
        out_ref[:, width:] = (high + low).astype(BF16)


def back_sum(kinds, own, core):
    slots, wide = own.shape
    block = slots // LOW

    def whole(shape):
        return pl.BlockSpec(shape, lambda i: (0, 0))

    return pl.pallas_call(
        functools.partial(back_sum_kernel, kinds),
        grid=(1,),
        in_specs=[whole(own.shape), whole(core.shape)],
        out_specs=[whole((block, wide)) for _ in range(LOW)],
        out_shape=[jax.ShapeDtypeStruct((block, wide), BF16) for _ in range(LOW)],
        compiler_params=pltpu.CompilerParams(vmem_limit_bytes=32 * 2**20),
        cost_estimate=cost_of(3),
        name="back_sum",
    )(own, core)


def feed_sum_kernel(own_ref, core_ref, *outs):
    block = outs[0].shape[0]
    for i, out_ref in enumerate(outs):
        rows = pl.ds(i * block, block)
        out_ref[...] = (own_ref[rows, :] + core_ref[rows, :].astype(F32)).astype(BF16)


def feed_sum(own, core):
    slots, width = own.shape
    block = slots // LOW

    def whole(shape):
        return pl.BlockSpec(shape, lambda i: (0, 0))

    return pl.pallas_call(
        feed_sum_kernel,
        grid=(1,),
        in_specs=[whole(own.shape), whole(core.shape)],
        out_specs=[whole((block, width)) for _ in range(LOW)],
        out_shape=[jax.ShapeDtypeStruct((block, width), BF16) for _ in range(LOW)],
        compiler_params=pltpu.CompilerParams(vmem_limit_bytes=32 * 2**20),
        cost_estimate=cost_of(3),
        name="feed_sum",
    )(own, core)


def spread_kernel(ids_ref, *refs):
    blocks, (near_ref, send_ref, slots_ref) = refs[:LOW], refs[LOW:]
    rows = near_ref.shape[1]
    slots = slots_ref.shape[0]
    block = slots // LOW

    @pl.when(pl.program_id(0) == 0)
    def _():
        for i in range(LOW):
            slots_ref[pl.ds(i * block, block), :] = blocks[i][...]

    for k, out_ref in enumerate((near_ref, send_ref)):
        slot = lax.broadcasted_iota(jnp.int32, (rows, slots), 1)
        ids = ids_ref[pl.ds(k * rows, rows), :]
        held = (slot == ids[:, 0:1]) | (slot == ids[:, 1:2])
        held = jnp.where(held, 1.0, 0.0).astype(BF16)
        total = jnp.dot(held, slots_ref[...], preferred_element_type=F32)
        out_ref[0] = total.astype(out_ref.dtype)


def spread(ids, values, rows):
    block, width = values[0].shape
    return pl.pallas_call(
        spread_kernel,
        grid=(2,),
        in_specs=[
            pl.BlockSpec((2 * rows, 8), lambda i: (i, 0)),
            *[pl.BlockSpec((block, width), lambda i: (0, 0)) for _ in range(LOW)],
        ],
        out_specs=[
            pl.BlockSpec((1, rows, width), lambda i: (i, 0, 0)),
            pl.BlockSpec((1, rows, width), lambda i: (i, 0, 0)),
        ],
        out_shape=[
            jax.ShapeDtypeStruct((2, rows, width), F32),
            jax.ShapeDtypeStruct((2, rows, width), BF16),
        ],
        scratch_shapes=[pltpu.VMEM((LOW * block, width), BF16)],
        compiler_params=pltpu.CompilerParams(vmem_limit_bytes=32 * 2**20),
        cost_estimate=cost_of(30),
        name="spread",
    )(ids, *values)


def slots_kernel(experts, capacity, scalars, routes_col, order_col, routes_row, order_row,
                 row_ref, col_ref, places_ref):
    group = routes_row.shape[1]
    rows = group // 4
    share = capacity // 2
    span = 2 * group
    bound = scalars[BOUNDS + 2]

    def target_of(routes, axis):
        place = lax.broadcasted_iota(jnp.int32, routes.shape, axis)
        return jnp.where((routes < experts) & (place < bound), routes, experts)

    target = target_of(routes_row[...], 1)
    code = target * span + order_row[...]
    block = 256

    def count(i, carry):
        first = pl.multiple_of(i * block, block)
        routes = routes_col[pl.ds(first, block), :]
        place = first + lax.broadcasted_iota(jnp.int32, routes.shape, 0)
        held = jnp.where((routes < experts) & (place < bound), routes, experts)
        others = held * span + order_col[pl.ds(first, block), :]
        result = []
        for k in range(2):
            total = carry[k]
            for j in range(2):
                smaller = jnp.where(others[:, j : j + 1] < code[k : k + 1, :], 1.0, 0.0)
                total = total + jnp.sum(smaller, axis=0, keepdims=True)
            result.append(total)
        return tuple(result)

    zero = jnp.zeros((1, group), F32)
    counts = lax.fori_loop(0, group // block, count, (zero, zero))
    for k in range(2):
        mine_target = target[k : k + 1, :]
        base = jnp.zeros((1, group), F32)
        for e in range(1, experts):
            earlier = jnp.sum(jnp.where(target < e, 1.0, 0.0))
            base = jnp.where(mine_target == e, earlier, base)
        place = (counts[k] - base).astype(jnp.int32)
        first = scalars[3] * share
        held = (
            (mine_target < experts)
            & (place >= first)
            & (place < first + share)
            & (place < capacity)
            & (jnp.bitwise_and(mine_target, 1) == scalars[2])
        )
        block = jnp.bitwise_xor(lax.shift_right_logical(mine_target, 1), scalars[LOW_PLACE])
        slot = block * share + place - first
        places_ref[k : k + 1, :] = jnp.where(held, slot, -1)
    for r in range(4):
        start = pl.multiple_of((scalars[1] ^ r) * rows, rows)
        piece = places_ref[:, pl.ds(start, rows)]
        row_ref[:, pl.ds(r * rows, rows)] = piece
        col_ref[pl.ds(r * rows, rows), :] = piece.T


def slots_of(scalars, routes, drop_order, experts, capacity):
    group = routes.shape[0]
    whole = pl.BlockSpec(memory_space=pltpu.VMEM)
    return pl.pallas_call(
        functools.partial(slots_kernel, experts, capacity),
        in_specs=[pl.BlockSpec(memory_space=pltpu.SMEM)] + [whole] * 4,
        out_specs=[whole] * 2,
        out_shape=[
            jax.ShapeDtypeStruct((8, group), jnp.int32),
            jax.ShapeDtypeStruct((group, 8), jnp.int32),
        ],
        scratch_shapes=[pltpu.VMEM((8, group), jnp.int32)],
        compiler_params=pltpu.CompilerParams(vmem_limit_bytes=32 * 2**20),
        cost_estimate=cost_of(8),
        name="slots",
    )(scalars, routes, drop_order, routes.T, drop_order.T)


def middle_kernel(kinds, scalars, mixed, p0, p1, p2, p3, x_ref, gain_ref, router_w, prior_ref,
                  prior_w, hidden_ref, sent_ref, router_ref, weight):
    hidden = x_ref[...]
    rows = p0.shape[2]
    for r, shards in enumerate((p0, p1, p2, p3)):
        for k in range(SHARDS):
            place = pl.multiple_of((scalars[0] ^ k) * rows, rows)
            weight[r, pl.ds(place, rows), :] = shards[k % LOW, k // LOW]
        hidden += lax.dot_general(
            mixed[scalars[1] ^ r].T, weight[r], (((1,), (1,)), ((), ())),
            preferred_element_type=F32,
        )
    hidden_ref[...] = hidden
    scale = lax.rsqrt(jnp.mean(hidden * hidden, axis=1, keepdims=True) + EPSILON)
    rounded = (hidden * scale * gain_ref[...]).astype(BF16)
    width = hidden.shape[1]
    sent_ref[:, :width] = rounded
    router_high, router_low = halves(router_w[...])
    logits = (
        jnp.dot(rounded, router_high, preferred_element_type=F32)
        + jnp.dot(rounded, router_low, preferred_element_type=F32)
        + split_dot(prior_ref[...], prior_w[...])
    )
    lanes = lax.broadcasted_iota(jnp.int32, logits.shape, 1)
    logits = jnp.where(lanes < 2 * kinds, logits, NEGATIVE)
    weights = jnp.exp(logits - jnp.max(logits, axis=1, keepdims=True))
    total = jnp.sum(jnp.where(lanes < kinds, weights, 0.0), axis=1, keepdims=True)
    router = weights / total
    router_ref[...] = router
    high = router.astype(BF16).astype(F32)
    sent_ref[:, width:] = jnp.where(lanes < kinds, high, router - high).astype(BF16)


def middle(kinds, scalars, mixed, weights, x, gain, router_w, prior, prior_w):
    rows, width = x.shape
    lanes = router_w.shape[1]

    def whole(shape):
        return pl.BlockSpec(shape, lambda i, _: (0,) * len(shape))

    return pl.pallas_call(
        functools.partial(middle_kernel, kinds),
        grid_spec=pltpu.PrefetchScalarGridSpec(
            num_scalar_prefetch=1,
            grid=(1,),
            in_specs=[
                whole(mixed.shape),
                *[whole(item.shape) for item in weights],
                whole(x.shape),
                whole(gain.shape),
                whole(router_w.shape),
                pl.BlockSpec((rows, kinds), lambda i, scalars: (scalars[1], 0)),
                whole(prior_w.shape),
            ],
            out_specs=[whole((rows, width)), whole((rows, width + lanes)), whole((rows, lanes))],
            scratch_shapes=[pltpu.VMEM((4, width, mixed.shape[1]), BF16)],
        ),
        out_shape=[
            jax.ShapeDtypeStruct((rows, width), F32),
            jax.ShapeDtypeStruct((rows, width + lanes), BF16),
            jax.ShapeDtypeStruct((rows, lanes), F32),
        ],
        compiler_params=pltpu.CompilerParams(vmem_limit_bytes=48 * 2**20),
        cost_estimate=cost_of(6),
        name="middle",
    )(scalars, mixed, *weights, x, gain, router_w, prior, prior_w)


def halves(value):
    high = value.astype(BF16)
    return high, (value - high.astype(F32)).astype(BF16)


def split_dot(left, right):
    (left_high, left_low), (right_high, right_low) = halves(left), halves(right)
    return (
        jnp.dot(left_high, right_high, preferred_element_type=F32)
        + jnp.dot(left_low, right_high, preferred_element_type=F32)
        + jnp.dot(left_high, right_low, preferred_element_type=F32)
    )


def turned_dot(left, right):
    high, low = halves(left.T)
    return jnp.dot(high, right, preferred_element_type=F32) + jnp.dot(
        low, right, preferred_element_type=F32
    )


def router_back_kernel(kinds, experts, scalars, near_ref, got_ref, far_ref, hidden_ref, router_ref,
                       routes_ref, cotangent_ref, prior_ref, gain_ref, small_ref, small_t_ref,
                       vector_ref, prior_w_ref,
                       grad_hidden_ref, grad_low_ref, partial_ref, grad_prior_ref, sums_ref):
    step = pl.program_id(0)
    rows, width = hidden_ref.shape
    place = scalars[1] * rows * pl.num_programs(0) + step * rows
    valid = place + lax.broadcasted_iota(jnp.int32, (rows, 1), 0) < scalars[BOUNDS + 2]
    valid = jnp.where(valid, 1.0, 0.0)
    back = near_ref[0] + got_ref[0].astype(F32) + far_ref[...].astype(F32)
    hidden = hidden_ref[...]
    grad_out = cotangent_ref[...] * valid
    scale = lax.rsqrt(jnp.mean(hidden * hidden, axis=1, keepdims=True) + EPSILON)
    unit = hidden * scale
    normed = unit * gain_ref[...]
    router = router_ref[...]
    lanes = lax.broadcasted_iota(jnp.int32, router.shape, 1)
    routes = routes_ref[...]

    def column(array, k):
        return jnp.sum(jnp.where(lanes == k, array, 0.0), axis=1, keepdims=True)

    def named(kind):
        return jnp.where((routes[:, 0:1] == kind) | (routes[:, 1:2] == kind), 1.0, 0.0)

    copy, first, second = (named(experts + k) for k in (1, 2, 3))
    weight_copy = column(router, experts + 1) * copy
    weight_first = column(router, experts + 2) * first
    weight_second = column(router, experts + 3) * second
    mixlog = split_dot(normed, small_ref[...])

    def softmax_two(k):
        one, two = column(mixlog, k), column(mixlog, k + 1)
        highest = jnp.maximum(one, two)
        one, two = jnp.exp(one - highest), jnp.exp(two - highest)
        return one / (one + two), two / (one + two)

    mix_one, mix_two = softmax_two(kinds), softmax_two(kinds + 2)
    vector_one, vector_two = vector_ref[0:1, :], vector_ref[1:2, :]
    along = jnp.sum(normed * grad_out, axis=1, keepdims=True)
    along_one = jnp.sum(vector_one * grad_out, axis=1, keepdims=True)
    along_two = jnp.sum(vector_two * grad_out, axis=1, keepdims=True)

    extra = back[:, width:]
    pairs = jnp.where(lanes < kinds, extra, 0.0) + jnp.where(
        lanes < kinds, pltpu.roll(extra, extra.shape[1] - kinds, 1), 0.0
    )
    grad_router = pairs + jnp.where(lanes == experts + 1, copy * along, 0.0)
    grad_router += jnp.where(
        lanes == experts + 2, first * (mix_one[0] * along + mix_one[1] * along_one), 0.0
    )
    grad_router += jnp.where(
        lanes == experts + 3, second * (mix_two[0] * along + mix_two[1] * along_two), 0.0
    )
    held = jnp.where(lanes < kinds, router, 0.0)
    grad_small = held * (grad_router - jnp.sum(held * grad_router, axis=1, keepdims=True))
    grad_prior_ref[...] = split_dot(grad_small, prior_w_ref[...])[:, :kinds]
    grad_logits = grad_small

    def mixed_back(weight, mix, other, k):
        one, two = weight * along, weight * other
        inner = mix[0] * one + mix[1] * two
        return jnp.where(lanes == k, mix[0] * (one - inner), 0.0) + jnp.where(
            lanes == k + 1, mix[1] * (two - inner), 0.0
        )

    grad_mixlog = mixed_back(weight_first, mix_one, along_one, kinds) + mixed_back(
        weight_second, mix_two, along_two, kinds + 2
    )
    grad_small = grad_logits + grad_mixlog
    share = weight_copy + weight_first * mix_one[0] + weight_second * mix_two[0]
    grad_normed = (
        back[:, :width]
        + share * grad_out
        + split_dot(grad_small, small_t_ref[...])
    )
    through = grad_normed * gain_ref[...]
    inner = jnp.mean(through * hidden, axis=1, keepdims=True)
    grad_hidden = grad_out + scale * through - (scale * scale * scale * inner) * hidden
    grad_hidden_ref[...] = grad_hidden
    grad_low_ref[...] = grad_hidden.astype(BF16)
    vector_first, vector_second = weight_first * mix_one[1], weight_second * mix_two[1]
    partial_ref[...] = valid * (
        hidden + share * normed + vector_first * vector_one + vector_second * vector_two
    )

    @pl.when(step == 0)
    def _():
        sums_ref[...] = jnp.zeros_like(sums_ref)

    vectors = jnp.where(lanes == kinds + 5, vector_first, 0.0) + jnp.where(
        lanes == kinds + 6, vector_second, 0.0
    )
    low = normed.astype(BF16)
    total = turned_dot(grad_small, low) + turned_dot(vectors, grad_out.astype(BF16))
    sums_ref[: kinds + 8, :] += total[: kinds + 8, :]
    sums_ref[kinds + 4 : kinds + 5, :] += jnp.sum(grad_normed * unit, axis=0, keepdims=True)
    prior = split_dot(prior_ref[...].T, grad_logits)
    sums_ref[pl.ds(kinds + 8, kinds), : lanes.shape[1]] += prior


def router_back(kinds, experts, scalars, near, got, far, hidden, router, routes, cotangent, prior,
                gain, small, small_t, vector, prior_w):
    rows, width = hidden.shape
    block = rows // 2
    lanes = router.shape[1]

    def whole(shape):
        return pl.BlockSpec(shape, lambda i, _: (0,) * len(shape))

    def part(columns):
        return pl.BlockSpec((block, columns), lambda i, _: (i, 0))

    def mine(columns):
        return pl.BlockSpec((block, columns), lambda i, scalars: (scalars[1] * 2 + i, 0))

    return pl.pallas_call(
        functools.partial(router_back_kernel, kinds, experts),
        grid_spec=pltpu.PrefetchScalarGridSpec(
            num_scalar_prefetch=1,
            grid=(2,),
            in_specs=[
                pl.BlockSpec((1, block, width + lanes), lambda i, _: (0, i, 0)),
                pl.BlockSpec((1, block, width + lanes), lambda i, _: (0, i, 0)),
                part(width + lanes),
                part(width),
                part(lanes),
                mine(2),
                part(width),
                mine(kinds),
                whole(gain.shape),
                whole(small.shape),
                whole(small_t.shape),
                whole(vector.shape),
                whole(prior_w.shape),
            ],
            out_specs=[
                part(width),
                part(width),
                part(width),
                part(kinds),
                whole((32, width)),
            ],
        ),
        out_shape=[
            jax.ShapeDtypeStruct((rows, width), F32),
            jax.ShapeDtypeStruct((rows, width), BF16),
            jax.ShapeDtypeStruct((rows, width), F32),
            jax.ShapeDtypeStruct((rows, kinds), F32),
            jax.ShapeDtypeStruct((32, width), F32),
        ],
        compiler_params=pltpu.CompilerParams(vmem_limit_bytes=48 * 2**20),
        cost_estimate=cost_of(8),
        name="router_back",
    )(scalars, near, got, far, hidden, router, routes, cotangent, prior, gain, small, small_t,
      vector, prior_w)


def two_parts(value):
    high = lax.reduce_precision(value, 8, 7)
    return jnp.concatenate([high, value - high], axis=-1).astype(BF16)


def everywhere(value, axes, count):
    copies = jnp.broadcast_to(value[None], (count, *value.shape))
    return lax.all_to_all(copies, axes, 0, 0, tiled=True)


def flip(value, axis, size, bit):
    return lax.ppermute(value, axis, [(i, i ^ bit) for i in range(size)])


def by_halves(value):
    if value.shape[0] == 2:
        return value
    rows, units = value.shape[-2:]
    middle_axes = tuple(range(2, value.ndim - 2))
    turned = value.transpose(*middle_axes, 0, 1, value.ndim - 2, value.ndim - 1)
    turned = turned.reshape(*turned.shape[:-4], 2, LOW, value.shape[0] * rows // 2, units)
    axes = turned.ndim
    return turned.transpose(axes - 4, axes - 3, *range(axes - 4), axes - 2, axes - 1)


def scatter_high(value, many):
    if many != 2:
        rows, units = value.shape[-2:]
        middle_axes = tuple(range(2, value.ndim - 2))
        turned = value.transpose(*middle_axes, 0, 1, value.ndim - 2, value.ndim - 1)
        turned = turned.reshape(*turned.shape[:-4], many, LOW, 2 * rows // many, units)
        axes = turned.ndim
        value = turned.transpose(axes - 4, axes - 3, *range(axes - 4), axes - 2, axes - 1)
    return lax.psum_scatter(value, "hi", scatter_dimension=0)


def gather_rows(value, later, many):
    if many != 2:
        full = lax.all_gather(value, ("hi", "lo"), axis=0, tiled=True)
        full = full.reshape(2, LOW, -1, full.shape[1])
        return [full[:, i] for i in range(LOW)], later
    far, *later = lax.optimization_barrier((swap(value, "hi"), *later))
    both = jnp.stack([value, far])
    return [both] + [flip(both, "lo", LOW, bit) for bit in range(1, LOW)], tuple(later)


def scatter_rows(near, far, many):
    if many != 2:
        full = jnp.stack([near, far]).astype(F32).reshape(-1, near.shape[2])
        return lax.psum_scatter(full, ("hi", "lo"), scatter_dimension=0, tiled=True)
    both = near.astype(F32) + far.astype(F32)
    total = both[0]
    for bit in range(1, LOW):
        total = total + flip(both[bit].astype(BF16), "lo", LOW, bit).astype(F32)
    return total


def per_device(
    many,
    inputs,
    cotangent,
    lengths,
    routes,
    drop_order,
    prior_logits,
    attn_gain,
    w_query,
    w_key,
    w_value,
    w_out,
    moe_gain,
    w_router,
    w_prior,
    w_const,
    const_vector,
    w_gate,
    w_up,
    w_down,
):
    tok_rows, width = inputs.shape
    group = tok_rows * 4
    kinds = w_router.shape[1]
    experts, shard_rows, shard_units = w_gate.shape
    capacity = 3 * group // 16
    share = capacity // 2
    slots = LOW * share
    local_width = w_query.shape[1]
    heads = local_width // HEAD
    tp_axes = ("y", "c")
    all_axes = ("hi", "lo", "y", "c")
    count = many * LOW * 4
    wide = width + 128
    high = lax.axis_index("hi")
    parity = lax.axis_index("y")
    core = lax.axis_index("c")
    place_in_group = parity * 2 + core
    mine = high * LOW + lax.axis_index("lo") if many == 2 else jnp.zeros_like(high)
    boundary = jnp.cumsum(lengths[0])
    scalars = jnp.concatenate(
        [jnp.stack([mine, place_in_group, parity, core, lax.axis_index("lo")]), boundary[:-1]]
    ).astype(jnp.int32)
    gain_one, gain_two = attn_gain.reshape(1, width), moe_gain.reshape(1, width)

    valid_mine = place_in_group * tok_rows + jnp.arange(tok_rows)[:, None] < boundary[-2]
    valid_mine = valid_mine.astype(F32)

    normed_one = rms_norm(inputs, attn_gain).astype(BF16)
    normed_other = swap(normed_one, "y")
    attn_shard = jnp.concatenate([w_query, w_key, w_value, w_out.T], axis=1)
    up_part = lax.all_to_all(w_up, ("lo", "y"), 0, 0, tiled=True)
    up_part = up_part.reshape(LOW, 2, shard_rows, shard_units)
    down_shard = w_down.transpose(0, 2, 1)
    attn_shards, (w_gate,) = gather_rows(attn_shard, (w_gate,), many)
    gate_far = swap(w_gate, "hi") if many == 2 else w_gate
    router_lanes = jnp.pad(
        jnp.concatenate([w_router, w_router], axis=1), ((0, 0), (0, 128 - 2 * kinds))
    )
    prior_lanes = jnp.pad(
        jnp.concatenate([w_prior, w_prior], axis=1), ((0, 0), (0, 128 - 2 * kinds))
    )
    const_flat = w_const.transpose(1, 0, 2).reshape(width, 4)
    small = jnp.pad(
        jnp.concatenate([w_router, const_flat], axis=1), ((0, 0), (0, 128 - kinds - 4))
    )
    small_t = small.T
    prior_back = jnp.pad(w_prior.T, ((0, 128 - kinds), (0, 128 - kinds)))
    (
        attn_shards[0], scalars, router_lanes, prior_lanes, small, small_t, prior_back, prior_logits
    ) = lax.optimization_barrier(
        (attn_shards[0], scalars, router_lanes, prior_lanes, small, small_t, prior_back, prior_logits)
    )
    ids_rows, ids_cols = slots_of(scalars, routes, drop_order, experts, capacity)
    grad_out_low = (cotangent * valid_mine).astype(BF16)
    (
        normed_other, attn_shards, ids_rows, down_shard, grad_out_low, up_part, gate_far
    ) = lax.optimization_barrier(
        (normed_other, attn_shards, ids_rows, down_shard, grad_out_low, up_part, gate_far)
    )
    grad_out_other = swap(grad_out_low, "y")
    down_part = lax.all_to_all(down_shard, ("lo", "y"), 0, 0, tiled=True)
    down_part = down_part.reshape(LOW, 2, shard_rows, shard_units)
    if many == 2:
        up_far = [swap(up_part[:2], "hi"), swap(up_part[2:], "hi")]
    else:
        up_all = by_halves(lax.all_gather(up_part, "hi"))
        up_part, up_far = up_all[0], [up_all[1, :2], up_all[1, 2:]]
    out_mine = jnp.stack([item[:, :, 3 * local_width :] for item in attn_shards])
    out_other = swap(out_mine, "y")
    normed_pieces = [normed_one, swap(normed_one, "c"), normed_other, swap(normed_other, "c")]
    mixed, lse, qkv, qkv_full = attend(normed_pieces, attn_shards, scalars, heads)
    mixed, out_other, out_mine, up_far[0], down_part, grad_out_other = lax.optimization_barrier(
        (mixed, out_other, out_mine, up_far[0], down_part, grad_out_other)
    )
    if many == 2:
        high_place = high
        down_far = [swap(down_part[:1], "hi"), swap(down_part[1:], "hi")]
        gate_both = jnp.where(
            high == 0, jnp.stack([w_gate, gate_far], axis=1), jnp.stack([gate_far, w_gate], axis=1)
        )
    else:
        high_place = jnp.zeros_like(high)
        down_all = by_halves(lax.all_gather(down_part, "hi"))
        down_part, down_far = down_all[0], [down_all[1, :1], down_all[1, 1:]]
        gate_both = lax.all_gather(w_gate, "hi", axis=1)
    out_pieces = [out_mine, swap(out_mine, "c"), out_other, swap(out_other, "c")]

    mixed_mine = lax.all_to_all(mixed, tp_axes, 0, 0, tiled=True)
    grad_out_pieces = [
        grad_out_low, swap(grad_out_low, "c"), grad_out_other, swap(grad_out_other, "c"),
    ]
    grad_out_slots = pick(ids_rows, grad_out_pieces, slots)
    mixed_mine, grad_out_slots, up_far[1], gate_both = lax.optimization_barrier(
        (mixed_mine, grad_out_slots, up_far[1], gate_both)
    )

    hidden, sent_two, router = middle(
        kinds, scalars, mixed_mine, out_pieces, inputs, gain_two, router_lanes, prior_logits, prior_lanes
    )

    gate_part = lax.all_to_all(gate_both, ("lo", "y"), 0, 0, tiled=True)
    gate_part = gate_part.reshape(LOW, 2, many, shard_rows, shard_units)
    if many != 2:
        gate_part = by_halves(gate_part.transpose(2, 0, 1, 3, 4)).transpose(1, 2, 0, 3, 4)
    other_two, grad_taken, gate_part, down_far[0] = lax.optimization_barrier(
        (swap(sent_two, "y"), to_experts(grad_out_slots), gate_part, down_far[0])
    )
    pieces_two = [sent_two, swap(sent_two, "c"), other_two, swap(other_two, "c")]

    grad_taken = [*grad_taken, swap(jnp.concatenate(grad_taken), "c")]
    sent_slots = pick(ids_rows, pieces_two, slots)
    sent_slots, qkv_full = lax.optimization_barrier((sent_slots, qkv_full))
    taken = to_experts(sent_slots)
    taken += [swap(item, "c") for item in taken]
    qkv_pieces = gather_pieces(qkv_full)
    taken, qkv_pieces, down_far[1] = lax.optimization_barrier((taken, qkv_pieces, down_far[1]))

    expert = lax.axis_index("lo") * 2 + parity
    back_own, back_send, feed_own, feed_send, grads_out = expert_pass(
        kinds, jnp.stack([expert, high_place]).astype(jnp.int32), taken, grad_taken,
        gate_part, [up_part, down_part], up_far + down_far,
    )

    weight_sum = scatter_high(grads_out, many)
    back_taken = to_experts(back_sum(kinds, back_own, swap(back_send, "c")))
    feed_core = swap(feed_send, "c")
    back_taken, feed_core = lax.optimization_barrier((back_taken, feed_core))

    back_near, back_sent = spread(ids_cols, back_taken, tok_rows)
    back_got, back_other = add_core(back_near, back_sent)
    back_other, feed_core = lax.optimization_barrier((back_other, feed_core))
    back_far, feed_blocks = lax.optimization_barrier(
        (swap(back_other, "y"), feed_sum(feed_own, feed_core))
    )

    grad_hidden, grad_low, partial, grad_prior, sums = router_back(
        kinds, experts, scalars, back_near, back_got, back_far, hidden, router, routes, cotangent,
        prior_logits, gain_two, small, small_t, const_vector, prior_back,
    )
    feed_taken = to_experts(feed_blocks)
    grad_mixed = to_heads(mixed_back(scalars, grad_low, out_pieces))
    grad_mixed, grad_low = lax.optimization_barrier((grad_mixed, grad_low))
    low_other = swap(grad_low, "y")
    share_sums = lax.all_to_all(sums.reshape(count, 32 * width // count), all_axes, 0, 0, tiled=True)
    grad_qkv = attend_back(scalars, qkv, lse, grad_mixed, heads).reshape(
        4, 3 * local_width, tok_rows
    )
    grad_qkv, feed_taken, weight_sum, low_other = lax.optimization_barrier(
        (grad_qkv, feed_taken, weight_sum, low_other)
    )
    grad_attn_pieces = [grad_low, swap(grad_low, "c"), low_other, swap(low_other, "c")]

    weight_own = lax.all_to_all(
        weight_sum.reshape(2 * LOW, 3, shard_rows, shard_units), ("lo", "y"), 0, 0, tiled=True
    )
    grad_qkv_mine = to_heads(grad_qkv)
    attn_near, attn_far = attn_grads(grad_qkv, mixed, normed_pieces, grad_attn_pieces, scalars)
    if many == 2:
        attn_far = swap(attn_far, "hi")
    feed_near, feed_sent = spread(ids_cols, feed_taken, tok_rows)
    feed_got, feed_other = add_core(feed_near, feed_sent)
    (
        grad_qkv_mine, share_sums, attn_near, attn_far, feed_near, feed_got, feed_other
    ) = lax.optimization_barrier(
        (grad_qkv_mine, share_sums, attn_near, attn_far, feed_near, feed_got, feed_other)
    )
    feed_far = swap(feed_other, "y")
    share_sums = jnp.sum(share_sums, axis=0)
    grad_inputs, gain_part = inputs_back(
        grad_qkv_mine, qkv_pieces, inputs, gain_one, grad_hidden
    )
    output = partial + valid_mine * (
        feed_near[0] + feed_got[0].astype(F32) + feed_far.astype(F32)
    )
    grad_attn_own = scatter_rows(attn_near, attn_far, many)
    last = jnp.concatenate([jnp.sum(gain_part, axis=0).reshape(-1), share_sums])
    last, weight_own = lax.optimization_barrier((last, weight_own))
    last = everywhere(last, all_axes, count)
    last, grad_attn_own = lax.optimization_barrier((last, grad_attn_own))
    grad_gain = jnp.sum(last[:, :width], axis=0)
    total = last[:, width:].reshape(32, width)
    return (
        output,
        grad_inputs,
        grad_prior,
        grad_gain,
        grad_attn_own[:, :local_width],
        grad_attn_own[:, local_width : 2 * local_width],
        grad_attn_own[:, 2 * local_width : 3 * local_width],
        grad_attn_own[:, 3 * local_width :].T,
        total[kinds + 4],
        total[:kinds].T,
        total[kinds + 8 : 2 * kinds + 8, :kinds],
        total[kinds : kinds + 4].reshape(2, 2, width).transpose(0, 2, 1),
        total[kinds + 5 : kinds + 7],
        weight_own[:, 0].astype(F32),
        weight_own[:, 1].astype(F32),
        weight_own[:, 2].transpose(0, 2, 1).astype(F32),
    )


def solution(mesh):
    many = mesh.shape["fsdp"] // LOW
    fine = Mesh(mesh.devices.reshape(many, LOW, 2, 2), ("hi", "lo", "y", "c"))
    fsdp, tp = ("hi", "lo"), ("y", "c")
    every = fsdp + tp
    return jax.shard_map(
        functools.partial(per_device, many),
        mesh=fine,
        in_specs=(
            P(every, None),
            P(every, None),
            P(fsdp, None),
            P(fsdp, None),
            P(fsdp, None),
            P(fsdp, None),
            P(),
            P(fsdp, tp),
            P(fsdp, tp),
            P(fsdp, tp),
            P(tp, fsdp),
            P(),
            P(),
            P(),
            P(),
            P(),
            P(None, fsdp, tp),
            P(None, fsdp, tp),
            P(None, tp, fsdp),
        ),
        out_specs=(
            P(every, None),
            P(every, None),
            P(every, None),
            P(),
            P(fsdp, tp),
            P(fsdp, tp),
            P(fsdp, tp),
            P(tp, fsdp),
            P(),
            P(),
            P(),
            P(),
            P(),
            P(None, fsdp, tp),
            P(None, fsdp, tp),
            P(None, tp, fsdp),
        ),
        check_vma=False,
    )
```
